32 devices in a mesh: gx: 4 (over y, core), gy: 8 (over z, x).
Axes of the slice: x: 2, y: 2, z: 4, core: 2. Of those that a mesh axis runs over, the one named last changes fastest.
Arguments:
- porosity: bfloat16 [512, 256, 1024], P(('gx', 'gy')), may hold values from 0.34960938 to 1
- grain_blocks: bfloat16 [8192, 16, 128], P(('gx', 'gy')), may hold values from 0 to 2
- owners: int32 [8192, 1], P(('gx', 'gy')), may hold values from 0 to 31; in each aligned block of 256 rows (0 to 255, 256 to 511, ...) at most 16 rows name the same one
- tiles: int32 [8192], P(('gx', 'gy')), may hold values from 0 to 2047
- live_counts: int32 [32], P(('gx', 'gy')), may hold values from 64 to 256, as said below
- ranks: int32 [32], replicated, may hold values from 0 to 31, as said below
- extinction: float32 [2], replicated, may hold values from 0.001 to 0.004
- color_weights: float32 [3, 3], replicated, may hold values from -3 to 3
Outputs:
- final_image: float32 [4, 262144], P(None, ('gx', 'gy'))
The draws below stay inside these ranges and needn't reach their ends.
Inputs may be any that keep to these rules, and one draw needn't show every extreme that they name: `owners`: among the 256 blocks of one device at most 16 name any one owner, a bound that some block reaches. Only the first live_counts[d] blocks of device d are used; some device uses all of them. ranks is a kd view order: bit b of ranks[d] equals bit b of d, flipped or not according to the bits of d above b only.
All inputs are finite; a program needn't handle non-finite values.
Results may differ from the reference program's by a relative error of at most 0.0015.
Values may be sent and summed in bfloat16 or wider, within the bound.
No kernel may reach another device: no remote copies, remote signals or barrier semaphores. Data moves between devices by JAX's collectives and lax.ppermute only.
A program may use at most 320 MiB of HBM per device.

```python
import math
import jax
import jax.numpy as jnp
import numpy as np
from jax import lax

DZ = 16
ROWS = 256
COLS = 1024
BCOL = 128
BLK_DEV = 256
CAP = 16
PIX = 262144
TILES = 2048
DEPTH = 512
GBLOCKS = 8192
DEVICES = 32


def draw_live_counts(key, part):
    base_counts = jax.random.randint(key, (DEVICES,), BLK_DEV // 4, BLK_DEV + 1)
    chosen = jax.random.randint(jax.random.fold_in(key, 7), (), 0, DEVICES)
    return jnp.where(jnp.arange(DEVICES) == chosen, BLK_DEV, base_counts).astype(jnp.int32)


def draw_ranks(key, part):
    bit_count = DEVICES.bit_length() - 1
    flips = jax.random.randint(jax.random.fold_in(key, 11), (bit_count, DEVICES), 0, 2).astype(jnp.int32)
    indices = jnp.arange(DEVICES, dtype=jnp.int32)
    result = jnp.zeros((DEVICES,), jnp.int32)
    for level in range(bit_count):
        upper = jnp.right_shift(indices, level + 1)
        own_bit = jnp.bitwise_and(jnp.right_shift(indices, level), 1)
        flipped = jnp.bitwise_xor(own_bit, flips[level][upper])
        result = result + jnp.left_shift(flipped, level)
    return result.astype(jnp.int32)


def set_ends(drawn, key, least, top_value):
    dims = drawn.shape
    place = [jax.random.randint(jax.random.fold_in(key, axis), (), 0, dims[axis]) for axis in range(len(dims))]
    drawn = drawn.at[tuple(place)].set(least)
    longest = dims.index(max(dims))
    place[longest] = (place[longest] + 1) % dims[longest]
    return drawn.at[tuple(place)].set(top_value)


def steps_of(key, extent, pieces, least, largest):
    loudness, own = 1.0, jax.random.fold_in(key, 6)
    for position, shards_of in pieces:
        steps = jnp.exp(jax.random.uniform(jax.random.fold_in(own, position), (shards_of,), jnp.float32, least / len(pieces), largest / len(pieces)))
        loudness = loudness * jnp.repeat(steps, extent[position] // shards_of).reshape([-1 if axis == position else 1 for axis in range(len(extent))])
    return loudness


def deal_out(own_key, own, number, rows, amount, top, bound, slope):
    sequence = jax.random.permutation(own_key, amount)
    crowded, ordinary = portions_of(amount, rows * top, bound, slope, True), portions_of(amount, rows * top, bound, slope, False)
    places = jnp.arange(amount)

    def named(lengths, offset_by):
        used = int((lengths > 0).sum())
        fixed = max(1, used // 4)
        moved = fixed + (places - fixed + offset_by * (used - fixed)) % max(1, amount - fixed)
        return jnp.zeros((amount,), jnp.int32).at[sequence[jnp.where(places < fixed, places, moved)]].set(jnp.asarray(lengths, jnp.int32))

    lengths = jnp.where(number % 4 == 0, named(crowded, number // 4), named(ordinary, number - number // 4 - 1))
    mixed = jax.random.permutation(jax.random.fold_in(own, 3), amount)
    source_of, sink = mixed[0:amount // 2 * 2:2], mixed[1:amount // 2 * 2:2]
    room = jnp.minimum(lengths[source_of] - 1, bound - lengths[sink]) // 2
    room = jnp.where((source_of == sequence[0]) | (sink == sequence[0]) | (lengths[sink] == 0), 0, jnp.maximum(room, 0))
    moved = jax.random.randint(jax.random.fold_in(own, 4), (amount // 2,), 0, 1 << 20) % (room + 1)
    lengths = lengths.at[source_of].add(-moved).at[sink].add(moved)
    items = jnp.searchsorted(jnp.cumsum(lengths), jnp.arange(rows * top), side="right").astype(jnp.int32)
    table = items.reshape(top, rows).T
    table = table[jax.random.permutation(jax.random.fold_in(own, 1), rows)]
    offset_by = jax.random.randint(jax.random.fold_in(own, 2), (rows, 1), 0, top)
    return jnp.take_along_axis(table, (jnp.arange(top)[None, :] + offset_by) % top, axis=1)


def portions_of(amount, total, limit, slope, full):
    portions = [(1 << 20) // math.isqrt(standing ** slope) + 1 for standing in range(1, amount + 1)]
    largest = limit if full else min(limit, max(-(-total // amount), total * portions[0] // sum(portions)))
    least = 1 if total - largest >= amount - 1 else 0
    holding, spare = [largest] + [least] * (amount - 1), total - largest - least * (amount - 1)
    while spare > 0:
        movable = [i for i in range(1, amount) if holding[i] < largest] or [i for i in range(1, amount) if holding[i] < limit]
        pool, left = sum([portions[i] for i in movable]), spare
        for i in movable:
            more = min(limit - holding[i], max(1, left * portions[i] // pool), spare)
            holding[i] = holding[i] + more
            spare = spare - more
    return np.array(holding)


def setup_inputs(seed: int = 0) -> dict:
    seeds = jax.random.split(jax.random.key(seed), 9)
    porosity = jnp.clip(0.34960938 + 0.6503906 * jax.random.uniform(seeds[0], (DEPTH, ROWS, COLS), jnp.float32) ** steps_of(seeds[0], (DEPTH, ROWS, COLS), ((0, 32),), -0.2, 0.2), 0.34960938, 1.0).astype(jnp.bfloat16)
    grain_blocks = jnp.clip(2.0 * jax.random.uniform(seeds[1], (GBLOCKS, DZ, BCOL), jnp.float32) ** steps_of(seeds[1], (GBLOCKS, DZ, BCOL), ((0, 32),), -0.2, 0.2), 0.0, 2.0).astype(jnp.bfloat16)
    owners_keys = jax.random.split(jax.random.fold_in(seeds[2], 1), GBLOCKS // BLK_DEV)
    owners_turns = jax.random.permutation(jax.random.fold_in(seeds[2], 3), GBLOCKS // BLK_DEV)
    owners = jax.vmap(lambda own, number: deal_out(jax.random.fold_in(seeds[2], 2), own, number, BLK_DEV, DEVICES, 1, CAP, 2))(owners_keys, owners_turns).reshape((GBLOCKS, 1))
    tiles = set_ends(jax.random.randint(seeds[3], (GBLOCKS,), 0, TILES), jax.random.fold_in(seeds[3], 1), 0, TILES - 1).astype(jnp.int32)
    live_counts = draw_live_counts(jax.random.fold_in(seeds[8], 71), 0)
    ranks = draw_ranks(jax.random.fold_in(seeds[8], 71), 0)
    extinction = jnp.clip(jnp.exp(jax.random.uniform(seeds[6], (2,), jnp.float32, math.log(0.001), math.log(0.004))), 0.001, 0.004)
    color_weights = jnp.clip(jax.random.uniform(seeds[7], (3, 3), jnp.float32, -3.0, 3.0), -3.0, 3.0)
    return {"porosity": porosity, "grain_blocks": grain_blocks, "owners": owners, "tiles": tiles, "live_counts": live_counts, "ranks": ranks, "extinction": extinction, "color_weights": color_weights}


def march_slab(porosity_slab, grain_field, extinction, color_weights):
    porous = porosity_slab.astype(jnp.float32)
    extinct = extinction[0] * (1.0 - porous) + extinction[1] * grain_field
    optical = jnp.cumsum(extinct, axis=0)
    before = optical - extinct
    weight = jnp.exp(-before) * (1.0 - jnp.exp(-extinct))
    channels = []
    for channel in range(3):
        colour = jax.nn.sigmoid(color_weights[channel, 0] * porous + color_weights[channel, 1] * grain_field + color_weights[channel, 2])
        channels.append(jnp.sum(weight * colour, axis=0))
    channels.append(1.0 - jnp.exp(-optical[-1]))
    stacked = jnp.stack(channels, axis=0)
    return stacked.reshape(4, stacked.shape[1] * stacked.shape[2])


def reference(porosity, grain_blocks, owners, tiles, live_counts, ranks, extinction, color_weights):
    block_ids = jnp.arange(GBLOCKS, dtype=jnp.int32)
    live_rows = (block_ids % BLK_DEV) < live_counts[block_ids // BLK_DEV]
    flat_target = owners[:, 0] * TILES + tiles
    grain_values = jnp.where(live_rows[:, None, None], grain_blocks.astype(jnp.float32), 0.0)
    grain_tiles = jnp.zeros((DEVICES * TILES, DZ, BCOL), jnp.float32).at[flat_target].add(grain_values)

    def one_slab(slab_index):
        porosity_slab = lax.dynamic_slice_in_dim(porosity, slab_index * DZ, DZ, 0)
        slab_tiles = lax.dynamic_slice_in_dim(grain_tiles, slab_index * TILES, TILES, 0)
        grain_field = jnp.transpose(slab_tiles, (1, 0, 2)).reshape(DZ, ROWS, COLS)
        return march_slab(porosity_slab, grain_field, extinction, color_weights)

    partial_value = lax.map(one_slab, jnp.arange(DEVICES, dtype=jnp.int32))
    inverse = jnp.zeros((DEVICES,), jnp.int32).at[ranks].set(jnp.arange(DEVICES, dtype=jnp.int32))
    ordered = partial_value[inverse]

    def blend(accumulated, farther):
        return accumulated + (1.0 - accumulated[3:4]) * farther, None

    final_image, unused = lax.scan(blend, jnp.zeros((4, PIX), jnp.float32), ordered)
    return final_image
```

```python
import functools

import jax
import jax.numpy as jnp
from jax import lax
from jax.experimental import pallas as pl
from jax.experimental.pallas import tpu as pltpu
from jax.sharding import PartitionSpec as P

LOG2E = 1.4426950408889634
VMEM_LIMIT = 56 * 1024 * 1024


def exchanged(block, axis, distance):
    route = [(low, low ^ distance) for low in range(lax.axis_size(axis))]
    return lax.ppermute(block, axis, route)


def over(nearer, farther, near_alpha):
    return nearer + (1.0 - near_alpha) * farther


def pack_kernel(
    owner_ref, tile_ref, live_ref, block_ref, out_ref, table, table_vec, table_sem, *, slots
):
    owners_all = out_ref.shape[0]

    def clear(owner, carry):
        table[owner, slots] = 0
        return carry

    lax.fori_loop(0, owners_all, clear, 0)

    def place(index, carry):
        owner = owner_ref[index]
        slot = table[owner, slots]
        table[owner, slots] = slot + 1
        table[owner, slot] = tile_ref[index]
        out_ref[owner, slot] = block_ref[index]
        return carry

    lax.fori_loop(0, live_ref[0], place, 0)
    copy = pltpu.make_async_copy(table, table_vec, table_sem)
    copy.start()
    copy.wait()
    first = lax.broadcasted_iota(jnp.int32, (16, 128), 0) == 0
    for owner in range(owners_all):
        row = jnp.broadcast_to(table_vec[owner : owner + 1, :], (16, 128))
        coded = jnp.where(first, row >> 6, row & 63)
        out_ref[owner, slots] = coded.astype(jnp.float32).astype(jnp.bfloat16)


def pack_blocks(grain_blocks, owner_dev, tiles, live_counts, device_count, slots):
    return pl.pallas_call(
        functools.partial(pack_kernel, slots=slots),
        out_shape=jax.ShapeDtypeStruct(
            (device_count, slots + 1) + grain_blocks.shape[1:], grain_blocks.dtype
        ),
        grid_spec=pltpu.PrefetchScalarGridSpec(
            num_scalar_prefetch=3,
            grid=(1,),
            in_specs=[pl.BlockSpec(grain_blocks.shape, lambda i, *s: (0, 0, 0))],
            out_specs=pl.BlockSpec(
                (device_count, slots + 1) + grain_blocks.shape[1:], lambda i, *s: (0, 0, 0, 0)
            ),
            scratch_shapes=[
                pltpu.SMEM((device_count, 128), jnp.int32),
                pltpu.VMEM((device_count, 128), jnp.int32),
                pltpu.SemaphoreType.DMA(()),
            ],
        ),
        compiler_params=pltpu.CompilerParams(vmem_limit_bytes=VMEM_LIMIT),
        name="pack_blocks",
    )(owner_dev, tiles, live_counts, grain_blocks)


def march_kernel(
    dev_ref,
    ext_ref,
    col_ref,
    got_ref,
    por_ref,
    keep_ref,
    send_ref,
    field,
    ids_vec,
    ids,
    ids_sem,
    *,
    slots,
    flip,
    width_y,
    chunk_rows,
):
    depth, block_rows, cols = por_ref.shape
    col_blocks = cols // 128
    device = dev_ref[0]
    chunk = (device // width_y) ^ flip
    step = pl.program_id(0)
    sources = got_ref.shape[0]

    @pl.when(step == 0)
    def _():
        for source in range(sources):
            coded = got_ref[source, slots].astype(jnp.float32)
            ids_vec[source : source + 1, :] = (coded[0:1, :] * 64.0 + coded[1:2, :]).astype(
                jnp.int32
            )
        copy = pltpu.make_async_copy(ids_vec, ids, ids_sem)
        copy.start()

        def wipe(col, carry):
            field[col] = jnp.zeros(field.shape[1:], jnp.float32)
            return carry

        lax.fori_loop(0, col_blocks, wipe, 0)
        copy.wait()

        def from_source(source, carry):
            def add_block(slot, carry):
                tile = ids[source, slot]
                row = tile // col_blocks

                @pl.when(row // chunk_rows == chunk)
                def _():
                    col = tile % col_blocks
                    where = pl.ds(row % chunk_rows, depth, stride=chunk_rows)
                    field[col, where, :] = field[col, where, :] + got_ref[source, slot].astype(
                        jnp.float32
                    )

                return carry

            return lax.fori_loop(0, ids[source, slots], add_block, carry)

        lax.fori_loop(0, sources, from_source, 0)

    first_half = device % 2 == 0
    base = -LOG2E * ext_ref[0]
    slope = LOG2E * ext_ref[0]
    grain_slope = -LOG2E * ext_ref[1]
    half_rows = block_rows // 2

    def one_column(col, carry):
        lanes = pl.ds(pl.multiple_of(col * 128, 128), 128)
        clear = jnp.ones((block_rows, 128), jnp.float32)
        sums = [jnp.zeros((block_rows, 128), jnp.float32) for _ in range(3)]
        for z in range(depth):
            porous = por_ref[z, :, lanes].astype(jnp.float32)
            start = pl.multiple_of(z * chunk_rows + step * block_rows, block_rows)
            grain = field[col, pl.ds(start, block_rows), :]
            passed = clear * jnp.exp2((base + slope * porous) + grain_slope * grain)
            weight = clear - passed
            clear = passed
            for c in range(3):
                half_logit = (
                    (0.5 * col_ref[c, 0]) * porous
                    + (0.5 * col_ref[c, 1]) * grain
                    + 0.5 * col_ref[c, 2]
                )
                sums[c] = sums[c] + weight * jnp.tanh(half_logit)
        alpha = 1.0 - clear
        parts = [0.5 * (alpha + total) for total in sums] + [alpha]
        kept = [jnp.where(first_half, part[:half_rows], part[half_rows:]) for part in parts]
        sent = [jnp.where(first_half, part[half_rows:], part[:half_rows]) for part in parts]
        for c in range(4):
            keep_ref[0, c * half_rows : (c + 1) * half_rows, lanes] = kept[c]
        for c in (0, 2):
            send_ref[0, c * half_rows : (c + 2) * half_rows, lanes] = jnp.concatenate(
                [sent[c], sent[c + 1]], axis=0
            ).astype(jnp.bfloat16)
        return carry

    lax.fori_loop(0, col_blocks, one_column, 0)


def march_chunk(got, porosity, dev, extinction, color_weights, slots, flip, width_x, width_y):
    depth, rows, cols = porosity.shape
    chunk_rows = rows // width_x
    block_rows = 16
    steps = chunk_rows // block_rows
    half_rows = block_rows // 2

    def rows_of(step, dev_ref):
        return (0, ((dev_ref[0] // width_y) ^ flip) * steps + step, 0)

    return pl.pallas_call(
        functools.partial(
            march_kernel, slots=slots, flip=flip, width_y=width_y, chunk_rows=chunk_rows
        ),
        out_shape=[
            jax.ShapeDtypeStruct((steps, 4 * half_rows, cols), jnp.float32),
            jax.ShapeDtypeStruct((steps, 4 * half_rows, cols), jnp.bfloat16),
        ],
        grid_spec=pltpu.PrefetchScalarGridSpec(
            num_scalar_prefetch=1,
            grid=(steps,),
            in_specs=[
                pl.BlockSpec(memory_space=pltpu.SMEM),
                pl.BlockSpec(memory_space=pltpu.SMEM),
                pl.BlockSpec(
                    got.shape, lambda step, d: (0, 0, 0, 0), pipeline_mode=pl.Buffered(1)
                ),
                pl.BlockSpec((depth, block_rows, cols), rows_of),
            ],
            out_specs=[
                pl.BlockSpec((1, 4 * half_rows, cols), lambda step, d: (step, 0, 0)),
                pl.BlockSpec((1, 4 * half_rows, cols), lambda step, d: (step, 0, 0)),
            ],
            scratch_shapes=[
                pltpu.VMEM((cols // 128, depth * chunk_rows, 128), jnp.float32),
                pltpu.VMEM((got.shape[0], 128), jnp.int32),
                pltpu.SMEM((got.shape[0], 128), jnp.int32),
                pltpu.SemaphoreType.DMA(()),
            ],
        ),
        compiler_params=pltpu.CompilerParams(vmem_limit_bytes=VMEM_LIMIT),
        cost_estimate=pl.CostEstimate(
            flops=30 * depth * chunk_rows * cols,
            bytes_accessed=2 * depth * chunk_rows * cols + 2 * got.size + 12 * chunk_rows * cols,
            transcendentals=4 * depth * chunk_rows * cols,
        ),
        name="march_chunk",
    )(dev, extinction, color_weights, got, porosity)


def ordered(mine, theirs, mine_near):
    nearer = [jnp.where(mine_near, a, b) for a, b in zip(mine, theirs)]
    farther = [jnp.where(mine_near, b, a) for a, b in zip(mine, theirs)]
    open_part = 1.0 - nearer[3]
    return [n + open_part * f for n, f in zip(nearer, farther)]


def channels_of(block):
    block = block.astype(jnp.float32)
    rows = block.shape[0] // 4
    return [block[c * rows : (c + 1) * rows] for c in range(4)]


def pair_kernel(dev_ref, rank_ref, keep_ref, got_ref, own_ref, *send_refs, width_y):
    device = dev_ref[0]
    mine_near = rank_ref[device] % 2 == 0
    place = (device % width_y) // 2

    def one_column(col, carry):
        lanes = pl.ds(pl.multiple_of(col * 128, 128), 128)
        for distance in range(keep_ref.shape[0]):
            group = place ^ distance
            merged = ordered(
                channels_of(keep_ref[group, :, lanes]),
                channels_of(got_ref[group, :, lanes]),
                mine_near,
            )
            if distance == 0:
                own_ref[:, lanes] = jnp.concatenate(merged, axis=0)
            else:
                send_refs[distance - 1][:, lanes] = jnp.concatenate(merged, axis=0).astype(
                    jnp.bfloat16
                )
        return carry

    lax.fori_loop(0, keep_ref.shape[2] // 128, one_column, 0)


def pair_chunk(keep, got, dev, ranks, width_y):
    groups, rows, cols = keep.shape
    smem = pl.BlockSpec(memory_space=pltpu.SMEM)
    vmem = pl.BlockSpec(memory_space=pltpu.VMEM)
    return pl.pallas_call(
        functools.partial(pair_kernel, width_y=width_y),
        out_shape=[jax.ShapeDtypeStruct((rows, cols), jnp.float32)]
        + [jax.ShapeDtypeStruct((rows, cols), jnp.bfloat16)] * (groups - 1),
        in_specs=[smem, smem, vmem, vmem],
        out_specs=[vmem] * groups,
        cost_estimate=pl.CostEstimate(
            flops=4 * groups * rows * cols, bytes_accessed=9 * groups * rows * cols, transcendentals=0
        ),
        name="pair_chunk",
    )(dev, ranks, keep, got)


def four_way(device, rank_ref, parts, stride, bit):
    low = (rank_ref[device] >> bit) % 2 == 0
    far_low = (rank_ref[device ^ (2 * stride)] >> bit) % 2 == 0
    high = (rank_ref[device] >> (bit + 1)) % 2 == 0
    return ordered(
        ordered(parts[0], parts[1], low), ordered(parts[2], parts[3], far_low), high
    )


def quad_kernel(dev_ref, rank_ref, p0, p1, p2, p3, out_ref):
    device = dev_ref[0]

    def one_column(col, carry):
        lanes = pl.ds(pl.multiple_of(col * 128, 128), 128)
        parts = [channels_of(ref[:, lanes]) for ref in (p0, p1, p2, p3)]
        merged = four_way(device, rank_ref, parts, 2, 1)
        out_ref[:, lanes] = jnp.concatenate(merged, axis=0)
        return carry

    lax.fori_loop(0, p0.shape[1] // 128, one_column, 0)


def quad_chunk(own, others, dev, ranks):
    rows, cols = own.shape
    smem = pl.BlockSpec(memory_space=pltpu.SMEM)
    vmem = pl.BlockSpec(memory_space=pltpu.VMEM)
    return pl.pallas_call(
        quad_kernel,
        out_shape=jax.ShapeDtypeStruct((rows, cols), jnp.float32),
        in_specs=[smem, smem] + [vmem] * 4,
        out_specs=vmem,
        cost_estimate=pl.CostEstimate(
            flops=12 * rows * cols, bytes_accessed=14 * rows * cols, transcendentals=0
        ),
        name="quad_chunk",
    )(dev, ranks, own, *others)


def last_kernel(dev_ref, rank_ref, p0, p1, p2, p3, q1, q2, q3, out_ref, *, width_y):
    device = dev_ref[0]
    cols = p0.shape[1]
    for col in range(cols // 128):
        lanes = slice(col * 128, (col + 1) * 128)
        parts = [channels_of(ref[:, lanes]) for ref in (p0, p1, p2, p3)]
        mine = four_way(device, rank_ref, parts, 2, 1)
        parts = [mine] + [channels_of(ref[:, lanes]) for ref in (q1, q2, q3)]
        bit = width_y.bit_length() - 1
        merged = four_way(device, rank_ref, parts, width_y, bit)
        for c in range(4):
            for row in range(merged[c].shape[0]):
                start = row * cols + col * 128
                out_ref[c : c + 1, start : start + 128] = merged[c][row : row + 1]


def last_chunk(own, others, ready, dev, ranks, width_y):
    rows, cols = own.shape
    smem = pl.BlockSpec(memory_space=pltpu.SMEM)
    vmem = pl.BlockSpec(memory_space=pltpu.VMEM)
    return pl.pallas_call(
        functools.partial(last_kernel, width_y=width_y),
        out_shape=jax.ShapeDtypeStruct((4, rows // 4 * cols), jnp.float32),
        in_specs=[smem, smem] + [vmem] * 7,
        out_specs=vmem,
        name="last_chunk",
    )(dev, ranks, own, *others, *ready)


def shards(porosity, grain_blocks, owners, tiles, live_counts, ranks, extinction, color_weights):
    width_x = lax.axis_size("gx")
    width_y = lax.axis_size("gy")
    device_count = width_x * width_y
    block_count = grain_blocks.shape[0]
    slots = max(2, 2 * block_count // device_count)
    dev = lax.axis_index(("gx", "gy")).astype(jnp.int32).reshape(1)
    packed = pack_blocks(grain_blocks, owners[:, 0], tiles, live_counts, device_count, slots)
    got = lax.all_to_all(packed, ("gx", "gy"), split_axis=0, concat_axis=0, tiled=True)
    ready = [None] * (width_x - 1)
    for flip in range(width_x - 1, -1, -1):
        keep, send = march_chunk(
            got, porosity, dev, extinction, color_weights, slots, flip, width_x, width_y
        )
        arrived = exchanged(send, "gy", 1)
        own, *outgoing = pair_chunk(keep, arrived, dev, ranks, width_y)
        others = [exchanged(out, "gy", 2 * (k + 1)) for k, out in enumerate(outgoing)]
        if flip:
            ready[flip - 1] = exchanged(quad_chunk(own, others, dev, ranks), "gx", flip)
    return last_chunk(own, others, ready, dev, ranks, width_y)


def march_flat(porous_flat, grain_flat, extinction, color_weights):
    porous = porous_flat.astype(jnp.float32)
    extinct = extinction[0] * (1.0 - porous) + extinction[1] * grain_flat
    optical = jnp.cumsum(extinct, axis=0)
    before = optical - extinct
    weight = jnp.exp(-before) * (1.0 - jnp.exp(-extinct))
    channels = []
    for channel in range(3):
        colour = jax.nn.sigmoid(
            color_weights[channel, 0] * porous
            + color_weights[channel, 1] * grain_flat
            + color_weights[channel, 2]
        )
        channels.append(jnp.sum(weight * colour, axis=0))
    channels.append(1.0 - jnp.exp(-optical[-1]))
    return jnp.stack(channels, axis=0)


def composite(nearer, farther):
    return nearer + (1.0 - nearer[3:4]) * farther


def shards_any(
    porosity, grain_blocks, owners, tiles, live_counts, ranks, extinction, color_weights
):
    width_x = lax.axis_size("gx")
    width_y = lax.axis_size("gy")
    device_count = width_x * width_y
    depth_cells, image_rows, image_cols = porosity.shape
    block_count, _, block_cols = grain_blocks.shape
    slots = max(2, 2 * block_count // device_count)
    tile_count = image_rows * image_cols // block_cols
    pixel_count = image_rows * image_cols
    block_len = pixel_count // device_count
    packed = pack_blocks(grain_blocks, owners[:, 0], tiles, live_counts, device_count, slots)
    got = lax.all_to_all(packed, ("gx", "gy"), split_axis=0, concat_axis=0, tiled=True)
    coded = got[:, slots, :2, : slots + 1].astype(jnp.int32)
    table = coded[:, 0] * 64 + coded[:, 1]
    used = jnp.arange(slots, dtype=jnp.int32)[None, :] < table[:, slots:]
    got_tile = jnp.where(used, table[:, :slots], tile_count)
    got_data = jnp.where(used[:, :, None, None], got[:, :slots], jnp.bfloat16(0))
    grain_tiles = (
        jnp.zeros((tile_count, depth_cells, block_cols), jnp.float32)
        .at[got_tile.reshape(-1)]
        .add(
            got_data.reshape(device_count * slots, depth_cells, block_cols).astype(jnp.float32),
            mode="drop",
        )
    )
    grain_flat = jnp.transpose(grain_tiles, (1, 0, 2)).reshape(depth_cells, pixel_count)
    porous_flat = porosity.reshape(depth_cells, pixel_count)
    partial_value = march_flat(porous_flat, grain_flat, extinction, color_weights)
    my_rank = ranks[lax.axis_index(("gx", "gy"))]
    bits_y = width_y.bit_length() - 1
    bits_x = width_x.bit_length() - 1
    current = partial_value.reshape(4, width_x, width_y, block_len)
    for axis, dim, bits, first in (("gy", 2, bits_y, 0), ("gx", 1, bits_x, bits_y)):
        for section_bit in range(bits):
            shape = current.shape
            paired = current.reshape(
                shape[:dim] + (shape[dim] // 2, 2) + shape[dim + 1 :]
            )
            own_bit = lax.axis_index(axis) >> section_bit & 1
            kept_half = lax.dynamic_index_in_dim(paired, own_bit, dim + 1, keepdims=False)
            sent_half = lax.dynamic_index_in_dim(paired, 1 - own_bit, dim + 1, keepdims=False)
            partner = exchanged(sent_half, axis, 1 << section_bit)
            nearer_side = my_rank >> first + section_bit & 1 == 0
            current = composite(
                jnp.where(nearer_side, kept_half, partner),
                jnp.where(nearer_side, partner, kept_half),
            )
        if dim == 2:
            current = current.reshape(4, width_x, 1, block_len).reshape(4, width_x, block_len)
    return current.reshape(4, block_len)


def solution(mesh):
    in_specs = (
        P(("gx", "gy"), None, None),
        P(("gx", "gy"), None, None),
        P(("gx", "gy"), None),
        P(("gx", "gy")),
        P(("gx", "gy")),
        P(),
        P(),
        P(),
    )
    out_specs = P(None, ("gx", "gy"))

    def run(porosity, *rest):
        rows = porosity.shape[1] // (mesh.shape["gx"] * mesh.shape["gy"])
        fits = mesh.shape["gx"] == 4 and mesh.shape["gy"] == 8 and rows == 8
        return jax.shard_map(
            shards if fits else shards_any,
            mesh=mesh,
            in_specs=in_specs,
            out_specs=out_specs,
            check_vma=False,
        )(porosity, *rest)

    return run
```

```python
import functools

import jax
import jax.numpy as jnp
from jax import lax
from jax.experimental import pallas as pl
from jax.experimental.pallas import tpu as pltpu
from jax.sharding import PartitionSpec as P

LOG2E = 1.4426950408889634
VMEM_LIMIT = 32 * 1024 * 1024
SMALL_LIMIT = 8 * 1024 * 1024
CHUNKS = ((3,), (2, 1), (0,))


def exchanged(block, axis, distance):
    route = [(low, low ^ distance) for low in range(lax.axis_size(axis))]
    return lax.ppermute(block, axis, route)


def over(nearer, farther, near_alpha):
    return nearer + (1.0 - near_alpha) * farther


def pack_kernel(
    owner_ref, tile_ref, live_ref, block_ref, out_ref, table, table_vec, table_sem, *, slots
):
    owners_all = out_ref.shape[0]

    def clear(owner, carry):
        table[owner, slots] = 0
        return carry

    lax.fori_loop(0, owners_all, clear, 0)

    def place(index, carry):
        owner = owner_ref[index]
        slot = table[owner, slots]
        table[owner, slots] = slot + 1
        table[owner, slot] = tile_ref[index]
        out_ref[owner, slot] = block_ref[index]
        return carry

    lax.fori_loop(0, live_ref[0], place, 0)
    copy = pltpu.make_async_copy(table, table_vec, table_sem)
    copy.start()
    copy.wait()
    first = lax.broadcasted_iota(jnp.int32, (16, 128), 0) == 0
    for owner in range(owners_all):
        row = jnp.broadcast_to(table_vec[owner : owner + 1, :], (16, 128))
        coded = jnp.where(first, row >> 6, row & 63)
        out_ref[owner, slots] = coded.astype(jnp.float32).astype(jnp.bfloat16)


def pack_blocks(grain_blocks, owner_dev, tiles, live_counts, device_count, slots):
    return pl.pallas_call(
        functools.partial(pack_kernel, slots=slots),
        out_shape=jax.ShapeDtypeStruct(
            (device_count, slots + 1) + grain_blocks.shape[1:], grain_blocks.dtype
        ),
        grid_spec=pltpu.PrefetchScalarGridSpec(
            num_scalar_prefetch=3,
            grid=(1,),
            in_specs=[pl.BlockSpec(grain_blocks.shape, lambda i, *s: (0, 0, 0))],
            out_specs=pl.BlockSpec(
                (device_count, slots + 1) + grain_blocks.shape[1:], lambda i, *s: (0, 0, 0, 0)
            ),
            scratch_shapes=[
                pltpu.SMEM((device_count, 128), jnp.int32),
                pltpu.VMEM((device_count, 128), jnp.int32),
                pltpu.SemaphoreType.DMA(()),
            ],
        ),
        compiler_params=pltpu.CompilerParams(vmem_limit_bytes=VMEM_LIMIT),
        name="pack_blocks",
    )(owner_dev, tiles, live_counts, grain_blocks)


def empty_kernel(ext_ref, col_ref, token_ref, por_ref, out_ref):
    depth, block_rows, cols = por_ref.shape
    half_rows = block_rows // 2
    base = -LOG2E * ext_ref[0]
    slope = LOG2E * ext_ref[0]

    def one_column(col, carry):
        lanes = pl.ds(pl.multiple_of(col * 128, 128), 128)
        clear = jnp.ones((block_rows, 128), jnp.float32)
        sums = [jnp.zeros((block_rows, 128), jnp.float32) for _ in range(3)]
        for z in range(depth):
            porous = por_ref[z, :, lanes].astype(jnp.float32)
            passed = clear * jnp.exp2(base + slope * porous)
            weight = clear - passed
            clear = passed
            for c in range(3):
                half_logit = (0.5 * col_ref[c, 0]) * porous + 0.5 * col_ref[c, 2]
                sums[c] = sums[c] + weight * jnp.tanh(half_logit)
        alpha = 1.0 - clear
        parts = [0.5 * (alpha + total) for total in sums] + [alpha]
        for c in range(4):
            for half in range(2):
                out_ref[half, col, c * half_rows : (c + 1) * half_rows, :] = parts[c][
                    half * half_rows : (half + 1) * half_rows
                ]
        return carry

    lax.fori_loop(0, cols // 128, one_column, 0)


def march_empty(porosity, token, extinction, color_weights):
    depth, rows, cols = porosity.shape
    smem = pl.BlockSpec(memory_space=pltpu.SMEM)
    return pl.pallas_call(
        empty_kernel,
        out_shape=jax.ShapeDtypeStruct((rows // 8, cols // 128, 32, 128), jnp.float32),
        grid=(rows // 16,),
        in_specs=[smem, smem, smem, pl.BlockSpec((depth, 16, cols), lambda step: (0, step, 0))],
        out_specs=pl.BlockSpec((2, cols // 128, 32, 128), lambda step: (step, 0, 0, 0)),
        cost_estimate=pl.CostEstimate(
            flops=20 * depth * rows * cols,
            bytes_accessed=2 * depth * rows * cols + 16 * rows * cols,
            transcendentals=4 * depth * rows * cols,
        ),
        name="march_empty",
    )(extinction, color_weights, token, porosity)


UNROLL = 4


def grain_kernel(
    dev_ref,
    ext_ref,
    col_ref,
    got_ref,
    por_hbm,
    part_hbm,
    keep_ref,
    send_ref,
    por,
    part,
    ids_vec,
    ids,
    entry,
    earlier,
    deeper,
    last,
    heads,
    sems,
    *,
    slots,
    flips,
    width_x,
    width_y,
):
    device = dev_ref[0]
    own_x = device % 2
    gx = device // width_y
    pieces = len(flips)
    piece_tiles = por_hbm.shape[0] // width_x
    piece_groups = part_hbm.shape[0] // width_x
    col_blocks = part_hbm.shape[1]
    sources = got_ref.shape[0] // (slots + 1)
    copies = []
    for piece, flip in enumerate(flips):
        chunk = gx ^ flip
        copies.append(
            pltpu.make_async_copy(
                por_hbm.at[pl.ds(chunk * piece_tiles, piece_tiles)],
                por.at[pl.ds(piece * piece_tiles, piece_tiles)],
                sems.at[2 * piece],
            )
        )
        copies.append(
            pltpu.make_async_copy(
                part_hbm.at[pl.ds(chunk * piece_groups, piece_groups)],
                part.at[pl.ds(piece * piece_groups, piece_groups)],
                sems.at[2 * piece + 1],
            )
        )
    for copy in copies:
        copy.start()

    for source in range(sources):
        coded = got_ref[source * (slots + 1) + slots].astype(jnp.float32)
        ids_vec[source : source + 1, :] = (coded[0:1, :] * 64.0 + coded[1:2, :]).astype(jnp.int32)
    copy = pltpu.make_async_copy(ids_vec, ids, sems.at[2 * pieces])
    copy.start()
    copy.wait()

    def from_source(source, count):
        def look(slot, count):
            tile = ids[source, slot]
            flip = (tile // piece_tiles) ^ gx
            local = jnp.int32(pieces * piece_tiles)
            for piece, wanted in enumerate(flips):
                local = jnp.where(flip == wanted, piece * piece_tiles + tile % piece_tiles, local)
            last[local] = -1
            entry[count] = (source * (slots + 1) + slot) + (local << 16)
            return count + jnp.where(local < pieces * piece_tiles, 1, 0)

        return lax.fori_loop(0, ids[source, slots], look, count)

    count = lax.fori_loop(0, sources, from_source, jnp.int32(0))

    def chain(index, carry):
        local = entry[index] >> 16
        before = last[local]
        earlier[index] = before
        deeper[index] = jnp.where(before >= 0, deeper[jnp.maximum(before, 0)] + 1, 0)
        last[local] = index
        return carry

    lax.fori_loop(0, count, chain, 0)

    def pick(index, found):
        heads[found] = index
        return found + jnp.where(last[entry[index] >> 16] == index, 1, 0)

    found = lax.fori_loop(0, count, pick, jnp.int32(0))

    @pl.when(found > 0)
    def _():
        for extra in range(UNROLL - 1):
            heads[found + extra] = heads[found - 1]

    base = -LOG2E * ext_ref[0]
    slope = LOG2E * ext_ref[0]
    grain_slope = -LOG2E * ext_ref[1]
    depth_of = lax.broadcasted_iota(jnp.int32, (8, 128), 0)

    def running(value):
        for shift in (1, 2, 4):
            value = value + jnp.where(depth_of >= shift, pltpu.roll(value, shift, 0), 0.0)
        return value

    for copy in copies:
        copy.wait()

    def some_tiles(batch, carry):
        work = []
        for place in range(UNROLL):
            index = heads[batch * UNROLL + place]
            code = entry[index]

            def add_earlier(_, state):
                at, total = state
                at = earlier[at]
                more = got_ref[entry[at] & 65535].astype(jnp.float32)
                return at, total + more

            grain = got_ref[code & 65535].astype(jnp.float32)
            _, grain = lax.fori_loop(0, deeper[index], add_earlier, (index, grain))
            work.append((code >> 16, grain))
        for local, grain in work:
            porous = por[local].astype(jnp.float32)
            exponent = (base + slope * porous) + grain_slope * grain
            front = running(exponent[:8])
            back = running(exponent[8:]) + front[7:8]
            optical = jnp.concatenate([front, back], axis=0)
            weight = jnp.exp2(optical - exponent) - jnp.exp2(optical)
            alpha = 1.0 - jnp.exp2(back[7:8])
            results = []
            for c in range(3):
                half_logit = (
                    (0.5 * col_ref[c, 0]) * porous
                    + (0.5 * col_ref[c, 1]) * grain
                    + 0.5 * col_ref[c, 2]
                )
                shaded = weight * jnp.tanh(half_logit)
                total = jnp.sum(shaded[:8] + shaded[8:], axis=0, keepdims=True)
                results.append(0.5 * (alpha + total))
            results.append(alpha)
            row = local // col_blocks
            for c in range(4):
                part[row // 8, local % col_blocks, pl.ds(c * 8 + row % 8, 1), :] = results[c]
        return carry

    lax.fori_loop(0, (found + UNROLL - 1) // UNROLL, some_tiles, 0)

    pairs = pieces * piece_groups // 2

    def split(pair, carry):
        keep_ref[pair] = part[2 * pair + own_x]
        send_ref[pair] = part[2 * pair + 1 - own_x].astype(jnp.bfloat16)
        return carry

    lax.fori_loop(0, pairs, split, 0)


def march_grain(
    got, porous_tiles, part, dev, extinction, color_weights, slots, flips, width_x, width_y
):
    groups = part.shape[0]
    pieces = len(flips)
    smem = pl.BlockSpec(memory_space=pltpu.SMEM)
    vmem = pl.BlockSpec(memory_space=pltpu.VMEM)
    hbm = pl.BlockSpec(memory_space=pltpu.HBM)
    sources = got.shape[0] // (slots + 1)
    most = sources * slots + UNROLL
    piece_tiles = porous_tiles.shape[0] // width_x
    piece_groups = groups // width_x
    out = (pieces * piece_groups // 2,) + part.shape[1:]
    return pl.pallas_call(
        functools.partial(
            grain_kernel, slots=slots, flips=flips, width_x=width_x, width_y=width_y
        ),
        out_shape=[
            jax.ShapeDtypeStruct(out, jnp.float32),
            jax.ShapeDtypeStruct(out, jnp.bfloat16),
        ],
        in_specs=[smem, smem, smem, vmem, hbm, hbm],
        out_specs=[vmem, vmem],
        scratch_shapes=[
            pltpu.VMEM((pieces * piece_tiles,) + porous_tiles.shape[1:], jnp.bfloat16),
            pltpu.VMEM((pieces * piece_groups,) + part.shape[1:], jnp.float32),
            pltpu.VMEM((sources, 128), jnp.int32),
            pltpu.SMEM((sources, 128), jnp.int32),
            pltpu.SMEM((most,), jnp.int32),
            pltpu.SMEM((most,), jnp.int32),
            pltpu.SMEM((most,), jnp.int32),
            pltpu.SMEM((pieces * piece_tiles + 1,), jnp.int32),
            pltpu.SMEM((most,), jnp.int32),
            pltpu.SemaphoreType.DMA((2 * pieces + 1,)),
        ],
        compiler_params=pltpu.CompilerParams(vmem_limit_bytes=VMEM_LIMIT),
        cost_estimate=pl.CostEstimate(
            flops=4_000_000 * pieces, bytes_accessed=6_000_000 * pieces, transcendentals=0
        ),
        name="march_grain",
    )(dev, extinction, color_weights, got, porous_tiles, part)


def ordered(mine, theirs, mine_near):
    nearer = [jnp.where(mine_near, a, b) for a, b in zip(mine, theirs)]
    farther = [jnp.where(mine_near, b, a) for a, b in zip(mine, theirs)]
    open_part = 1.0 - nearer[3]
    return [n + open_part * f for n, f in zip(nearer, farther)]


def channels_of(block):
    block = block.astype(jnp.float32)
    rows = block.shape[0] // 4
    return [block[c * rows : (c + 1) * rows] for c in range(4)]


def pair_kernel(dev_ref, rank_ref, keep_ref, got_ref, own_ref, *send_refs, width_y):
    device = dev_ref[0]
    mine_near = rank_ref[device] % 2 == 0
    place = (device % width_y) // 2
    around = width_y // 2

    def one_column(col, carry):
        for piece in range(own_ref.shape[0]):
            for distance in range(around):
                group = piece * around + (place ^ distance)
                merged = ordered(
                    channels_of(keep_ref[group, col]),
                    channels_of(got_ref[group, col]),
                    mine_near,
                )
                merged = jnp.concatenate(merged, axis=0)
                if distance == 0:
                    own_ref[piece, col] = merged
                else:
                    send_refs[distance - 1][piece, col] = merged.astype(jnp.bfloat16)
        return carry

    lax.fori_loop(0, keep_ref.shape[1], one_column, 0)


def pair_chunk(keep, got, dev, ranks, width_y):
    around = width_y // 2
    shape = (keep.shape[0] // around,) + keep.shape[1:]
    smem = pl.BlockSpec(memory_space=pltpu.SMEM)
    vmem = pl.BlockSpec(memory_space=pltpu.VMEM)
    return pl.pallas_call(
        functools.partial(pair_kernel, width_y=width_y),
        out_shape=[jax.ShapeDtypeStruct(shape, jnp.float32)]
        + [jax.ShapeDtypeStruct(shape, jnp.bfloat16)] * (around - 1),
        in_specs=[smem, smem, vmem, vmem],
        out_specs=[vmem] * around,
        cost_estimate=pl.CostEstimate(
            flops=4 * keep.size, bytes_accessed=9 * keep.size, transcendentals=0
        ),
        compiler_params=pltpu.CompilerParams(vmem_limit_bytes=SMALL_LIMIT),
        name="pair_chunk",
    )(dev, ranks, keep, got)


def four_way(device, rank_ref, parts, stride, bit):
    low = (rank_ref[device] >> bit) % 2 == 0
    far_low = (rank_ref[device ^ (2 * stride)] >> bit) % 2 == 0
    high = (rank_ref[device] >> (bit + 1)) % 2 == 0
    return ordered(
        ordered(parts[0], parts[1], low), ordered(parts[2], parts[3], far_low), high
    )


def quad_kernel(dev_ref, rank_ref, p0, p1, p2, p3, *out_refs):
    device = dev_ref[0]

    def one_column(col, carry):
        for piece, out_ref in enumerate(out_refs):
            parts = [channels_of(ref[piece, col]) for ref in (p0, p1, p2, p3)]
            merged = four_way(device, rank_ref, parts, 2, 1)
            out_ref[col] = jnp.concatenate(merged, axis=0)
        return carry

    lax.fori_loop(0, p0.shape[1], one_column, 0)


def quad_chunk(own, others, dev, ranks):
    pieces = own.shape[0]
    smem = pl.BlockSpec(memory_space=pltpu.SMEM)
    vmem = pl.BlockSpec(memory_space=pltpu.VMEM)
    return pl.pallas_call(
        quad_kernel,
        out_shape=[jax.ShapeDtypeStruct(own.shape[1:], jnp.float32)] * pieces,
        in_specs=[smem, smem] + [vmem] * 4,
        out_specs=[vmem] * pieces,
        cost_estimate=pl.CostEstimate(
            flops=12 * own.size, bytes_accessed=14 * own.size, transcendentals=0
        ),
        compiler_params=pltpu.CompilerParams(vmem_limit_bytes=SMALL_LIMIT),
        name="quad_chunk",
    )(dev, ranks, own, *others)


def last_kernel(dev_ref, rank_ref, p0, p1, p2, p3, q1, q2, q3, out_ref, *, width_y):
    device = dev_ref[0]
    col_blocks = p0.shape[1]
    for col in range(col_blocks):
        parts = [channels_of(ref[0, col]) for ref in (p0, p1, p2, p3)]
        mine = four_way(device, rank_ref, parts, 2, 1)
        parts = [mine] + [channels_of(ref[col]) for ref in (q1, q2, q3)]
        bit = width_y.bit_length() - 1
        merged = four_way(device, rank_ref, parts, width_y, bit)
        for c in range(4):
            for row in range(merged[c].shape[0]):
                start = (row * col_blocks + col) * 128
                out_ref[c : c + 1, start : start + 128] = merged[c][row : row + 1]


def last_chunk(own, others, ready, dev, ranks, width_y):
    smem = pl.BlockSpec(memory_space=pltpu.SMEM)
    vmem = pl.BlockSpec(memory_space=pltpu.VMEM)
    return pl.pallas_call(
        functools.partial(last_kernel, width_y=width_y),
        out_shape=jax.ShapeDtypeStruct((4, own.size // 4), jnp.float32),
        in_specs=[smem, smem] + [vmem] * 7,
        out_specs=vmem,
        compiler_params=pltpu.CompilerParams(vmem_limit_bytes=SMALL_LIMIT),
        name="last_chunk",
    )(dev, ranks, own, *others, *ready)


def shards(porosity, grain_blocks, owners, tiles, live_counts, ranks, extinction, color_weights):
    width_x = lax.axis_size("gx")
    width_y = lax.axis_size("gy")
    device_count = width_x * width_y
    block_count = grain_blocks.shape[0]
    slots = max(2, 2 * block_count // device_count)
    dev = lax.axis_index(("gx", "gy")).astype(jnp.int32).reshape(1)
    packed = pack_blocks(grain_blocks, owners[:, 0], tiles, live_counts, device_count, slots)
    got = lax.all_to_all(packed, ("gx", "gy"), split_axis=0, concat_axis=0, tiled=True)
    got = got.reshape((-1,) + got.shape[2:])
    depth, rows, cols = porosity.shape
    porosity, _ = lax.optimization_barrier((porosity, packed))
    part = march_empty(porosity, dev, extinction, color_weights)
    porous_tiles = (
        porosity.reshape(depth, rows, cols // 128, 128)
        .transpose(1, 2, 0, 3)
        .reshape(-1, depth, 128)
    )
    ready = [None] * (width_x - 1)
    for flips in CHUNKS:
        keep, send = march_grain(
            got, porous_tiles, part, dev, extinction, color_weights, slots, flips, width_x, width_y
        )
        got, _ = lax.optimization_barrier((got, send))
        arrived = exchanged(send, "gy", 1)
        own, *outgoing = pair_chunk(keep, arrived, dev, ranks, width_y)
        others = [exchanged(out, "gy", 2 * (k + 1)) for k, out in enumerate(outgoing)]
        if flips != (0,):
            for flip, done in zip(flips, quad_chunk(own, others, dev, ranks)):
                ready[flip - 1] = exchanged(done, "gx", flip)
    return last_chunk(own, others, ready, dev, ranks, width_y)


def march_flat(porous_flat, grain_flat, extinction, color_weights):
    porous = porous_flat.astype(jnp.float32)
    extinct = extinction[0] * (1.0 - porous) + extinction[1] * grain_flat
    optical = jnp.cumsum(extinct, axis=0)
    before = optical - extinct
    weight = jnp.exp(-before) * (1.0 - jnp.exp(-extinct))
    channels = []
    for channel in range(3):
        colour = jax.nn.sigmoid(
            color_weights[channel, 0] * porous
            + color_weights[channel, 1] * grain_flat
            + color_weights[channel, 2]
        )
        channels.append(jnp.sum(weight * colour, axis=0))
    channels.append(1.0 - jnp.exp(-optical[-1]))
    return jnp.stack(channels, axis=0)


def composite(nearer, farther):
    return nearer + (1.0 - nearer[3:4]) * farther


def shards_any(
    porosity, grain_blocks, owners, tiles, live_counts, ranks, extinction, color_weights
):
    width_x = lax.axis_size("gx")
    width_y = lax.axis_size("gy")
    device_count = width_x * width_y
    depth_cells, image_rows, image_cols = porosity.shape
    block_count, _, block_cols = grain_blocks.shape
    slots = max(2, 2 * block_count // device_count)
    tile_count = image_rows * image_cols // block_cols
    pixel_count = image_rows * image_cols
    block_len = pixel_count // device_count
    packed = pack_blocks(grain_blocks, owners[:, 0], tiles, live_counts, device_count, slots)
    got = lax.all_to_all(packed, ("gx", "gy"), split_axis=0, concat_axis=0, tiled=True)
    coded = got[:, slots, :2, : slots + 1].astype(jnp.int32)
    table = coded[:, 0] * 64 + coded[:, 1]
    used = jnp.arange(slots, dtype=jnp.int32)[None, :] < table[:, slots:]
    got_tile = jnp.where(used, table[:, :slots], tile_count)
    got_data = jnp.where(used[:, :, None, None], got[:, :slots], jnp.bfloat16(0))
    grain_tiles = (
        jnp.zeros((tile_count, depth_cells, block_cols), jnp.float32)
        .at[got_tile.reshape(-1)]
        .add(
            got_data.reshape(device_count * slots, depth_cells, block_cols).astype(jnp.float32),
            mode="drop",
        )
    )
    grain_flat = jnp.transpose(grain_tiles, (1, 0, 2)).reshape(depth_cells, pixel_count)
    porous_flat = porosity.reshape(depth_cells, pixel_count)
    partial_value = march_flat(porous_flat, grain_flat, extinction, color_weights)
    my_rank = ranks[lax.axis_index(("gx", "gy"))]
    bits_y = width_y.bit_length() - 1
    bits_x = width_x.bit_length() - 1
    current = partial_value.reshape(4, width_x, width_y, block_len)
    for axis, dim, bits, first in (("gy", 2, bits_y, 0), ("gx", 1, bits_x, bits_y)):
        for section_bit in range(bits):
            shape = current.shape
            paired = current.reshape(
                shape[:dim] + (shape[dim] // 2, 2) + shape[dim + 1 :]
            )
            own_bit = lax.axis_index(axis) >> section_bit & 1
            kept_half = lax.dynamic_index_in_dim(paired, own_bit, dim + 1, keepdims=False)
            sent_half = lax.dynamic_index_in_dim(paired, 1 - own_bit, dim + 1, keepdims=False)
            partner = exchanged(sent_half, axis, 1 << section_bit)
            nearer_side = my_rank >> first + section_bit & 1 == 0
            current = composite(
                jnp.where(nearer_side, kept_half, partner),
                jnp.where(nearer_side, partner, kept_half),
            )
        if dim == 2:
            current = current.reshape(4, width_x, 1, block_len).reshape(4, width_x, block_len)
    return current.reshape(4, block_len)


def solution(mesh):
    in_specs = (
        P(("gx", "gy"), None, None),
        P(("gx", "gy"), None, None),
        P(("gx", "gy"), None),
        P(("gx", "gy")),
        P(("gx", "gy")),
        P(),
        P(),
        P(),
    )
    out_specs = P(None, ("gx", "gy"))

    def run(porosity, *rest):
        rows = porosity.shape[1] // (mesh.shape["gx"] * mesh.shape["gy"])
        fits = mesh.shape["gx"] == 4 and mesh.shape["gy"] == 8 and rows == 8
        return jax.shard_map(
            shards if fits else shards_any,
            mesh=mesh,
            in_specs=in_specs,
            out_specs=out_specs,
            check_vma=False,
        )(porosity, *rest)

    return run
```

```python
import functools

import jax
import jax.numpy as jnp
from jax import lax
from jax.experimental import pallas as pl
from jax.experimental.pallas import tpu as pltpu
from jax.sharding import PartitionSpec as P

LOG2E = 1.4426950408889634
PACK_LIMIT = 56 * 1024 * 1024
GRAIN_LIMIT = 16 * 1024 * 1024
SMALL_LIMIT = 8 * 1024 * 1024
UNROLL = 4
CHUNKS = ((3,), (2, 1), (0,))


def exchanged(block, axis, distance):
    route = [(low, low ^ distance) for low in range(lax.axis_size(axis))]
    return lax.ppermute(block, axis, route)


def bits_of(size):
    assert size & (size - 1) == 0
    return size.bit_length() - 1


def pack_kernel(
    owner_ref, tile_ref, live_ref, block_ref, out_ref, table_ref, table, table_sem, *, slots
):
    owners_all = out_ref.shape[0]

    def clear(owner, carry):
        table[owner, slots] = 0
        return carry

    lax.fori_loop(0, owners_all, clear, 0)

    def place(index, carry):
        owner = owner_ref[index]
        slot = table[owner, slots]
        table[owner, slots] = slot + 1
        table[owner, slot] = tile_ref[index]
        out_ref[owner, slot] = block_ref[index]
        return carry

    lax.fori_loop(0, live_ref[0], place, 0)
    copy = pltpu.make_async_copy(table, table_ref, table_sem)
    copy.start()
    copy.wait()


def pack_blocks(grain_blocks, owner_dev, tiles, live_counts, device_count, slots):
    packed = (device_count, slots) + grain_blocks.shape[1:]
    smem = pl.BlockSpec(memory_space=pltpu.SMEM)
    vmem = pl.BlockSpec(memory_space=pltpu.VMEM)
    return pl.pallas_call(
        functools.partial(pack_kernel, slots=slots),
        out_shape=[
            jax.ShapeDtypeStruct(packed, grain_blocks.dtype),
            jax.ShapeDtypeStruct((device_count, 128), jnp.int32),
        ],
        in_specs=[smem, smem, smem, vmem],
        out_specs=[vmem, vmem],
        scratch_shapes=[
            pltpu.SMEM((device_count, 128), jnp.int32),
            pltpu.SemaphoreType.DMA(()),
        ],
        compiler_params=pltpu.CompilerParams(vmem_limit_bytes=PACK_LIMIT),
        name="pack_blocks",
    )(owner_dev, tiles, live_counts, grain_blocks)


def exchange_table(table, width_x, width_y):
    device = lax.axis_index(("gx", "gy"))
    row = lax.broadcasted_iota(jnp.int32, table.shape, 0)
    for bit in range(bits_of(width_x * width_y)):
        bits_y = bits_of(width_y)
        axis, distance = ("gy", 1 << bit) if bit < bits_y else ("gx", 1 << bit - bits_y)
        other = exchanged(table, axis, distance)
        other = other.reshape(-1, 2, 1 << bit, other.shape[1])[:, ::-1].reshape(table.shape)
        table = jnp.where((row >> bit & 1) == (device >> bit & 1), table, other)
    return table


def plan_kernel(dev_ref, ids_ref, heads, earlier, deeper, last, *, slots, width_x, width_y):
    sources = ids_ref.shape[0]
    piece_tiles = last.shape[0] // width_x
    piece_bits = bits_of(piece_tiles)
    gx = dev_ref[0] >> bits_of(width_y)
    counter = heads.shape[1] - 1

    def of_source(body):
        def run(source, carry):
            def one(slot, carry):
                body(ids_ref[source, slot], source * slots + slot)
                return carry

            return lax.fori_loop(0, ids_ref[source, slots], one, carry)

        lax.fori_loop(0, sources, run, 0)

    def forget(tile, entry):
        last[tile] = -1

    def chain(tile, entry):
        before = last[tile]
        earlier[entry] = before
        deeper[entry] = jnp.where(before >= 0, deeper[jnp.maximum(before, 0)] + 1, 0)
        last[tile] = entry

    def pick(tile, entry):
        flip = (tile >> piece_bits) ^ gx
        found = heads[flip, counter]
        heads[flip, found] = entry + ((tile & (piece_tiles - 1)) << 16)
        heads[flip, counter] = found + jnp.where(last[tile] == entry, 1, 0)

    of_source(forget)
    deeper[0] = 0
    of_source(chain)
    for chunk in range(width_x):
        heads[chunk, counter] = 0
    of_source(pick)

    for chunk in range(width_x):
        found = heads[chunk, counter]

        @pl.when(found > 0)
        def _():
            for extra in range(UNROLL - 1):
                heads[chunk, found + extra] = heads[chunk, found - 1]


def plan_tiles(ids, dev, tile_count, slots, width_x, width_y):
    sources = ids.shape[0]
    smem = pl.BlockSpec(memory_space=pltpu.SMEM)
    most = -(-(sources * slots + UNROLL + 1) // 128) * 128
    return pl.pallas_call(
        functools.partial(plan_kernel, slots=slots, width_x=width_x, width_y=width_y),
        out_shape=[
            jax.ShapeDtypeStruct((width_x, most), jnp.int32),
            jax.ShapeDtypeStruct((sources * slots,), jnp.int32),
            jax.ShapeDtypeStruct((sources * slots,), jnp.int32),
        ],
        in_specs=[smem, smem],
        out_specs=[smem, smem, smem],
        scratch_shapes=[pltpu.SMEM((tile_count,), jnp.int32)],
        compiler_params=pltpu.CompilerParams(vmem_limit_bytes=SMALL_LIMIT),
        cost_estimate=pl.CostEstimate(flops=1_000_000, bytes_accessed=10_000_000, transcendentals=0),
        name="plan_tiles",
    )(dev, ids)


def empty_kernel(
    dev_ref, ext_ref, col_ref, por_hbm, part, por_tiles, por, turned, sems, *, flip, width_x, width_y
):
    depth, rows, cols = por_hbm.shape
    block_rows = por.shape[2]
    half_rows = block_rows // 2
    col_blocks = cols // 128
    steps = rows // width_x // block_rows
    first_row = ((dev_ref[0] >> bits_of(width_y)) ^ flip) * (rows // width_x)
    base = -LOG2E * ext_ref[0]
    slope = LOG2E * ext_ref[0]

    def fetch(step, slot):
        start = pl.multiple_of(first_row + step * block_rows, block_rows)
        return pltpu.make_async_copy(
            por_hbm.at[:, pl.ds(start, block_rows), :], por.at[slot], sems.at[slot]
        )

    fetch(0, 0).start()

    def one_step(step, carry):
        slot = lax.rem(step, 2)

        @pl.when(step + 1 < steps)
        def _():
            fetch(step + 1, 1 - slot).start()

        fetch(step, slot).wait()

        def one_column(col, carry):
            lanes = pl.ds(pl.multiple_of(col * 128, 128), 128)
            clear = jnp.ones((block_rows, 128), jnp.float32)
            sums = [jnp.zeros((block_rows, 128), jnp.float32) for _ in range(3)]
            for z in range(depth):
                porous = por[slot, z, :, lanes].astype(jnp.float32)
                turned[z * block_rows : (z + 1) * block_rows, :] = porous
                passed = clear * jnp.exp2(base + slope * porous)
                weight = clear - passed
                clear = passed
                for c in range(3):
                    half_logit = (0.5 * col_ref[c, 0]) * porous + 0.5 * col_ref[c, 2]
                    sums[c] = sums[c] + weight * jnp.tanh(half_logit)
            for row in range(block_rows):
                tile = (step * block_rows + row) * col_blocks + col
                por_tiles[tile] = turned[pl.ds(row, depth, stride=block_rows), :].astype(
                    jnp.bfloat16
                )
            alpha = 1.0 - clear
            parts = [0.5 * (alpha + total) for total in sums] + [alpha]
            for c in range(4):
                for half in range(2):
                    part[2 * step + half, col, c * half_rows : (c + 1) * half_rows, :] = parts[c][
                        half * half_rows : (half + 1) * half_rows
                    ]
            return carry

        lax.fori_loop(0, col_blocks, one_column, 0)
        return carry

    lax.fori_loop(0, steps, one_step, 0)


def march_empty(porosity, dev, extinction, color_weights, flip, width_x, width_y):
    depth, rows, cols = porosity.shape
    rows = rows // width_x
    block_rows = 16
    smem = pl.BlockSpec(memory_space=pltpu.SMEM)
    vmem = pl.BlockSpec(memory_space=pltpu.VMEM)
    return pl.pallas_call(
        functools.partial(empty_kernel, flip=flip, width_x=width_x, width_y=width_y),
        out_shape=[
            jax.ShapeDtypeStruct((rows // 8, cols // 128, 32, 128), jnp.float32),
            jax.ShapeDtypeStruct((rows * cols // 128, depth, 128), porosity.dtype),
        ],
        in_specs=[smem, smem, smem, pl.BlockSpec(memory_space=pl.ANY)],
        out_specs=[vmem, vmem],
        scratch_shapes=[
            pltpu.VMEM((2, depth, block_rows, cols), porosity.dtype),
            pltpu.VMEM((depth * block_rows, 128), jnp.float32),
            pltpu.SemaphoreType.DMA((2,)),
        ],
        compiler_params=pltpu.CompilerParams(vmem_limit_bytes=SMALL_LIMIT),
        cost_estimate=pl.CostEstimate(
            flops=20 * depth * rows * cols,
            bytes_accessed=4 * depth * rows * cols + 16 * rows * cols,
            transcendentals=4 * depth * rows * cols,
        ),
        name="march_empty",
    )(dev, extinction, color_weights, porosity)


def grain_kernel(dev_ref, ext_ref, col_ref, heads, earlier, deeper, got_ref, *refs, flips):
    pieces = len(flips)
    por_refs, parts, send_ref = refs[:pieces], refs[2 * pieces : 3 * pieces], refs[3 * pieces]
    own_x = dev_ref[0] & 1
    col_bits = bits_of(parts[0].shape[1])
    pairs = parts[0].shape[0] // 2
    counter = heads.shape[1] - 1
    base = -LOG2E * ext_ref[0]
    slope = LOG2E * ext_ref[0]
    grain_slope = -LOG2E * ext_ref[1]
    depth_of = lax.broadcasted_iota(jnp.int32, (8, 128), 0)

    def running(value):
        for shift in (1, 2, 4):
            value = value + jnp.where(depth_of >= shift, pltpu.roll(value, shift, 0), 0.0)
        return value

    for piece, flip in enumerate(flips):
        part, por_ref = parts[piece], por_refs[piece]

        def some_tiles(batch, carry):
            work = []
            for place in range(UNROLL):
                code = heads[flip, batch * UNROLL + place]
                entry = code & 65535

                def add_earlier(_, state):
                    at, total = state
                    at = earlier[at]
                    return at, total + got_ref[at].astype(jnp.float32)

                grain = got_ref[entry].astype(jnp.float32)
                _, grain = lax.fori_loop(0, deeper[entry], add_earlier, (entry, grain))
                work.append((code >> 16, grain))
            for tile, grain in work:
                porous = por_ref[tile].astype(jnp.float32)
                exponent = (base + slope * porous) + grain_slope * grain
                front = running(exponent[:8])
                back = running(exponent[8:]) + front[7:8]
                optical = jnp.concatenate([front, back], axis=0)
                weight = jnp.exp2(optical - exponent) - jnp.exp2(optical)
                alpha = 1.0 - jnp.exp2(back[7:8])
                results = []
                for c in range(3):
                    half_logit = (
                        (0.5 * col_ref[c, 0]) * porous
                        + (0.5 * col_ref[c, 1]) * grain
                        + 0.5 * col_ref[c, 2]
                    )
                    shaded = weight * jnp.tanh(half_logit)
                    total = jnp.sum(shaded[:8] + shaded[8:], axis=0, keepdims=True)
                    results.append(0.5 * (alpha + total))
                results.append(alpha)
                group, row = tile >> (3 + col_bits), (tile >> col_bits) & 7
                col = tile & ((1 << col_bits) - 1)
                for c in range(4):
                    part[group, col, pl.ds(c * 8 + row, 1), :] = results[c]
            return carry

        lax.fori_loop(0, (heads[flip, counter] + UNROLL - 1) >> bits_of(UNROLL), some_tiles, 0)

        def cast(pair, carry):
            send_ref[piece * pairs + pair] = part[2 * pair + 1 - own_x].astype(jnp.bfloat16)
            return carry

        lax.fori_loop(0, pairs, cast, 0)


def march_grain(plan, got, porous_tiles, parts, dev, extinction, color_weights, flips):
    smem = pl.BlockSpec(memory_space=pltpu.SMEM)
    vmem = pl.BlockSpec(memory_space=pltpu.VMEM)
    pieces = len(flips)
    shape = parts[0].shape
    sent = (pieces * shape[0] // 2,) + shape[1:]
    *parts, send = pl.pallas_call(
        functools.partial(grain_kernel, flips=flips),
        out_shape=[jax.ShapeDtypeStruct(shape, jnp.float32)] * pieces
        + [jax.ShapeDtypeStruct(sent, jnp.bfloat16)],
        in_specs=[smem] * 6 + [vmem] * (1 + 2 * pieces),
        out_specs=[vmem] * (pieces + 1),
        input_output_aliases={7 + pieces + piece: piece for piece in range(pieces)},
        compiler_params=pltpu.CompilerParams(vmem_limit_bytes=GRAIN_LIMIT),
        cost_estimate=pl.CostEstimate(
            flops=4_000_000 * pieces, bytes_accessed=6_000_000 * pieces, transcendentals=0
        ),
        name="march_grain",
    )(dev, extinction, color_weights, *plan, got, *porous_tiles, *parts)
    return parts, send


def ordered(mine, theirs, mine_near):
    nearer = [jnp.where(mine_near, a, b) for a, b in zip(mine, theirs)]
    farther = [jnp.where(mine_near, b, a) for a, b in zip(mine, theirs)]
    open_part = 1.0 - nearer[3]
    return [n + open_part * f for n, f in zip(nearer, farther)]


def channels_of(block):
    block = block.astype(jnp.float32)
    rows = block.shape[0] // 4
    return [block[c * rows : (c + 1) * rows] for c in range(4)]


def pair_kernel(dev_ref, rank_ref, got_ref, *refs, pieces, width_y):
    parts, own_ref, send_refs = refs[:pieces], refs[pieces], refs[pieces + 1 :]
    device = dev_ref[0]
    mine_near = rank_ref[device] & 1 == 0
    around = width_y // 2
    place = (device & (width_y - 1)) >> 1

    def one_column(col, carry):
        for piece, part_ref in enumerate(parts):
            for distance in range(around):
                group = place ^ distance
                merged = ordered(
                    channels_of(part_ref[2 * group + (device & 1), col]),
                    channels_of(got_ref[piece * around + group, col]),
                    mine_near,
                )
                merged = jnp.concatenate(merged, axis=0)
                if distance == 0:
                    own_ref[piece, col] = merged
                else:
                    send_refs[distance - 1][piece, col] = merged.astype(jnp.bfloat16)
        return carry

    lax.fori_loop(0, got_ref.shape[1], one_column, 0)


def pair_chunk(parts, got, dev, ranks, width_y):
    around = width_y // 2
    pieces = len(parts)
    shape = (pieces,) + got.shape[1:]
    smem = pl.BlockSpec(memory_space=pltpu.SMEM)
    vmem = pl.BlockSpec(memory_space=pltpu.VMEM)
    return pl.pallas_call(
        functools.partial(pair_kernel, pieces=pieces, width_y=width_y),
        out_shape=[jax.ShapeDtypeStruct(shape, jnp.float32)]
        + [jax.ShapeDtypeStruct(shape, jnp.bfloat16)] * (around - 1),
        in_specs=[smem, smem] + [vmem] * (1 + pieces),
        out_specs=[vmem] * around,
        cost_estimate=pl.CostEstimate(
            flops=4 * got.size, bytes_accessed=9 * got.size, transcendentals=0
        ),
        compiler_params=pltpu.CompilerParams(vmem_limit_bytes=SMALL_LIMIT),
        name="pair_chunk",
    )(dev, ranks, got, *parts)


def four_way(device, rank_ref, parts, stride, bit):
    low = (rank_ref[device] >> bit) & 1 == 0
    far_low = (rank_ref[device ^ (2 * stride)] >> bit) & 1 == 0
    high = (rank_ref[device] >> (bit + 1)) & 1 == 0
    return ordered(
        ordered(parts[0], parts[1], low), ordered(parts[2], parts[3], far_low), high
    )


def quad_kernel(dev_ref, rank_ref, p0, p1, p2, p3, *out_refs):
    device = dev_ref[0]

    def one_column(col, carry):
        for piece, out_ref in enumerate(out_refs):
            parts = [channels_of(ref[piece, col]) for ref in (p0, p1, p2, p3)]
            merged = four_way(device, rank_ref, parts, 2, 1)
            out_ref[col] = jnp.concatenate(merged, axis=0)
        return carry

    lax.fori_loop(0, p0.shape[1], one_column, 0)


def quad_chunk(own, others, dev, ranks):
    pieces = own.shape[0]
    smem = pl.BlockSpec(memory_space=pltpu.SMEM)
    vmem = pl.BlockSpec(memory_space=pltpu.VMEM)
    return pl.pallas_call(
        quad_kernel,
        out_shape=[jax.ShapeDtypeStruct(own.shape[1:], jnp.float32)] * pieces,
        in_specs=[smem, smem] + [vmem] * 4,
        out_specs=[vmem] * pieces,
        cost_estimate=pl.CostEstimate(
            flops=12 * own.size, bytes_accessed=14 * own.size, transcendentals=0
        ),
        compiler_params=pltpu.CompilerParams(vmem_limit_bytes=SMALL_LIMIT),
        name="quad_chunk",
    )(dev, ranks, own, *others)


def last_kernel(dev_ref, rank_ref, p0, p1, p2, p3, q1, q2, q3, out_ref, *, width_y):
    device = dev_ref[0]
    col_blocks = p0.shape[1]
    for col in range(col_blocks):
        parts = [channels_of(ref[0, col]) for ref in (p0, p1, p2, p3)]
        mine = four_way(device, rank_ref, parts, 2, 1)
        parts = [mine] + [channels_of(ref[col]) for ref in (q1, q2, q3)]
        bit = width_y.bit_length() - 1
        merged = four_way(device, rank_ref, parts, width_y, bit)
        for c in range(4):
            for row in range(merged[c].shape[0]):
                start = (row * col_blocks + col) * 128
                out_ref[c : c + 1, start : start + 128] = merged[c][row : row + 1]


def last_chunk(own, others, ready, dev, ranks, width_y):
    smem = pl.BlockSpec(memory_space=pltpu.SMEM)
    vmem = pl.BlockSpec(memory_space=pltpu.VMEM)
    return pl.pallas_call(
        functools.partial(last_kernel, width_y=width_y),
        out_shape=jax.ShapeDtypeStruct((4, own.size // 4), jnp.float32),
        in_specs=[smem, smem] + [vmem] * 7,
        out_specs=vmem,
        compiler_params=pltpu.CompilerParams(vmem_limit_bytes=SMALL_LIMIT),
        name="last_chunk",
    )(dev, ranks, own, *others, *ready)


def shards(porosity, grain_blocks, owners, tiles, live_counts, ranks, extinction, color_weights):
    width_x = lax.axis_size("gx")
    width_y = lax.axis_size("gy")
    device_count = width_x * width_y
    block_count = grain_blocks.shape[0]
    slots = max(2, 2 * block_count // device_count)
    dev = lax.axis_index(("gx", "gy")).astype(jnp.int32).reshape(1)
    packed, table = pack_blocks(
        grain_blocks, owners[:, 0], tiles, live_counts, device_count, slots
    )
    got = lax.all_to_all(packed, ("gx", "gy"), split_axis=0, concat_axis=0, tiled=True)
    got = got.reshape((-1,) + got.shape[2:])
    porosity, table = lax.optimization_barrier((porosity, table))
    ids = exchange_table(table, width_x, width_y)
    tile_count = porosity.shape[1] * porosity.shape[2] // 128
    plan = plan_tiles(ids, dev, tile_count, slots, width_x, width_y)
    empty = [
        march_empty(porosity, dev, extinction, color_weights, flip, width_x, width_y)
        for flip in range(width_x)
    ]
    got, empty = lax.optimization_barrier((got, empty))
    ready = [None] * (width_x - 1)
    for flips in CHUNKS:
        parts, send = march_grain(
            plan,
            got,
            [empty[flip][1] for flip in flips],
            [empty[flip][0] for flip in flips],
            dev,
            extinction,
            color_weights,
            flips,
        )
        got, _ = lax.optimization_barrier((got, send))
        block = exchanged(send, "gy", 1)
        own, *outgoing = pair_chunk(parts, block, dev, ranks, width_y)
        others = [exchanged(out, "gy", 2 * (k + 1)) for k, out in enumerate(outgoing)]
        if flips != (0,):
            for flip, done in zip(flips, quad_chunk(own, others, dev, ranks)):
                ready[flip - 1] = exchanged(done, "gx", flip)
    return last_chunk(own, others, ready, dev, ranks, width_y)


def march_flat(porous_flat, grain_flat, extinction, color_weights):
    porous = porous_flat.astype(jnp.float32)
    extinct = extinction[0] * (1.0 - porous) + extinction[1] * grain_flat
    optical = jnp.cumsum(extinct, axis=0)
    before = optical - extinct
    weight = jnp.exp(-before) * (1.0 - jnp.exp(-extinct))
    channels = []
    for channel in range(3):
        colour = jax.nn.sigmoid(
            color_weights[channel, 0] * porous
            + color_weights[channel, 1] * grain_flat
            + color_weights[channel, 2]
        )
        channels.append(jnp.sum(weight * colour, axis=0))
    channels.append(1.0 - jnp.exp(-optical[-1]))
    return jnp.stack(channels, axis=0)


def composite(nearer, farther):
    return nearer + (1.0 - nearer[3:4]) * farther


def shards_any(
    porosity, grain_blocks, owners, tiles, live_counts, ranks, extinction, color_weights
):
    width_x = lax.axis_size("gx")
    width_y = lax.axis_size("gy")
    device_count = width_x * width_y
    depth_cells, image_rows, image_cols = porosity.shape
    block_count, _, block_cols = grain_blocks.shape
    slots = max(2, 2 * block_count // device_count)
    tile_count = image_rows * image_cols // block_cols
    pixel_count = image_rows * image_cols
    block_len = pixel_count // device_count
    packed, table = pack_blocks(
        grain_blocks, owners[:, 0], tiles, live_counts, device_count, slots
    )
    got = lax.all_to_all(packed, ("gx", "gy"), split_axis=0, concat_axis=0, tiled=True)
    table = lax.all_to_all(table, ("gx", "gy"), split_axis=0, concat_axis=0, tiled=True)
    table = table[:, : slots + 1]
    used = jnp.arange(slots, dtype=jnp.int32)[None, :] < table[:, slots:]
    got_tile = jnp.where(used, table[:, :slots], tile_count)
    got_data = jnp.where(used[:, :, None, None], got, jnp.bfloat16(0))
    grain_tiles = (
        jnp.zeros((tile_count, depth_cells, block_cols), jnp.float32)
        .at[got_tile.reshape(-1)]
        .add(
            got_data.reshape(device_count * slots, depth_cells, block_cols).astype(jnp.float32),
            mode="drop",
        )
    )
    grain_flat = jnp.transpose(grain_tiles, (1, 0, 2)).reshape(depth_cells, pixel_count)
    porous_flat = porosity.reshape(depth_cells, pixel_count)
    partial_value = march_flat(porous_flat, grain_flat, extinction, color_weights)
    my_rank = ranks[lax.axis_index(("gx", "gy"))]
    bits_y = width_y.bit_length() - 1
    bits_x = width_x.bit_length() - 1
    current = partial_value.reshape(4, width_x, width_y, block_len)
    for axis, dim, bits, first in (("gy", 2, bits_y, 0), ("gx", 1, bits_x, bits_y)):
        for section_bit in range(bits):
            shape = current.shape
            paired = current.reshape(
                shape[:dim] + (shape[dim] // 2, 2) + shape[dim + 1 :]
            )
            own_bit = lax.axis_index(axis) >> section_bit & 1
            kept_half = lax.dynamic_index_in_dim(paired, own_bit, dim + 1, keepdims=False)
            sent_half = lax.dynamic_index_in_dim(paired, 1 - own_bit, dim + 1, keepdims=False)
            partner = exchanged(sent_half, axis, 1 << section_bit)
            nearer_side = my_rank >> first + section_bit & 1 == 0
            current = composite(
                jnp.where(nearer_side, kept_half, partner),
                jnp.where(nearer_side, partner, kept_half),
            )
        if dim == 2:
            current = current.reshape(4, width_x, 1, block_len).reshape(4, width_x, block_len)
    return current.reshape(4, block_len)


def solution(mesh):
    in_specs = (
        P(("gx", "gy"), None, None),
        P(("gx", "gy"), None, None),
        P(("gx", "gy"), None),
        P(("gx", "gy")),
        P(("gx", "gy")),
        P(),
        P(),
        P(),
    )
    out_specs = P(None, ("gx", "gy"))

    def run(porosity, *rest):
        rows = porosity.shape[1] // (mesh.shape["gx"] * mesh.shape["gy"])
        fits = mesh.shape["gx"] == 4 and mesh.shape["gy"] == 8 and rows == 8
        return jax.shard_map(
            shards if fits else shards_any,
            mesh=mesh,
            in_specs=in_specs,
            out_specs=out_specs,
            check_vma=False,
        )(porosity, *rest)

    return run
```

```python
import functools

import jax
import jax.numpy as jnp
from jax import lax
from jax.experimental import pallas as pl
from jax.experimental.pallas import tpu as pltpu
from jax.sharding import PartitionSpec as P

LOG2E = 1.4426950408889634
PACK_LIMIT = 56 * 1024 * 1024
GRAIN_LIMIT = 16 * 1024 * 1024
SMALL_LIMIT = 8 * 1024 * 1024
UNROLL = 4
CHUNKS = ((3,), (2, 1), (0,))


def exchanged(block, axis, distance):
    route = [(low, low ^ distance) for low in range(lax.axis_size(axis))]
    return lax.ppermute(block, axis, route)


def bits_of(size):
    assert size & (size - 1) == 0
    return size.bit_length() - 1


def pack_kernel(
    owner_ref, tile_ref, live_ref, block_ref, out_ref, table, table_vec, table_sem, *, slots
):
    owners_all = out_ref.shape[0]

    def clear(owner, carry):
        table[owner, slots] = 0
        return carry

    lax.fori_loop(0, owners_all, clear, 0)

    def place(index, carry):
        owner = owner_ref[index]
        slot = table[owner, slots]
        table[owner, slots] = slot + 1
        table[owner, slot] = tile_ref[index]
        out_ref[owner, slot] = block_ref[index]
        return carry

    lax.fori_loop(0, live_ref[0], place, 0)
    copy = pltpu.make_async_copy(table, table_vec, table_sem)
    copy.start()
    copy.wait()
    first = lax.broadcasted_iota(jnp.int32, (16, 128), 0) == 0
    for owner in range(owners_all):
        row = jnp.broadcast_to(table_vec[owner : owner + 1, :], (16, 128))
        coded = jnp.where(first, row >> 6, row & 63)
        out_ref[owner, slots] = coded.astype(jnp.float32).astype(jnp.bfloat16)


def pack_blocks(grain_blocks, owner_dev, tiles, live_counts, device_count, slots):
    smem = pl.BlockSpec(memory_space=pltpu.SMEM)
    vmem = pl.BlockSpec(memory_space=pltpu.VMEM)
    return pl.pallas_call(
        functools.partial(pack_kernel, slots=slots),
        out_shape=jax.ShapeDtypeStruct(
            (device_count, slots + 1) + grain_blocks.shape[1:], grain_blocks.dtype
        ),
        in_specs=[smem, smem, smem, vmem],
        out_specs=vmem,
        scratch_shapes=[
            pltpu.SMEM((device_count, 128), jnp.int32),
            pltpu.VMEM((device_count, 128), jnp.int32),
            pltpu.SemaphoreType.DMA(()),
        ],
        compiler_params=pltpu.CompilerParams(vmem_limit_bytes=PACK_LIMIT),
        name="pack_blocks",
    )(owner_dev, tiles, live_counts, grain_blocks)


def plan_tiles(gx, nowhere, got_ref, heads, earlier, deeper, ids_vec, ids, last, sems, slots):
    sources = ids.shape[0]
    piece_bits = bits_of(last.shape[0] // heads.shape[0])
    counter = heads.shape[1] - 1
    forget = pltpu.make_async_copy(nowhere, last, sems.at[0])
    forget.start()
    for source in range(sources):
        coded = got_ref[source * (slots + 1) + slots].astype(jnp.float32)
        ids_vec[source : source + 1, :] = (coded[0:1, :] * 64.0 + coded[1:2, :]).astype(jnp.int32)
    fetch = pltpu.make_async_copy(ids_vec, ids, sems.at[1])
    fetch.start()
    for flip in range(heads.shape[0]):
        heads[flip, counter] = 0
    fetch.wait()
    forget.wait()

    def from_source(source, carry):
        def one(slot, carry):
            tile = ids[source, slot]
            entry = source * (slots + 1) + slot
            flip = (tile >> piece_bits) ^ gx
            before = last[tile]
            found = heads[flip, counter]
            heads[flip, found] = entry + ((tile & ((1 << piece_bits) - 1)) << 16)
            heads[flip, counter] = found + jnp.where(before < 0, 1, 0)
            last[tile] = jnp.where(before < 0, entry, before)
            earlier[entry] = -1
            deeper[entry] = 0

            @pl.when(before >= 0)
            def _():
                earlier[entry] = earlier[before]
                earlier[before] = entry
                deeper[before] = deeper[before] + 1

            return carry

        return lax.fori_loop(0, ids[source, slots], one, carry)

    lax.fori_loop(0, sources, from_source, 0)

    for flip in range(heads.shape[0]):
        found = heads[flip, counter]

        @pl.when(found > 0)
        def _():
            for extra in range(UNROLL - 1):
                heads[flip, found + extra] = heads[flip, found - 1]


def empty_kernel(
    dev_ref, ext_ref, col_ref, por_hbm, part, por_tiles, por, turned, sems, *, flip, width_x, width_y
):
    depth, rows, cols = por_hbm.shape
    block_rows = por.shape[2]
    half_rows = block_rows // 2
    col_blocks = cols // 128
    steps = rows // width_x // block_rows
    first_row = ((dev_ref[0] >> bits_of(width_y)) ^ flip) * (rows // width_x)
    base = -LOG2E * ext_ref[0]
    slope = LOG2E * ext_ref[0]

    def fetch(step, slot):
        start = pl.multiple_of(first_row + step * block_rows, block_rows)
        return pltpu.make_async_copy(
            por_hbm.at[:, pl.ds(start, block_rows), :], por.at[slot], sems.at[slot]
        )

    fetch(0, 0).start()

    def one_step(step, carry):
        slot = lax.rem(step, 2)

        @pl.when(step + 1 < steps)
        def _():
            fetch(step + 1, 1 - slot).start()

        fetch(step, slot).wait()

        def one_column(col, carry):
            lanes = pl.ds(pl.multiple_of(col * 128, 128), 128)
            clear = jnp.ones((block_rows, 128), jnp.float32)
            sums = [jnp.zeros((block_rows, 128), jnp.float32) for _ in range(3)]
            for z in range(depth):
                porous = por[slot, z, :, lanes].astype(jnp.float32)
                turned[z * block_rows : (z + 1) * block_rows, :] = porous
                passed = clear * jnp.exp2(base + slope * porous)
                weight = clear - passed
                clear = passed
                for c in range(3):
                    half_logit = (0.5 * col_ref[c, 0]) * porous + 0.5 * col_ref[c, 2]
                    sums[c] = sums[c] + weight * jnp.tanh(half_logit)
            for row in range(block_rows):
                tile = (step * block_rows + row) * col_blocks + col
                por_tiles[tile] = turned[pl.ds(row, depth, stride=block_rows), :].astype(
                    jnp.bfloat16
                )
            alpha = 1.0 - clear
            parts = [0.5 * (alpha + total) for total in sums] + [alpha]
            for c in range(4):
                for half in range(2):
                    part[2 * step + half, col, c * half_rows : (c + 1) * half_rows, :] = parts[c][
                        half * half_rows : (half + 1) * half_rows
                    ]
            return carry

        lax.fori_loop(0, col_blocks, one_column, 0)
        return carry

    lax.fori_loop(0, steps, one_step, 0)


def march_empty(porosity, dev, extinction, color_weights, flip, width_x, width_y):
    depth, rows, cols = porosity.shape
    rows = rows // width_x
    block_rows = 16
    smem = pl.BlockSpec(memory_space=pltpu.SMEM)
    vmem = pl.BlockSpec(memory_space=pltpu.VMEM)
    return pl.pallas_call(
        functools.partial(empty_kernel, flip=flip, width_x=width_x, width_y=width_y),
        out_shape=[
            jax.ShapeDtypeStruct((rows // 8, cols // 128, 32, 128), jnp.float32),
            jax.ShapeDtypeStruct((rows * cols // 128, depth, 128), porosity.dtype),
        ],
        in_specs=[smem, smem, smem, pl.BlockSpec(memory_space=pl.ANY)],
        out_specs=[vmem, vmem],
        scratch_shapes=[
            pltpu.VMEM((2, depth, block_rows, cols), porosity.dtype),
            pltpu.VMEM((depth * block_rows, 128), jnp.float32),
            pltpu.SemaphoreType.DMA((2,)),
        ],
        compiler_params=pltpu.CompilerParams(vmem_limit_bytes=SMALL_LIMIT),
        cost_estimate=pl.CostEstimate(
            flops=20 * depth * rows * cols,
            bytes_accessed=4 * depth * rows * cols + 16 * rows * cols,
            transcendentals=4 * depth * rows * cols,
        ),
        name="march_empty",
    )(dev, extinction, color_weights, porosity)


def grain_kernel(dev_ref, ext_ref, col_ref, *refs, flips, slots, gy_bits, planned):
    pieces = len(flips)
    if planned:
        heads, earlier, deeper, *refs = refs
    else:
        nowhere, *refs = refs
    got_ref, por_refs, parts = refs[0], refs[1 : 1 + pieces], refs[1 + 2 * pieces : 1 + 3 * pieces]
    send_ref, *rest = refs[1 + 3 * pieces :]
    if not planned:
        heads, earlier, deeper, *scratch = rest
        plan_tiles(
            dev_ref[0] >> gy_bits, nowhere, got_ref, heads, earlier, deeper, *scratch, slots
        )
    own_x = dev_ref[0] & 1
    col_bits = bits_of(parts[0].shape[1])
    pairs = parts[0].shape[0] // 2
    counter = heads.shape[1] - 1
    base = -LOG2E * ext_ref[0]
    slope = LOG2E * ext_ref[0]
    grain_slope = -LOG2E * ext_ref[1]
    depth_of = lax.broadcasted_iota(jnp.int32, (8, 128), 0)

    def running(value):
        for shift in (1, 2, 4):
            value = value + jnp.where(depth_of >= shift, pltpu.roll(value, shift, 0), 0.0)
        return value

    for piece, flip in enumerate(flips):
        part, por_ref = parts[piece], por_refs[piece]

        def some_tiles(batch, carry):
            work = []
            for place in range(UNROLL):
                code = heads[flip, batch * UNROLL + place]
                entry = code & 65535

                def add_earlier(_, state):
                    at, total = state
                    at = earlier[at]
                    return at, total + got_ref[at].astype(jnp.float32)

                grain = got_ref[entry].astype(jnp.float32)
                _, grain = lax.fori_loop(0, deeper[entry], add_earlier, (entry, grain))
                work.append((code >> 16, grain))
            for tile, grain in work:
                porous = por_ref[tile].astype(jnp.float32)
                exponent = (base + slope * porous) + grain_slope * grain
                front = running(exponent[:8])
                back = running(exponent[8:]) + front[7:8]
                optical = jnp.concatenate([front, back], axis=0)
                weight = jnp.exp2(optical - exponent) - jnp.exp2(optical)
                alpha = 1.0 - jnp.exp2(back[7:8])
                results = []
                for c in range(3):
                    half_logit = (
                        (0.5 * col_ref[c, 0]) * porous
                        + (0.5 * col_ref[c, 1]) * grain
                        + 0.5 * col_ref[c, 2]
                    )
                    shaded = weight * jnp.tanh(half_logit)
                    total = jnp.sum(shaded[:8] + shaded[8:], axis=0, keepdims=True)
                    results.append(0.5 * (alpha + total))
                results.append(alpha)
                group, row = tile >> (3 + col_bits), (tile >> col_bits) & 7
                col = tile & ((1 << col_bits) - 1)
                for c in range(4):
                    part[group, col, pl.ds(c * 8 + row, 1), :] = results[c]
            return carry

        lax.fori_loop(0, (heads[flip, counter] + UNROLL - 1) >> bits_of(UNROLL), some_tiles, 0)

        def cast(pair, carry):
            send_ref[piece * pairs + pair] = part[2 * pair + 1 - own_x].astype(jnp.bfloat16)
            return carry

        lax.fori_loop(0, pairs, cast, 0)


def march_grain(
    plan, got, porous_tiles, parts, dev, extinction, color_weights, flips, slots, width_x, width_y
):
    smem = pl.BlockSpec(memory_space=pltpu.SMEM)
    vmem = pl.BlockSpec(memory_space=pltpu.VMEM)
    pieces = len(flips)
    shape = parts[0].shape
    sent = (pieces * shape[0] // 2,) + shape[1:]
    entries = got.shape[0]
    sources = entries // (slots + 1)
    tile_count = porous_tiles[0].shape[0] * width_x
    most = -(-(entries + UNROLL + 1) // 128) * 128
    plan_shapes, plan_specs, scratch = [], [], []
    if plan is None:
        plan_shapes = [
            jax.ShapeDtypeStruct((width_x, most), jnp.int32),
            jax.ShapeDtypeStruct((entries,), jnp.int32),
            jax.ShapeDtypeStruct((entries,), jnp.int32),
        ]
        plan_specs = [smem] * 3
        scratch = [
            pltpu.VMEM((sources, 128), jnp.int32),
            pltpu.SMEM((sources, 128), jnp.int32),
            pltpu.SMEM((tile_count,), jnp.int32),
            pltpu.SemaphoreType.DMA((2,)),
        ]
        before = [jnp.full((tile_count,), -1, jnp.int32)]
        before_specs = [pl.BlockSpec(memory_space=pl.ANY)]
    else:
        before, before_specs = list(plan), [smem] * 3
    first_part = 3 + len(before) + 1 + pieces
    outs = pl.pallas_call(
        functools.partial(
            grain_kernel,
            flips=flips,
            slots=slots,
            gy_bits=bits_of(width_y),
            planned=plan is not None,
        ),
        out_shape=[jax.ShapeDtypeStruct(shape, jnp.float32)] * pieces
        + [jax.ShapeDtypeStruct(sent, jnp.bfloat16)]
        + plan_shapes,
        in_specs=[smem] * 3 + before_specs + [vmem] * (1 + 2 * pieces),
        out_specs=[vmem] * (pieces + 1) + plan_specs,
        scratch_shapes=scratch,
        input_output_aliases={first_part + piece: piece for piece in range(pieces)},
        compiler_params=pltpu.CompilerParams(vmem_limit_bytes=GRAIN_LIMIT),
        cost_estimate=pl.CostEstimate(
            flops=1000, bytes_accessed=1000, transcendentals=0
        ),
        name="march_grain",
    )(dev, extinction, color_weights, *before, got, *porous_tiles, *parts)
    return outs[:pieces], outs[pieces], outs[pieces + 1 :] or plan


def ordered(mine, theirs, mine_near):
    nearer = [jnp.where(mine_near, a, b) for a, b in zip(mine, theirs)]
    farther = [jnp.where(mine_near, b, a) for a, b in zip(mine, theirs)]
    open_part = 1.0 - nearer[3]
    return [n + open_part * f for n, f in zip(nearer, farther)]


def channels_of(block):
    block = block.astype(jnp.float32)
    rows = block.shape[0] // 4
    return [block[c * rows : (c + 1) * rows] for c in range(4)]


def pair_kernel(dev_ref, rank_ref, got_ref, *refs, pieces, width_y):
    parts, own_ref, send_refs = refs[:pieces], refs[pieces], refs[pieces + 1 :]
    device = dev_ref[0]
    mine_near = rank_ref[device] & 1 == 0
    around = width_y // 2
    place = (device & (width_y - 1)) >> 1

    def one_column(col, carry):
        for piece, part_ref in enumerate(parts):
            for distance in range(around):
                group = place ^ distance
                merged = ordered(
                    channels_of(part_ref[2 * group + (device & 1), col]),
                    channels_of(got_ref[piece * around + group, col]),
                    mine_near,
                )
                merged = jnp.concatenate(merged, axis=0)
                if distance == 0:
                    own_ref[piece, col] = merged
                else:
                    send_refs[distance - 1][piece, col] = merged.astype(jnp.bfloat16)
        return carry

    lax.fori_loop(0, got_ref.shape[1], one_column, 0)


def pair_chunk(parts, got, dev, ranks, width_y):
    around = width_y // 2
    pieces = len(parts)
    shape = (pieces,) + got.shape[1:]
    smem = pl.BlockSpec(memory_space=pltpu.SMEM)
    vmem = pl.BlockSpec(memory_space=pltpu.VMEM)
    return pl.pallas_call(
        functools.partial(pair_kernel, pieces=pieces, width_y=width_y),
        out_shape=[jax.ShapeDtypeStruct(shape, jnp.float32)]
        + [jax.ShapeDtypeStruct(shape, jnp.bfloat16)] * (around - 1),
        in_specs=[smem, smem] + [vmem] * (1 + pieces),
        out_specs=[vmem] * around,
        cost_estimate=pl.CostEstimate(
            flops=1000, bytes_accessed=1000, transcendentals=0
        ),
        compiler_params=pltpu.CompilerParams(vmem_limit_bytes=SMALL_LIMIT),
        name="pair_chunk",
    )(dev, ranks, got, *parts)


def four_way(device, rank_ref, parts, stride, bit):
    low = (rank_ref[device] >> bit) & 1 == 0
    far_low = (rank_ref[device ^ (2 * stride)] >> bit) & 1 == 0
    high = (rank_ref[device] >> (bit + 1)) & 1 == 0
    return ordered(
        ordered(parts[0], parts[1], low), ordered(parts[2], parts[3], far_low), high
    )


def quad_kernel(dev_ref, rank_ref, p0, p1, p2, p3, *out_refs):
    device = dev_ref[0]

    def one_column(col, carry):
        for piece, out_ref in enumerate(out_refs):
            parts = [channels_of(ref[piece, col]) for ref in (p0, p1, p2, p3)]
            merged = four_way(device, rank_ref, parts, 2, 1)
            out_ref[col] = jnp.concatenate(merged, axis=0)
        return carry

    lax.fori_loop(0, p0.shape[1], one_column, 0)


def quad_chunk(own, others, dev, ranks):
    pieces = own.shape[0]
    smem = pl.BlockSpec(memory_space=pltpu.SMEM)
    vmem = pl.BlockSpec(memory_space=pltpu.VMEM)
    return pl.pallas_call(
        quad_kernel,
        out_shape=[jax.ShapeDtypeStruct(own.shape[1:], jnp.float32)] * pieces,
        in_specs=[smem, smem] + [vmem] * 4,
        out_specs=[vmem] * pieces,
        cost_estimate=pl.CostEstimate(
            flops=1000, bytes_accessed=1000, transcendentals=0
        ),
        compiler_params=pltpu.CompilerParams(vmem_limit_bytes=SMALL_LIMIT),
        name="quad_chunk",
    )(dev, ranks, own, *others)


def last_kernel(dev_ref, rank_ref, p0, p1, p2, p3, q1, q2, q3, out_ref, *, width_y):
    device = dev_ref[0]
    col_blocks = p0.shape[1]
    for col in range(col_blocks):
        parts = [channels_of(ref[0, col]) for ref in (p0, p1, p2, p3)]
        mine = four_way(device, rank_ref, parts, 2, 1)
        parts = [mine] + [channels_of(ref[col]) for ref in (q1, q2, q3)]
        bit = width_y.bit_length() - 1
        merged = four_way(device, rank_ref, parts, width_y, bit)
        for c in range(4):
            for row in range(merged[c].shape[0]):
                start = (row * col_blocks + col) * 128
                out_ref[c : c + 1, start : start + 128] = merged[c][row : row + 1]


def last_chunk(own, others, ready, dev, ranks, width_y):
    smem = pl.BlockSpec(memory_space=pltpu.SMEM)
    vmem = pl.BlockSpec(memory_space=pltpu.VMEM)
    return pl.pallas_call(
        functools.partial(last_kernel, width_y=width_y),
        out_shape=jax.ShapeDtypeStruct((4, own.size // 4), jnp.float32),
        in_specs=[smem, smem] + [vmem] * 7,
        out_specs=vmem,
        compiler_params=pltpu.CompilerParams(vmem_limit_bytes=SMALL_LIMIT),
        name="last_chunk",
    )(dev, ranks, own, *others, *ready)


def shards(porosity, grain_blocks, owners, tiles, live_counts, ranks, extinction, color_weights):
    width_x = lax.axis_size("gx")
    width_y = lax.axis_size("gy")
    device_count = width_x * width_y
    block_count = grain_blocks.shape[0]
    slots = max(2, 2 * block_count // device_count)
    dev = lax.axis_index(("gx", "gy")).astype(jnp.int32).reshape(1)
    packed = pack_blocks(grain_blocks, owners[:, 0], tiles, live_counts, device_count, slots)
    got = lax.all_to_all(packed, ("gx", "gy"), split_axis=0, concat_axis=0, tiled=True)
    got = got.reshape((-1,) + got.shape[2:])
    porosity, _ = lax.optimization_barrier((porosity, packed))
    empty = [
        march_empty(porosity, dev, extinction, color_weights, flip, width_x, width_y)
        for flip in range(width_x)
    ]
    got, empty = lax.optimization_barrier((got, empty))
    ready = [None] * (width_x - 1)
    plan = None
    for flips in CHUNKS:
        parts, send, plan = march_grain(
            plan,
            got,
            [empty[flip][1] for flip in flips],
            [empty[flip][0] for flip in flips],
            dev,
            extinction,
            color_weights,
            flips,
            slots,
            width_x,
            width_y,
        )
        got, _ = lax.optimization_barrier((got, send))
        block = exchanged(send, "gy", 1)
        own, *outgoing = pair_chunk(parts, block, dev, ranks, width_y)
        others = [exchanged(out, "gy", 2 * (k + 1)) for k, out in enumerate(outgoing)]
        if flips != (0,):
            for flip, done in zip(flips, quad_chunk(own, others, dev, ranks)):
                ready[flip - 1] = exchanged(done, "gx", flip)
    return last_chunk(own, others, ready, dev, ranks, width_y)


def march_flat(porous_flat, grain_flat, extinction, color_weights):
    porous = porous_flat.astype(jnp.float32)
    extinct = extinction[0] * (1.0 - porous) + extinction[1] * grain_flat
    optical = jnp.cumsum(extinct, axis=0)
    before = optical - extinct
    weight = jnp.exp(-before) * (1.0 - jnp.exp(-extinct))
    channels = []
    for channel in range(3):
        colour = jax.nn.sigmoid(
            color_weights[channel, 0] * porous
            + color_weights[channel, 1] * grain_flat
            + color_weights[channel, 2]
        )
        channels.append(jnp.sum(weight * colour, axis=0))
    channels.append(1.0 - jnp.exp(-optical[-1]))
    return jnp.stack(channels, axis=0)


def composite(nearer, farther):
    return nearer + (1.0 - nearer[3:4]) * farther


def shards_any(
    porosity, grain_blocks, owners, tiles, live_counts, ranks, extinction, color_weights
):
    width_x = lax.axis_size("gx")
    width_y = lax.axis_size("gy")
    device_count = width_x * width_y
    depth_cells, image_rows, image_cols = porosity.shape
    block_count, _, block_cols = grain_blocks.shape
    slots = max(2, 2 * block_count // device_count)
    tile_count = image_rows * image_cols // block_cols
    pixel_count = image_rows * image_cols
    block_len = pixel_count // device_count
    packed = pack_blocks(grain_blocks, owners[:, 0], tiles, live_counts, device_count, slots)
    got = lax.all_to_all(packed, ("gx", "gy"), split_axis=0, concat_axis=0, tiled=True)
    coded = got[:, slots, :2, : slots + 1].astype(jnp.int32)
    table = coded[:, 0] * 64 + coded[:, 1]
    used = jnp.arange(slots, dtype=jnp.int32)[None, :] < table[:, slots:]
    got_tile = jnp.where(used, table[:, :slots], tile_count)
    got_data = jnp.where(used[:, :, None, None], got[:, :slots], jnp.bfloat16(0))
    grain_tiles = (
        jnp.zeros((tile_count, depth_cells, block_cols), jnp.float32)
        .at[got_tile.reshape(-1)]
        .add(
            got_data.reshape(device_count * slots, depth_cells, block_cols).astype(jnp.float32),
            mode="drop",
        )
    )
    grain_flat = jnp.transpose(grain_tiles, (1, 0, 2)).reshape(depth_cells, pixel_count)
    porous_flat = porosity.reshape(depth_cells, pixel_count)
    partial_value = march_flat(porous_flat, grain_flat, extinction, color_weights)
    my_rank = ranks[lax.axis_index(("gx", "gy"))]
    bits_y = width_y.bit_length() - 1
    bits_x = width_x.bit_length() - 1
    current = partial_value.reshape(4, width_x, width_y, block_len)
    for axis, dim, bits, first in (("gy", 2, bits_y, 0), ("gx", 1, bits_x, bits_y)):
        for section_bit in range(bits):
            shape = current.shape
            paired = current.reshape(
                shape[:dim] + (shape[dim] // 2, 2) + shape[dim + 1 :]
            )
            own_bit = lax.axis_index(axis) >> section_bit & 1
            kept_half = lax.dynamic_index_in_dim(paired, own_bit, dim + 1, keepdims=False)
            sent_half = lax.dynamic_index_in_dim(paired, 1 - own_bit, dim + 1, keepdims=False)
            partner = exchanged(sent_half, axis, 1 << section_bit)
            nearer_side = my_rank >> first + section_bit & 1 == 0
            current = composite(
                jnp.where(nearer_side, kept_half, partner),
                jnp.where(nearer_side, partner, kept_half),
            )
        if dim == 2:
            current = current.reshape(4, width_x, 1, block_len).reshape(4, width_x, block_len)
    return current.reshape(4, block_len)


def solution(mesh):
    in_specs = (
        P(("gx", "gy"), None, None),
        P(("gx", "gy"), None, None),
        P(("gx", "gy"), None),
        P(("gx", "gy")),
        P(("gx", "gy")),
        P(),
        P(),
        P(),
    )
    out_specs = P(None, ("gx", "gy"))

    def run(porosity, *rest):
        rows = porosity.shape[1] // (mesh.shape["gx"] * mesh.shape["gy"])
        fits = mesh.shape["gx"] == 4 and mesh.shape["gy"] == 8 and rows == 8
        return jax.shard_map(
            shards if fits else shards_any,
            mesh=mesh,
            in_specs=in_specs,
            out_specs=out_specs,
            check_vma=False,
        )(porosity, *rest)

    return run
```

```python
import functools

import jax
import jax.numpy as jnp
from jax import lax
from jax.experimental import pallas as pl
from jax.experimental.pallas import tpu as pltpu
from jax.sharding import PartitionSpec as P

LOG2E = 1.4426950408889634
PACK_LIMIT = 56 * 1024 * 1024
EMPTY_LIMIT = 24 * 1024 * 1024
GRAIN_LIMIT = 50 * 1024 * 1024
SMALL_LIMIT = 8 * 1024 * 1024
UNROLL = 4
CHUNKS = ((3,), (2, 1), (0,))


def exchanged(block, axis, distance):
    route = [(low, low ^ distance) for low in range(lax.axis_size(axis))]
    return lax.ppermute(block, axis, route)


def bits_of(size):
    assert size & (size - 1) == 0
    return size.bit_length() - 1


def pack_kernel(
    owner_ref, tile_ref, live_ref, block_ref, out_ref, table, table_vec, table_sem, *, slots
):
    owners_all = out_ref.shape[0]

    def clear(owner, carry):
        table[owner, slots] = 0
        return carry

    lax.fori_loop(0, owners_all, clear, 0)

    def place(index, carry):
        owner = owner_ref[index]
        slot = table[owner, slots]
        table[owner, slots] = slot + 1
        table[owner, slot] = tile_ref[index]
        out_ref[owner, slot] = block_ref[index]
        return carry

    lax.fori_loop(0, live_ref[0], place, 0)
    copy = pltpu.make_async_copy(table, table_vec, table_sem)
    copy.start()
    copy.wait()
    first = lax.broadcasted_iota(jnp.int32, (16, 128), 0) == 0
    for owner in range(owners_all):
        row = jnp.broadcast_to(table_vec[owner : owner + 1, :], (16, 128))
        coded = jnp.where(first, row >> 6, row & 63)
        out_ref[owner, slots] = coded.astype(jnp.float32).astype(jnp.bfloat16)


def pack_blocks(grain_blocks, owner_dev, tiles, live_counts, device_count, slots):
    smem = pl.BlockSpec(memory_space=pltpu.SMEM)
    vmem = pl.BlockSpec(memory_space=pltpu.VMEM)
    return pl.pallas_call(
        functools.partial(pack_kernel, slots=slots),
        out_shape=jax.ShapeDtypeStruct(
            (device_count, slots + 1) + grain_blocks.shape[1:], grain_blocks.dtype
        ),
        in_specs=[smem, smem, smem, vmem],
        out_specs=vmem,
        scratch_shapes=[
            pltpu.SMEM((device_count, 128), jnp.int32),
            pltpu.VMEM((device_count, 128), jnp.int32),
            pltpu.SemaphoreType.DMA(()),
        ],
        compiler_params=pltpu.CompilerParams(vmem_limit_bytes=PACK_LIMIT),
        name="pack_blocks",
    )(owner_dev, tiles, live_counts, grain_blocks)


def plan_tiles(nowhere, got_ref, heads, earlier, deeper, ids_vec, ids, last, sems, slots):
    sources = ids.shape[0]
    forget = pltpu.make_async_copy(nowhere, last, sems.at[0])
    forget.start()
    for source in range(sources):
        coded = got_ref[source * (slots + 1) + slots].astype(jnp.float32)
        ids_vec[source : source + 1, :] = (coded[0:1, :] * 64.0 + coded[1:2, :]).astype(jnp.int32)
    fetch = pltpu.make_async_copy(ids_vec, ids, sems.at[1])
    fetch.start()
    fetch.wait()
    forget.wait()

    def from_source(source, found):
        def one(slot, found):
            tile = ids[source, slot]
            entry = source * (slots + 1) + slot
            before = last[tile]
            fresh = before < 0
            heads[found] = entry + (tile << 16)
            last[tile] = jnp.where(fresh, entry, before)
            deeper[entry] = 0

            @pl.when(jnp.logical_not(fresh))
            def _():
                earlier[entry] = earlier[before]
                earlier[before] = entry
                deeper[before] = deeper[before] + 1

            return found + jnp.where(fresh, 1, 0)

        return lax.fori_loop(0, ids[source, slots], one, found)

    found = lax.fori_loop(0, sources, from_source, jnp.int32(0))

    @pl.when(found > 0)
    def _():
        for extra in range(UNROLL - 1):
            heads[found + extra] = heads[found - 1]

    return found


def empty_kernel(ext_ref, col_ref, por_hbm, part, por_tiles, por, turned, sems):
    depth, rows, cols = por_hbm.shape
    block_rows = por.shape[2]
    half_rows = block_rows // 2
    col_blocks = cols // 128
    steps = rows // block_rows
    base = -LOG2E * ext_ref[0]
    slope = LOG2E * ext_ref[0]

    def fetch(step, slot):
        start = pl.multiple_of(step * block_rows, block_rows)
        return pltpu.make_async_copy(
            por_hbm.at[:, pl.ds(start, block_rows), :], por.at[slot], sems.at[slot]
        )

    fetch(0, 0).start()

    def one_step(step, carry):
        slot = lax.rem(step, 2)

        @pl.when(step + 1 < steps)
        def _():
            fetch(step + 1, 1 - slot).start()

        fetch(step, slot).wait()

        def one_column(col, carry):
            lanes = pl.ds(pl.multiple_of(col * 128, 128), 128)
            clear = jnp.ones((block_rows, 128), jnp.float32)
            sums = [jnp.zeros((block_rows, 128), jnp.float32) for _ in range(3)]
            for z in range(depth):
                porous = por[slot, z, :, lanes].astype(jnp.float32)
                turned[z * block_rows : (z + 1) * block_rows, :] = porous
                passed = clear * jnp.exp2(base + slope * porous)
                weight = clear - passed
                clear = passed
                for c in range(3):
                    half_logit = (0.5 * col_ref[c, 0]) * porous + 0.5 * col_ref[c, 2]
                    sums[c] = sums[c] + weight * jnp.tanh(half_logit)
            for row in range(block_rows):
                tile = (step * block_rows + row) * col_blocks + col
                por_tiles[tile] = turned[pl.ds(row, depth, stride=block_rows), :].astype(
                    jnp.bfloat16
                )
            alpha = 1.0 - clear
            parts = [0.5 * (alpha + total) for total in sums] + [alpha]
            for c in range(4):
                for half in range(2):
                    part[2 * step + half, col, c * half_rows : (c + 1) * half_rows, :] = parts[c][
                        half * half_rows : (half + 1) * half_rows
                    ]
            return carry

        lax.fori_loop(0, col_blocks, one_column, 0)
        return carry

    lax.fori_loop(0, steps, one_step, 0)


def march_empty(porosity, extinction, color_weights):
    depth, rows, cols = porosity.shape
    block_rows = 16
    smem = pl.BlockSpec(memory_space=pltpu.SMEM)
    vmem = pl.BlockSpec(memory_space=pltpu.VMEM)
    return pl.pallas_call(
        empty_kernel,
        out_shape=[
            jax.ShapeDtypeStruct((rows // 8, cols // 128, 32, 128), jnp.float32),
            jax.ShapeDtypeStruct((rows * cols // 128, depth, 128), porosity.dtype),
        ],
        in_specs=[smem, smem, pl.BlockSpec(memory_space=pl.ANY)],
        out_specs=[vmem, vmem],
        scratch_shapes=[
            pltpu.VMEM((2, depth, block_rows, cols), porosity.dtype),
            pltpu.VMEM((depth * block_rows, 128), jnp.float32),
            pltpu.SemaphoreType.DMA((2,)),
        ],
        compiler_params=pltpu.CompilerParams(vmem_limit_bytes=EMPTY_LIMIT),
        cost_estimate=pl.CostEstimate(
            flops=20 * depth * rows * cols,
            bytes_accessed=4 * depth * rows * cols + 16 * rows * cols,
            transcendentals=4 * depth * rows * cols,
        ),
        name="march_empty",
    )(extinction, color_weights, porosity)


def grain_kernel(
    dev_ref, ext_ref, col_ref, nowhere, por_hbm, part_hbm, got_ref, *refs, slots, gy_bits
):
    keep_refs, send_refs = refs[: len(CHUNKS)], refs[len(CHUNKS) : 2 * len(CHUNKS)]
    por_ref, part, sems, *scratch = refs[2 * len(CHUNKS) :]
    fetches = [
        pltpu.make_async_copy(part_hbm, part, sems.at[0]),
        pltpu.make_async_copy(por_hbm, por_ref, sems.at[1]),
    ]
    for fetch in fetches:
        fetch.start()
    heads, earlier, deeper, *_ = scratch
    found = plan_tiles(nowhere, got_ref, *scratch, slots)
    for fetch in fetches:
        fetch.wait()
    own_x = dev_ref[0] & 1
    gx = dev_ref[0] >> gy_bits
    col_bits = bits_of(part.shape[1])
    base = -LOG2E * ext_ref[0]
    slope = LOG2E * ext_ref[0]
    grain_slope = -LOG2E * ext_ref[1]
    depth_of = lax.broadcasted_iota(jnp.int32, (8, 128), 0)

    def running(value):
        for shift in (1, 2, 4):
            value = value + jnp.where(depth_of >= shift, pltpu.roll(value, shift, 0), 0.0)
        return value

    def some_tiles(batch, carry):
        work = []
        for place in range(UNROLL):
            code = heads[batch * UNROLL + place]
            entry = code & 65535

            def add_earlier(_, state):
                at, total = state
                at = earlier[at]
                return at, total + got_ref[at].astype(jnp.float32)

            grain = got_ref[entry].astype(jnp.float32)
            _, grain = lax.fori_loop(0, deeper[entry], add_earlier, (entry, grain))
            work.append((code >> 16, grain))
        for tile, grain in work:
            porous = por_ref[tile].astype(jnp.float32)
            exponent = (base + slope * porous) + grain_slope * grain
            front = running(exponent[:8])
            back = running(exponent[8:]) + front[7:8]
            optical = jnp.concatenate([front, back], axis=0)
            weight = jnp.exp2(optical - exponent) - jnp.exp2(optical)
            alpha = 1.0 - jnp.exp2(back[7:8])
            results = []
            for c in range(3):
                half_logit = (
                    (0.5 * col_ref[c, 0]) * porous
                    + (0.5 * col_ref[c, 1]) * grain
                    + 0.5 * col_ref[c, 2]
                )
                shaded = weight * jnp.tanh(half_logit)
                total = jnp.sum(shaded[:8] + shaded[8:], axis=0, keepdims=True)
                results.append(0.5 * (alpha + total))
            results.append(alpha)
            group, row = tile >> (3 + col_bits), (tile >> col_bits) & 7
            col = tile & ((1 << col_bits) - 1)
            for c in range(4):
                part[group, col, pl.ds(c * 8 + row, 1), :] = results[c]
        return carry

    lax.fori_loop(0, (found + UNROLL - 1) >> bits_of(UNROLL), some_tiles, 0)

    for flips, keep_ref, send_ref in zip(CHUNKS, keep_refs, send_refs):
        pairs = send_ref.shape[0] // len(flips)
        for piece, flip in enumerate(flips):
            first = (gx ^ flip) * 2 * pairs

            def split(pair, carry):
                group = first + 2 * pair
                send_ref[piece * pairs + pair] = part[group + 1 - own_x].astype(jnp.bfloat16)
                keep_ref[piece * pairs + pair] = part[group + own_x]
                return carry

            lax.fori_loop(0, pairs, split, 0)


def march_grain(got, porous_tiles, part, dev, extinction, color_weights, slots, width_x, width_y):
    smem = pl.BlockSpec(memory_space=pltpu.SMEM)
    vmem = pl.BlockSpec(memory_space=pltpu.VMEM)
    entries = got.shape[0]
    sources = entries // (slots + 1)
    tile_count = porous_tiles.shape[0]
    pairs = part.shape[0] // width_x // 2
    split = [(len(flips) * pairs,) + part.shape[1:] for flips in CHUNKS]
    outs = pl.pallas_call(
        functools.partial(grain_kernel, slots=slots, gy_bits=bits_of(width_y)),
        out_shape=[jax.ShapeDtypeStruct(shape, jnp.float32) for shape in split]
        + [jax.ShapeDtypeStruct(shape, jnp.bfloat16) for shape in split],
        in_specs=[smem] * 3 + [pl.BlockSpec(memory_space=pltpu.HBM)] * 3 + [vmem],
        out_specs=[vmem] * (2 * len(CHUNKS)),
        scratch_shapes=[
            pltpu.VMEM(porous_tiles.shape, porous_tiles.dtype),
            pltpu.VMEM(part.shape, part.dtype),
            pltpu.SemaphoreType.DMA((2,)),
            pltpu.SMEM((entries + UNROLL,), jnp.int32),
            pltpu.SMEM((entries,), jnp.int32),
            pltpu.SMEM((entries,), jnp.int32),
            pltpu.VMEM((sources, 128), jnp.int32),
            pltpu.SMEM((sources, 128), jnp.int32),
            pltpu.SMEM((tile_count,), jnp.int32),
            pltpu.SemaphoreType.DMA((2,)),
        ],
        compiler_params=pltpu.CompilerParams(vmem_limit_bytes=GRAIN_LIMIT),
        cost_estimate=pl.CostEstimate(flops=1000, bytes_accessed=1000, transcendentals=0),
        name="march_grain",
    )(
        dev,
        extinction,
        color_weights,
        jnp.full((tile_count,), -1, jnp.int32),
        porous_tiles,
        part,
        got,
    )
    return outs[: len(CHUNKS)], outs[len(CHUNKS) :]


def ordered(mine, theirs, mine_near):
    nearer = [jnp.where(mine_near, a, b) for a, b in zip(mine, theirs)]
    farther = [jnp.where(mine_near, b, a) for a, b in zip(mine, theirs)]
    open_part = 1.0 - nearer[3]
    return [n + open_part * f for n, f in zip(nearer, farther)]


def channels_of(block):
    block = block.astype(jnp.float32)
    rows = block.shape[0] // 4
    return [block[c * rows : (c + 1) * rows] for c in range(4)]


def swap_kernel(dev_ref, rank_ref, mine_ref, got_ref, *out_refs, stage, pieces):
    device = dev_ref[0]
    mine_near = (rank_ref[device] >> stage) & 1 == 0
    low, high = (device >> 1) & 1, (device >> 2) & 1
    piece_groups = got_ref.shape[0] // pieces

    def one_column(col, carry):
        for piece in range(pieces):
            for way, out_ref in enumerate(out_refs):
                for place in range(out_ref.shape[0] // pieces):
                    group = [2 * place + (low ^ way), high ^ way, 0][stage] + piece * piece_groups
                    merged = ordered(
                        channels_of(mine_ref[group, col]),
                        channels_of(got_ref[group, col]),
                        mine_near,
                    )
                    merged = jnp.concatenate(merged, axis=0).astype(out_ref.dtype)
                    out_ref[piece * (out_ref.shape[0] // pieces) + place, col] = merged
        return carry

    lax.fori_loop(0, got_ref.shape[1], one_column, 0)


def swap_rows(mine, got, dev, ranks, stage, pieces):
    smem = pl.BlockSpec(memory_space=pltpu.SMEM)
    vmem = pl.BlockSpec(memory_space=pltpu.VMEM)
    kept = (max(1, got.shape[0] // 2) if stage < 2 else got.shape[0],) + got.shape[1:]
    out_shape = [jax.ShapeDtypeStruct(kept, jnp.float32)]
    if stage < 2:
        out_shape.append(jax.ShapeDtypeStruct(kept, jnp.bfloat16))
    return pl.pallas_call(
        functools.partial(swap_kernel, stage=stage, pieces=pieces),
        out_shape=out_shape,
        in_specs=[smem, smem, vmem, vmem],
        out_specs=[vmem] * len(out_shape),
        compiler_params=pltpu.CompilerParams(vmem_limit_bytes=SMALL_LIMIT),
        cost_estimate=pl.CostEstimate(flops=1000, bytes_accessed=1000, transcendentals=0),
        name=f"swap_rows_{stage}",
    )(dev, ranks, mine, got)


def four_way(device, rank_ref, parts, stride, bit):
    low = (rank_ref[device] >> bit) & 1 == 0
    far_low = (rank_ref[device ^ (2 * stride)] >> bit) & 1 == 0
    high = (rank_ref[device] >> (bit + 1)) & 1 == 0
    return ordered(
        ordered(parts[0], parts[1], low), ordered(parts[2], parts[3], far_low), high
    )


def last_kernel(dev_ref, rank_ref, mine_ref, got_ref, q1, q2, q3, out_ref, *, width_y):
    device = dev_ref[0]
    mine_near = (rank_ref[device] >> 2) & 1 == 0
    col_blocks = mine_ref.shape[1]
    for col in range(col_blocks):
        mine = ordered(channels_of(mine_ref[0, col]), channels_of(got_ref[0, col]), mine_near)
        parts = [mine] + [channels_of(ref[0, col]) for ref in (q1, q2, q3)]
        merged = four_way(device, rank_ref, parts, width_y, bits_of(width_y))
        for c in range(4):
            for row in range(merged[c].shape[0]):
                start = (row * col_blocks + col) * 128
                out_ref[c : c + 1, start : start + 128] = merged[c][row : row + 1]


def last_rows(mine, got, ready, dev, ranks, width_y):
    smem = pl.BlockSpec(memory_space=pltpu.SMEM)
    vmem = pl.BlockSpec(memory_space=pltpu.VMEM)
    return pl.pallas_call(
        functools.partial(last_kernel, width_y=width_y),
        out_shape=jax.ShapeDtypeStruct((4, mine.size // 4), jnp.float32),
        in_specs=[smem, smem] + [vmem] * 5,
        out_specs=vmem,
        compiler_params=pltpu.CompilerParams(vmem_limit_bytes=SMALL_LIMIT),
        name="last_rows",
    )(dev, ranks, mine, got, *ready)


def shards(porosity, grain_blocks, owners, tiles, live_counts, ranks, extinction, color_weights):
    width_x = lax.axis_size("gx")
    width_y = lax.axis_size("gy")
    device_count = width_x * width_y
    block_count = grain_blocks.shape[0]
    slots = max(2, 2 * block_count // device_count)
    dev = lax.axis_index(("gx", "gy")).astype(jnp.int32).reshape(1)
    packed = pack_blocks(grain_blocks, owners[:, 0], tiles, live_counts, device_count, slots)
    got = lax.all_to_all(packed, ("gx", "gy"), split_axis=0, concat_axis=0, tiled=True)
    got = got.reshape((-1,) + got.shape[2:])
    porosity, _ = lax.optimization_barrier((porosity, packed))
    part, porous_tiles = march_empty(porosity, extinction, color_weights)
    got, part, porous_tiles = lax.optimization_barrier((got, part, porous_tiles))
    keeps, sends = march_grain(
        got, porous_tiles, part, dev, extinction, color_weights, slots, width_x, width_y
    )
    ready = [None] * (width_x - 1)
    for flips, mine, send in zip(CHUNKS, keeps, sends):
        got = exchanged(send, "gy", 1)
        for stage in range(2):
            mine, send = swap_rows(mine, got, dev, ranks, stage, len(flips))
            got = exchanged(send, "gy", 2 << stage)
        if flips == (0,):
            return last_rows(mine, got, ready, dev, ranks, width_y)
        (done,) = swap_rows(mine, got, dev, ranks, 2, len(flips))
        for piece, flip in enumerate(flips):
            ready[flip - 1] = exchanged(done[piece : piece + 1], "gx", flip)


def march_flat(porous_flat, grain_flat, extinction, color_weights):
    porous = porous_flat.astype(jnp.float32)
    extinct = extinction[0] * (1.0 - porous) + extinction[1] * grain_flat
    optical = jnp.cumsum(extinct, axis=0)
    before = optical - extinct
    weight = jnp.exp(-before) * (1.0 - jnp.exp(-extinct))
    channels = []
    for channel in range(3):
        colour = jax.nn.sigmoid(
            color_weights[channel, 0] * porous
            + color_weights[channel, 1] * grain_flat
            + color_weights[channel, 2]
        )
        channels.append(jnp.sum(weight * colour, axis=0))
    channels.append(1.0 - jnp.exp(-optical[-1]))
    return jnp.stack(channels, axis=0)


def composite(nearer, farther):
    return nearer + (1.0 - nearer[3:4]) * farther


def shards_any(
    porosity, grain_blocks, owners, tiles, live_counts, ranks, extinction, color_weights
):
    width_x = lax.axis_size("gx")
    width_y = lax.axis_size("gy")
    device_count = width_x * width_y
    depth_cells, image_rows, image_cols = porosity.shape
    block_count, _, block_cols = grain_blocks.shape
    slots = max(2, 2 * block_count // device_count)
    tile_count = image_rows * image_cols // block_cols
    pixel_count = image_rows * image_cols
    block_len = pixel_count // device_count
    packed = pack_blocks(grain_blocks, owners[:, 0], tiles, live_counts, device_count, slots)
    got = lax.all_to_all(packed, ("gx", "gy"), split_axis=0, concat_axis=0, tiled=True)
    coded = got[:, slots, :2, : slots + 1].astype(jnp.int32)
    table = coded[:, 0] * 64 + coded[:, 1]
    used = jnp.arange(slots, dtype=jnp.int32)[None, :] < table[:, slots:]
    got_tile = jnp.where(used, table[:, :slots], tile_count)
    got_data = jnp.where(used[:, :, None, None], got[:, :slots], jnp.bfloat16(0))
    grain_tiles = (
        jnp.zeros((tile_count, depth_cells, block_cols), jnp.float32)
        .at[got_tile.reshape(-1)]
        .add(
            got_data.reshape(device_count * slots, depth_cells, block_cols).astype(jnp.float32),
            mode="drop",
        )
    )
    grain_flat = jnp.transpose(grain_tiles, (1, 0, 2)).reshape(depth_cells, pixel_count)
    porous_flat = porosity.reshape(depth_cells, pixel_count)
    partial_value = march_flat(porous_flat, grain_flat, extinction, color_weights)
    my_rank = ranks[lax.axis_index(("gx", "gy"))]
    bits_y = width_y.bit_length() - 1
    bits_x = width_x.bit_length() - 1
    current = partial_value.reshape(4, width_x, width_y, block_len)
    for axis, dim, bits, first in (("gy", 2, bits_y, 0), ("gx", 1, bits_x, bits_y)):
        for section_bit in range(bits):
            shape = current.shape
            paired = current.reshape(
                shape[:dim] + (shape[dim] // 2, 2) + shape[dim + 1 :]
            )
            own_bit = lax.axis_index(axis) >> section_bit & 1
            kept_half = lax.dynamic_index_in_dim(paired, own_bit, dim + 1, keepdims=False)
            sent_half = lax.dynamic_index_in_dim(paired, 1 - own_bit, dim + 1, keepdims=False)
            partner = exchanged(sent_half, axis, 1 << section_bit)
            nearer_side = my_rank >> first + section_bit & 1 == 0
            current = composite(
                jnp.where(nearer_side, kept_half, partner),
                jnp.where(nearer_side, partner, kept_half),
            )
        if dim == 2:
            current = current.reshape(4, width_x, 1, block_len).reshape(4, width_x, block_len)
    return current.reshape(4, block_len)


def solution(mesh):
    in_specs = (
        P(("gx", "gy"), None, None),
        P(("gx", "gy"), None, None),
        P(("gx", "gy"), None),
        P(("gx", "gy")),
        P(("gx", "gy")),
        P(),
        P(),
        P(),
    )
    out_specs = P(None, ("gx", "gy"))

    def run(porosity, *rest):
        rows = porosity.shape[1] // (mesh.shape["gx"] * mesh.shape["gy"])
        fits = mesh.shape["gx"] == 4 and mesh.shape["gy"] == 8 and rows == 8
        return jax.shard_map(
            shards if fits else shards_any,
            mesh=mesh,
            in_specs=in_specs,
            out_specs=out_specs,
            check_vma=False,
        )(porosity, *rest)

    return run
```

```python
import functools

import jax
import jax.numpy as jnp
from jax import lax
from jax.experimental import pallas as pl
from jax.experimental.pallas import tpu as pltpu
from jax.sharding import PartitionSpec as P

LOG2E = 1.4426950408889634
PACK_LIMIT = 56 * 1024 * 1024
EMPTY_LIMIT = 24 * 1024 * 1024
GRAIN_LIMIT = 47 * 1024 * 1024
SMALL_LIMIT = 8 * 1024 * 1024
UNROLL = 4
KERNELS = (((3, 2),), ((1,), (0,)))


def exchanged(block, axis, distance):
    route = [(low, low ^ distance) for low in range(lax.axis_size(axis))]
    return lax.ppermute(block, axis, route)


def bits_of(size):
    assert size & (size - 1) == 0
    return size.bit_length() - 1


def pack_kernel(
    owner_ref, tile_ref, live_ref, block_ref, out_ref, table, table_vec, table_sem, *, slots
):
    owners_all = out_ref.shape[0]

    def clear(owner, carry):
        table[owner, slots] = 0
        return carry

    lax.fori_loop(0, owners_all, clear, 0)

    def place(index, carry):
        owner = owner_ref[index]
        slot = table[owner, slots]
        table[owner, slots] = slot + 1
        table[owner, slot] = tile_ref[index]
        out_ref[owner, slot] = block_ref[index]
        return carry

    lax.fori_loop(0, live_ref[0], place, 0)
    copy = pltpu.make_async_copy(table, table_vec, table_sem)
    copy.start()
    copy.wait()
    first = lax.broadcasted_iota(jnp.int32, (16, 128), 0) == 0
    for owner in range(owners_all):
        row = jnp.broadcast_to(table_vec[owner : owner + 1, :], (16, 128))
        coded = jnp.where(first, row >> 6, row & 63)
        out_ref[owner, slots] = coded.astype(jnp.float32).astype(jnp.bfloat16)


def pack_blocks(grain_blocks, owner_dev, tiles, live_counts, device_count, slots):
    smem = pl.BlockSpec(memory_space=pltpu.SMEM)
    vmem = pl.BlockSpec(memory_space=pltpu.VMEM)
    return pl.pallas_call(
        functools.partial(pack_kernel, slots=slots),
        out_shape=jax.ShapeDtypeStruct(
            (device_count, slots + 1) + grain_blocks.shape[1:], grain_blocks.dtype
        ),
        in_specs=[smem, smem, smem, vmem],
        out_specs=vmem,
        scratch_shapes=[
            pltpu.SMEM((device_count, 128), jnp.int32),
            pltpu.VMEM((device_count, 128), jnp.int32),
            pltpu.SemaphoreType.DMA(()),
        ],
        compiler_params=pltpu.CompilerParams(vmem_limit_bytes=PACK_LIMIT),
        name="pack_blocks",
    )(owner_dev, tiles, live_counts, grain_blocks)


def plan_tiles(gx, piece_bits, nowhere, got_ref, plan, ids_vec, ids, last, sems, slots):
    heads, earlier, deeper = plan
    sources = ids.shape[0]
    forget = pltpu.make_async_copy(nowhere, last, sems.at[0])
    forget.start()
    for source in range(sources):
        coded = got_ref[source * (slots + 1) + slots].astype(jnp.float32)
        ids_vec[source : source + 1, :] = (coded[0:1, :] * 64.0 + coded[1:2, :]).astype(jnp.int32)
    fetch = pltpu.make_async_copy(ids_vec, ids, sems.at[1])
    fetch.start()
    fetch.wait()
    forget.wait()

    def from_source(source, counts):
        def one(slot, counts):
            tile = ids[source, slot]
            entry = source * (slots + 1) + slot
            kernel = 1 - (((tile >> piece_bits) ^ gx) >> 1)
            before = last[tile]
            fresh = before < 0
            heads[kernel, jnp.where(kernel == 0, counts[0], counts[1])] = entry + (tile << 16)
            last[tile] = jnp.where(fresh, entry, before)
            deeper[entry] = 0

            @pl.when(jnp.logical_not(fresh))
            def _():
                earlier[entry] = earlier[before]
                earlier[before] = entry
                deeper[before] = deeper[before] + 1

            new = jnp.where(fresh, 1, 0)
            return counts[0] + (1 - kernel) * new, counts[1] + kernel * new

        return lax.fori_loop(0, ids[source, slots], one, counts)

    counts = lax.fori_loop(0, sources, from_source, (jnp.int32(0), jnp.int32(0)))

    for kernel, found in enumerate(counts):
        heads[kernel, heads.shape[1] - 1] = found

        @pl.when(found > 0)
        def _():
            for extra in range(UNROLL - 1):
                heads[kernel, found + extra] = heads[kernel, found - 1]


def empty_kernel(ext_ref, col_ref, por_hbm, part, por_tiles, por, turned, sems):
    depth, rows, cols = por_hbm.shape
    block_rows = por.shape[2]
    half_rows = block_rows // 2
    col_blocks = cols // 128
    steps = rows // block_rows
    base = -LOG2E * ext_ref[0]
    slope = LOG2E * ext_ref[0]

    def fetch(step, slot):
        start = pl.multiple_of(step * block_rows, block_rows)
        return pltpu.make_async_copy(
            por_hbm.at[:, pl.ds(start, block_rows), :], por.at[slot], sems.at[slot]
        )

    fetch(0, 0).start()

    def one_step(step, carry):
        slot = lax.rem(step, 2)

        @pl.when(step + 1 < steps)
        def _():
            fetch(step + 1, 1 - slot).start()

        fetch(step, slot).wait()

        def one_column(col, carry):
            lanes = pl.ds(pl.multiple_of(col * 128, 128), 128)
            clear = jnp.ones((block_rows, 128), jnp.float32)
            sums = [jnp.zeros((block_rows, 128), jnp.float32) for _ in range(3)]
            for z in range(depth):
                porous = por[slot, z, :, lanes].astype(jnp.float32)
                turned[z * block_rows : (z + 1) * block_rows, :] = porous
                passed = clear * jnp.exp2(base + slope * porous)
                weight = clear - passed
                clear = passed
                for c in range(3):
                    half_logit = (0.5 * col_ref[c, 0]) * porous + 0.5 * col_ref[c, 2]
                    sums[c] = sums[c] + weight * jnp.tanh(half_logit)
            for row in range(block_rows):
                tile = (step * block_rows + row) * col_blocks + col
                por_tiles[tile] = turned[pl.ds(row, depth, stride=block_rows), :].astype(
                    jnp.bfloat16
                )
            alpha = 1.0 - clear
            parts = [0.5 * (alpha + total) for total in sums] + [alpha]
            for c in range(4):
                for half in range(2):
                    part[2 * step + half, col, c * half_rows : (c + 1) * half_rows, :] = parts[c][
                        half * half_rows : (half + 1) * half_rows
                    ]
            return carry

        lax.fori_loop(0, col_blocks, one_column, 0)
        return carry

    lax.fori_loop(0, steps, one_step, 0)


def march_empty(porosity, extinction, color_weights):
    depth, rows, cols = porosity.shape
    block_rows = 16
    smem = pl.BlockSpec(memory_space=pltpu.SMEM)
    vmem = pl.BlockSpec(memory_space=pltpu.VMEM)
    return pl.pallas_call(
        empty_kernel,
        out_shape=[
            jax.ShapeDtypeStruct((rows // 8, cols // 128, 32, 128), jnp.float32),
            jax.ShapeDtypeStruct((rows * cols // 128, depth, 128), porosity.dtype),
        ],
        in_specs=[smem, smem, pl.BlockSpec(memory_space=pl.ANY)],
        out_specs=[vmem, vmem],
        scratch_shapes=[
            pltpu.VMEM((2, depth, block_rows, cols), porosity.dtype),
            pltpu.VMEM((depth * block_rows, 128), jnp.float32),
            pltpu.SemaphoreType.DMA((2,)),
        ],
        compiler_params=pltpu.CompilerParams(vmem_limit_bytes=EMPTY_LIMIT),
        cost_estimate=pl.CostEstimate(
            flops=20 * depth * rows * cols,
            bytes_accessed=4 * depth * rows * cols + 16 * rows * cols,
            transcendentals=4 * depth * rows * cols,
        ),
        name="march_empty",
    )(extinction, color_weights, porosity)


def grain_kernel(dev_ref, ext_ref, col_ref, *refs, kernel, slots, gy_bits):
    chunks = KERNELS[kernel]
    if kernel == 0:
        nowhere, *refs = refs
    else:
        plan, refs = refs[:3], refs[3:]
    por_hbm, part_hbm, got_ref, *refs = refs
    keep_refs, send_refs = refs[: len(chunks)], refs[len(chunks) : 2 * len(chunks)]
    refs = refs[2 * len(chunks) :]
    if kernel == 0:
        plan, refs = refs[:3], refs[3:]
    por_ref, part, sems, *scratch = refs
    own_x = dev_ref[0] & 1
    gx = dev_ref[0] >> gy_bits
    col_bits = bits_of(part.shape[2])
    piece_bits = bits_of(por_ref.shape[1])
    fetches = []
    for piece in range(2):
        chunk = gx ^ (piece + 2 * (1 - kernel))
        for place, (hbm, ref) in enumerate(((part_hbm, part), (por_hbm, por_ref))):
            rows = pl.ds(chunk * ref.shape[1], ref.shape[1])
            fetches.append(
                pltpu.make_async_copy(hbm.at[rows], ref.at[piece], sems.at[2 * piece + place])
            )
    for fetch in fetches:
        fetch.start()
    if kernel == 0:
        plan_tiles(gx, piece_bits, nowhere, got_ref, plan, *scratch, slots)
    heads, earlier, deeper = plan
    for fetch in fetches:
        fetch.wait()
    base = -LOG2E * ext_ref[0]
    slope = LOG2E * ext_ref[0]
    grain_slope = -LOG2E * ext_ref[1]
    depth_of = lax.broadcasted_iota(jnp.int32, (8, 128), 0)

    def running(value):
        for shift in (1, 2, 4):
            value = value + jnp.where(depth_of >= shift, pltpu.roll(value, shift, 0), 0.0)
        return value

    def some_tiles(batch, carry):
        work = []
        for place in range(UNROLL):
            code = heads[kernel, batch * UNROLL + place]
            entry = code & 65535

            def add_earlier(_, state):
                at, total = state
                at = earlier[at]
                return at, total + got_ref[at].astype(jnp.float32)

            grain = got_ref[entry].astype(jnp.float32)
            _, grain = lax.fori_loop(0, deeper[entry], add_earlier, (entry, grain))
            work.append((code >> 16, grain))
        for tile, grain in work:
            piece = ((tile >> piece_bits) ^ gx) & 1
            tile = tile & ((1 << piece_bits) - 1)
            porous = por_ref[piece, tile].astype(jnp.float32)
            exponent = (base + slope * porous) + grain_slope * grain
            front = running(exponent[:8])
            back = running(exponent[8:]) + front[7:8]
            optical = jnp.concatenate([front, back], axis=0)
            weight = jnp.exp2(optical - exponent) - jnp.exp2(optical)
            alpha = 1.0 - jnp.exp2(back[7:8])
            results = []
            for c in range(3):
                half_logit = (
                    (0.5 * col_ref[c, 0]) * porous
                    + (0.5 * col_ref[c, 1]) * grain
                    + 0.5 * col_ref[c, 2]
                )
                shaded = weight * jnp.tanh(half_logit)
                total = jnp.sum(shaded[:8] + shaded[8:], axis=0, keepdims=True)
                results.append(0.5 * (alpha + total))
            results.append(alpha)
            group, row = tile >> (3 + col_bits), (tile >> col_bits) & 7
            col = tile & ((1 << col_bits) - 1)
            for c in range(4):
                part[piece, group, col, pl.ds(c * 8 + row, 1), :] = results[c]
        return carry

    found = heads[kernel, heads.shape[1] - 1]
    lax.fori_loop(0, (found + UNROLL - 1) >> bits_of(UNROLL), some_tiles, 0)

    pairs = part.shape[1] // 2
    for flips, keep_ref, send_ref in zip(chunks, keep_refs, send_refs):
        for place, flip in enumerate(flips):

            def split(pair, carry):
                at = place * pairs + pair
                send_ref[at] = part[flip & 1, 2 * pair + 1 - own_x].astype(jnp.bfloat16)
                keep_ref[at] = part[flip & 1, 2 * pair + own_x]
                return carry

            lax.fori_loop(0, pairs, split, 0)


def march_grain(kernel, plan, got, porous_tiles, part, dev, extinction, color_weights, slots, mesh):
    width_x, width_y = mesh
    chunks = KERNELS[kernel]
    smem = pl.BlockSpec(memory_space=pltpu.SMEM)
    vmem = pl.BlockSpec(memory_space=pltpu.VMEM)
    hbm = pl.BlockSpec(memory_space=pltpu.HBM)
    entries = got.shape[0]
    sources = entries // (slots + 1)
    tile_count = porous_tiles.shape[0]
    groups = part.shape[0] // width_x
    split = [(len(flips) * groups // 2,) + part.shape[1:] for flips in chunks]
    scratch = [
        pltpu.VMEM((2, tile_count // width_x) + porous_tiles.shape[1:], porous_tiles.dtype),
        pltpu.VMEM((2, groups) + part.shape[1:], part.dtype),
        pltpu.SemaphoreType.DMA((4,)),
    ]
    plan_shapes = []
    if kernel == 0:
        most = -(-(entries + UNROLL + 1) // 128) * 128
        plan_shapes = [
            jax.ShapeDtypeStruct((2, most), jnp.int32),
            jax.ShapeDtypeStruct((entries,), jnp.int32),
            jax.ShapeDtypeStruct((entries,), jnp.int32),
        ]
        scratch += [
            pltpu.VMEM((sources, 128), jnp.int32),
            pltpu.SMEM((sources, 128), jnp.int32),
            pltpu.SMEM((tile_count,), jnp.int32),
            pltpu.SemaphoreType.DMA((2,)),
        ]
        before, before_specs = [jnp.full((tile_count,), -1, jnp.int32)], [hbm]
    else:
        before, before_specs = plan, [smem] * 3
    outs = pl.pallas_call(
        functools.partial(grain_kernel, kernel=kernel, slots=slots, gy_bits=bits_of(width_y)),
        out_shape=[jax.ShapeDtypeStruct(shape, jnp.float32) for shape in split]
        + [jax.ShapeDtypeStruct(shape, jnp.bfloat16) for shape in split]
        + plan_shapes,
        in_specs=[smem] * 3 + before_specs + [hbm] * 2 + [vmem],
        out_specs=[vmem] * (2 * len(chunks)) + [smem] * len(plan_shapes),
        scratch_shapes=scratch,
        compiler_params=pltpu.CompilerParams(vmem_limit_bytes=GRAIN_LIMIT),
        cost_estimate=pl.CostEstimate(flops=1000, bytes_accessed=1000, transcendentals=0),
        name=f"march_grain_{kernel}",
    )(dev, extinction, color_weights, *before, porous_tiles, part, got)
    keeps, sends = outs[: len(chunks)], outs[len(chunks) : 2 * len(chunks)]
    return list(zip(chunks, keeps, sends)), outs[2 * len(chunks) :]


def ordered(mine, theirs, mine_near):
    nearer = [jnp.where(mine_near, a, b) for a, b in zip(mine, theirs)]
    farther = [jnp.where(mine_near, b, a) for a, b in zip(mine, theirs)]
    open_part = 1.0 - nearer[3]
    return [n + open_part * f for n, f in zip(nearer, farther)]


def channels_of(block):
    block = block.astype(jnp.float32)
    rows = block.shape[0] // 4
    return [block[c * rows : (c + 1) * rows] for c in range(4)]


def swap_kernel(dev_ref, rank_ref, mine_ref, got_ref, *out_refs, stage, pieces):
    device = dev_ref[0]
    mine_near = (rank_ref[device] >> stage) & 1 == 0
    low, high = (device >> 1) & 1, (device >> 2) & 1
    piece_groups = got_ref.shape[0] // pieces

    def one_column(col, carry):
        for piece in range(pieces):
            for way, out_ref in enumerate(out_refs):
                for place in range(out_ref.shape[0] // pieces):
                    group = [2 * place + (low ^ way), high ^ way, 0][stage] + piece * piece_groups
                    merged = ordered(
                        channels_of(mine_ref[group, col]),
                        channels_of(got_ref[group, col]),
                        mine_near,
                    )
                    merged = jnp.concatenate(merged, axis=0).astype(out_ref.dtype)
                    out_ref[piece * (out_ref.shape[0] // pieces) + place, col] = merged
        return carry

    lax.fori_loop(0, got_ref.shape[1], one_column, 0)


def swap_rows(mine, got, dev, ranks, stage, pieces):
    smem = pl.BlockSpec(memory_space=pltpu.SMEM)
    vmem = pl.BlockSpec(memory_space=pltpu.VMEM)
    kept = (max(1, got.shape[0] // 2) if stage < 2 else got.shape[0],) + got.shape[1:]
    out_shape = [jax.ShapeDtypeStruct(kept, jnp.float32)]
    if stage < 2:
        out_shape.append(jax.ShapeDtypeStruct(kept, jnp.bfloat16))
    return pl.pallas_call(
        functools.partial(swap_kernel, stage=stage, pieces=pieces),
        out_shape=out_shape,
        in_specs=[smem, smem, vmem, vmem],
        out_specs=[vmem] * len(out_shape),
        compiler_params=pltpu.CompilerParams(vmem_limit_bytes=SMALL_LIMIT),
        cost_estimate=pl.CostEstimate(flops=1000, bytes_accessed=1000, transcendentals=0),
        name=f"swap_rows_{stage}",
    )(dev, ranks, mine, got)


def four_way(device, rank_ref, parts, stride, bit):
    low = (rank_ref[device] >> bit) & 1 == 0
    far_low = (rank_ref[device ^ (2 * stride)] >> bit) & 1 == 0
    high = (rank_ref[device] >> (bit + 1)) & 1 == 0
    return ordered(
        ordered(parts[0], parts[1], low), ordered(parts[2], parts[3], far_low), high
    )


def last_kernel(dev_ref, rank_ref, mine_ref, got_ref, q1, q2, q3, out_ref, *, width_y):
    device = dev_ref[0]
    mine_near = (rank_ref[device] >> 2) & 1 == 0
    col_blocks = mine_ref.shape[1]
    for col in range(col_blocks):
        mine = ordered(channels_of(mine_ref[0, col]), channels_of(got_ref[0, col]), mine_near)
        parts = [mine] + [channels_of(ref[0, col]) for ref in (q1, q2, q3)]
        merged = four_way(device, rank_ref, parts, width_y, bits_of(width_y))
        for c in range(4):
            for row in range(merged[c].shape[0]):
                start = (row * col_blocks + col) * 128
                out_ref[c : c + 1, start : start + 128] = merged[c][row : row + 1]


def last_rows(mine, got, ready, dev, ranks, width_y):
    smem = pl.BlockSpec(memory_space=pltpu.SMEM)
    vmem = pl.BlockSpec(memory_space=pltpu.VMEM)
    return pl.pallas_call(
        functools.partial(last_kernel, width_y=width_y),
        out_shape=jax.ShapeDtypeStruct((4, mine.size // 4), jnp.float32),
        in_specs=[smem, smem] + [vmem] * 5,
        out_specs=vmem,
        compiler_params=pltpu.CompilerParams(vmem_limit_bytes=SMALL_LIMIT),
        name="last_rows",
    )(dev, ranks, mine, got, *ready)


def shards(porosity, grain_blocks, owners, tiles, live_counts, ranks, extinction, color_weights):
    width_x = lax.axis_size("gx")
    width_y = lax.axis_size("gy")
    device_count = width_x * width_y
    block_count = grain_blocks.shape[0]
    slots = max(2, 2 * block_count // device_count)
    dev = lax.axis_index(("gx", "gy")).astype(jnp.int32).reshape(1)
    packed = pack_blocks(grain_blocks, owners[:, 0], tiles, live_counts, device_count, slots)
    got = lax.all_to_all(packed, ("gx", "gy"), split_axis=0, concat_axis=0, tiled=True)
    got = got.reshape((-1,) + got.shape[2:])
    porosity, _ = lax.optimization_barrier((porosity, packed))
    part, porous_tiles = march_empty(porosity, extinction, color_weights)
    got, part, porous_tiles = lax.optimization_barrier((got, part, porous_tiles))
    work, plan = [], None
    for kernel in range(len(KERNELS)):
        made, planned = march_grain(
            kernel,
            plan,
            got,
            porous_tiles,
            part,
            dev,
            extinction,
            color_weights,
            slots,
            (width_x, width_y),
        )
        plan = plan or planned
        for flips, keep, send in made:
            work.append((flips, keep, exchanged(send, "gy", 1)))
    ready = [None] * (width_x - 1)
    for flips, mine, got in work:
        for stage in range(2):
            mine, send = swap_rows(mine, got, dev, ranks, stage, len(flips))
            got = exchanged(send, "gy", 2 << stage)
        if flips == (0,):
            return last_rows(mine, got, ready, dev, ranks, width_y)
        (done,) = swap_rows(mine, got, dev, ranks, 2, len(flips))
        for piece, flip in enumerate(flips):
            ready[flip - 1] = exchanged(done[piece : piece + 1], "gx", flip)


def march_flat(porous_flat, grain_flat, extinction, color_weights):
    porous = porous_flat.astype(jnp.float32)
    extinct = extinction[0] * (1.0 - porous) + extinction[1] * grain_flat
    optical = jnp.cumsum(extinct, axis=0)
    before = optical - extinct
    weight = jnp.exp(-before) * (1.0 - jnp.exp(-extinct))
    channels = []
    for channel in range(3):
        colour = jax.nn.sigmoid(
            color_weights[channel, 0] * porous
            + color_weights[channel, 1] * grain_flat
            + color_weights[channel, 2]
        )
        channels.append(jnp.sum(weight * colour, axis=0))
    channels.append(1.0 - jnp.exp(-optical[-1]))
    return jnp.stack(channels, axis=0)


def composite(nearer, farther):
    return nearer + (1.0 - nearer[3:4]) * farther


def shards_any(
    porosity, grain_blocks, owners, tiles, live_counts, ranks, extinction, color_weights
):
    width_x = lax.axis_size("gx")
    width_y = lax.axis_size("gy")
    device_count = width_x * width_y
    depth_cells, image_rows, image_cols = porosity.shape
    block_count, _, block_cols = grain_blocks.shape
    slots = max(2, 2 * block_count // device_count)
    tile_count = image_rows * image_cols // block_cols
    pixel_count = image_rows * image_cols
    block_len = pixel_count // device_count
    packed = pack_blocks(grain_blocks, owners[:, 0], tiles, live_counts, device_count, slots)
    got = lax.all_to_all(packed, ("gx", "gy"), split_axis=0, concat_axis=0, tiled=True)
    coded = got[:, slots, :2, : slots + 1].astype(jnp.int32)
    table = coded[:, 0] * 64 + coded[:, 1]
    used = jnp.arange(slots, dtype=jnp.int32)[None, :] < table[:, slots:]
    got_tile = jnp.where(used, table[:, :slots], tile_count)
    got_data = jnp.where(used[:, :, None, None], got[:, :slots], jnp.bfloat16(0))
    grain_tiles = (
        jnp.zeros((tile_count, depth_cells, block_cols), jnp.float32)
        .at[got_tile.reshape(-1)]
        .add(
            got_data.reshape(device_count * slots, depth_cells, block_cols).astype(jnp.float32),
            mode="drop",
        )
    )
    grain_flat = jnp.transpose(grain_tiles, (1, 0, 2)).reshape(depth_cells, pixel_count)
    porous_flat = porosity.reshape(depth_cells, pixel_count)
    partial_value = march_flat(porous_flat, grain_flat, extinction, color_weights)
    my_rank = ranks[lax.axis_index(("gx", "gy"))]
    bits_y = width_y.bit_length() - 1
    bits_x = width_x.bit_length() - 1
    current = partial_value.reshape(4, width_x, width_y, block_len)
    for axis, dim, bits, first in (("gy", 2, bits_y, 0), ("gx", 1, bits_x, bits_y)):
        for section_bit in range(bits):
            shape = current.shape
            paired = current.reshape(
                shape[:dim] + (shape[dim] // 2, 2) + shape[dim + 1 :]
            )
            own_bit = lax.axis_index(axis) >> section_bit & 1
            kept_half = lax.dynamic_index_in_dim(paired, own_bit, dim + 1, keepdims=False)
            sent_half = lax.dynamic_index_in_dim(paired, 1 - own_bit, dim + 1, keepdims=False)
            partner = exchanged(sent_half, axis, 1 << section_bit)
            nearer_side = my_rank >> first + section_bit & 1 == 0
            current = composite(
                jnp.where(nearer_side, kept_half, partner),
                jnp.where(nearer_side, partner, kept_half),
            )
        if dim == 2:
            current = current.reshape(4, width_x, 1, block_len).reshape(4, width_x, block_len)
    return current.reshape(4, block_len)


def solution(mesh):
    in_specs = (
        P(("gx", "gy"), None, None),
        P(("gx", "gy"), None, None),
        P(("gx", "gy"), None),
        P(("gx", "gy")),
        P(("gx", "gy")),
        P(),
        P(),
        P(),
    )
    out_specs = P(None, ("gx", "gy"))

    def run(porosity, *rest):
        rows = porosity.shape[1] // (mesh.shape["gx"] * mesh.shape["gy"])
        fits = mesh.shape["gx"] == 4 and mesh.shape["gy"] == 8 and rows == 8
        return jax.shard_map(
            shards if fits else shards_any,
            mesh=mesh,
            in_specs=in_specs,
            out_specs=out_specs,
            check_vma=False,
        )(porosity, *rest)

    return run
```

```python
import functools

import jax
import jax.numpy as jnp
from jax import lax
from jax.experimental import pallas as pl
from jax.experimental.pallas import tpu as pltpu
from jax.sharding import PartitionSpec as P

LOG2E = 1.4426950408889634
PACK_LIMIT = 56 * 1024 * 1024
EMPTY_LIMIT = 24 * 1024 * 1024
GRAIN_LIMIT = 47 * 1024 * 1024
SMALL_LIMIT = 8 * 1024 * 1024
UNROLL = 4
KERNELS = (((3, 2),), ((1,), (0,)))
ORDER = ((3, 0), (2, 0), (3, 1), (1, 0), (2, 1), (3, 2), (0, 0), (1, 1), (2, 2), (1, 2), (0, 1), (0, 2))


def exchanged(block, axis, distance):
    route = [(low, low ^ distance) for low in range(lax.axis_size(axis))]
    return lax.ppermute(block, axis, route)


def bits_of(size):
    assert size & (size - 1) == 0
    return size.bit_length() - 1


def pack_kernel(
    owner_ref, tile_ref, live_ref, block_ref, out_ref, table, table_vec, table_sem, *, slots
):
    owners_all = out_ref.shape[0]

    def clear(owner, carry):
        table[owner, slots] = 0
        return carry

    lax.fori_loop(0, owners_all, clear, 0)

    def place(index, carry):
        owner = owner_ref[index]
        slot = table[owner, slots]
        table[owner, slots] = slot + 1
        table[owner, slot] = tile_ref[index]
        out_ref[owner, slot] = block_ref[index]
        return carry

    lax.fori_loop(0, live_ref[0], place, 0)
    copy = pltpu.make_async_copy(table, table_vec, table_sem)
    copy.start()
    copy.wait()
    first = lax.broadcasted_iota(jnp.int32, (16, 128), 0) == 0
    for owner in range(owners_all):
        row = jnp.broadcast_to(table_vec[owner : owner + 1, :], (16, 128))
        coded = jnp.where(first, row >> 6, row & 63)
        out_ref[owner, slots] = coded.astype(jnp.float32).astype(jnp.bfloat16)


def pack_blocks(grain_blocks, owner_dev, tiles, live_counts, device_count, slots):
    smem = pl.BlockSpec(memory_space=pltpu.SMEM)
    vmem = pl.BlockSpec(memory_space=pltpu.VMEM)
    return pl.pallas_call(
        functools.partial(pack_kernel, slots=slots),
        out_shape=jax.ShapeDtypeStruct(
            (device_count, slots + 1) + grain_blocks.shape[1:], grain_blocks.dtype
        ),
        in_specs=[smem, smem, smem, vmem],
        out_specs=vmem,
        scratch_shapes=[
            pltpu.SMEM((device_count, 128), jnp.int32),
            pltpu.VMEM((device_count, 128), jnp.int32),
            pltpu.SemaphoreType.DMA(()),
        ],
        compiler_params=pltpu.CompilerParams(vmem_limit_bytes=PACK_LIMIT),
        name="pack_blocks",
    )(owner_dev, tiles, live_counts, grain_blocks)


def plan_tiles(gx, piece_bits, nowhere, got_ref, plan, ids_vec, ids, last, sems, slots):
    heads, earlier = plan
    sources = ids.shape[0]
    forget = pltpu.make_async_copy(nowhere, last, sems.at[0])
    forget.start()
    for source in range(sources):
        coded = got_ref[source * (slots + 1) + slots].astype(jnp.float32)
        ids_vec[source : source + 1, :] = (coded[0:1, :] * 64.0 + coded[1:2, :]).astype(jnp.int32)
    fetch = pltpu.make_async_copy(ids_vec, ids, sems.at[1])
    fetch.start()
    fetch.wait()
    forget.wait()

    def from_source(source, counts):
        def one(slot, counts):
            tile = ids[source, slot]
            entry = source * (slots + 1) + slot
            kernel = 1 - (((tile >> piece_bits) ^ gx) >> 1)
            heads[kernel, jnp.where(kernel == 0, counts[0], counts[1])] = entry + (tile << 16)
            earlier[entry] = last[tile]
            last[tile] = entry
            return counts[0] + 1 - kernel, counts[1] + kernel

        return lax.fori_loop(0, ids[source, slots], one, counts)

    counts = lax.fori_loop(0, sources, from_source, (jnp.int32(0), jnp.int32(0)))

    for kernel, found in enumerate(counts):
        heads[kernel, heads.shape[1] - 1] = found

        @pl.when(found > 0)
        def _():
            for extra in range(UNROLL - 1):
                heads[kernel, found + extra] = heads[kernel, found - 1]


def empty_kernel(ext_ref, col_ref, por_hbm, part, por_tiles, por, turned, sems):
    depth, rows, cols = por_hbm.shape
    block_rows = por.shape[2]
    half_rows = block_rows // 2
    col_blocks = cols // 128
    steps = rows // block_rows
    base = -LOG2E * ext_ref[0]
    slope = LOG2E * ext_ref[0]

    def fetch(step, slot):
        start = pl.multiple_of(step * block_rows, block_rows)
        return pltpu.make_async_copy(
            por_hbm.at[:, pl.ds(start, block_rows), :], por.at[slot], sems.at[slot]
        )

    fetch(0, 0).start()

    def one_step(step, carry):
        slot = lax.rem(step, 2)

        @pl.when(step + 1 < steps)
        def _():
            fetch(step + 1, 1 - slot).start()

        fetch(step, slot).wait()

        def one_column(col, carry):
            lanes = pl.ds(pl.multiple_of(col * 128, 128), 128)
            clear = jnp.ones((block_rows, 128), jnp.float32)
            sums = [jnp.zeros((block_rows, 128), jnp.float32) for _ in range(3)]
            for z in range(depth):
                porous = por[slot, z, :, lanes].astype(jnp.float32)
                turned[z * block_rows : (z + 1) * block_rows, :] = porous
                passed = clear * jnp.exp2(base + slope * porous)
                weight = clear - passed
                clear = passed
                for c in range(3):
                    half_logit = (0.5 * col_ref[c, 0]) * porous + 0.5 * col_ref[c, 2]
                    sums[c] = sums[c] + weight * jnp.tanh(half_logit)
            for row in range(block_rows):
                tile = (step * block_rows + row) * col_blocks + col
                por_tiles[tile] = turned[pl.ds(row, depth, stride=block_rows), :].astype(
                    jnp.bfloat16
                )
            alpha = 1.0 - clear
            parts = [0.5 * (alpha + total) for total in sums] + [alpha]
            for c in range(4):
                for half in range(2):
                    part[2 * step + half, col, c * half_rows : (c + 1) * half_rows, :] = parts[c][
                        half * half_rows : (half + 1) * half_rows
                    ]
            return carry

        lax.fori_loop(0, col_blocks, one_column, 0)
        return carry

    lax.fori_loop(0, steps, one_step, 0)


def march_empty(porosity, extinction, color_weights):
    depth, rows, cols = porosity.shape
    block_rows = 16
    smem = pl.BlockSpec(memory_space=pltpu.SMEM)
    vmem = pl.BlockSpec(memory_space=pltpu.VMEM)
    return pl.pallas_call(
        empty_kernel,
        out_shape=[
            jax.ShapeDtypeStruct((rows // 8, cols // 128, 32, 128), jnp.float32),
            jax.ShapeDtypeStruct((rows * cols // 128, depth, 128), porosity.dtype),
        ],
        in_specs=[smem, smem, pl.BlockSpec(memory_space=pl.ANY)],
        out_specs=[vmem, vmem],
        scratch_shapes=[
            pltpu.VMEM((2, depth, block_rows, cols), porosity.dtype),
            pltpu.VMEM((depth * block_rows, 128), jnp.float32),
            pltpu.SemaphoreType.DMA((2,)),
        ],
        compiler_params=pltpu.CompilerParams(vmem_limit_bytes=EMPTY_LIMIT),
        cost_estimate=pl.CostEstimate(
            flops=20 * depth * rows * cols,
            bytes_accessed=4 * depth * rows * cols + 16 * rows * cols,
            transcendentals=4 * depth * rows * cols,
        ),
        name="march_empty",
    )(extinction, color_weights, porosity)


def grain_kernel(dev_ref, ext_ref, col_ref, *refs, kernel, slots, gy_bits):
    chunks = KERNELS[kernel]
    if kernel == 0:
        nowhere, *refs = refs
    else:
        plan, refs = refs[:2], refs[2:]
    por_hbm, part_hbm, got_ref, *refs = refs
    keep_refs, send_refs = refs[: len(chunks)], refs[len(chunks) : 2 * len(chunks)]
    refs = refs[2 * len(chunks) :]
    if kernel == 0:
        plan, refs = refs[:2], refs[2:]
    por_ref, part, sems, *scratch = refs
    own_x = dev_ref[0] & 1
    gx = dev_ref[0] >> gy_bits
    col_bits = bits_of(part.shape[2])
    piece_bits = bits_of(por_ref.shape[1])
    fetches = []
    for piece in range(2):
        chunk = gx ^ (piece + 2 * (1 - kernel))
        for place, (hbm, ref) in enumerate(((part_hbm, part), (por_hbm, por_ref))):
            rows = pl.ds(chunk * ref.shape[1], ref.shape[1])
            fetches.append(
                pltpu.make_async_copy(hbm.at[rows], ref.at[piece], sems.at[2 * piece + place])
            )
    for fetch in fetches:
        fetch.start()
    if kernel == 0:
        plan_tiles(gx, piece_bits, nowhere, got_ref, plan, *scratch, slots)
    heads, earlier = plan
    for fetch in fetches:
        fetch.wait()
    base = -LOG2E * ext_ref[0]
    slope = LOG2E * ext_ref[0]
    grain_slope = -LOG2E * ext_ref[1]
    depth_of = lax.broadcasted_iota(jnp.int32, (8, 128), 0)

    def running(value):
        for shift in (1, 2, 4):
            value = value + jnp.where(depth_of >= shift, pltpu.roll(value, shift, 0), 0.0)
        return value

    def some_tiles(batch, carry):
        work = []
        for place in range(UNROLL):
            code = heads[kernel, batch * UNROLL + place]
            entry = code & 65535

            def add_earlier(state):
                at, total = state
                return earlier[at], total + got_ref[at].astype(jnp.float32)

            grain = got_ref[entry].astype(jnp.float32)
            _, grain = lax.while_loop(
                lambda state: state[0] >= 0, add_earlier, (earlier[entry], grain)
            )
            work.append((code >> 16, grain))
        for tile, grain in work:
            piece = ((tile >> piece_bits) ^ gx) & 1
            tile = tile & ((1 << piece_bits) - 1)
            porous = por_ref[piece, tile].astype(jnp.float32)
            exponent = (base + slope * porous) + grain_slope * grain
            front = running(exponent[:8])
            back = running(exponent[8:]) + front[7:8]
            optical = jnp.concatenate([front, back], axis=0)
            weight = jnp.exp2(optical - exponent) - jnp.exp2(optical)
            alpha = 1.0 - jnp.exp2(back[7:8])
            results = []
            for c in range(3):
                half_logit = (
                    (0.5 * col_ref[c, 0]) * porous
                    + (0.5 * col_ref[c, 1]) * grain
                    + 0.5 * col_ref[c, 2]
                )
                shaded = weight * jnp.tanh(half_logit)
                total = jnp.sum(shaded[:8] + shaded[8:], axis=0, keepdims=True)
                results.append(0.5 * (alpha + total))
            results.append(alpha)
            group, row = tile >> (3 + col_bits), (tile >> col_bits) & 7
            col = tile & ((1 << col_bits) - 1)
            for c in range(4):
                part[piece, group, col, pl.ds(c * 8 + row, 1), :] = results[c]
        return carry

    found = heads[kernel, heads.shape[1] - 1]
    lax.fori_loop(0, (found + UNROLL - 1) >> bits_of(UNROLL), some_tiles, 0)

    pairs = part.shape[1] // 2
    for flips, keep_ref, send_ref in zip(chunks, keep_refs, send_refs):
        for place, flip in enumerate(flips):

            def split(pair, carry):
                at = place * pairs + pair
                send_ref[at] = part[flip & 1, 2 * pair + 1 - own_x].astype(jnp.bfloat16)
                keep_ref[at] = part[flip & 1, 2 * pair + own_x]
                return carry

            lax.fori_loop(0, pairs, split, 0)


def march_grain(kernel, plan, got, porous_tiles, part, dev, extinction, color_weights, slots, mesh):
    width_x, width_y = mesh
    chunks = KERNELS[kernel]
    smem = pl.BlockSpec(memory_space=pltpu.SMEM)
    vmem = pl.BlockSpec(memory_space=pltpu.VMEM)
    hbm = pl.BlockSpec(memory_space=pltpu.HBM)
    entries = got.shape[0]
    sources = entries // (slots + 1)
    tile_count = porous_tiles.shape[0]
    groups = part.shape[0] // width_x
    split = [(len(flips) * groups // 2,) + part.shape[1:] for flips in chunks]
    scratch = [
        pltpu.VMEM((2, tile_count // width_x) + porous_tiles.shape[1:], porous_tiles.dtype),
        pltpu.VMEM((2, groups) + part.shape[1:], part.dtype),
        pltpu.SemaphoreType.DMA((4,)),
    ]
    plan_shapes = []
    if kernel == 0:
        most = -(-(entries + UNROLL + 1) // 128) * 128
        plan_shapes = [
            jax.ShapeDtypeStruct((2, most), jnp.int32),
            jax.ShapeDtypeStruct((entries,), jnp.int32),
        ]
        scratch += [
            pltpu.VMEM((sources, 128), jnp.int32),
            pltpu.SMEM((sources, 128), jnp.int32),
            pltpu.SMEM((tile_count,), jnp.int32),
            pltpu.SemaphoreType.DMA((2,)),
        ]
        before, before_specs = [jnp.full((tile_count,), -1, jnp.int32)], [hbm]
    else:
        before, before_specs = plan, [smem] * 2
    outs = pl.pallas_call(
        functools.partial(grain_kernel, kernel=kernel, slots=slots, gy_bits=bits_of(width_y)),
        out_shape=[jax.ShapeDtypeStruct(shape, jnp.float32) for shape in split]
        + [jax.ShapeDtypeStruct(shape, jnp.bfloat16) for shape in split]
        + plan_shapes,
        in_specs=[smem] * 3 + before_specs + [hbm] * 2 + [vmem],
        out_specs=[vmem] * (2 * len(chunks)) + [smem] * len(plan_shapes),
        scratch_shapes=scratch,
        compiler_params=pltpu.CompilerParams(vmem_limit_bytes=GRAIN_LIMIT),
        cost_estimate=pl.CostEstimate(flops=1000, bytes_accessed=1000, transcendentals=0),
        name=f"march_grain_{kernel}",
    )(dev, extinction, color_weights, *before, porous_tiles, part, got)
    keeps, sends = outs[: len(chunks)], outs[len(chunks) : 2 * len(chunks)]
    return list(zip(chunks, keeps, sends)), outs[2 * len(chunks) :]


def ordered(mine, theirs, mine_near):
    nearer = [jnp.where(mine_near, a, b) for a, b in zip(mine, theirs)]
    farther = [jnp.where(mine_near, b, a) for a, b in zip(mine, theirs)]
    open_part = 1.0 - nearer[3]
    return [n + open_part * f for n, f in zip(nearer, farther)]


def channels_of(block):
    block = block.astype(jnp.float32)
    rows = block.shape[0] // 4
    return [block[c * rows : (c + 1) * rows] for c in range(4)]


def swap_kernel(dev_ref, rank_ref, mine_ref, got_ref, *out_refs, stage, first):
    device = dev_ref[0]
    mine_near = (rank_ref[device] >> stage) & 1 == 0
    low, high = (device >> 1) & 1, (device >> 2) & 1

    def one_column(col, carry):
        for way, out_ref in enumerate(out_refs):
            for place in range(out_ref.shape[0]):
                group = first + [2 * place + (low ^ way), high ^ way, 0][stage]
                merged = ordered(
                    channels_of(mine_ref[group, col]), channels_of(got_ref[group, col]), mine_near
                )
                out_ref[place, col] = jnp.concatenate(merged, axis=0).astype(out_ref.dtype)
        return carry

    lax.fori_loop(0, got_ref.shape[1], one_column, 0)


def swap_rows(mine, got, dev, ranks, stage, first=0):
    smem = pl.BlockSpec(memory_space=pltpu.SMEM)
    vmem = pl.BlockSpec(memory_space=pltpu.VMEM)
    kept = ((2, 1, 1)[stage],) + got.shape[1:]
    out_shape = [jax.ShapeDtypeStruct(kept, jnp.float32)]
    if stage < 2:
        out_shape.append(jax.ShapeDtypeStruct(kept, jnp.bfloat16))
    return pl.pallas_call(
        functools.partial(swap_kernel, stage=stage, first=first),
        out_shape=out_shape,
        in_specs=[smem, smem, vmem, vmem],
        out_specs=[vmem] * len(out_shape),
        compiler_params=pltpu.CompilerParams(vmem_limit_bytes=SMALL_LIMIT),
        cost_estimate=pl.CostEstimate(flops=1000, bytes_accessed=1000, transcendentals=0),
        name=f"swap_rows_{stage}",
    )(dev, ranks, mine, got)


def four_way(device, rank_ref, parts, stride, bit):
    low = (rank_ref[device] >> bit) & 1 == 0
    far_low = (rank_ref[device ^ (2 * stride)] >> bit) & 1 == 0
    high = (rank_ref[device] >> (bit + 1)) & 1 == 0
    return ordered(
        ordered(parts[0], parts[1], low), ordered(parts[2], parts[3], far_low), high
    )


def last_kernel(dev_ref, rank_ref, mine_ref, got_ref, q1, q2, q3, out_ref, *, width_y):
    device = dev_ref[0]
    mine_near = (rank_ref[device] >> 2) & 1 == 0
    col_blocks = mine_ref.shape[1]
    for col in range(col_blocks):
        mine = ordered(channels_of(mine_ref[0, col]), channels_of(got_ref[0, col]), mine_near)
        parts = [mine] + [channels_of(ref[0, col]) for ref in (q1, q2, q3)]
        merged = four_way(device, rank_ref, parts, width_y, bits_of(width_y))
        for c in range(4):
            for row in range(merged[c].shape[0]):
                start = (row * col_blocks + col) * 128
                out_ref[c : c + 1, start : start + 128] = merged[c][row : row + 1]


def last_rows(mine, got, ready, dev, ranks, width_y):
    smem = pl.BlockSpec(memory_space=pltpu.SMEM)
    vmem = pl.BlockSpec(memory_space=pltpu.VMEM)
    return pl.pallas_call(
        functools.partial(last_kernel, width_y=width_y),
        out_shape=jax.ShapeDtypeStruct((4, mine.size // 4), jnp.float32),
        in_specs=[smem, smem] + [vmem] * 5,
        out_specs=vmem,
        compiler_params=pltpu.CompilerParams(vmem_limit_bytes=SMALL_LIMIT),
        name="last_rows",
    )(dev, ranks, mine, got, *ready)


def shards(porosity, grain_blocks, owners, tiles, live_counts, ranks, extinction, color_weights):
    width_x = lax.axis_size("gx")
    width_y = lax.axis_size("gy")
    device_count = width_x * width_y
    block_count = grain_blocks.shape[0]
    slots = max(2, 2 * block_count // device_count)
    dev = lax.axis_index(("gx", "gy")).astype(jnp.int32).reshape(1)
    packed = pack_blocks(grain_blocks, owners[:, 0], tiles, live_counts, device_count, slots)
    got = lax.all_to_all(packed, ("gx", "gy"), split_axis=0, concat_axis=0, tiled=True)
    got = got.reshape((-1,) + got.shape[2:])
    porosity, _ = lax.optimization_barrier((porosity, packed))
    part, porous_tiles = march_empty(porosity, extinction, color_weights)
    got, part, porous_tiles = lax.optimization_barrier((got, part, porous_tiles))
    work, plan = [], None
    for kernel in range(len(KERNELS)):
        made, planned = march_grain(
            kernel,
            plan,
            got,
            porous_tiles,
            part,
            dev,
            extinction,
            color_weights,
            slots,
            (width_x, width_y),
        )
        plan = plan or planned
        for flips, keep, send in made:
            arrived = exchanged(send, "gy", 1)
            for piece, flip in enumerate(flips):
                work.append((flip, piece * keep.shape[0] // len(flips), keep, arrived))
    ready = [None] * (width_x - 1)
    token = work[-1][2]
    state = {flip: (mine, got, first) for flip, first, mine, got in work}
    for flip, stage in ORDER:
        mine, got, first = state[flip]
        got, token = lax.optimization_barrier((got, token))
        if flip == 0 and stage == 2:
            return last_rows(mine, got, ready, dev, ranks, width_y)
        mine, *send = swap_rows(mine, got, dev, ranks, stage, first)
        token = mine
        if stage == 2:
            ready[flip - 1] = exchanged(mine, "gx", flip)
        else:
            state[flip] = mine, exchanged(send[0], "gy", 2 << stage), 0


def march_flat(porous_flat, grain_flat, extinction, color_weights):
    porous = porous_flat.astype(jnp.float32)
    extinct = extinction[0] * (1.0 - porous) + extinction[1] * grain_flat
    optical = jnp.cumsum(extinct, axis=0)
    before = optical - extinct
    weight = jnp.exp(-before) * (1.0 - jnp.exp(-extinct))
    channels = []
    for channel in range(3):
        colour = jax.nn.sigmoid(
            color_weights[channel, 0] * porous
            + color_weights[channel, 1] * grain_flat
            + color_weights[channel, 2]
        )
        channels.append(jnp.sum(weight * colour, axis=0))
    channels.append(1.0 - jnp.exp(-optical[-1]))
    return jnp.stack(channels, axis=0)


def composite(nearer, farther):
    return nearer + (1.0 - nearer[3:4]) * farther


def shards_any(
    porosity, grain_blocks, owners, tiles, live_counts, ranks, extinction, color_weights
):
    width_x = lax.axis_size("gx")
    width_y = lax.axis_size("gy")
    device_count = width_x * width_y
    depth_cells, image_rows, image_cols = porosity.shape
    block_count, _, block_cols = grain_blocks.shape
    slots = max(2, 2 * block_count // device_count)
    tile_count = image_rows * image_cols // block_cols
    pixel_count = image_rows * image_cols
    block_len = pixel_count // device_count
    packed = pack_blocks(grain_blocks, owners[:, 0], tiles, live_counts, device_count, slots)
    got = lax.all_to_all(packed, ("gx", "gy"), split_axis=0, concat_axis=0, tiled=True)
    coded = got[:, slots, :2, : slots + 1].astype(jnp.int32)
    table = coded[:, 0] * 64 + coded[:, 1]
    used = jnp.arange(slots, dtype=jnp.int32)[None, :] < table[:, slots:]
    got_tile = jnp.where(used, table[:, :slots], tile_count)
    got_data = jnp.where(used[:, :, None, None], got[:, :slots], jnp.bfloat16(0))
    grain_tiles = (
        jnp.zeros((tile_count, depth_cells, block_cols), jnp.float32)
        .at[got_tile.reshape(-1)]
        .add(
            got_data.reshape(device_count * slots, depth_cells, block_cols).astype(jnp.float32),
            mode="drop",
        )
    )
    grain_flat = jnp.transpose(grain_tiles, (1, 0, 2)).reshape(depth_cells, pixel_count)
    porous_flat = porosity.reshape(depth_cells, pixel_count)
    partial_value = march_flat(porous_flat, grain_flat, extinction, color_weights)
    my_rank = ranks[lax.axis_index(("gx", "gy"))]
    bits_y = width_y.bit_length() - 1
    bits_x = width_x.bit_length() - 1
    current = partial_value.reshape(4, width_x, width_y, block_len)
    for axis, dim, bits, first in (("gy", 2, bits_y, 0), ("gx", 1, bits_x, bits_y)):
        for section_bit in range(bits):
            shape = current.shape
            paired = current.reshape(
                shape[:dim] + (shape[dim] // 2, 2) + shape[dim + 1 :]
            )
            own_bit = lax.axis_index(axis) >> section_bit & 1
            kept_half = lax.dynamic_index_in_dim(paired, own_bit, dim + 1, keepdims=False)
            sent_half = lax.dynamic_index_in_dim(paired, 1 - own_bit, dim + 1, keepdims=False)
            partner = exchanged(sent_half, axis, 1 << section_bit)
            nearer_side = my_rank >> first + section_bit & 1 == 0
            current = composite(
                jnp.where(nearer_side, kept_half, partner),
                jnp.where(nearer_side, partner, kept_half),
            )
        if dim == 2:
            current = current.reshape(4, width_x, 1, block_len).reshape(4, width_x, block_len)
    return current.reshape(4, block_len)


def solution(mesh):
    in_specs = (
        P(("gx", "gy"), None, None),
        P(("gx", "gy"), None, None),
        P(("gx", "gy"), None),
        P(("gx", "gy")),
        P(("gx", "gy")),
        P(),
        P(),
        P(),
    )
    out_specs = P(None, ("gx", "gy"))

    def run(porosity, *rest):
        rows = porosity.shape[1] // (mesh.shape["gx"] * mesh.shape["gy"])
        fits = mesh.shape["gx"] == 4 and mesh.shape["gy"] == 8 and rows == 8
        return jax.shard_map(
            shards if fits else shards_any,
            mesh=mesh,
            in_specs=in_specs,
            out_specs=out_specs,
            check_vma=False,
        )(porosity, *rest)

    return run
```

```python
import functools

import jax
import jax.numpy as jnp
from jax import lax
from jax.experimental import pallas as pl
from jax.experimental.pallas import tpu as pltpu
from jax.sharding import PartitionSpec as P

LOG2E = 1.4426950408889634
PACK_LIMIT = 56 * 1024 * 1024
EMPTY_LIMIT = 24 * 1024 * 1024
GRAIN_LIMIT = 47 * 1024 * 1024
SMALL_LIMIT = 8 * 1024 * 1024
UNROLL = 4
KERNELS = (((3, 2),), ((1,), (0,)))
ORDER = (
    (3, 0),
    (2, 0),
    (3, 1),
    (1, 0),
    (2, 1),
    (3, 2),
    (1, 1),
    (0, 0),
    (2, 2),
    (1, 2),
    (0, 1),
    (0, 2),
)


def exchanged(block, axis, distance):
    route = [(low, low ^ distance) for low in range(lax.axis_size(axis))]
    return lax.ppermute(block, axis, route)


def bits_of(size):
    assert size & (size - 1) == 0
    return size.bit_length() - 1


def pack_kernel(
    owner_ref, tile_ref, live_ref, block_ref, out_ref, table, table_vec, table_sem, *, slots
):
    owners_all = out_ref.shape[0]

    def clear(owner, carry):
        table[owner, slots] = 0
        return carry

    lax.fori_loop(0, owners_all, clear, 0)

    def place(index, carry):
        owner = owner_ref[index]
        slot = table[owner, slots]
        table[owner, slots] = slot + 1
        table[owner, slot] = tile_ref[index]
        out_ref[owner, slot] = block_ref[index]
        return carry

    lax.fori_loop(0, live_ref[0], place, 0)
    copy = pltpu.make_async_copy(table, table_vec, table_sem)
    copy.start()
    copy.wait()
    first = lax.broadcasted_iota(jnp.int32, (16, 128), 0) == 0
    for owner in range(owners_all):
        row = jnp.broadcast_to(table_vec[owner : owner + 1, :], (16, 128))
        coded = jnp.where(first, row >> 6, row & 63)
        out_ref[owner, slots] = coded.astype(jnp.float32).astype(jnp.bfloat16)


def pack_blocks(grain_blocks, owner_dev, tiles, live_counts, device_count, slots):
    smem = pl.BlockSpec(memory_space=pltpu.SMEM)
    vmem = pl.BlockSpec(memory_space=pltpu.VMEM)
    return pl.pallas_call(
        functools.partial(pack_kernel, slots=slots),
        out_shape=jax.ShapeDtypeStruct(
            (device_count, slots + 1) + grain_blocks.shape[1:], grain_blocks.dtype
        ),
        in_specs=[smem, smem, smem, vmem],
        out_specs=vmem,
        scratch_shapes=[
            pltpu.SMEM((device_count, 128), jnp.int32),
            pltpu.VMEM((device_count, 128), jnp.int32),
            pltpu.SemaphoreType.DMA(()),
        ],
        compiler_params=pltpu.CompilerParams(vmem_limit_bytes=PACK_LIMIT),
        name="pack_blocks",
    )(owner_dev, tiles, live_counts, grain_blocks)


def plan_tiles(gx, piece_bits, nowhere, got_ref, plan, ids_vec, ids, last, sems, slots):
    heads, again, earlier = plan
    nowhere_tile = last.shape[0] - 1
    sources = ids.shape[0]
    forget = pltpu.make_async_copy(nowhere, last.at[pl.ds(0, nowhere.shape[0])], sems.at[0])
    forget.start()
    for source in range(sources):
        coded = got_ref[source * (slots + 1) + slots].astype(jnp.float32)
        ids_vec[source : source + 1, :] = (coded[0:1, :] * 64.0 + coded[1:2, :]).astype(jnp.int32)
    fetch = pltpu.make_async_copy(ids_vec, ids, sems.at[1])
    fetch.start()
    last[nowhere_tile] = -1
    fetch.wait()
    forget.wait()

    def from_source(source, counts):
        live = ids[source, slots]

        def some(batch, counts):
            count = list(counts)
            found = []
            for place in range(UNROLL):
                slot = batch * UNROLL + place
                entry = source * (slots + 1) + slot
                valid = slot < live
                tile = jnp.where(valid, ids[source, slot], nowhere_tile)
                before = last[tile]
                last[tile] = entry
                found.append((entry, tile, valid, before))
            for entry, tile, valid, before in found:
                earlier[entry] = before
                code = entry + (tile << 16)
                kernel = 1 - (((tile >> piece_bits) ^ gx) >> 1) & 1
                heads[kernel, jnp.where(kernel == 0, count[0], count[1])] = code
                again[kernel, jnp.where(kernel == 0, count[2], count[3])] = code
                one = jnp.where(valid, 1, 0)
                more = jnp.where(jnp.logical_and(valid, before >= 0), 1, 0)
                count[0] = count[0] + (1 - kernel) * one
                count[1] = count[1] + kernel * one
                count[2] = count[2] + (1 - kernel) * more
                count[3] = count[3] + kernel * more
            return tuple(count)

        return lax.fori_loop(0, (live + UNROLL - 1) >> bits_of(UNROLL), some, counts)

    counts = lax.fori_loop(0, sources, from_source, (jnp.int32(0),) * 4)

    for kernel in range(2):
        found = counts[kernel]
        heads[kernel, heads.shape[1] - 1] = found
        again[kernel, heads.shape[1] - 1] = counts[2 + kernel]

        @pl.when(found > 0)
        def _():
            for extra in range(UNROLL - 1):
                heads[kernel, found + extra] = heads[kernel, found - 1]


def empty_kernel(ext_ref, col_ref, por_hbm, part, por_tiles, por, turned, sems):
    depth, rows, cols = por_hbm.shape
    block_rows = por.shape[2]
    half_rows = block_rows // 2
    col_blocks = cols // 128
    steps = rows // block_rows
    base = -LOG2E * ext_ref[0]
    slope = LOG2E * ext_ref[0]

    def fetch(step, slot):
        start = pl.multiple_of(step * block_rows, block_rows)
        return pltpu.make_async_copy(
            por_hbm.at[:, pl.ds(start, block_rows), :], por.at[slot], sems.at[slot]
        )

    fetch(0, 0).start()

    def one_step(step, carry):
        slot = lax.rem(step, 2)

        @pl.when(step + 1 < steps)
        def _():
            fetch(step + 1, 1 - slot).start()

        fetch(step, slot).wait()

        def one_column(col, carry):
            lanes = pl.ds(pl.multiple_of(col * 128, 128), 128)
            clear = jnp.ones((block_rows, 128), jnp.float32)
            sums = [jnp.zeros((block_rows, 128), jnp.float32) for _ in range(3)]
            for z in range(depth):
                porous = por[slot, z, :, lanes].astype(jnp.float32)
                turned[z * block_rows : (z + 1) * block_rows, :] = porous
                passed = clear * jnp.exp2(base + slope * porous)
                weight = clear - passed
                clear = passed
                for c in range(3):
                    half_logit = (0.5 * col_ref[c, 0]) * porous + 0.5 * col_ref[c, 2]
                    sums[c] = sums[c] + weight * jnp.tanh(half_logit)
            for row in range(block_rows):
                tile = (step * block_rows + row) * col_blocks + col
                por_tiles[tile] = turned[pl.ds(row, depth, stride=block_rows), :].astype(
                    jnp.bfloat16
                )
            alpha = 1.0 - clear
            parts = [0.5 * (alpha + total) for total in sums] + [alpha]
            for c in range(4):
                for half in range(2):
                    part[2 * step + half, col, c * half_rows : (c + 1) * half_rows, :] = parts[c][
                        half * half_rows : (half + 1) * half_rows
                    ]
            return carry

        lax.fori_loop(0, col_blocks, one_column, 0)
        return carry

    lax.fori_loop(0, steps, one_step, 0)


def march_empty(porosity, extinction, color_weights):
    depth, rows, cols = porosity.shape
    block_rows = 16
    smem = pl.BlockSpec(memory_space=pltpu.SMEM)
    vmem = pl.BlockSpec(memory_space=pltpu.VMEM)
    return pl.pallas_call(
        empty_kernel,
        out_shape=[
            jax.ShapeDtypeStruct((rows // 8, cols // 128, 32, 128), jnp.float32),
            jax.ShapeDtypeStruct((rows * cols // 128, depth, 128), porosity.dtype),
        ],
        in_specs=[smem, smem, pl.BlockSpec(memory_space=pl.ANY)],
        out_specs=[vmem, vmem],
        scratch_shapes=[
            pltpu.VMEM((2, depth, block_rows, cols), porosity.dtype),
            pltpu.VMEM((depth * block_rows, 128), jnp.float32),
            pltpu.SemaphoreType.DMA((2,)),
        ],
        compiler_params=pltpu.CompilerParams(vmem_limit_bytes=EMPTY_LIMIT),
        cost_estimate=pl.CostEstimate(
            flops=20 * depth * rows * cols,
            bytes_accessed=4 * depth * rows * cols + 16 * rows * cols,
            transcendentals=4 * depth * rows * cols,
        ),
        name="march_empty",
    )(extinction, color_weights, porosity)


def grain_kernel(dev_ref, ext_ref, col_ref, *refs, kernel, slots, gy_bits):
    chunks = KERNELS[kernel]
    if kernel == 0:
        nowhere, *refs = refs
    else:
        plan, refs = refs[:3], refs[3:]
    por_hbm, part_hbm, got_ref, *refs = refs
    keep_refs, send_refs = refs[: len(chunks)], refs[len(chunks) : 2 * len(chunks)]
    refs = refs[2 * len(chunks) :]
    if kernel == 0:
        plan, refs = refs[:3], refs[3:]
    por_ref, part, sems, *scratch = refs
    own_x = dev_ref[0] & 1
    gx = dev_ref[0] >> gy_bits
    col_bits = bits_of(part.shape[2])
    piece_bits = bits_of(por_ref.shape[1])
    fetches = []
    for piece in range(2):
        chunk = gx ^ (piece + 2 * (1 - kernel))
        for place, (hbm, ref) in enumerate(((part_hbm, part), (por_hbm, por_ref))):
            rows = pl.ds(chunk * ref.shape[1], ref.shape[1])
            fetches.append(
                pltpu.make_async_copy(hbm.at[rows], ref.at[piece], sems.at[2 * piece + place])
            )
    for fetch in fetches:
        fetch.start()
    if kernel == 0:
        plan_tiles(gx, piece_bits, nowhere, got_ref, plan, *scratch, slots)
    heads, again, earlier = plan
    for fetch in fetches:
        fetch.wait()
    base = -LOG2E * ext_ref[0]
    slope = LOG2E * ext_ref[0]
    grain_slope = -LOG2E * ext_ref[1]
    depth_of = lax.broadcasted_iota(jnp.int32, (8, 128), 0)

    def running(value):
        for shift in (1, 2, 4):
            value = value + jnp.where(depth_of >= shift, pltpu.roll(value, shift, 0), 0.0)
        return value

    def march_tiles(work):
        for code, grain in work:
            tile = code >> 16
            piece = ((tile >> piece_bits) ^ gx) & 1
            tile = tile & ((1 << piece_bits) - 1)
            porous = por_ref[piece, tile].astype(jnp.float32)
            exponent = (base + slope * porous) + grain_slope * grain
            front = running(exponent[:8])
            back = running(exponent[8:]) + front[7:8]
            optical = jnp.concatenate([front, back], axis=0)
            weight = jnp.exp2(optical - exponent) - jnp.exp2(optical)
            alpha = 1.0 - jnp.exp2(back[7:8])
            results = []
            for c in range(3):
                half_logit = (
                    (0.5 * col_ref[c, 0]) * porous
                    + (0.5 * col_ref[c, 1]) * grain
                    + 0.5 * col_ref[c, 2]
                )
                shaded = weight * jnp.tanh(half_logit)
                total = jnp.sum(shaded[:8] + shaded[8:], axis=0, keepdims=True)
                results.append(0.5 * (alpha + total))
            results.append(alpha)
            group, row = tile >> (3 + col_bits), (tile >> col_bits) & 7
            col = tile & ((1 << col_bits) - 1)
            for c in range(4):
                part[piece, group, col, pl.ds(c * 8 + row, 1), :] = results[c]

    def some_tiles(batch, carry):
        codes = [heads[kernel, batch * UNROLL + place] for place in range(UNROLL)]
        march_tiles([(code, got_ref[code & 65535].astype(jnp.float32)) for code in codes])
        return carry

    found = heads[kernel, heads.shape[1] - 1]
    lax.fori_loop(0, (found + UNROLL - 1) >> bits_of(UNROLL), some_tiles, 0)

    def one_again(index, carry):
        code = again[kernel, index]
        entry = code & 65535

        def add_earlier(state):
            at, total = state
            return earlier[at], total + got_ref[at].astype(jnp.float32)

        grain = got_ref[entry].astype(jnp.float32)
        _, grain = lax.while_loop(
            lambda state: state[0] >= 0, add_earlier, (earlier[entry], grain)
        )
        march_tiles([(code, grain)])
        return carry

    lax.fori_loop(0, again[kernel, heads.shape[1] - 1], one_again, 0)

    pairs = part.shape[1] // 2
    for flips, keep_ref, send_ref in zip(chunks, keep_refs, send_refs):
        for place, flip in enumerate(flips):

            def split(pair, carry):
                at = place * pairs + pair
                send_ref[at] = part[flip & 1, 2 * pair + 1 - own_x].astype(jnp.bfloat16)
                keep_ref[at] = part[flip & 1, 2 * pair + own_x]
                return carry

            lax.fori_loop(0, pairs, split, 0)


def march_grain(kernel, plan, got, porous_tiles, part, dev, extinction, color_weights, slots, mesh):
    width_x, width_y = mesh
    chunks = KERNELS[kernel]
    smem = pl.BlockSpec(memory_space=pltpu.SMEM)
    vmem = pl.BlockSpec(memory_space=pltpu.VMEM)
    hbm = pl.BlockSpec(memory_space=pltpu.HBM)
    entries = got.shape[0]
    sources = entries // (slots + 1)
    tile_count = porous_tiles.shape[0]
    groups = part.shape[0] // width_x
    split = [(len(flips) * groups // 2,) + part.shape[1:] for flips in chunks]
    scratch = [
        pltpu.VMEM((2, tile_count // width_x) + porous_tiles.shape[1:], porous_tiles.dtype),
        pltpu.VMEM((2, groups) + part.shape[1:], part.dtype),
        pltpu.SemaphoreType.DMA((4,)),
    ]
    plan_shapes = []
    if kernel == 0:
        most = -(-(entries + UNROLL + 1) // 128) * 128
        plan_shapes = [
            jax.ShapeDtypeStruct((2, most), jnp.int32),
            jax.ShapeDtypeStruct((2, most), jnp.int32),
            jax.ShapeDtypeStruct((entries + UNROLL,), jnp.int32),
        ]
        scratch += [
            pltpu.VMEM((sources, 128), jnp.int32),
            pltpu.SMEM((sources, 128), jnp.int32),
            pltpu.SMEM((tile_count + 1,), jnp.int32),
            pltpu.SemaphoreType.DMA((2,)),
        ]
        before, before_specs = [jnp.full((tile_count,), -1, jnp.int32)], [hbm]
    else:
        before, before_specs = plan, [smem] * 3
    outs = pl.pallas_call(
        functools.partial(grain_kernel, kernel=kernel, slots=slots, gy_bits=bits_of(width_y)),
        out_shape=[jax.ShapeDtypeStruct(shape, jnp.float32) for shape in split]
        + [jax.ShapeDtypeStruct(shape, jnp.bfloat16) for shape in split]
        + plan_shapes,
        in_specs=[smem] * 3 + before_specs + [hbm] * 2 + [vmem],
        out_specs=[vmem] * (2 * len(chunks)) + [smem] * len(plan_shapes),
        scratch_shapes=scratch,
        compiler_params=pltpu.CompilerParams(vmem_limit_bytes=GRAIN_LIMIT),
        cost_estimate=pl.CostEstimate(flops=1000, bytes_accessed=1000, transcendentals=0),
        name=f"march_grain_{kernel}",
    )(dev, extinction, color_weights, *before, porous_tiles, part, got)
    keeps, sends = outs[: len(chunks)], outs[len(chunks) : 2 * len(chunks)]
    return list(zip(chunks, keeps, sends)), outs[2 * len(chunks) :]


def ordered(mine, theirs, mine_near):
    nearer = [jnp.where(mine_near, a, b) for a, b in zip(mine, theirs)]
    farther = [jnp.where(mine_near, b, a) for a, b in zip(mine, theirs)]
    open_part = 1.0 - nearer[3]
    return [n + open_part * f for n, f in zip(nearer, farther)]


def channels_of(block):
    block = block.astype(jnp.float32)
    rows = block.shape[0] // 4
    return [block[c * rows : (c + 1) * rows] for c in range(4)]


def swap_kernel(dev_ref, rank_ref, mine_ref, got_ref, *out_refs, stage, first):
    device = dev_ref[0]
    mine_near = (rank_ref[device] >> stage) & 1 == 0
    low, high = (device >> 1) & 1, (device >> 2) & 1

    def one_column(col, carry):
        for way, out_ref in enumerate(out_refs):
            for place in range(out_ref.shape[0]):
                group = first + [2 * place + (low ^ way), high ^ way, 0][stage]
                merged = ordered(
                    channels_of(mine_ref[group, col]), channels_of(got_ref[group, col]), mine_near
                )
                out_ref[place, col] = jnp.concatenate(merged, axis=0).astype(out_ref.dtype)
        return carry

    lax.fori_loop(0, got_ref.shape[1], one_column, 0)


def swap_rows(mine, got, dev, ranks, stage, first=0):
    smem = pl.BlockSpec(memory_space=pltpu.SMEM)
    vmem = pl.BlockSpec(memory_space=pltpu.VMEM)
    kept = ((2, 1, 1)[stage],) + got.shape[1:]
    out_shape = [jax.ShapeDtypeStruct(kept, jnp.float32)]
    if stage < 2:
        out_shape.append(jax.ShapeDtypeStruct(kept, jnp.bfloat16))
    return pl.pallas_call(
        functools.partial(swap_kernel, stage=stage, first=first),
        out_shape=out_shape,
        in_specs=[smem, smem, vmem, vmem],
        out_specs=[vmem] * len(out_shape),
        compiler_params=pltpu.CompilerParams(vmem_limit_bytes=SMALL_LIMIT),
        cost_estimate=pl.CostEstimate(flops=1000, bytes_accessed=1000, transcendentals=0),
        name=f"swap_rows_{stage}",
    )(dev, ranks, mine, got)


def four_way(device, rank_ref, parts, stride, bit):
    low = (rank_ref[device] >> bit) & 1 == 0
    far_low = (rank_ref[device ^ (2 * stride)] >> bit) & 1 == 0
    high = (rank_ref[device] >> (bit + 1)) & 1 == 0
    return ordered(
        ordered(parts[0], parts[1], low), ordered(parts[2], parts[3], far_low), high
    )


def last_kernel(dev_ref, rank_ref, mine_ref, got_ref, q1, q2, q3, out_ref, *, width_y):
    device = dev_ref[0]
    mine_near = (rank_ref[device] >> 2) & 1 == 0
    col_blocks = mine_ref.shape[1]
    for col in range(col_blocks):
        mine = ordered(channels_of(mine_ref[0, col]), channels_of(got_ref[0, col]), mine_near)
        parts = [mine] + [channels_of(ref[0, col]) for ref in (q1, q2, q3)]
        merged = four_way(device, rank_ref, parts, width_y, bits_of(width_y))
        for c in range(4):
            for row in range(merged[c].shape[0]):
                start = (row * col_blocks + col) * 128
                out_ref[c : c + 1, start : start + 128] = merged[c][row : row + 1]


def last_rows(mine, got, ready, dev, ranks, width_y):
    smem = pl.BlockSpec(memory_space=pltpu.SMEM)
    vmem = pl.BlockSpec(memory_space=pltpu.VMEM)
    return pl.pallas_call(
        functools.partial(last_kernel, width_y=width_y),
        out_shape=jax.ShapeDtypeStruct((4, mine.size // 4), jnp.float32),
        in_specs=[smem, smem] + [vmem] * 5,
        out_specs=vmem,
        compiler_params=pltpu.CompilerParams(vmem_limit_bytes=SMALL_LIMIT),
        name="last_rows",
    )(dev, ranks, mine, got, *ready)


def shards(porosity, grain_blocks, owners, tiles, live_counts, ranks, extinction, color_weights):
    width_x = lax.axis_size("gx")
    width_y = lax.axis_size("gy")
    device_count = width_x * width_y
    block_count = grain_blocks.shape[0]
    slots = max(2, 2 * block_count // device_count)
    dev = lax.axis_index(("gx", "gy")).astype(jnp.int32).reshape(1)
    packed = pack_blocks(grain_blocks, owners[:, 0], tiles, live_counts, device_count, slots)
    got = lax.all_to_all(packed, ("gx", "gy"), split_axis=0, concat_axis=0, tiled=True)
    got = got.reshape((-1,) + got.shape[2:])
    porosity, _ = lax.optimization_barrier((porosity, packed))
    part, porous_tiles = march_empty(porosity, extinction, color_weights)
    got, part, porous_tiles = lax.optimization_barrier((got, part, porous_tiles))
    work, plan = [], None
    for kernel in range(len(KERNELS)):
        made, planned = march_grain(
            kernel,
            plan,
            got,
            porous_tiles,
            part,
            dev,
            extinction,
            color_weights,
            slots,
            (width_x, width_y),
        )
        plan = plan or planned
        for flips, keep, send in made:
            arrived = exchanged(send, "gy", 1)
            for piece, flip in enumerate(flips):
                work.append((flip, piece * keep.shape[0] // len(flips), keep, arrived))
    ready = [None] * (width_x - 1)
    token = work[-1][2]
    state = {flip: (mine, got, first) for flip, first, mine, got in work}
    for flip, stage in ORDER:
        mine, got, first = state[flip]
        got, token = lax.optimization_barrier((got, token))
        if flip == 0 and stage == 2:
            return last_rows(mine, got, ready, dev, ranks, width_y)
        mine, *send = swap_rows(mine, got, dev, ranks, stage, first)
        token = mine
        if stage == 2:
            ready[flip - 1] = exchanged(mine, "gx", flip)
        else:
            state[flip] = mine, exchanged(send[0], "gy", 2 << stage), 0


def march_flat(porous_flat, grain_flat, extinction, color_weights):
    porous = porous_flat.astype(jnp.float32)
    extinct = extinction[0] * (1.0 - porous) + extinction[1] * grain_flat
    optical = jnp.cumsum(extinct, axis=0)
    before = optical - extinct
    weight = jnp.exp(-before) * (1.0 - jnp.exp(-extinct))
    channels = []
    for channel in range(3):
        colour = jax.nn.sigmoid(
            color_weights[channel, 0] * porous
            + color_weights[channel, 1] * grain_flat
            + color_weights[channel, 2]
        )
        channels.append(jnp.sum(weight * colour, axis=0))
    channels.append(1.0 - jnp.exp(-optical[-1]))
    return jnp.stack(channels, axis=0)


def composite(nearer, farther):
    return nearer + (1.0 - nearer[3:4]) * farther


def shards_any(
    porosity, grain_blocks, owners, tiles, live_counts, ranks, extinction, color_weights
):
    width_x = lax.axis_size("gx")
    width_y = lax.axis_size("gy")
    device_count = width_x * width_y
    depth_cells, image_rows, image_cols = porosity.shape
    block_count, _, block_cols = grain_blocks.shape
    slots = max(2, 2 * block_count // device_count)
    tile_count = image_rows * image_cols // block_cols
    pixel_count = image_rows * image_cols
    block_len = pixel_count // device_count
    packed = pack_blocks(grain_blocks, owners[:, 0], tiles, live_counts, device_count, slots)
    got = lax.all_to_all(packed, ("gx", "gy"), split_axis=0, concat_axis=0, tiled=True)
    coded = got[:, slots, :2, : slots + 1].astype(jnp.int32)
    table = coded[:, 0] * 64 + coded[:, 1]
    used = jnp.arange(slots, dtype=jnp.int32)[None, :] < table[:, slots:]
    got_tile = jnp.where(used, table[:, :slots], tile_count)
    got_data = jnp.where(used[:, :, None, None], got[:, :slots], jnp.bfloat16(0))
    grain_tiles = (
        jnp.zeros((tile_count, depth_cells, block_cols), jnp.float32)
        .at[got_tile.reshape(-1)]
        .add(
            got_data.reshape(device_count * slots, depth_cells, block_cols).astype(jnp.float32),
            mode="drop",
        )
    )
    grain_flat = jnp.transpose(grain_tiles, (1, 0, 2)).reshape(depth_cells, pixel_count)
    porous_flat = porosity.reshape(depth_cells, pixel_count)
    partial_value = march_flat(porous_flat, grain_flat, extinction, color_weights)
    my_rank = ranks[lax.axis_index(("gx", "gy"))]
    bits_y = width_y.bit_length() - 1
    bits_x = width_x.bit_length() - 1
    current = partial_value.reshape(4, width_x, width_y, block_len)
    for axis, dim, bits, first in (("gy", 2, bits_y, 0), ("gx", 1, bits_x, bits_y)):
        for section_bit in range(bits):
            shape = current.shape
            paired = current.reshape(
                shape[:dim] + (shape[dim] // 2, 2) + shape[dim + 1 :]
            )
            own_bit = lax.axis_index(axis) >> section_bit & 1
            kept_half = lax.dynamic_index_in_dim(paired, own_bit, dim + 1, keepdims=False)
            sent_half = lax.dynamic_index_in_dim(paired, 1 - own_bit, dim + 1, keepdims=False)
            partner = exchanged(sent_half, axis, 1 << section_bit)
            nearer_side = my_rank >> first + section_bit & 1 == 0
            current = composite(
                jnp.where(nearer_side, kept_half, partner),
                jnp.where(nearer_side, partner, kept_half),
            )
        if dim == 2:
            current = current.reshape(4, width_x, 1, block_len).reshape(4, width_x, block_len)
    return current.reshape(4, block_len)


def solution(mesh):
    in_specs = (
        P(("gx", "gy"), None, None),
        P(("gx", "gy"), None, None),
        P(("gx", "gy"), None),
        P(("gx", "gy")),
        P(("gx", "gy")),
        P(),
        P(),
        P(),
    )
    out_specs = P(None, ("gx", "gy"))

    def run(porosity, *rest):
        rows = porosity.shape[1] // (mesh.shape["gx"] * mesh.shape["gy"])
        fits = mesh.shape["gx"] == 4 and mesh.shape["gy"] == 8 and rows == 8
        return jax.shard_map(
            shards if fits else shards_any,
            mesh=mesh,
            in_specs=in_specs,
            out_specs=out_specs,
            check_vma=False,
        )(porosity, *rest)

    return run
```

```python
import functools
import math

import jax
import jax.numpy as jnp
from jax import lax
from jax.experimental import pallas as pl
from jax.experimental.pallas import tpu as pltpu
from jax.sharding import PartitionSpec as P

LOG2E = 1.4426950408889634
PACK_LIMIT = 56 * 1024 * 1024
EMPTY_LIMIT = 24 * 1024 * 1024
GRAIN_LIMIT = 47 * 1024 * 1024
SMALL_LIMIT = 8 * 1024 * 1024
UNROLL = 4
KERNELS = (((3, 2),), ((1,), (0,)))
ORDER = ((3, 0), (2, 0), (3, 1), (1, 0), (2, 1), (1, 1), (0, 0))


def exchanged(block, axis, distance):
    axes = axis if isinstance(axis, tuple) else (axis,)
    count = math.prod(lax.axis_size(name) for name in axes)
    route = [(low, low ^ distance) for low in range(count)]
    return lax.ppermute(block, axis, route)


def bits_of(size):
    assert size & (size - 1) == 0
    return size.bit_length() - 1


def pack_kernel(
    owner_ref, tile_ref, live_ref, block_ref, out_ref, table, table_vec, table_sem, *, slots
):
    owners_all = out_ref.shape[0]

    def clear(owner, carry):
        table[owner, slots] = 0
        return carry

    lax.fori_loop(0, owners_all, clear, 0)

    def place(index, carry):
        owner = owner_ref[index]
        slot = table[owner, slots]
        table[owner, slots] = slot + 1
        table[owner, slot] = tile_ref[index]
        out_ref[owner, slot] = block_ref[index]
        return carry

    lax.fori_loop(0, live_ref[0], place, 0)
    copy = pltpu.make_async_copy(table, table_vec, table_sem)
    copy.start()
    copy.wait()
    first = lax.broadcasted_iota(jnp.int32, (16, 128), 0) == 0
    for owner in range(owners_all):
        row = jnp.broadcast_to(table_vec[owner : owner + 1, :], (16, 128))
        coded = jnp.where(first, row >> 6, row & 63)
        out_ref[owner, slots] = coded.astype(jnp.float32).astype(jnp.bfloat16)


def pack_blocks(grain_blocks, owner_dev, tiles, live_counts, device_count, slots):
    smem = pl.BlockSpec(memory_space=pltpu.SMEM)
    vmem = pl.BlockSpec(memory_space=pltpu.VMEM)
    return pl.pallas_call(
        functools.partial(pack_kernel, slots=slots),
        out_shape=jax.ShapeDtypeStruct(
            (device_count, slots + 1) + grain_blocks.shape[1:], grain_blocks.dtype
        ),
        in_specs=[smem, smem, smem, vmem],
        out_specs=vmem,
        scratch_shapes=[
            pltpu.SMEM((device_count, 128), jnp.int32),
            pltpu.VMEM((device_count, 128), jnp.int32),
            pltpu.SemaphoreType.DMA(()),
        ],
        compiler_params=pltpu.CompilerParams(vmem_limit_bytes=PACK_LIMIT),
        name="pack_blocks",
    )(owner_dev, tiles, live_counts, grain_blocks)


def plan_tiles(gx, piece_bits, nowhere, got_ref, plan, ids_vec, ids, last, sems, slots):
    heads, again, earlier = plan
    nowhere_tile = last.shape[0] - 1
    sources = ids.shape[0]
    forget = pltpu.make_async_copy(nowhere, last.at[pl.ds(0, nowhere.shape[0])], sems.at[0])
    forget.start()
    for source in range(sources):
        coded = got_ref[source * (slots + 1) + slots].astype(jnp.float32)
        ids_vec[source : source + 1, :] = (coded[0:1, :] * 64.0 + coded[1:2, :]).astype(jnp.int32)
    fetch = pltpu.make_async_copy(ids_vec, ids, sems.at[1])
    fetch.start()
    last[nowhere_tile] = -1
    fetch.wait()
    forget.wait()

    def from_source(source, counts):
        live = ids[source, slots]

        def some(batch, counts):
            count = list(counts)
            found = []
            for place in range(UNROLL):
                slot = batch * UNROLL + place
                entry = source * (slots + 1) + slot
                valid = slot < live
                tile = jnp.where(valid, ids[source, slot], nowhere_tile)
                before = last[tile]
                last[tile] = entry
                found.append((entry, tile, valid, before))
            for entry, tile, valid, before in found:
                earlier[entry] = before
                code = entry + (tile << 16)
                kernel = 1 - (((tile >> piece_bits) ^ gx) >> 1) & 1
                heads[kernel, jnp.where(kernel == 0, count[0], count[1])] = code
                again[kernel, jnp.where(kernel == 0, count[2], count[3])] = code
                one = jnp.where(valid, 1, 0)
                more = jnp.where(jnp.logical_and(valid, before >= 0), 1, 0)
                count[0] = count[0] + (1 - kernel) * one
                count[1] = count[1] + kernel * one
                count[2] = count[2] + (1 - kernel) * more
                count[3] = count[3] + kernel * more
            return tuple(count)

        return lax.fori_loop(0, (live + UNROLL - 1) >> bits_of(UNROLL), some, counts)

    counts = lax.fori_loop(0, sources, from_source, (jnp.int32(0),) * 4)

    for kernel in range(2):
        found = counts[kernel]
        heads[kernel, heads.shape[1] - 1] = found
        again[kernel, heads.shape[1] - 1] = counts[2 + kernel]

        @pl.when(found > 0)
        def _():
            for extra in range(UNROLL - 1):
                heads[kernel, found + extra] = heads[kernel, found - 1]


def empty_kernel(ext_ref, col_ref, por_hbm, part, por_tiles, por, turned, sems):
    depth, rows, cols = por_hbm.shape
    block_rows = por.shape[2]
    half_rows = block_rows // 2
    col_blocks = cols // 128
    steps = rows // block_rows
    base = -LOG2E * ext_ref[0]
    slope = LOG2E * ext_ref[0]

    def fetch(step, slot):
        start = pl.multiple_of(step * block_rows, block_rows)
        return pltpu.make_async_copy(
            por_hbm.at[:, pl.ds(start, block_rows), :], por.at[slot], sems.at[slot]
        )

    fetch(0, 0).start()

    def one_step(step, carry):
        slot = lax.rem(step, 2)

        @pl.when(step + 1 < steps)
        def _():
            fetch(step + 1, 1 - slot).start()

        fetch(step, slot).wait()

        def one_column(col, carry):
            lanes = pl.ds(pl.multiple_of(col * 128, 128), 128)
            clear = jnp.ones((block_rows, 128), jnp.float32)
            sums = [jnp.zeros((block_rows, 128), jnp.float32) for _ in range(3)]
            for z in range(depth):
                porous = por[slot, z, :, lanes].astype(jnp.float32)
                turned[z * block_rows : (z + 1) * block_rows, :] = porous
                passed = clear * jnp.exp2(base + slope * porous)
                weight = clear - passed
                clear = passed
                for c in range(3):
                    half_logit = (0.5 * col_ref[c, 0]) * porous + 0.5 * col_ref[c, 2]
                    sums[c] = sums[c] + weight * jnp.tanh(half_logit)
            for row in range(block_rows):
                tile = (step * block_rows + row) * col_blocks + col
                por_tiles[tile] = turned[pl.ds(row, depth, stride=block_rows), :].astype(
                    jnp.bfloat16
                )
            alpha = 1.0 - clear
            parts = [0.5 * (alpha + total) for total in sums] + [alpha]
            for c in range(4):
                for half in range(2):
                    part[2 * step + half, col, c * half_rows : (c + 1) * half_rows, :] = parts[c][
                        half * half_rows : (half + 1) * half_rows
                    ]
            return carry

        lax.fori_loop(0, col_blocks, one_column, 0)
        return carry

    lax.fori_loop(0, steps, one_step, 0)


def march_empty(porosity, extinction, color_weights):
    depth, rows, cols = porosity.shape
    block_rows = 16
    smem = pl.BlockSpec(memory_space=pltpu.SMEM)
    vmem = pl.BlockSpec(memory_space=pltpu.VMEM)
    return pl.pallas_call(
        empty_kernel,
        out_shape=[
            jax.ShapeDtypeStruct((rows // 8, cols // 128, 32, 128), jnp.float32),
            jax.ShapeDtypeStruct((rows * cols // 128, depth, 128), porosity.dtype),
        ],
        in_specs=[smem, smem, pl.BlockSpec(memory_space=pl.ANY)],
        out_specs=[vmem, vmem],
        scratch_shapes=[
            pltpu.VMEM((2, depth, block_rows, cols), porosity.dtype),
            pltpu.VMEM((depth * block_rows, 128), jnp.float32),
            pltpu.SemaphoreType.DMA((2,)),
        ],
        compiler_params=pltpu.CompilerParams(vmem_limit_bytes=EMPTY_LIMIT),
        cost_estimate=pl.CostEstimate(
            flops=20 * depth * rows * cols,
            bytes_accessed=4 * depth * rows * cols + 16 * rows * cols,
            transcendentals=4 * depth * rows * cols,
        ),
        name="march_empty",
    )(extinction, color_weights, porosity)


def grain_kernel(dev_ref, ext_ref, col_ref, *refs, kernel, slots, gy_bits):
    chunks = KERNELS[kernel]
    if kernel == 0:
        nowhere, *refs = refs
    else:
        plan, refs = refs[:3], refs[3:]
    por_hbm, part_hbm, got_ref, *refs = refs
    keep_refs, send_refs = refs[: len(chunks)], refs[len(chunks) : 2 * len(chunks)]
    refs = refs[2 * len(chunks) :]
    if kernel == 0:
        plan, refs = refs[:3], refs[3:]
    por_ref, part, sems, *scratch = refs
    own_x = dev_ref[0] & 1
    gx = dev_ref[0] >> gy_bits
    col_bits = bits_of(part.shape[2])
    piece_bits = bits_of(por_ref.shape[1])
    fetches = []
    for piece in range(2):
        chunk = gx ^ (piece + 2 * (1 - kernel))
        for place, (hbm, ref) in enumerate(((part_hbm, part), (por_hbm, por_ref))):
            rows = pl.ds(chunk * ref.shape[1], ref.shape[1])
            fetches.append(
                pltpu.make_async_copy(hbm.at[rows], ref.at[piece], sems.at[2 * piece + place])
            )
    for fetch in fetches:
        fetch.start()
    if kernel == 0:
        plan_tiles(gx, piece_bits, nowhere, got_ref, plan, *scratch, slots)
    heads, again, earlier = plan
    for fetch in fetches:
        fetch.wait()
    base = -LOG2E * ext_ref[0]
    slope = LOG2E * ext_ref[0]
    grain_slope = -LOG2E * ext_ref[1]
    depth_of = lax.broadcasted_iota(jnp.int32, (8, 128), 0)

    def running(value):
        for shift in (1, 2, 4):
            value = value + jnp.where(depth_of >= shift, pltpu.roll(value, shift, 0), 0.0)
        return value

    def march_tiles(work):
        for code, grain in work:
            tile = code >> 16
            piece = ((tile >> piece_bits) ^ gx) & 1
            tile = tile & ((1 << piece_bits) - 1)
            porous = por_ref[piece, tile].astype(jnp.float32)
            exponent = (base + slope * porous) + grain_slope * grain
            front = running(exponent[:8])
            back = running(exponent[8:]) + front[7:8]
            optical = jnp.concatenate([front, back], axis=0)
            weight = jnp.exp2(optical - exponent) - jnp.exp2(optical)
            alpha = 1.0 - jnp.exp2(back[7:8])
            results = []
            for c in range(3):
                half_logit = (
                    (0.5 * col_ref[c, 0]) * porous
                    + (0.5 * col_ref[c, 1]) * grain
                    + 0.5 * col_ref[c, 2]
                )
                shaded = weight * jnp.tanh(half_logit)
                total = jnp.sum(shaded[:8] + shaded[8:], axis=0, keepdims=True)
                results.append(0.5 * (alpha + total))
            results.append(alpha)
            group, row = tile >> (3 + col_bits), (tile >> col_bits) & 7
            col = tile & ((1 << col_bits) - 1)
            for c in range(4):
                part[piece, group, col, pl.ds(c * 8 + row, 1), :] = results[c]

    def some_tiles(batch, carry):
        codes = [heads[kernel, batch * UNROLL + place] for place in range(UNROLL)]
        march_tiles([(code, got_ref[code & 65535].astype(jnp.float32)) for code in codes])
        return carry

    found = heads[kernel, heads.shape[1] - 1]
    lax.fori_loop(0, (found + UNROLL - 1) >> bits_of(UNROLL), some_tiles, 0)

    def one_again(index, carry):
        code = again[kernel, index]
        entry = code & 65535

        def add_earlier(state):
            at, total = state
            return earlier[at], total + got_ref[at].astype(jnp.float32)

        grain = got_ref[entry].astype(jnp.float32)
        _, grain = lax.while_loop(
            lambda state: state[0] >= 0, add_earlier, (earlier[entry], grain)
        )
        march_tiles([(code, grain)])
        return carry

    lax.fori_loop(0, again[kernel, heads.shape[1] - 1], one_again, 0)

    pairs = part.shape[1] // 2
    for flips, keep_ref, send_ref in zip(chunks, keep_refs, send_refs):
        for place, flip in enumerate(flips):

            def split(pair, carry):
                at = place * pairs + pair
                send_ref[at] = part[flip & 1, 2 * pair + 1 - own_x].astype(jnp.bfloat16)
                keep_ref[at] = part[flip & 1, 2 * pair + own_x]
                return carry

            lax.fori_loop(0, pairs, split, 0)


def march_grain(kernel, plan, got, porous_tiles, part, dev, extinction, color_weights, slots, mesh):
    width_x, width_y = mesh
    chunks = KERNELS[kernel]
    smem = pl.BlockSpec(memory_space=pltpu.SMEM)
    vmem = pl.BlockSpec(memory_space=pltpu.VMEM)
    hbm = pl.BlockSpec(memory_space=pltpu.HBM)
    entries = got.shape[0]
    sources = entries // (slots + 1)
    tile_count = porous_tiles.shape[0]
    groups = part.shape[0] // width_x
    split = [(len(flips) * groups // 2,) + part.shape[1:] for flips in chunks]
    scratch = [
        pltpu.VMEM((2, tile_count // width_x) + porous_tiles.shape[1:], porous_tiles.dtype),
        pltpu.VMEM((2, groups) + part.shape[1:], part.dtype),
        pltpu.SemaphoreType.DMA((4,)),
    ]
    plan_shapes = []
    if kernel == 0:
        most = -(-(entries + UNROLL + 1) // 128) * 128
        plan_shapes = [
            jax.ShapeDtypeStruct((2, most), jnp.int32),
            jax.ShapeDtypeStruct((2, most), jnp.int32),
            jax.ShapeDtypeStruct((entries + UNROLL,), jnp.int32),
        ]
        scratch += [
            pltpu.VMEM((sources, 128), jnp.int32),
            pltpu.SMEM((sources, 128), jnp.int32),
            pltpu.SMEM((tile_count + 1,), jnp.int32),
            pltpu.SemaphoreType.DMA((2,)),
        ]
        before, before_specs = [jnp.full((tile_count,), -1, jnp.int32)], [hbm]
    else:
        before, before_specs = plan, [smem] * 3
    outs = pl.pallas_call(
        functools.partial(grain_kernel, kernel=kernel, slots=slots, gy_bits=bits_of(width_y)),
        out_shape=[jax.ShapeDtypeStruct(shape, jnp.float32) for shape in split]
        + [jax.ShapeDtypeStruct(shape, jnp.bfloat16) for shape in split]
        + plan_shapes,
        in_specs=[smem] * 3 + before_specs + [hbm] * 2 + [vmem],
        out_specs=[vmem] * (2 * len(chunks)) + [smem] * len(plan_shapes),
        scratch_shapes=scratch,
        compiler_params=pltpu.CompilerParams(vmem_limit_bytes=GRAIN_LIMIT),
        cost_estimate=pl.CostEstimate(flops=1000, bytes_accessed=1000, transcendentals=0),
        name=f"march_grain_{kernel}",
    )(dev, extinction, color_weights, *before, porous_tiles, part, got)
    keeps, sends = outs[: len(chunks)], outs[len(chunks) : 2 * len(chunks)]
    return list(zip(chunks, keeps, sends)), outs[2 * len(chunks) :]


def ordered(mine, theirs, mine_near):
    nearer = [jnp.where(mine_near, a, b) for a, b in zip(mine, theirs)]
    farther = [jnp.where(mine_near, b, a) for a, b in zip(mine, theirs)]
    open_part = 1.0 - nearer[3]
    return [n + open_part * f for n, f in zip(nearer, farther)]


def channels_of(block):
    block = block.astype(jnp.float32)
    rows = block.shape[0] // 4
    return [block[c * rows : (c + 1) * rows] for c in range(4)]


def swap_kernel(dev_ref, rank_ref, mine_ref, got_ref, *out_refs, stage, first):
    device = dev_ref[0]
    mine_near = (rank_ref[device] >> stage) & 1 == 0
    low, high = (device >> 1) & 1, (device >> 2) & 1

    def one_column(col, carry):
        for way, out_ref in enumerate(out_refs):
            for place in range(out_ref.shape[0]):
                group = first + (2 * place + (low ^ way) if stage == 0 else high ^ way)
                merged = ordered(
                    channels_of(mine_ref[group, col]), channels_of(got_ref[group, col]), mine_near
                )
                out_ref[place, col] = jnp.concatenate(merged, axis=0).astype(out_ref.dtype)
        return carry

    lax.fori_loop(0, got_ref.shape[1], one_column, 0)


def swap_rows(mine, got, dev, ranks, stage, first=0):
    smem = pl.BlockSpec(memory_space=pltpu.SMEM)
    vmem = pl.BlockSpec(memory_space=pltpu.VMEM)
    kept = (2 - stage,) + got.shape[1:]
    out_shape = [jax.ShapeDtypeStruct(kept, dtype) for dtype in (jnp.float32, jnp.bfloat16)]
    return pl.pallas_call(
        functools.partial(swap_kernel, stage=stage, first=first),
        out_shape=out_shape,
        in_specs=[smem, smem, vmem, vmem],
        out_specs=[vmem] * len(out_shape),
        compiler_params=pltpu.CompilerParams(vmem_limit_bytes=SMALL_LIMIT),
        cost_estimate=pl.CostEstimate(flops=1000, bytes_accessed=1000, transcendentals=0),
        name=f"swap_rows_{stage}",
    )(dev, ranks, mine, got)


def spread_kernel(dev_ref, rank_ref, mine_ref, got_ref, own_ref, *send_refs, around):
    device = dev_ref[0]
    mine_near = rank_ref[device] & 1 == 0
    place = (device >> 1) & (around - 1)

    def one_column(col, carry):
        for distance, out_ref in enumerate((own_ref, *send_refs)):
            group = place ^ distance
            merged = ordered(
                channels_of(mine_ref[group, col]), channels_of(got_ref[group, col]), mine_near
            )
            out_ref[col] = jnp.concatenate(merged, axis=0).astype(out_ref.dtype)
        return carry

    lax.fori_loop(0, got_ref.shape[1], one_column, 0)


def spread_rows(mine, got, dev, ranks, width_y):
    smem = pl.BlockSpec(memory_space=pltpu.SMEM)
    vmem = pl.BlockSpec(memory_space=pltpu.VMEM)
    around = width_y // 2
    return pl.pallas_call(
        functools.partial(spread_kernel, around=around),
        out_shape=[jax.ShapeDtypeStruct(got.shape[1:], jnp.float32)]
        + [jax.ShapeDtypeStruct(got.shape[1:], jnp.bfloat16)] * (around - 1),
        in_specs=[smem, smem, vmem, vmem],
        out_specs=[vmem] * around,
        compiler_params=pltpu.CompilerParams(vmem_limit_bytes=SMALL_LIMIT),
        cost_estimate=pl.CostEstimate(flops=1000, bytes_accessed=1000, transcendentals=0),
        name="spread_rows",
    )(dev, ranks, mine, got)


def four_way(device, rank_ref, parts, stride, bit):
    low = (rank_ref[device] >> bit) & 1 == 0
    far_low = (rank_ref[device ^ (2 * stride)] >> bit) & 1 == 0
    high = (rank_ref[device] >> (bit + 1)) & 1 == 0
    return ordered(
        ordered(parts[0], parts[1], low), ordered(parts[2], parts[3], far_low), high
    )


def last_kernel(dev_ref, rank_ref, *refs, width_y):
    own_refs, pair_refs, out_ref = refs[:4], refs[4:10], refs[10]
    device = dev_ref[0]
    col_blocks = own_refs[0].shape[0]
    nears = [(rank_ref[device ^ (flip * width_y)] >> 2) & 1 == 0 for flip in range(4)]
    for col in range(col_blocks):
        own = [channels_of(ref[col]) for ref in own_refs]
        parts = [four_way(device, rank_ref, own, 2, 1)]
        for flip in range(1, 4):
            mine, theirs = (ref[0, col] for ref in pair_refs[2 * flip - 2 : 2 * flip])
            parts.append(ordered(channels_of(mine), channels_of(theirs), nears[flip]))
        merged = four_way(device, rank_ref, parts, width_y, bits_of(width_y))
        for c in range(4):
            for row in range(merged[c].shape[0]):
                start = (row * col_blocks + col) * 128
                out_ref[c : c + 1, start : start + 128] = merged[c][row : row + 1]


def last_rows(own, others, ready, dev, ranks, width_y):
    smem = pl.BlockSpec(memory_space=pltpu.SMEM)
    vmem = pl.BlockSpec(memory_space=pltpu.VMEM)
    return pl.pallas_call(
        functools.partial(last_kernel, width_y=width_y),
        out_shape=jax.ShapeDtypeStruct((4, own.size // 4), jnp.float32),
        in_specs=[smem, smem] + [vmem] * 10,
        out_specs=vmem,
        compiler_params=pltpu.CompilerParams(vmem_limit_bytes=SMALL_LIMIT),
        name="last_rows",
    )(dev, ranks, own, *others, *ready[1], *ready[2], *ready[3])


def shards(porosity, grain_blocks, owners, tiles, live_counts, ranks, extinction, color_weights):
    width_x = lax.axis_size("gx")
    width_y = lax.axis_size("gy")
    device_count = width_x * width_y
    block_count = grain_blocks.shape[0]
    slots = max(2, 2 * block_count // device_count)
    dev = lax.axis_index(("gx", "gy")).astype(jnp.int32).reshape(1)
    packed = pack_blocks(grain_blocks, owners[:, 0], tiles, live_counts, device_count, slots)
    got = lax.all_to_all(packed, ("gx", "gy"), split_axis=0, concat_axis=0, tiled=True)
    got = got.reshape((-1,) + got.shape[2:])
    porosity, _ = lax.optimization_barrier((porosity, packed))
    part, porous_tiles = march_empty(porosity, extinction, color_weights)
    got, part, porous_tiles = lax.optimization_barrier((got, part, porous_tiles))
    work, plan = [], None
    for kernel in range(len(KERNELS)):
        made, planned = march_grain(
            kernel,
            plan,
            got,
            porous_tiles,
            part,
            dev,
            extinction,
            color_weights,
            slots,
            (width_x, width_y),
        )
        plan = plan or planned
        for flips, keep, send in made:
            arrived = exchanged(send, "gy", 1)
            for piece, flip in enumerate(flips):
                work.append((flip, piece * keep.shape[0] // len(flips), keep, arrived))
    ready = [None] * width_x
    token = work[-1][2]
    state = {flip: (mine, got, first) for flip, first, mine, got in work}
    for flip, stage in ORDER:
        mine, got, first = state[flip]
        got, token = lax.optimization_barrier((got, token))
        if flip == 0:
            own, *sends = spread_rows(mine, got, dev, ranks, width_y)
            others = [exchanged(send, "gy", 2 * (k + 1)) for k, send in enumerate(sends)]
            token = own
            continue
        mine, *send = swap_rows(mine, got, dev, ranks, stage, first)
        token = mine
        if stage == 0:
            state[flip] = mine, exchanged(send[0], "gy", 2), 0
        else:
            far = exchanged(send[0], ("gx", "gy"), flip * width_y + 4)
            ready[flip] = exchanged(mine, "gx", flip), far
    return last_rows(own, others, ready, dev, ranks, width_y)


def march_flat(porous_flat, grain_flat, extinction, color_weights):
    porous = porous_flat.astype(jnp.float32)
    extinct = extinction[0] * (1.0 - porous) + extinction[1] * grain_flat
    optical = jnp.cumsum(extinct, axis=0)
    before = optical - extinct
    weight = jnp.exp(-before) * (1.0 - jnp.exp(-extinct))
    channels = []
    for channel in range(3):
        colour = jax.nn.sigmoid(
            color_weights[channel, 0] * porous
            + color_weights[channel, 1] * grain_flat
            + color_weights[channel, 2]
        )
        channels.append(jnp.sum(weight * colour, axis=0))
    channels.append(1.0 - jnp.exp(-optical[-1]))
    return jnp.stack(channels, axis=0)


def composite(nearer, farther):
    return nearer + (1.0 - nearer[3:4]) * farther


def shards_any(
    porosity, grain_blocks, owners, tiles, live_counts, ranks, extinction, color_weights
):
    width_x = lax.axis_size("gx")
    width_y = lax.axis_size("gy")
    device_count = width_x * width_y
    depth_cells, image_rows, image_cols = porosity.shape
    block_count, _, block_cols = grain_blocks.shape
    slots = max(2, 2 * block_count // device_count)
    tile_count = image_rows * image_cols // block_cols
    pixel_count = image_rows * image_cols
    block_len = pixel_count // device_count
    packed = pack_blocks(grain_blocks, owners[:, 0], tiles, live_counts, device_count, slots)
    got = lax.all_to_all(packed, ("gx", "gy"), split_axis=0, concat_axis=0, tiled=True)
    coded = got[:, slots, :2, : slots + 1].astype(jnp.int32)
    table = coded[:, 0] * 64 + coded[:, 1]
    used = jnp.arange(slots, dtype=jnp.int32)[None, :] < table[:, slots:]
    got_tile = jnp.where(used, table[:, :slots], tile_count)
    got_data = jnp.where(used[:, :, None, None], got[:, :slots], jnp.bfloat16(0))
    grain_tiles = (
        jnp.zeros((tile_count, depth_cells, block_cols), jnp.float32)
        .at[got_tile.reshape(-1)]
        .add(
            got_data.reshape(device_count * slots, depth_cells, block_cols).astype(jnp.float32),
            mode="drop",
        )
    )
    grain_flat = jnp.transpose(grain_tiles, (1, 0, 2)).reshape(depth_cells, pixel_count)
    porous_flat = porosity.reshape(depth_cells, pixel_count)
    partial_value = march_flat(porous_flat, grain_flat, extinction, color_weights)
    my_rank = ranks[lax.axis_index(("gx", "gy"))]
    bits_y = width_y.bit_length() - 1
    bits_x = width_x.bit_length() - 1
    current = partial_value.reshape(4, width_x, width_y, block_len)
    for axis, dim, bits, first in (("gy", 2, bits_y, 0), ("gx", 1, bits_x, bits_y)):
        for section_bit in range(bits):
            shape = current.shape
            paired = current.reshape(
                shape[:dim] + (shape[dim] // 2, 2) + shape[dim + 1 :]
            )
            own_bit = lax.axis_index(axis) >> section_bit & 1
            kept_half = lax.dynamic_index_in_dim(paired, own_bit, dim + 1, keepdims=False)
            sent_half = lax.dynamic_index_in_dim(paired, 1 - own_bit, dim + 1, keepdims=False)
            partner = exchanged(sent_half, axis, 1 << section_bit)
            nearer_side = my_rank >> first + section_bit & 1 == 0
            current = composite(
                jnp.where(nearer_side, kept_half, partner),
                jnp.where(nearer_side, partner, kept_half),
            )
        if dim == 2:
            current = current.reshape(4, width_x, 1, block_len).reshape(4, width_x, block_len)
    return current.reshape(4, block_len)


def solution(mesh):
    in_specs = (
        P(("gx", "gy"), None, None),
        P(("gx", "gy"), None, None),
        P(("gx", "gy"), None),
        P(("gx", "gy")),
        P(("gx", "gy")),
        P(),
        P(),
        P(),
    )
    out_specs = P(None, ("gx", "gy"))

    def run(porosity, *rest):
        rows = porosity.shape[1] // (mesh.shape["gx"] * mesh.shape["gy"])
        fits = mesh.shape["gx"] == 4 and mesh.shape["gy"] == 8 and rows == 8
        return jax.shard_map(
            shards if fits else shards_any,
            mesh=mesh,
            in_specs=in_specs,
            out_specs=out_specs,
            check_vma=False,
        )(porosity, *rest)

    return run
```

```python
import functools
import math

import jax
import jax.numpy as jnp
from jax import lax
from jax.experimental import pallas as pl
from jax.experimental.pallas import tpu as pltpu
from jax.sharding import PartitionSpec as P

LOG2E = 1.4426950408889634
PACK_LIMIT = 56 * 1024 * 1024
EMPTY_LIMIT = 24 * 1024 * 1024
GRAIN_LIMIT = 47 * 1024 * 1024
SMALL_LIMIT = 8 * 1024 * 1024
UNROLL = 4
KERNELS = (((3, 2),), ((1,), (0,)))
ORDER = ((3, 0), (2, 0), (3, 1), (2, 1), (1, 0), (3, 2), (2, 2), (1, 1), (0, 0))


def exchanged(block, axis, distance):
    axes = axis if isinstance(axis, tuple) else (axis,)
    count = math.prod(lax.axis_size(name) for name in axes)
    route = [(low, low ^ distance) for low in range(count)]
    return lax.ppermute(block, axis, route)


def bits_of(size):
    assert size & (size - 1) == 0
    return size.bit_length() - 1


def pack_kernel(
    owner_ref, tile_ref, live_ref, block_ref, out_ref, table, table_vec, table_sem, *, slots
):
    owners_all = out_ref.shape[0]

    def clear(owner, carry):
        table[owner, slots] = 0
        return carry

    lax.fori_loop(0, owners_all, clear, 0)

    def place(index, carry):
        owner = owner_ref[index]
        slot = table[owner, slots]
        table[owner, slots] = slot + 1
        table[owner, slot] = tile_ref[index]
        out_ref[owner, slot] = block_ref[index]
        return carry

    lax.fori_loop(0, live_ref[0], place, 0)
    copy = pltpu.make_async_copy(table, table_vec, table_sem)
    copy.start()
    copy.wait()
    first = lax.broadcasted_iota(jnp.int32, (16, 128), 0) == 0
    for owner in range(owners_all):
        row = jnp.broadcast_to(table_vec[owner : owner + 1, :], (16, 128))
        coded = jnp.where(first, row >> 6, row & 63)
        out_ref[owner, slots] = coded.astype(jnp.float32).astype(jnp.bfloat16)


def pack_blocks(grain_blocks, owner_dev, tiles, live_counts, device_count, slots):
    smem = pl.BlockSpec(memory_space=pltpu.SMEM)
    vmem = pl.BlockSpec(memory_space=pltpu.VMEM)
    return pl.pallas_call(
        functools.partial(pack_kernel, slots=slots),
        out_shape=jax.ShapeDtypeStruct(
            (device_count, slots + 1) + grain_blocks.shape[1:], grain_blocks.dtype
        ),
        in_specs=[smem, smem, smem, vmem],
        out_specs=vmem,
        scratch_shapes=[
            pltpu.SMEM((device_count, 128), jnp.int32),
            pltpu.VMEM((device_count, 128), jnp.int32),
            pltpu.SemaphoreType.DMA(()),
        ],
        compiler_params=pltpu.CompilerParams(vmem_limit_bytes=PACK_LIMIT),
        name="pack_blocks",
    )(owner_dev, tiles, live_counts, grain_blocks)


def plan_tiles(gx, piece_bits, nowhere, got_ref, plan, ids_vec, ids, last, sems, slots):
    heads, again, earlier = plan
    nowhere_tile = last.shape[0] - 1
    sources = ids.shape[0]
    forget = pltpu.make_async_copy(nowhere, last.at[pl.ds(0, nowhere.shape[0])], sems.at[0])
    forget.start()
    for source in range(sources):
        coded = got_ref[source * (slots + 1) + slots].astype(jnp.float32)
        ids_vec[source : source + 1, :] = (coded[0:1, :] * 64.0 + coded[1:2, :]).astype(jnp.int32)
    fetch = pltpu.make_async_copy(ids_vec, ids, sems.at[1])
    fetch.start()
    last[nowhere_tile] = -1
    fetch.wait()
    forget.wait()

    def from_source(source, counts):
        live = ids[source, slots]

        def some(batch, counts):
            count = list(counts)
            found = []
            for place in range(UNROLL):
                slot = batch * UNROLL + place
                entry = source * (slots + 1) + slot
                valid = slot < live
                tile = jnp.where(valid, ids[source, slot], nowhere_tile)
                before = last[tile]
                last[tile] = entry
                found.append((entry, tile, valid, before))
            for entry, tile, valid, before in found:
                earlier[entry] = before
                code = entry + (tile << 16)
                kernel = 1 - (((tile >> piece_bits) ^ gx) >> 1) & 1
                heads[kernel, jnp.where(kernel == 0, count[0], count[1])] = code
                again[kernel, jnp.where(kernel == 0, count[2], count[3])] = code
                one = jnp.where(valid, 1, 0)
                more = jnp.where(jnp.logical_and(valid, before >= 0), 1, 0)
                count[0] = count[0] + (1 - kernel) * one
                count[1] = count[1] + kernel * one
                count[2] = count[2] + (1 - kernel) * more
                count[3] = count[3] + kernel * more
            return tuple(count)

        return lax.fori_loop(0, (live + UNROLL - 1) >> bits_of(UNROLL), some, counts)

    counts = lax.fori_loop(0, sources, from_source, (jnp.int32(0),) * 4)

    for kernel in range(2):
        found = counts[kernel]
        heads[kernel, heads.shape[1] - 1] = found
        again[kernel, heads.shape[1] - 1] = counts[2 + kernel]

        @pl.when(found > 0)
        def _():
            for extra in range(UNROLL - 1):
                heads[kernel, found + extra] = heads[kernel, found - 1]


def empty_kernel(ext_ref, col_ref, por_hbm, part, por_tiles, por, turned, sems):
    depth, rows, cols = por_hbm.shape
    block_rows = por.shape[2]
    half_rows = block_rows // 2
    col_blocks = cols // 128
    steps = rows // block_rows
    base = -LOG2E * ext_ref[0]
    slope = LOG2E * ext_ref[0]

    def fetch(step, slot):
        start = pl.multiple_of(step * block_rows, block_rows)
        return pltpu.make_async_copy(
            por_hbm.at[:, pl.ds(start, block_rows), :], por.at[slot], sems.at[slot]
        )

    fetch(0, 0).start()

    def one_step(step, carry):
        slot = lax.rem(step, 2)

        @pl.when(step + 1 < steps)
        def _():
            fetch(step + 1, 1 - slot).start()

        fetch(step, slot).wait()

        def one_column(col, carry):
            lanes = pl.ds(pl.multiple_of(col * 128, 128), 128)
            clear = jnp.ones((block_rows, 128), jnp.float32)
            sums = [jnp.zeros((block_rows, 128), jnp.float32) for _ in range(3)]
            for z in range(depth):
                porous = por[slot, z, :, lanes].astype(jnp.float32)
                turned[z * block_rows : (z + 1) * block_rows, :] = porous
                passed = clear * jnp.exp2(base + slope * porous)
                weight = clear - passed
                clear = passed
                for c in range(3):
                    half_logit = (0.5 * col_ref[c, 0]) * porous + 0.5 * col_ref[c, 2]
                    sums[c] = sums[c] + weight * jnp.tanh(half_logit)
            for row in range(block_rows):
                tile = (step * block_rows + row) * col_blocks + col
                por_tiles[tile] = turned[pl.ds(row, depth, stride=block_rows), :].astype(
                    jnp.bfloat16
                )
            alpha = 1.0 - clear
            parts = [0.5 * (alpha + total) for total in sums] + [alpha]
            for c in range(4):
                for half in range(2):
                    part[2 * step + half, col, c * half_rows : (c + 1) * half_rows, :] = parts[c][
                        half * half_rows : (half + 1) * half_rows
                    ]
            return carry

        lax.fori_loop(0, col_blocks, one_column, 0)
        return carry

    lax.fori_loop(0, steps, one_step, 0)


def march_empty(porosity, extinction, color_weights):
    depth, rows, cols = porosity.shape
    block_rows = 16
    smem = pl.BlockSpec(memory_space=pltpu.SMEM)
    vmem = pl.BlockSpec(memory_space=pltpu.VMEM)
    return pl.pallas_call(
        empty_kernel,
        out_shape=[
            jax.ShapeDtypeStruct((rows // 8, cols // 128, 32, 128), jnp.float32),
            jax.ShapeDtypeStruct((rows * cols // 128, depth, 128), porosity.dtype),
        ],
        in_specs=[smem, smem, pl.BlockSpec(memory_space=pl.ANY)],
        out_specs=[vmem, vmem],
        scratch_shapes=[
            pltpu.VMEM((2, depth, block_rows, cols), porosity.dtype),
            pltpu.VMEM((depth * block_rows, 128), jnp.float32),
            pltpu.SemaphoreType.DMA((2,)),
        ],
        compiler_params=pltpu.CompilerParams(vmem_limit_bytes=EMPTY_LIMIT),
        cost_estimate=pl.CostEstimate(
            flops=20 * depth * rows * cols,
            bytes_accessed=4 * depth * rows * cols + 16 * rows * cols,
            transcendentals=4 * depth * rows * cols,
        ),
        name="march_empty",
    )(extinction, color_weights, porosity)


def grain_kernel(dev_ref, ext_ref, col_ref, *refs, kernel, slots, gy_bits):
    chunks = KERNELS[kernel]
    if kernel == 0:
        nowhere, *refs = refs
    else:
        plan, refs = refs[:3], refs[3:]
    por_hbm, part_hbm, got_ref, *refs = refs
    keep_refs, send_refs = refs[: len(chunks)], refs[len(chunks) : 2 * len(chunks)]
    refs = refs[2 * len(chunks) :]
    if kernel == 0:
        plan, refs = refs[:3], refs[3:]
    por_ref, part, sems, *scratch = refs
    own_x = dev_ref[0] & 1
    gx = dev_ref[0] >> gy_bits
    col_bits = bits_of(part.shape[2])
    piece_bits = bits_of(por_ref.shape[1])
    fetches = []
    for piece in range(2):
        chunk = gx ^ (piece + 2 * (1 - kernel))
        for place, (hbm, ref) in enumerate(((part_hbm, part), (por_hbm, por_ref))):
            rows = pl.ds(chunk * ref.shape[1], ref.shape[1])
            fetches.append(
                pltpu.make_async_copy(hbm.at[rows], ref.at[piece], sems.at[2 * piece + place])
            )
    for fetch in fetches:
        fetch.start()
    if kernel == 0:
        plan_tiles(gx, piece_bits, nowhere, got_ref, plan, *scratch, slots)
    heads, again, earlier = plan
    for fetch in fetches:
        fetch.wait()
    base = -LOG2E * ext_ref[0]
    slope = LOG2E * ext_ref[0]
    grain_slope = -LOG2E * ext_ref[1]
    depth_of = lax.broadcasted_iota(jnp.int32, (8, 128), 0)

    def running(value):
        for shift in (1, 2, 4):
            value = value + jnp.where(depth_of >= shift, pltpu.roll(value, shift, 0), 0.0)
        return value

    def march_tiles(work):
        for code, grain in work:
            tile = code >> 16
            piece = ((tile >> piece_bits) ^ gx) & 1
            tile = tile & ((1 << piece_bits) - 1)
            porous = por_ref[piece, tile].astype(jnp.float32)
            exponent = (base + slope * porous) + grain_slope * grain
            front = running(exponent[:8])
            back = running(exponent[8:]) + front[7:8]
            optical = jnp.concatenate([front, back], axis=0)
            weight = jnp.exp2(optical - exponent) - jnp.exp2(optical)
            alpha = 1.0 - jnp.exp2(back[7:8])
            results = []
            for c in range(3):
                half_logit = (
                    (0.5 * col_ref[c, 0]) * porous
                    + (0.5 * col_ref[c, 1]) * grain
                    + 0.5 * col_ref[c, 2]
                )
                shaded = weight * jnp.tanh(half_logit)
                total = jnp.sum(shaded[:8] + shaded[8:], axis=0, keepdims=True)
                results.append(0.5 * (alpha + total))
            results.append(alpha)
            group, row = tile >> (3 + col_bits), (tile >> col_bits) & 7
            col = tile & ((1 << col_bits) - 1)
            for c in range(4):
                part[piece, group, col, pl.ds(c * 8 + row, 1), :] = results[c]

    def some_tiles(batch, carry):
        codes = [heads[kernel, batch * UNROLL + place] for place in range(UNROLL)]
        march_tiles([(code, got_ref[code & 65535].astype(jnp.float32)) for code in codes])
        return carry

    found = heads[kernel, heads.shape[1] - 1]
    lax.fori_loop(0, (found + UNROLL - 1) >> bits_of(UNROLL), some_tiles, 0)

    def one_again(index, carry):
        code = again[kernel, index]
        entry = code & 65535

        def add_earlier(state):
            at, total = state
            return earlier[at], total + got_ref[at].astype(jnp.float32)

        grain = got_ref[entry].astype(jnp.float32)
        _, grain = lax.while_loop(
            lambda state: state[0] >= 0, add_earlier, (earlier[entry], grain)
        )
        march_tiles([(code, grain)])
        return carry

    lax.fori_loop(0, again[kernel, heads.shape[1] - 1], one_again, 0)

    pairs = part.shape[1] // 2
    for flips, keep_ref, send_ref in zip(chunks, keep_refs, send_refs):
        for place, flip in enumerate(flips):

            def split(pair, carry):
                at = place * pairs + pair
                send_ref[at] = part[flip & 1, 2 * pair + 1 - own_x].astype(jnp.bfloat16)
                keep_ref[at] = part[flip & 1, 2 * pair + own_x]
                return carry

            lax.fori_loop(0, pairs, split, 0)


def march_grain(kernel, plan, got, porous_tiles, part, dev, extinction, color_weights, slots, mesh):
    width_x, width_y = mesh
    chunks = KERNELS[kernel]
    smem = pl.BlockSpec(memory_space=pltpu.SMEM)
    vmem = pl.BlockSpec(memory_space=pltpu.VMEM)
    hbm = pl.BlockSpec(memory_space=pltpu.HBM)
    entries = got.shape[0]
    sources = entries // (slots + 1)
    tile_count = porous_tiles.shape[0]
    groups = part.shape[0] // width_x
    split = [(len(flips) * groups // 2,) + part.shape[1:] for flips in chunks]
    scratch = [
        pltpu.VMEM((2, tile_count // width_x) + porous_tiles.shape[1:], porous_tiles.dtype),
        pltpu.VMEM((2, groups) + part.shape[1:], part.dtype),
        pltpu.SemaphoreType.DMA((4,)),
    ]
    plan_shapes = []
    if kernel == 0:
        most = -(-(entries + UNROLL + 1) // 128) * 128
        plan_shapes = [
            jax.ShapeDtypeStruct((2, most), jnp.int32),
            jax.ShapeDtypeStruct((2, most), jnp.int32),
            jax.ShapeDtypeStruct((entries + UNROLL,), jnp.int32),
        ]
        scratch += [
            pltpu.VMEM((sources, 128), jnp.int32),
            pltpu.SMEM((sources, 128), jnp.int32),
            pltpu.SMEM((tile_count + 1,), jnp.int32),
            pltpu.SemaphoreType.DMA((2,)),
        ]
        before, before_specs = [jnp.full((tile_count,), -1, jnp.int32)], [hbm]
    else:
        before, before_specs = plan, [smem] * 3
    outs = pl.pallas_call(
        functools.partial(grain_kernel, kernel=kernel, slots=slots, gy_bits=bits_of(width_y)),
        out_shape=[jax.ShapeDtypeStruct(shape, jnp.float32) for shape in split]
        + [jax.ShapeDtypeStruct(shape, jnp.bfloat16) for shape in split]
        + plan_shapes,
        in_specs=[smem] * 3 + before_specs + [hbm] * 2 + [vmem],
        out_specs=[vmem] * (2 * len(chunks)) + [smem] * len(plan_shapes),
        scratch_shapes=scratch,
        compiler_params=pltpu.CompilerParams(vmem_limit_bytes=GRAIN_LIMIT),
        cost_estimate=pl.CostEstimate(flops=1000, bytes_accessed=1000, transcendentals=0),
        name=f"march_grain_{kernel}",
    )(dev, extinction, color_weights, *before, porous_tiles, part, got)
    keeps, sends = outs[: len(chunks)], outs[len(chunks) : 2 * len(chunks)]
    return list(zip(chunks, keeps, sends)), outs[2 * len(chunks) :]


def ordered(mine, theirs, mine_near):
    nearer = [jnp.where(mine_near, a, b) for a, b in zip(mine, theirs)]
    farther = [jnp.where(mine_near, b, a) for a, b in zip(mine, theirs)]
    open_part = 1.0 - nearer[3]
    return [n + open_part * f for n, f in zip(nearer, farther)]


def channels_of(block):
    block = block.astype(jnp.float32)
    rows = block.shape[0] // 4
    return [block[c * rows : (c + 1) * rows] for c in range(4)]


def swap_kernel(dev_ref, rank_ref, mine_ref, got_ref, *out_refs, stage, first):
    device = dev_ref[0]
    mine_near = (rank_ref[device] >> stage) & 1 == 0
    low, high = (device >> 1) & 1, (device >> 2) & 1

    def one_column(col, carry):
        for way, out_ref in enumerate(out_refs):
            for place in range(out_ref.shape[0]):
                group = first + [2 * place + (low ^ way), high ^ way, 0][stage]
                merged = ordered(
                    channels_of(mine_ref[group, col]), channels_of(got_ref[group, col]), mine_near
                )
                out_ref[place, col] = jnp.concatenate(merged, axis=0).astype(out_ref.dtype)
        return carry

    lax.fori_loop(0, got_ref.shape[1], one_column, 0)


def swap_rows(mine, got, dev, ranks, stage, first=0):
    smem = pl.BlockSpec(memory_space=pltpu.SMEM)
    vmem = pl.BlockSpec(memory_space=pltpu.VMEM)
    kept = ((2, 1, 1)[stage],) + got.shape[1:]
    dtypes = (jnp.float32, jnp.bfloat16) if stage < 2 else (jnp.float32,)
    out_shape = [jax.ShapeDtypeStruct(kept, dtype) for dtype in dtypes]
    return pl.pallas_call(
        functools.partial(swap_kernel, stage=stage, first=first),
        out_shape=out_shape,
        in_specs=[smem, smem, vmem, vmem],
        out_specs=[vmem] * len(out_shape),
        compiler_params=pltpu.CompilerParams(vmem_limit_bytes=SMALL_LIMIT),
        cost_estimate=pl.CostEstimate(flops=1000, bytes_accessed=1000, transcendentals=0),
        name=f"swap_rows_{stage}",
    )(dev, ranks, mine, got)


def spread_kernel(dev_ref, rank_ref, mine_ref, got_ref, own_ref, *send_refs, around):
    device = dev_ref[0]
    mine_near = rank_ref[device] & 1 == 0
    place = (device >> 1) & (around - 1)

    def one_column(col, carry):
        for distance, out_ref in enumerate((own_ref, *send_refs)):
            group = place ^ distance
            merged = ordered(
                channels_of(mine_ref[group, col]), channels_of(got_ref[group, col]), mine_near
            )
            out_ref[col] = jnp.concatenate(merged, axis=0).astype(out_ref.dtype)
        return carry

    lax.fori_loop(0, got_ref.shape[1], one_column, 0)


def spread_rows(mine, got, dev, ranks, width_y):
    smem = pl.BlockSpec(memory_space=pltpu.SMEM)
    vmem = pl.BlockSpec(memory_space=pltpu.VMEM)
    around = width_y // 2
    return pl.pallas_call(
        functools.partial(spread_kernel, around=around),
        out_shape=[jax.ShapeDtypeStruct(got.shape[1:], jnp.float32)]
        + [jax.ShapeDtypeStruct(got.shape[1:], jnp.bfloat16)] * (around - 1),
        in_specs=[smem, smem, vmem, vmem],
        out_specs=[vmem] * around,
        compiler_params=pltpu.CompilerParams(vmem_limit_bytes=SMALL_LIMIT),
        cost_estimate=pl.CostEstimate(flops=1000, bytes_accessed=1000, transcendentals=0),
        name="spread_rows",
    )(dev, ranks, mine, got)


def four_way(device, rank_ref, parts, stride, bit):
    low = (rank_ref[device] >> bit) & 1 == 0
    far_low = (rank_ref[device ^ (2 * stride)] >> bit) & 1 == 0
    high = (rank_ref[device] >> (bit + 1)) & 1 == 0
    return ordered(
        ordered(parts[0], parts[1], low), ordered(parts[2], parts[3], far_low), high
    )


def last_kernel(dev_ref, rank_ref, *refs, width_y):
    own_refs, pair_refs, far_refs, out_ref = refs[:4], refs[4:6], refs[6:8], refs[8]
    device = dev_ref[0]
    col_blocks = own_refs[0].shape[0]
    next_near = (rank_ref[device ^ width_y] >> 2) & 1 == 0
    for col in range(col_blocks):
        own = [channels_of(ref[col]) for ref in own_refs]
        parts = [four_way(device, rank_ref, own, 2, 1)]
        parts.append(ordered(*(channels_of(ref[0, col]) for ref in pair_refs), next_near))
        parts += [channels_of(ref[0, col]) for ref in far_refs]
        merged = four_way(device, rank_ref, parts, width_y, bits_of(width_y))
        for c in range(4):
            for row in range(merged[c].shape[0]):
                start = (row * col_blocks + col) * 128
                out_ref[c : c + 1, start : start + 128] = merged[c][row : row + 1]


def last_rows(own, others, ready, dev, ranks, width_y):
    smem = pl.BlockSpec(memory_space=pltpu.SMEM)
    vmem = pl.BlockSpec(memory_space=pltpu.VMEM)
    return pl.pallas_call(
        functools.partial(last_kernel, width_y=width_y),
        out_shape=jax.ShapeDtypeStruct((4, own.size // 4), jnp.float32),
        in_specs=[smem, smem] + [vmem] * 8,
        out_specs=vmem,
        compiler_params=pltpu.CompilerParams(vmem_limit_bytes=SMALL_LIMIT),
        name="last_rows",
    )(dev, ranks, own, *others, *ready[1], *ready[2], *ready[3])


def shards(porosity, grain_blocks, owners, tiles, live_counts, ranks, extinction, color_weights):
    width_x = lax.axis_size("gx")
    width_y = lax.axis_size("gy")
    device_count = width_x * width_y
    block_count = grain_blocks.shape[0]
    slots = max(2, 2 * block_count // device_count)
    dev = lax.axis_index(("gx", "gy")).astype(jnp.int32).reshape(1)
    packed = pack_blocks(grain_blocks, owners[:, 0], tiles, live_counts, device_count, slots)
    got = lax.all_to_all(packed, ("gx", "gy"), split_axis=0, concat_axis=0, tiled=True)
    got = got.reshape((-1,) + got.shape[2:])
    porosity, _ = lax.optimization_barrier((porosity, packed))
    part, porous_tiles = march_empty(porosity, extinction, color_weights)
    got, part, porous_tiles = lax.optimization_barrier((got, part, porous_tiles))
    work, plan = [], None
    for kernel in range(len(KERNELS)):
        made, planned = march_grain(
            kernel,
            plan,
            got,
            porous_tiles,
            part,
            dev,
            extinction,
            color_weights,
            slots,
            (width_x, width_y),
        )
        plan = plan or planned
        for flips, keep, send in made:
            arrived = exchanged(send, "gy", 1)
            for piece, flip in enumerate(flips):
                work.append((flip, piece * keep.shape[0] // len(flips), keep, arrived))
    ready = [None] * width_x
    token = work[-1][2]
    state = {flip: (mine, got, first) for flip, first, mine, got in work}
    for flip, stage in ORDER:
        mine, got, first = state[flip]
        got, token = lax.optimization_barrier((got, token))
        if flip == 0:
            own, *sends = spread_rows(mine, got, dev, ranks, width_y)
            others = [exchanged(send, "gy", 2 * (k + 1)) for k, send in enumerate(sends)]
            token = own
            continue
        mine, *send = swap_rows(mine, got, dev, ranks, stage, first)
        token = mine
        if stage == 0:
            state[flip] = mine, exchanged(send[0], "gy", 2), 0
        elif flip == 1:
            far = exchanged(send[0], ("gx", "gy"), flip * width_y + 4)
            ready[flip] = exchanged(mine, "gx", flip), far
        elif stage == 1:
            state[flip] = mine, exchanged(send[0], "gy", 4), 0
        else:
            ready[flip] = (exchanged(mine, "gx", flip),)
    return last_rows(own, others, ready, dev, ranks, width_y)


def march_flat(porous_flat, grain_flat, extinction, color_weights):
    porous = porous_flat.astype(jnp.float32)
    extinct = extinction[0] * (1.0 - porous) + extinction[1] * grain_flat
    optical = jnp.cumsum(extinct, axis=0)
    before = optical - extinct
    weight = jnp.exp(-before) * (1.0 - jnp.exp(-extinct))
    channels = []
    for channel in range(3):
        colour = jax.nn.sigmoid(
            color_weights[channel, 0] * porous
            + color_weights[channel, 1] * grain_flat
            + color_weights[channel, 2]
        )
        channels.append(jnp.sum(weight * colour, axis=0))
    channels.append(1.0 - jnp.exp(-optical[-1]))
    return jnp.stack(channels, axis=0)


def composite(nearer, farther):
    return nearer + (1.0 - nearer[3:4]) * farther


def shards_any(
    porosity, grain_blocks, owners, tiles, live_counts, ranks, extinction, color_weights
):
    width_x = lax.axis_size("gx")
    width_y = lax.axis_size("gy")
    device_count = width_x * width_y
    depth_cells, image_rows, image_cols = porosity.shape
    block_count, _, block_cols = grain_blocks.shape
    slots = max(2, 2 * block_count // device_count)
    tile_count = image_rows * image_cols // block_cols
    pixel_count = image_rows * image_cols
    block_len = pixel_count // device_count
    packed = pack_blocks(grain_blocks, owners[:, 0], tiles, live_counts, device_count, slots)
    got = lax.all_to_all(packed, ("gx", "gy"), split_axis=0, concat_axis=0, tiled=True)
    coded = got[:, slots, :2, : slots + 1].astype(jnp.int32)
    table = coded[:, 0] * 64 + coded[:, 1]
    used = jnp.arange(slots, dtype=jnp.int32)[None, :] < table[:, slots:]
    got_tile = jnp.where(used, table[:, :slots], tile_count)
    got_data = jnp.where(used[:, :, None, None], got[:, :slots], jnp.bfloat16(0))
    grain_tiles = (
        jnp.zeros((tile_count, depth_cells, block_cols), jnp.float32)
        .at[got_tile.reshape(-1)]
        .add(
            got_data.reshape(device_count * slots, depth_cells, block_cols).astype(jnp.float32),
            mode="drop",
        )
    )
    grain_flat = jnp.transpose(grain_tiles, (1, 0, 2)).reshape(depth_cells, pixel_count)
    porous_flat = porosity.reshape(depth_cells, pixel_count)
    partial_value = march_flat(porous_flat, grain_flat, extinction, color_weights)
    my_rank = ranks[lax.axis_index(("gx", "gy"))]
    bits_y = width_y.bit_length() - 1
    bits_x = width_x.bit_length() - 1
    current = partial_value.reshape(4, width_x, width_y, block_len)
    for axis, dim, bits, first in (("gy", 2, bits_y, 0), ("gx", 1, bits_x, bits_y)):
        for section_bit in range(bits):
            shape = current.shape
            paired = current.reshape(
                shape[:dim] + (shape[dim] // 2, 2) + shape[dim + 1 :]
            )
            own_bit = lax.axis_index(axis) >> section_bit & 1
            kept_half = lax.dynamic_index_in_dim(paired, own_bit, dim + 1, keepdims=False)
            sent_half = lax.dynamic_index_in_dim(paired, 1 - own_bit, dim + 1, keepdims=False)
            partner = exchanged(sent_half, axis, 1 << section_bit)
            nearer_side = my_rank >> first + section_bit & 1 == 0
            current = composite(
                jnp.where(nearer_side, kept_half, partner),
                jnp.where(nearer_side, partner, kept_half),
            )
        if dim == 2:
            current = current.reshape(4, width_x, 1, block_len).reshape(4, width_x, block_len)
    return current.reshape(4, block_len)


def solution(mesh):
    in_specs = (
        P(("gx", "gy"), None, None),
        P(("gx", "gy"), None, None),
        P(("gx", "gy"), None),
        P(("gx", "gy")),
        P(("gx", "gy")),
        P(),
        P(),
        P(),
    )
    out_specs = P(None, ("gx", "gy"))

    def run(porosity, *rest):
        rows = porosity.shape[1] // (mesh.shape["gx"] * mesh.shape["gy"])
        fits = mesh.shape["gx"] == 4 and mesh.shape["gy"] == 8 and rows == 8
        return jax.shard_map(
            shards if fits else shards_any,
            mesh=mesh,
            in_specs=in_specs,
            out_specs=out_specs,
            check_vma=False,
        )(porosity, *rest)

    return run
```

```python
import functools

import jax
import jax.numpy as jnp
from jax import lax
from jax.experimental import pallas as pl
from jax.experimental.pallas import tpu as pltpu
from jax.sharding import PartitionSpec as P

LOG2E = 1.4426950408889634
PACK_LIMIT = 56 * 1024 * 1024
EMPTY_LIMIT = 24 * 1024 * 1024
GRAIN_LIMIT = 47 * 1024 * 1024
SMALL_LIMIT = 8 * 1024 * 1024
UNROLL = 4
KERNELS = (((3, 2),), ((1,), (0,)))
ORDER = ((0, 0), (1, 0), (0, 1), (1, 1), (2, 0), (1, 2), (0, 2), (2, 1), (2, 2))


def exchanged(block, axis, distance):
    route = [(low, low ^ distance) for low in range(lax.axis_size(axis))]
    return lax.ppermute(block, axis, route)


def bits_of(size):
    assert size & (size - 1) == 0
    return size.bit_length() - 1


def pack_kernel(
    owner_ref, tile_ref, live_ref, block_ref, out_ref, table, table_vec, table_sem, *, slots
):
    owners_all = out_ref.shape[0]

    def clear(owner, carry):
        table[owner, slots] = 0
        return carry

    lax.fori_loop(0, owners_all, clear, 0)

    def place(index, carry):
        owner = owner_ref[index]
        slot = table[owner, slots]
        table[owner, slots] = slot + 1
        table[owner, slot] = tile_ref[index]
        out_ref[owner, slot] = block_ref[index]
        return carry

    lax.fori_loop(0, live_ref[0], place, 0)
    copy = pltpu.make_async_copy(table, table_vec, table_sem)
    copy.start()
    copy.wait()
    first = lax.broadcasted_iota(jnp.int32, (16, 128), 0) == 0
    for owner in range(owners_all):
        row = jnp.broadcast_to(table_vec[owner : owner + 1, :], (16, 128))
        coded = jnp.where(first, row >> 6, row & 63)
        out_ref[owner, slots] = coded.astype(jnp.float32).astype(jnp.bfloat16)


def pack_blocks(grain_blocks, owner_dev, tiles, live_counts, device_count, slots):
    smem = pl.BlockSpec(memory_space=pltpu.SMEM)
    vmem = pl.BlockSpec(memory_space=pltpu.VMEM)
    return pl.pallas_call(
        functools.partial(pack_kernel, slots=slots),
        out_shape=jax.ShapeDtypeStruct(
            (device_count, slots + 1) + grain_blocks.shape[1:], grain_blocks.dtype
        ),
        in_specs=[smem, smem, smem, vmem],
        out_specs=vmem,
        scratch_shapes=[
            pltpu.SMEM((device_count, 128), jnp.int32),
            pltpu.VMEM((device_count, 128), jnp.int32),
            pltpu.SemaphoreType.DMA(()),
        ],
        compiler_params=pltpu.CompilerParams(vmem_limit_bytes=PACK_LIMIT),
        name="pack_blocks",
    )(owner_dev, tiles, live_counts, grain_blocks)


def plan_tiles(gx, piece_bits, nowhere, got_ref, plan, ids_vec, ids, last, sems, slots):
    heads, again, earlier = plan
    nowhere_tile = last.shape[0] - 1
    sources = ids.shape[0]
    forget = pltpu.make_async_copy(nowhere, last.at[pl.ds(0, nowhere.shape[0])], sems.at[0])
    forget.start()
    for source in range(sources):
        coded = got_ref[source * (slots + 1) + slots].astype(jnp.float32)
        ids_vec[source : source + 1, :] = (coded[0:1, :] * 64.0 + coded[1:2, :]).astype(jnp.int32)
    fetch = pltpu.make_async_copy(ids_vec, ids, sems.at[1])
    fetch.start()
    last[nowhere_tile] = -1
    fetch.wait()
    forget.wait()

    def from_source(source, counts):
        live = ids[source, slots]

        def some(batch, counts):
            count = list(counts)
            found = []
            for place in range(UNROLL):
                slot = batch * UNROLL + place
                entry = source * (slots + 1) + slot
                valid = slot < live
                tile = jnp.where(valid, ids[source, slot], nowhere_tile)
                before = last[tile]
                last[tile] = entry
                found.append((entry, tile, valid, before))
            for entry, tile, valid, before in found:
                earlier[entry] = before
                code = entry + (tile << 16)
                kernel = 1 - (((tile >> piece_bits) ^ gx) >> 1) & 1
                heads[kernel, jnp.where(kernel == 0, count[0], count[1])] = code
                again[kernel, jnp.where(kernel == 0, count[2], count[3])] = code
                one = jnp.where(valid, 1, 0)
                more = jnp.where(jnp.logical_and(valid, before >= 0), 1, 0)
                count[0] = count[0] + (1 - kernel) * one
                count[1] = count[1] + kernel * one
                count[2] = count[2] + (1 - kernel) * more
                count[3] = count[3] + kernel * more
            return tuple(count)

        return lax.fori_loop(0, (live + UNROLL - 1) >> bits_of(UNROLL), some, counts)

    counts = lax.fori_loop(0, sources, from_source, (jnp.int32(0),) * 4)

    for kernel in range(2):
        found = counts[kernel]
        heads[kernel, heads.shape[1] - 1] = found
        again[kernel, heads.shape[1] - 1] = counts[2 + kernel]

        @pl.when(found > 0)
        def _():
            for extra in range(UNROLL - 1):
                heads[kernel, found + extra] = heads[kernel, found - 1]


def empty_kernel(ext_ref, col_ref, por_hbm, part, por_tiles, por, turned, sems):
    depth, rows, cols = por_hbm.shape
    block_rows = por.shape[2]
    half_rows = block_rows // 2
    col_blocks = cols // 128
    steps = rows // block_rows
    base = -LOG2E * ext_ref[0]
    slope = LOG2E * ext_ref[0]

    def fetch(step, slot):
        start = pl.multiple_of(step * block_rows, block_rows)
        return pltpu.make_async_copy(
            por_hbm.at[:, pl.ds(start, block_rows), :], por.at[slot], sems.at[slot]
        )

    fetch(0, 0).start()

    def one_step(step, carry):
        slot = lax.rem(step, 2)

        @pl.when(step + 1 < steps)
        def _():
            fetch(step + 1, 1 - slot).start()

        fetch(step, slot).wait()

        def one_column(col, carry):
            lanes = pl.ds(pl.multiple_of(col * 128, 128), 128)
            clear = jnp.ones((block_rows, 128), jnp.float32)
            sums = [jnp.zeros((block_rows, 128), jnp.float32) for _ in range(3)]
            for z in range(depth):
                porous = por[slot, z, :, lanes].astype(jnp.float32)
                turned[z * block_rows : (z + 1) * block_rows, :] = porous
                passed = clear * jnp.exp2(base + slope * porous)
                weight = clear - passed
                clear = passed
                for c in range(3):
                    half_logit = (0.5 * col_ref[c, 0]) * porous + 0.5 * col_ref[c, 2]
                    sums[c] = sums[c] + weight * jnp.tanh(half_logit)
            for row in range(block_rows):
                tile = (step * block_rows + row) * col_blocks + col
                por_tiles[tile] = turned[pl.ds(row, depth, stride=block_rows), :].astype(
                    jnp.bfloat16
                )
            alpha = 1.0 - clear
            parts = [0.5 * (alpha + total) for total in sums] + [alpha]
            for c in range(4):
                for half in range(2):
                    part[2 * step + half, col, c * half_rows : (c + 1) * half_rows, :] = parts[c][
                        half * half_rows : (half + 1) * half_rows
                    ]
            return carry

        lax.fori_loop(0, col_blocks, one_column, 0)
        return carry

    lax.fori_loop(0, steps, one_step, 0)


def march_empty(porosity, extinction, color_weights):
    depth, rows, cols = porosity.shape
    block_rows = 16
    smem = pl.BlockSpec(memory_space=pltpu.SMEM)
    vmem = pl.BlockSpec(memory_space=pltpu.VMEM)
    return pl.pallas_call(
        empty_kernel,
        out_shape=[
            jax.ShapeDtypeStruct((rows // 8, cols // 128, 32, 128), jnp.float32),
            jax.ShapeDtypeStruct((rows * cols // 128, depth, 128), porosity.dtype),
        ],
        in_specs=[smem, smem, pl.BlockSpec(memory_space=pl.ANY)],
        out_specs=[vmem, vmem],
        scratch_shapes=[
            pltpu.VMEM((2, depth, block_rows, cols), porosity.dtype),
            pltpu.VMEM((depth * block_rows, 128), jnp.float32),
            pltpu.SemaphoreType.DMA((2,)),
        ],
        compiler_params=pltpu.CompilerParams(vmem_limit_bytes=EMPTY_LIMIT),
        cost_estimate=pl.CostEstimate(
            flops=20 * depth * rows * cols,
            bytes_accessed=4 * depth * rows * cols + 16 * rows * cols,
            transcendentals=4 * depth * rows * cols,
        ),
        name="march_empty",
    )(extinction, color_weights, porosity)


def grain_kernel(dev_ref, ext_ref, col_ref, *refs, kernel, slots, gy_bits):
    chunks = KERNELS[kernel]
    if kernel == 0:
        nowhere, *refs = refs
    else:
        plan, refs = refs[:3], refs[3:]
    por_hbm, part_hbm, got_ref, *refs = refs
    keep_refs, send_refs = refs[: len(chunks)], refs[len(chunks) : 2 * len(chunks)]
    refs = refs[2 * len(chunks) :]
    if kernel == 0:
        plan, refs = refs[:3], refs[3:]
    por_ref, part, sems, *scratch = refs
    own_x = dev_ref[0] & 1
    gx = dev_ref[0] >> gy_bits
    col_bits = bits_of(part.shape[2])
    piece_bits = bits_of(por_ref.shape[1])
    fetches = []
    for piece in range(2):
        chunk = gx ^ (piece + 2 * (1 - kernel))
        for place, (hbm, ref) in enumerate(((part_hbm, part), (por_hbm, por_ref))):
            rows = pl.ds(chunk * ref.shape[1], ref.shape[1])
            fetches.append(
                pltpu.make_async_copy(hbm.at[rows], ref.at[piece], sems.at[2 * piece + place])
            )
    for fetch in fetches:
        fetch.start()
    if kernel == 0:
        plan_tiles(gx, piece_bits, nowhere, got_ref, plan, *scratch, slots)
    heads, again, earlier = plan
    for fetch in fetches:
        fetch.wait()
    base = -LOG2E * ext_ref[0]
    slope = LOG2E * ext_ref[0]
    grain_slope = -LOG2E * ext_ref[1]
    depth_of = lax.broadcasted_iota(jnp.int32, (8, 128), 0)

    def running(value):
        for shift in (1, 2, 4):
            value = value + jnp.where(depth_of >= shift, pltpu.roll(value, shift, 0), 0.0)
        return value

    def march_tiles(work):
        for code, grain in work:
            tile = code >> 16
            piece = ((tile >> piece_bits) ^ gx) & 1
            tile = tile & ((1 << piece_bits) - 1)
            porous = por_ref[piece, tile].astype(jnp.float32)
            exponent = (base + slope * porous) + grain_slope * grain
            front = running(exponent[:8])
            back = running(exponent[8:]) + front[7:8]
            optical = jnp.concatenate([front, back], axis=0)
            weight = jnp.exp2(optical - exponent) - jnp.exp2(optical)
            alpha = 1.0 - jnp.exp2(back[7:8])
            results = []
            for c in range(3):
                half_logit = (
                    (0.5 * col_ref[c, 0]) * porous
                    + (0.5 * col_ref[c, 1]) * grain
                    + 0.5 * col_ref[c, 2]
                )
                shaded = weight * jnp.tanh(half_logit)
                total = jnp.sum(shaded[:8] + shaded[8:], axis=0, keepdims=True)
                results.append(0.5 * (alpha + total))
            results.append(alpha)
            group, row = tile >> (3 + col_bits), (tile >> col_bits) & 7
            col = tile & ((1 << col_bits) - 1)
            for c in range(4):
                part[piece, group, col, pl.ds(c * 8 + row, 1), :] = results[c]

    def some_tiles(batch, carry):
        codes = [heads[kernel, batch * UNROLL + place] for place in range(UNROLL)]
        march_tiles([(code, got_ref[code & 65535].astype(jnp.float32)) for code in codes])
        return carry

    found = heads[kernel, heads.shape[1] - 1]
    lax.fori_loop(0, (found + UNROLL - 1) >> bits_of(UNROLL), some_tiles, 0)

    def one_again(index, carry):
        code = again[kernel, index]
        entry = code & 65535

        def add_earlier(state):
            at, total = state
            return earlier[at], total + got_ref[at].astype(jnp.float32)

        grain = got_ref[entry].astype(jnp.float32)
        _, grain = lax.while_loop(
            lambda state: state[0] >= 0, add_earlier, (earlier[entry], grain)
        )
        march_tiles([(code, grain)])
        return carry

    lax.fori_loop(0, again[kernel, heads.shape[1] - 1], one_again, 0)

    pairs = part.shape[1] // 2
    for flips, keep_ref, send_ref in zip(chunks, keep_refs, send_refs):
        for place, flip in enumerate(flips):

            def split(pair, carry):
                at = place * pairs + pair
                send_ref[at] = part[flip & 1, 2 * pair + 1 - own_x].astype(jnp.bfloat16)
                keep_ref[at] = part[flip & 1, 2 * pair + own_x]
                return carry

            lax.fori_loop(0, pairs, split, 0)


def march_grain(kernel, plan, got, porous_tiles, part, dev, extinction, color_weights, slots, mesh):
    width_x, width_y = mesh
    chunks = KERNELS[kernel]
    smem = pl.BlockSpec(memory_space=pltpu.SMEM)
    vmem = pl.BlockSpec(memory_space=pltpu.VMEM)
    hbm = pl.BlockSpec(memory_space=pltpu.HBM)
    entries = got.shape[0]
    sources = entries // (slots + 1)
    tile_count = porous_tiles.shape[0]
    groups = part.shape[0] // width_x
    split = [(len(flips) * groups // 2,) + part.shape[1:] for flips in chunks]
    scratch = [
        pltpu.VMEM((2, tile_count // width_x) + porous_tiles.shape[1:], porous_tiles.dtype),
        pltpu.VMEM((2, groups) + part.shape[1:], part.dtype),
        pltpu.SemaphoreType.DMA((4,)),
    ]
    plan_shapes = []
    if kernel == 0:
        most = -(-(entries + UNROLL + 1) // 128) * 128
        plan_shapes = [
            jax.ShapeDtypeStruct((2, most), jnp.int32),
            jax.ShapeDtypeStruct((2, most), jnp.int32),
            jax.ShapeDtypeStruct((entries + UNROLL,), jnp.int32),
        ]
        scratch += [
            pltpu.VMEM((sources, 128), jnp.int32),
            pltpu.SMEM((sources, 128), jnp.int32),
            pltpu.SMEM((tile_count + 1,), jnp.int32),
            pltpu.SemaphoreType.DMA((2,)),
        ]
        before, before_specs = [jnp.full((tile_count,), -1, jnp.int32)], [hbm]
    else:
        before, before_specs = plan, [smem] * 3
    outs = pl.pallas_call(
        functools.partial(grain_kernel, kernel=kernel, slots=slots, gy_bits=bits_of(width_y)),
        out_shape=[jax.ShapeDtypeStruct(shape, jnp.float32) for shape in split]
        + [jax.ShapeDtypeStruct(shape, jnp.bfloat16) for shape in split]
        + plan_shapes,
        in_specs=[smem] * 3 + before_specs + [hbm] * 2 + [vmem],
        out_specs=[vmem] * (2 * len(chunks)) + [smem] * len(plan_shapes),
        scratch_shapes=scratch,
        compiler_params=pltpu.CompilerParams(vmem_limit_bytes=GRAIN_LIMIT),
        cost_estimate=pl.CostEstimate(flops=1000, bytes_accessed=1000, transcendentals=0),
        name=f"march_grain_{kernel}",
    )(dev, extinction, color_weights, *before, porous_tiles, part, got)
    keeps, sends = outs[: len(chunks)], outs[len(chunks) : 2 * len(chunks)]
    return list(zip(chunks, keeps, sends)), outs[2 * len(chunks) :]


def ordered(mine, theirs, mine_near):
    nearer = [jnp.where(mine_near, a, b) for a, b in zip(mine, theirs)]
    farther = [jnp.where(mine_near, b, a) for a, b in zip(mine, theirs)]
    open_part = 1.0 - nearer[3]
    return [n + open_part * f for n, f in zip(nearer, farther)]


def channels_of(block):
    block = block.astype(jnp.float32)
    rows = block.shape[0] // 4
    return [block[c * rows : (c + 1) * rows] for c in range(4)]


def swap_kernel(dev_ref, rank_ref, mine_ref, got_ref, *out_refs, stage, pieces):
    device = dev_ref[0]
    mine_near = (rank_ref[device] >> stage) & 1 == 0
    low, high = (device >> 1) & 1, (device >> 2) & 1
    piece_groups = got_ref.shape[0] // pieces

    def one_column(col, carry):
        for piece in range(pieces):
            for way, out_ref in enumerate(out_refs):
                for place in range(out_ref.shape[0] // pieces):
                    group = [2 * place + (low ^ way), high ^ way, 0][stage] + piece * piece_groups
                    merged = ordered(
                        channels_of(mine_ref[group, col]),
                        channels_of(got_ref[group, col]),
                        mine_near,
                    )
                    merged = jnp.concatenate(merged, axis=0).astype(out_ref.dtype)
                    out_ref[piece * (out_ref.shape[0] // pieces) + place, col] = merged
        return carry

    lax.fori_loop(0, got_ref.shape[1], one_column, 0)


def swap_rows(mine, got, dev, ranks, stage, pieces):
    smem = pl.BlockSpec(memory_space=pltpu.SMEM)
    vmem = pl.BlockSpec(memory_space=pltpu.VMEM)
    kept = (max(1, got.shape[0] // 2) if stage < 2 else got.shape[0],) + got.shape[1:]
    out_shape = [jax.ShapeDtypeStruct(kept, jnp.float32)]
    if stage < 2:
        out_shape.append(jax.ShapeDtypeStruct(kept, jnp.bfloat16))
    return pl.pallas_call(
        functools.partial(swap_kernel, stage=stage, pieces=pieces),
        out_shape=out_shape,
        in_specs=[smem, smem, vmem, vmem],
        out_specs=[vmem] * len(out_shape),
        compiler_params=pltpu.CompilerParams(vmem_limit_bytes=SMALL_LIMIT),
        cost_estimate=pl.CostEstimate(flops=1000, bytes_accessed=1000, transcendentals=0),
        name=f"swap_rows_{stage}",
    )(dev, ranks, mine, got)


def four_way(device, rank_ref, parts, stride, bit):
    low = (rank_ref[device] >> bit) & 1 == 0
    far_low = (rank_ref[device ^ (2 * stride)] >> bit) & 1 == 0
    high = (rank_ref[device] >> (bit + 1)) & 1 == 0
    return ordered(
        ordered(parts[0], parts[1], low), ordered(parts[2], parts[3], far_low), high
    )


def last_kernel(dev_ref, rank_ref, mine_ref, got_ref, q1, q2, q3, out_ref, *, width_y):
    device = dev_ref[0]
    mine_near = (rank_ref[device] >> 2) & 1 == 0
    col_blocks = mine_ref.shape[1]
    for col in range(col_blocks):
        mine = ordered(channels_of(mine_ref[0, col]), channels_of(got_ref[0, col]), mine_near)
        parts = [mine] + [channels_of(ref[0, col]) for ref in (q1, q2, q3)]
        merged = four_way(device, rank_ref, parts, width_y, bits_of(width_y))
        for c in range(4):
            for row in range(merged[c].shape[0]):
                start = (row * col_blocks + col) * 128
                out_ref[c : c + 1, start : start + 128] = merged[c][row : row + 1]


def last_rows(mine, got, ready, dev, ranks, width_y):
    smem = pl.BlockSpec(memory_space=pltpu.SMEM)
    vmem = pl.BlockSpec(memory_space=pltpu.VMEM)
    return pl.pallas_call(
        functools.partial(last_kernel, width_y=width_y),
        out_shape=jax.ShapeDtypeStruct((4, mine.size // 4), jnp.float32),
        in_specs=[smem, smem] + [vmem] * 5,
        out_specs=vmem,
        compiler_params=pltpu.CompilerParams(vmem_limit_bytes=SMALL_LIMIT),
        name="last_rows",
    )(dev, ranks, mine, got, *ready)


def shards(porosity, grain_blocks, owners, tiles, live_counts, ranks, extinction, color_weights):
    width_x = lax.axis_size("gx")
    width_y = lax.axis_size("gy")
    device_count = width_x * width_y
    block_count = grain_blocks.shape[0]
    slots = max(2, 2 * block_count // device_count)
    dev = lax.axis_index(("gx", "gy")).astype(jnp.int32).reshape(1)
    packed = pack_blocks(grain_blocks, owners[:, 0], tiles, live_counts, device_count, slots)
    got = lax.all_to_all(packed, ("gx", "gy"), split_axis=0, concat_axis=0, tiled=True)
    got = got.reshape((-1,) + got.shape[2:])
    porosity, _ = lax.optimization_barrier((porosity, packed))
    part, porous_tiles = march_empty(porosity, extinction, color_weights)
    got, part, porous_tiles = lax.optimization_barrier((got, part, porous_tiles))
    work, plan = [], None
    for kernel in range(len(KERNELS)):
        made, planned = march_grain(
            kernel,
            plan,
            got,
            porous_tiles,
            part,
            dev,
            extinction,
            color_weights,
            slots,
            (width_x, width_y),
        )
        plan = plan or planned
        for flips, keep, send in made:
            work.append((flips, keep, exchanged(send, "gy", 1)))
    ready = [None] * (width_x - 1)
    token = work[-1][1]
    for chunk, stage in ORDER:
        flips, mine, got = work[chunk]
        got, token = lax.optimization_barrier((got, token))
        if flips == (0,) and stage == 2:
            return last_rows(mine, got, ready, dev, ranks, width_y)
        mine, *send = swap_rows(mine, got, dev, ranks, stage, len(flips))
        token = mine
        if stage < 2:
            work[chunk] = flips, mine, exchanged(send[0], "gy", 2 << stage)
            continue
        for piece, flip in enumerate(flips):
            ready[flip - 1] = exchanged(mine[piece : piece + 1], "gx", flip)


def march_flat(porous_flat, grain_flat, extinction, color_weights):
    porous = porous_flat.astype(jnp.float32)
    extinct = extinction[0] * (1.0 - porous) + extinction[1] * grain_flat
    optical = jnp.cumsum(extinct, axis=0)
    before = optical - extinct
    weight = jnp.exp(-before) * (1.0 - jnp.exp(-extinct))
    channels = []
    for channel in range(3):
        colour = jax.nn.sigmoid(
            color_weights[channel, 0] * porous
            + color_weights[channel, 1] * grain_flat
            + color_weights[channel, 2]
        )
        channels.append(jnp.sum(weight * colour, axis=0))
    channels.append(1.0 - jnp.exp(-optical[-1]))
    return jnp.stack(channels, axis=0)


def composite(nearer, farther):
    return nearer + (1.0 - nearer[3:4]) * farther


def shards_any(
    porosity, grain_blocks, owners, tiles, live_counts, ranks, extinction, color_weights
):
    width_x = lax.axis_size("gx")
    width_y = lax.axis_size("gy")
    device_count = width_x * width_y
    depth_cells, image_rows, image_cols = porosity.shape
    block_count, _, block_cols = grain_blocks.shape
    slots = max(2, 2 * block_count // device_count)
    tile_count = image_rows * image_cols // block_cols
    pixel_count = image_rows * image_cols
    block_len = pixel_count // device_count
    packed = pack_blocks(grain_blocks, owners[:, 0], tiles, live_counts, device_count, slots)
    got = lax.all_to_all(packed, ("gx", "gy"), split_axis=0, concat_axis=0, tiled=True)
    coded = got[:, slots, :2, : slots + 1].astype(jnp.int32)
    table = coded[:, 0] * 64 + coded[:, 1]
    used = jnp.arange(slots, dtype=jnp.int32)[None, :] < table[:, slots:]
    got_tile = jnp.where(used, table[:, :slots], tile_count)
    got_data = jnp.where(used[:, :, None, None], got[:, :slots], jnp.bfloat16(0))
    grain_tiles = (
        jnp.zeros((tile_count, depth_cells, block_cols), jnp.float32)
        .at[got_tile.reshape(-1)]
        .add(
            got_data.reshape(device_count * slots, depth_cells, block_cols).astype(jnp.float32),
            mode="drop",
        )
    )
    grain_flat = jnp.transpose(grain_tiles, (1, 0, 2)).reshape(depth_cells, pixel_count)
    porous_flat = porosity.reshape(depth_cells, pixel_count)
    partial_value = march_flat(porous_flat, grain_flat, extinction, color_weights)
    my_rank = ranks[lax.axis_index(("gx", "gy"))]
    bits_y = width_y.bit_length() - 1
    bits_x = width_x.bit_length() - 1
    current = partial_value.reshape(4, width_x, width_y, block_len)
    for axis, dim, bits, first in (("gy", 2, bits_y, 0), ("gx", 1, bits_x, bits_y)):
        for section_bit in range(bits):
            shape = current.shape
            paired = current.reshape(
                shape[:dim] + (shape[dim] // 2, 2) + shape[dim + 1 :]
            )
            own_bit = lax.axis_index(axis) >> section_bit & 1
            kept_half = lax.dynamic_index_in_dim(paired, own_bit, dim + 1, keepdims=False)
            sent_half = lax.dynamic_index_in_dim(paired, 1 - own_bit, dim + 1, keepdims=False)
            partner = exchanged(sent_half, axis, 1 << section_bit)
            nearer_side = my_rank >> first + section_bit & 1 == 0
            current = composite(
                jnp.where(nearer_side, kept_half, partner),
                jnp.where(nearer_side, partner, kept_half),
            )
        if dim == 2:
            current = current.reshape(4, width_x, 1, block_len).reshape(4, width_x, block_len)
    return current.reshape(4, block_len)


def solution(mesh):
    in_specs = (
        P(("gx", "gy"), None, None),
        P(("gx", "gy"), None, None),
        P(("gx", "gy"), None),
        P(("gx", "gy")),
        P(("gx", "gy")),
        P(),
        P(),
        P(),
    )
    out_specs = P(None, ("gx", "gy"))

    def run(porosity, *rest):
        rows = porosity.shape[1] // (mesh.shape["gx"] * mesh.shape["gy"])
        fits = mesh.shape["gx"] == 4 and mesh.shape["gy"] == 8 and rows == 8
        return jax.shard_map(
            shards if fits else shards_any,
            mesh=mesh,
            in_specs=in_specs,
            out_specs=out_specs,
            check_vma=False,
        )(porosity, *rest)

    return run
```

```python
import functools

import jax
import jax.numpy as jnp
from jax import lax
from jax.experimental import pallas as pl
from jax.experimental.pallas import tpu as pltpu
from jax.sharding import PartitionSpec as P

LOG2E = 1.4426950408889634
PACK_LIMIT = 56 * 1024 * 1024
EMPTY_LIMIT = 24 * 1024 * 1024
GRAIN_LIMIT = 47 * 1024 * 1024
SMALL_LIMIT = 8 * 1024 * 1024
UNROLL = 4
KERNELS = (((3, 2),), ((1,), (0,)))
ORDER = ((0, 0), (1, 0), (0, 1), (1, 1), (2, 0), (1, 2), (0, 2), (2, 1), (2, 2))


def exchanged(block, axis, distance):
    route = [(low, low ^ distance) for low in range(lax.axis_size(axis))]
    return lax.ppermute(block, axis, route)


def bits_of(size):
    assert size & (size - 1) == 0
    return size.bit_length() - 1


def pack_kernel(
    owner_ref, tile_ref, live_ref, block_ref, out_ref, table, table_vec, table_sem, *, slots
):
    owners_all = out_ref.shape[0]
    depth = block_ref.shape[1]

    def clear(owner, carry):
        table[owner, slots] = 0
        return carry

    lax.fori_loop(0, owners_all, clear, 0)

    def place(index, carry):
        owner = owner_ref[index]
        slot = table[owner, slots]
        table[owner, slots] = slot + 1
        table[owner, slot] = tile_ref[index]
        out_ref[owner, pl.ds(pl.multiple_of(slot * depth, depth), depth), :] = block_ref[index]
        return carry

    lax.fori_loop(0, live_ref[0], place, 0)
    copy = pltpu.make_async_copy(table, table_vec, table_sem)
    copy.start()
    copy.wait()
    first = lax.broadcasted_iota(jnp.int32, (8, 128), 0) == 0
    for owner in range(owners_all):
        row = jnp.broadcast_to(table_vec[owner : owner + 1, :], (8, 128))
        coded = jnp.where(first, row >> 6, row & 63)
        out_ref[owner, slots * depth :, :] = coded.astype(jnp.float32).astype(jnp.bfloat16)


def pack_blocks(grain_blocks, owner_dev, tiles, live_counts, device_count, slots):
    smem = pl.BlockSpec(memory_space=pltpu.SMEM)
    vmem = pl.BlockSpec(memory_space=pltpu.VMEM)
    return pl.pallas_call(
        functools.partial(pack_kernel, slots=slots),
        out_shape=jax.ShapeDtypeStruct(
            (device_count, slots * grain_blocks.shape[1] + 8, grain_blocks.shape[2]),
            grain_blocks.dtype,
        ),
        in_specs=[smem, smem, smem, vmem],
        out_specs=vmem,
        scratch_shapes=[
            pltpu.SMEM((device_count, 128), jnp.int32),
            pltpu.VMEM((device_count, 128), jnp.int32),
            pltpu.SemaphoreType.DMA(()),
        ],
        compiler_params=pltpu.CompilerParams(vmem_limit_bytes=PACK_LIMIT),
        name="pack_blocks",
    )(owner_dev, tiles, live_counts, grain_blocks)


def plan_tiles(gx, piece_bits, nowhere, got_ref, plan, ids_vec, ids, last, sems, slots):
    heads, again, earlier = plan
    nowhere_tile = last.shape[0] - 1
    sources = ids.shape[0]
    forget = pltpu.make_async_copy(nowhere, last.at[pl.ds(0, nowhere.shape[0])], sems.at[0])
    forget.start()
    for source in range(sources):
        coded = got_ref[source, got_ref.shape[1] - 8 :, :].astype(jnp.float32)
        ids_vec[source : source + 1, :] = (coded[0:1, :] * 64.0 + coded[1:2, :]).astype(jnp.int32)
    fetch = pltpu.make_async_copy(ids_vec, ids, sems.at[1])
    fetch.start()
    last[nowhere_tile] = -1
    fetch.wait()
    forget.wait()

    def from_source(source, counts):
        live = ids[source, slots]

        def some(batch, counts):
            count = list(counts)
            found = []
            for place in range(UNROLL):
                slot = batch * UNROLL + place
                entry = source * slots + slot
                valid = slot < live
                tile = jnp.where(valid, ids[source, slot], nowhere_tile)
                before = last[tile]
                last[tile] = entry
                found.append((entry, tile, valid, before))
            for entry, tile, valid, before in found:
                earlier[entry] = before
                code = entry + (tile << 16)
                kernel = 1 - (((tile >> piece_bits) ^ gx) >> 1) & 1
                heads[kernel, jnp.where(kernel == 0, count[0], count[1])] = code
                again[kernel, jnp.where(kernel == 0, count[2], count[3])] = code
                one = jnp.where(valid, 1, 0)
                more = jnp.where(jnp.logical_and(valid, before >= 0), 1, 0)
                count[0] = count[0] + (1 - kernel) * one
                count[1] = count[1] + kernel * one
                count[2] = count[2] + (1 - kernel) * more
                count[3] = count[3] + kernel * more
            return tuple(count)

        return lax.fori_loop(0, (live + UNROLL - 1) >> bits_of(UNROLL), some, counts)

    counts = lax.fori_loop(0, sources, from_source, (jnp.int32(0),) * 4)

    for kernel in range(2):
        found = counts[kernel]
        heads[kernel, heads.shape[1] - 1] = found
        again[kernel, heads.shape[1] - 1] = counts[2 + kernel]

        @pl.when(found > 0)
        def _():
            for extra in range(UNROLL - 1):
                heads[kernel, found + extra] = heads[kernel, found - 1]


def empty_kernel(ext_ref, col_ref, por_hbm, part, por_tiles, por, turned, sems):
    depth, rows, cols = por_hbm.shape
    block_rows = por.shape[2]
    half_rows = block_rows // 2
    col_blocks = cols // 128
    steps = rows // block_rows
    base = -LOG2E * ext_ref[0]
    slope = LOG2E * ext_ref[0]

    def fetch(step, slot):
        start = pl.multiple_of(step * block_rows, block_rows)
        return pltpu.make_async_copy(
            por_hbm.at[:, pl.ds(start, block_rows), :], por.at[slot], sems.at[slot]
        )

    fetch(0, 0).start()

    def one_step(step, carry):
        slot = lax.rem(step, 2)

        @pl.when(step + 1 < steps)
        def _():
            fetch(step + 1, 1 - slot).start()

        fetch(step, slot).wait()

        def one_column(col, carry):
            lanes = pl.ds(pl.multiple_of(col * 128, 128), 128)
            clear = jnp.ones((block_rows, 128), jnp.float32)
            sums = [jnp.zeros((block_rows, 128), jnp.float32) for _ in range(3)]
            for z in range(depth):
                porous = por[slot, z, :, lanes].astype(jnp.float32)
                turned[z * block_rows : (z + 1) * block_rows, :] = porous
                passed = clear * jnp.exp2(base + slope * porous)
                weight = clear - passed
                clear = passed
                for c in range(3):
                    half_logit = (0.5 * col_ref[c, 0]) * porous + 0.5 * col_ref[c, 2]
                    sums[c] = sums[c] + weight * jnp.tanh(half_logit)
            for row in range(block_rows):
                tile = (step * block_rows + row) * col_blocks + col
                por_tiles[tile] = turned[pl.ds(row, depth, stride=block_rows), :].astype(
                    jnp.bfloat16
                )
            alpha = 1.0 - clear
            parts = [0.5 * (alpha + total) for total in sums] + [alpha]
            for c in range(4):
                for half in range(2):
                    part[2 * step + half, col, c * half_rows : (c + 1) * half_rows, :] = parts[c][
                        half * half_rows : (half + 1) * half_rows
                    ]
            return carry

        lax.fori_loop(0, col_blocks, one_column, 0)
        return carry

    lax.fori_loop(0, steps, one_step, 0)


def march_empty(porosity, extinction, color_weights):
    depth, rows, cols = porosity.shape
    block_rows = 16
    smem = pl.BlockSpec(memory_space=pltpu.SMEM)
    vmem = pl.BlockSpec(memory_space=pltpu.VMEM)
    return pl.pallas_call(
        empty_kernel,
        out_shape=[
            jax.ShapeDtypeStruct((rows // 8, cols // 128, 32, 128), jnp.float32),
            jax.ShapeDtypeStruct((rows * cols // 128, depth, 128), porosity.dtype),
        ],
        in_specs=[smem, smem, pl.BlockSpec(memory_space=pl.ANY)],
        out_specs=[vmem, vmem],
        scratch_shapes=[
            pltpu.VMEM((2, depth, block_rows, cols), porosity.dtype),
            pltpu.VMEM((depth * block_rows, 128), jnp.float32),
            pltpu.SemaphoreType.DMA((2,)),
        ],
        compiler_params=pltpu.CompilerParams(vmem_limit_bytes=EMPTY_LIMIT),
        cost_estimate=pl.CostEstimate(
            flops=20 * depth * rows * cols,
            bytes_accessed=4 * depth * rows * cols + 16 * rows * cols,
            transcendentals=4 * depth * rows * cols,
        ),
        name="march_empty",
    )(extinction, color_weights, porosity)


def grain_kernel(dev_ref, ext_ref, col_ref, *refs, kernel, slots, gy_bits):
    chunks = KERNELS[kernel]
    if kernel == 0:
        nowhere, *refs = refs
    else:
        plan, refs = refs[:3], refs[3:]
    por_hbm, part_hbm, got_ref, *refs = refs
    keep_refs, send_refs = refs[: len(chunks)], refs[len(chunks) : 2 * len(chunks)]
    refs = refs[2 * len(chunks) :]
    if kernel == 0:
        plan, refs = refs[:3], refs[3:]
    por_ref, part, sems, *scratch = refs
    own_x = dev_ref[0] & 1
    gx = dev_ref[0] >> gy_bits
    col_bits = bits_of(part.shape[2])
    piece_bits = bits_of(por_ref.shape[1])
    fetches = []
    for piece in range(2):
        chunk = gx ^ (piece + 2 * (1 - kernel))
        for place, (hbm, ref) in enumerate(((part_hbm, part), (por_hbm, por_ref))):
            rows = pl.ds(chunk * ref.shape[1], ref.shape[1])
            fetches.append(
                pltpu.make_async_copy(hbm.at[rows], ref.at[piece], sems.at[2 * piece + place])
            )
    for fetch in fetches:
        fetch.start()
    if kernel == 0:
        plan_tiles(gx, piece_bits, nowhere, got_ref, plan, *scratch, slots)
    heads, again, earlier = plan
    for fetch in fetches:
        fetch.wait()

    def block_of(entry):
        depth = por_ref.shape[2]
        start = pl.multiple_of((entry & (slots - 1)) * depth, depth)
        block = got_ref[entry >> bits_of(slots), pl.ds(start, depth), :]
        return block.astype(jnp.float32)

    base = -LOG2E * ext_ref[0]
    slope = LOG2E * ext_ref[0]
    grain_slope = -LOG2E * ext_ref[1]
    depth_of = lax.broadcasted_iota(jnp.int32, (8, 128), 0)

    def running(value):
        for shift in (1, 2, 4):
            value = value + jnp.where(depth_of >= shift, pltpu.roll(value, shift, 0), 0.0)
        return value

    def march_tiles(work):
        for code, grain in work:
            tile = code >> 16
            piece = ((tile >> piece_bits) ^ gx) & 1
            tile = tile & ((1 << piece_bits) - 1)
            porous = por_ref[piece, tile].astype(jnp.float32)
            exponent = (base + slope * porous) + grain_slope * grain
            front = running(exponent[:8])
            back = running(exponent[8:]) + front[7:8]
            optical = jnp.concatenate([front, back], axis=0)
            weight = jnp.exp2(optical - exponent) - jnp.exp2(optical)
            alpha = 1.0 - jnp.exp2(back[7:8])
            results = []
            for c in range(3):
                half_logit = (
                    (0.5 * col_ref[c, 0]) * porous
                    + (0.5 * col_ref[c, 1]) * grain
                    + 0.5 * col_ref[c, 2]
                )
                shaded = weight * jnp.tanh(half_logit)
                total = jnp.sum(shaded[:8] + shaded[8:], axis=0, keepdims=True)
                results.append(0.5 * (alpha + total))
            results.append(alpha)
            group, row = tile >> (3 + col_bits), (tile >> col_bits) & 7
            col = tile & ((1 << col_bits) - 1)
            for c in range(4):
                part[piece, group, col, pl.ds(c * 8 + row, 1), :] = results[c]

    def some_tiles(batch, carry):
        codes = [heads[kernel, batch * UNROLL + place] for place in range(UNROLL)]
        march_tiles([(code, block_of(code & 65535)) for code in codes])
        return carry

    found = heads[kernel, heads.shape[1] - 1]
    lax.fori_loop(0, (found + UNROLL - 1) >> bits_of(UNROLL), some_tiles, 0)

    def one_again(index, carry):
        code = again[kernel, index]
        entry = code & 65535

        def add_earlier(state):
            at, total = state
            return earlier[at], total + block_of(at)

        _, grain = lax.while_loop(
            lambda state: state[0] >= 0, add_earlier, (earlier[entry], block_of(entry))
        )
        march_tiles([(code, grain)])
        return carry

    lax.fori_loop(0, again[kernel, heads.shape[1] - 1], one_again, 0)

    pairs = part.shape[1] // 2
    for flips, keep_ref, send_ref in zip(chunks, keep_refs, send_refs):
        for place, flip in enumerate(flips):

            def split(pair, carry):
                at = place * pairs + pair
                send_ref[at] = part[flip & 1, 2 * pair + 1 - own_x].astype(jnp.bfloat16)
                keep_ref[at] = part[flip & 1, 2 * pair + own_x]
                return carry

            lax.fori_loop(0, pairs, split, 0)


def march_grain(kernel, plan, got, porous_tiles, part, dev, extinction, color_weights, slots, mesh):
    width_x, width_y = mesh
    chunks = KERNELS[kernel]
    smem = pl.BlockSpec(memory_space=pltpu.SMEM)
    vmem = pl.BlockSpec(memory_space=pltpu.VMEM)
    hbm = pl.BlockSpec(memory_space=pltpu.HBM)
    sources = got.shape[0]
    entries = sources * slots
    tile_count = porous_tiles.shape[0]
    groups = part.shape[0] // width_x
    split = [(len(flips) * groups // 2,) + part.shape[1:] for flips in chunks]
    scratch = [
        pltpu.VMEM((2, tile_count // width_x) + porous_tiles.shape[1:], porous_tiles.dtype),
        pltpu.VMEM((2, groups) + part.shape[1:], part.dtype),
        pltpu.SemaphoreType.DMA((4,)),
    ]
    plan_shapes = []
    if kernel == 0:
        most = -(-(entries + UNROLL + 1) // 128) * 128
        plan_shapes = [
            jax.ShapeDtypeStruct((2, most), jnp.int32),
            jax.ShapeDtypeStruct((2, most), jnp.int32),
            jax.ShapeDtypeStruct((entries + UNROLL,), jnp.int32),
        ]
        scratch += [
            pltpu.VMEM((sources, 128), jnp.int32),
            pltpu.SMEM((sources, 128), jnp.int32),
            pltpu.SMEM((tile_count + 1,), jnp.int32),
            pltpu.SemaphoreType.DMA((2,)),
        ]
        before, before_specs = [jnp.full((tile_count,), -1, jnp.int32)], [hbm]
    else:
        before, before_specs = plan, [smem] * 3
    outs = pl.pallas_call(
        functools.partial(grain_kernel, kernel=kernel, slots=slots, gy_bits=bits_of(width_y)),
        out_shape=[jax.ShapeDtypeStruct(shape, jnp.float32) for shape in split]
        + [jax.ShapeDtypeStruct(shape, jnp.bfloat16) for shape in split]
        + plan_shapes,
        in_specs=[smem] * 3 + before_specs + [hbm] * 2 + [vmem],
        out_specs=[vmem] * (2 * len(chunks)) + [smem] * len(plan_shapes),
        scratch_shapes=scratch,
        compiler_params=pltpu.CompilerParams(vmem_limit_bytes=GRAIN_LIMIT),
        cost_estimate=pl.CostEstimate(flops=1000, bytes_accessed=1000, transcendentals=0),
        name=f"march_grain_{kernel}",
    )(dev, extinction, color_weights, *before, porous_tiles, part, got)
    keeps, sends = outs[: len(chunks)], outs[len(chunks) : 2 * len(chunks)]
    return list(zip(chunks, keeps, sends)), outs[2 * len(chunks) :]


def ordered(mine, theirs, mine_near):
    nearer = [jnp.where(mine_near, a, b) for a, b in zip(mine, theirs)]
    farther = [jnp.where(mine_near, b, a) for a, b in zip(mine, theirs)]
    open_part = 1.0 - nearer[3]
    return [n + open_part * f for n, f in zip(nearer, farther)]


def channels_of(block):
    block = block.astype(jnp.float32)
    rows = block.shape[0] // 4
    return [block[c * rows : (c + 1) * rows] for c in range(4)]


def swap_kernel(dev_ref, rank_ref, mine_ref, got_ref, *out_refs, stage, pieces):
    device = dev_ref[0]
    mine_near = (rank_ref[device] >> stage) & 1 == 0
    low, high = (device >> 1) & 1, (device >> 2) & 1
    piece_groups = got_ref.shape[0] // pieces

    def one_column(col, carry):
        for piece in range(pieces):
            for way, out_ref in enumerate(out_refs):
                for place in range(out_ref.shape[0] // pieces):
                    group = [2 * place + (low ^ way), high ^ way, 0][stage] + piece * piece_groups
                    merged = ordered(
                        channels_of(mine_ref[group, col]),
                        channels_of(got_ref[group, col]),
                        mine_near,
                    )
                    merged = jnp.concatenate(merged, axis=0).astype(out_ref.dtype)
                    out_ref[piece * (out_ref.shape[0] // pieces) + place, col] = merged
        return carry

    lax.fori_loop(0, got_ref.shape[1], one_column, 0)


def swap_rows(mine, got, dev, ranks, stage, pieces):
    smem = pl.BlockSpec(memory_space=pltpu.SMEM)
    vmem = pl.BlockSpec(memory_space=pltpu.VMEM)
    kept = (max(1, got.shape[0] // 2) if stage < 2 else got.shape[0],) + got.shape[1:]
    out_shape = [jax.ShapeDtypeStruct(kept, jnp.float32)]
    if stage < 2:
        out_shape.append(jax.ShapeDtypeStruct(kept, jnp.bfloat16))
    return pl.pallas_call(
        functools.partial(swap_kernel, stage=stage, pieces=pieces),
        out_shape=out_shape,
        in_specs=[smem, smem, vmem, vmem],
        out_specs=[vmem] * len(out_shape),
        compiler_params=pltpu.CompilerParams(vmem_limit_bytes=SMALL_LIMIT),
        cost_estimate=pl.CostEstimate(flops=1000, bytes_accessed=1000, transcendentals=0),
        name=f"swap_rows_{stage}",
    )(dev, ranks, mine, got)


def four_way(device, rank_ref, parts, stride, bit):
    low = (rank_ref[device] >> bit) & 1 == 0
    far_low = (rank_ref[device ^ (2 * stride)] >> bit) & 1 == 0
    high = (rank_ref[device] >> (bit + 1)) & 1 == 0
    return ordered(
        ordered(parts[0], parts[1], low), ordered(parts[2], parts[3], far_low), high
    )


def last_kernel(dev_ref, rank_ref, mine_ref, got_ref, q1, q2, q3, out_ref, *, width_y):
    device = dev_ref[0]
    mine_near = (rank_ref[device] >> 2) & 1 == 0
    col_blocks = mine_ref.shape[1]
    for col in range(col_blocks):
        mine = ordered(channels_of(mine_ref[0, col]), channels_of(got_ref[0, col]), mine_near)
        parts = [mine] + [channels_of(ref[0, col]) for ref in (q1, q2, q3)]
        merged = four_way(device, rank_ref, parts, width_y, bits_of(width_y))
        for c in range(4):
            for row in range(merged[c].shape[0]):
                start = (row * col_blocks + col) * 128
                out_ref[c : c + 1, start : start + 128] = merged[c][row : row + 1]


def last_rows(mine, got, ready, dev, ranks, width_y):
    smem = pl.BlockSpec(memory_space=pltpu.SMEM)
    vmem = pl.BlockSpec(memory_space=pltpu.VMEM)
    return pl.pallas_call(
        functools.partial(last_kernel, width_y=width_y),
        out_shape=jax.ShapeDtypeStruct((4, mine.size // 4), jnp.float32),
        in_specs=[smem, smem] + [vmem] * 5,
        out_specs=vmem,
        compiler_params=pltpu.CompilerParams(vmem_limit_bytes=SMALL_LIMIT),
        name="last_rows",
    )(dev, ranks, mine, got, *ready)


def shards(porosity, grain_blocks, owners, tiles, live_counts, ranks, extinction, color_weights):
    width_x = lax.axis_size("gx")
    width_y = lax.axis_size("gy")
    device_count = width_x * width_y
    block_count = grain_blocks.shape[0]
    slots = max(2, 2 * block_count // device_count)
    dev = lax.axis_index(("gx", "gy")).astype(jnp.int32).reshape(1)
    packed = pack_blocks(grain_blocks, owners[:, 0], tiles, live_counts, device_count, slots)
    got = lax.all_to_all(packed, ("gx", "gy"), split_axis=0, concat_axis=0, tiled=True)
    porosity, _ = lax.optimization_barrier((porosity, packed))
    part, porous_tiles = march_empty(porosity, extinction, color_weights)
    got, part, porous_tiles = lax.optimization_barrier((got, part, porous_tiles))
    work, plan = [], None
    for kernel in range(len(KERNELS)):
        made, planned = march_grain(
            kernel,
            plan,
            got,
            porous_tiles,
            part,
            dev,
            extinction,
            color_weights,
            slots,
            (width_x, width_y),
        )
        plan = plan or planned
        for flips, keep, send in made:
            work.append((flips, keep, exchanged(send, "gy", 1)))
    ready = [None] * (width_x - 1)
    token = work[-1][1]
    for chunk, stage in ORDER:
        flips, mine, got = work[chunk]
        got, token = lax.optimization_barrier((got, token))
        if flips == (0,) and stage == 2:
            return last_rows(mine, got, ready, dev, ranks, width_y)
        mine, *send = swap_rows(mine, got, dev, ranks, stage, len(flips))
        token = mine
        if stage < 2:
            work[chunk] = flips, mine, exchanged(send[0], "gy", 2 << stage)
            continue
        for piece, flip in enumerate(flips):
            ready[flip - 1] = exchanged(mine[piece : piece + 1], "gx", flip)


def march_flat(porous_flat, grain_flat, extinction, color_weights):
    porous = porous_flat.astype(jnp.float32)
    extinct = extinction[0] * (1.0 - porous) + extinction[1] * grain_flat
    optical = jnp.cumsum(extinct, axis=0)
    before = optical - extinct
    weight = jnp.exp(-before) * (1.0 - jnp.exp(-extinct))
    channels = []
    for channel in range(3):
        colour = jax.nn.sigmoid(
            color_weights[channel, 0] * porous
            + color_weights[channel, 1] * grain_flat
            + color_weights[channel, 2]
        )
        channels.append(jnp.sum(weight * colour, axis=0))
    channels.append(1.0 - jnp.exp(-optical[-1]))
    return jnp.stack(channels, axis=0)


def composite(nearer, farther):
    return nearer + (1.0 - nearer[3:4]) * farther


def shards_any(
    porosity, grain_blocks, owners, tiles, live_counts, ranks, extinction, color_weights
):
    width_x = lax.axis_size("gx")
    width_y = lax.axis_size("gy")
    device_count = width_x * width_y
    depth_cells, image_rows, image_cols = porosity.shape
    block_count, _, block_cols = grain_blocks.shape
    slots = max(2, 2 * block_count // device_count)
    tile_count = image_rows * image_cols // block_cols
    pixel_count = image_rows * image_cols
    block_len = pixel_count // device_count
    packed = pack_blocks(grain_blocks, owners[:, 0], tiles, live_counts, device_count, slots)
    got = lax.all_to_all(packed, ("gx", "gy"), split_axis=0, concat_axis=0, tiled=True)
    coded = got[:, slots * depth_cells : slots * depth_cells + 2, : slots + 1].astype(jnp.int32)
    table = coded[:, 0] * 64 + coded[:, 1]
    used = jnp.arange(slots, dtype=jnp.int32)[None, :] < table[:, slots:]
    got_tile = jnp.where(used, table[:, :slots], tile_count)
    got_data = got[:, : slots * depth_cells].reshape(-1, slots, depth_cells, block_cols)
    got_data = jnp.where(used[:, :, None, None], got_data, jnp.bfloat16(0))
    grain_tiles = (
        jnp.zeros((tile_count, depth_cells, block_cols), jnp.float32)
        .at[got_tile.reshape(-1)]
        .add(
            got_data.reshape(device_count * slots, depth_cells, block_cols).astype(jnp.float32),
            mode="drop",
        )
    )
    grain_flat = jnp.transpose(grain_tiles, (1, 0, 2)).reshape(depth_cells, pixel_count)
    porous_flat = porosity.reshape(depth_cells, pixel_count)
    partial_value = march_flat(porous_flat, grain_flat, extinction, color_weights)
    my_rank = ranks[lax.axis_index(("gx", "gy"))]
    bits_y = width_y.bit_length() - 1
    bits_x = width_x.bit_length() - 1
    current = partial_value.reshape(4, width_x, width_y, block_len)
    for axis, dim, bits, first in (("gy", 2, bits_y, 0), ("gx", 1, bits_x, bits_y)):
        for section_bit in range(bits):
            shape = current.shape
            paired = current.reshape(
                shape[:dim] + (shape[dim] // 2, 2) + shape[dim + 1 :]
            )
            own_bit = lax.axis_index(axis) >> section_bit & 1
            kept_half = lax.dynamic_index_in_dim(paired, own_bit, dim + 1, keepdims=False)
            sent_half = lax.dynamic_index_in_dim(paired, 1 - own_bit, dim + 1, keepdims=False)
            partner = exchanged(sent_half, axis, 1 << section_bit)
            nearer_side = my_rank >> first + section_bit & 1 == 0
            current = composite(
                jnp.where(nearer_side, kept_half, partner),
                jnp.where(nearer_side, partner, kept_half),
            )
        if dim == 2:
            current = current.reshape(4, width_x, 1, block_len).reshape(4, width_x, block_len)
    return current.reshape(4, block_len)


def solution(mesh):
    in_specs = (
        P(("gx", "gy"), None, None),
        P(("gx", "gy"), None, None),
        P(("gx", "gy"), None),
        P(("gx", "gy")),
        P(("gx", "gy")),
        P(),
        P(),
        P(),
    )
    out_specs = P(None, ("gx", "gy"))

    def run(porosity, *rest):
        rows = porosity.shape[1] // (mesh.shape["gx"] * mesh.shape["gy"])
        fits = mesh.shape["gx"] == 4 and mesh.shape["gy"] == 8 and rows == 8
        return jax.shard_map(
            shards if fits else shards_any,
            mesh=mesh,
            in_specs=in_specs,
            out_specs=out_specs,
            check_vma=False,
        )(porosity, *rest)

    return run
```

```python
import functools

import jax
import jax.numpy as jnp
from jax import lax
from jax.experimental import pallas as pl
from jax.experimental.pallas import tpu as pltpu
from jax.sharding import PartitionSpec as P

LOG2E = 1.4426950408889634
PACK_LIMIT = 56 * 1024 * 1024
EMPTY_LIMIT = 24 * 1024 * 1024
GRAIN_LIMIT = 47 * 1024 * 1024
SMALL_LIMIT = 8 * 1024 * 1024
UNROLL = 4
KERNELS = (((3, 2),), ((1,), (0,)))
ORDER = ((0, 0), (1, 0), (0, 1), (1, 1), (2, 0), (1, 2), (0, 2), (2, 1), (2, 2))


def exchanged(block, axis, distance):
    route = [(low, low ^ distance) for low in range(lax.axis_size(axis))]
    return lax.ppermute(block, axis, route)


def bits_of(size):
    assert size & (size - 1) == 0
    return size.bit_length() - 1


def pack_kernel(
    owner_ref, tile_ref, live_ref, block_ref, out_hbm, rows, table, table_vec, coded, sems, *, slots
):
    owners_all = rows.shape[0]
    depth = block_ref.shape[1]

    def clear(owner, carry):
        table[owner, slots] = 0
        return carry

    lax.fori_loop(0, owners_all, clear, 0)

    def place(index, carry):
        owner = owner_ref[index]
        slot = table[owner, slots]
        table[owner, slots] = slot + 1
        table[owner, slot] = tile_ref[index]
        rows[owner, pl.ds(pl.multiple_of(slot * depth, depth), depth), :] = block_ref[index]
        return carry

    lax.fori_loop(0, live_ref[0], place, 0)
    data = pltpu.make_async_copy(rows, out_hbm.at[:, pl.ds(0, rows.shape[1]), :], sems.at[0])
    data.start()
    copy = pltpu.make_async_copy(table, table_vec, sems.at[1])
    copy.start()
    copy.wait()
    first = lax.broadcasted_iota(jnp.int32, (8, 128), 0) == 0
    for owner in range(owners_all):
        row = jnp.broadcast_to(table_vec[owner : owner + 1, :], (8, 128))
        coded[owner] = jnp.where(first, row >> 6, row & 63).astype(jnp.float32).astype(jnp.bfloat16)
    copy = pltpu.make_async_copy(coded, out_hbm.at[:, pl.ds(rows.shape[1], 8), :], sems.at[2])
    copy.start()
    copy.wait()
    data.wait()


def pack_blocks(grain_blocks, owner_dev, tiles, live_counts, device_count, slots):
    _, depth, lanes = grain_blocks.shape
    smem = pl.BlockSpec(memory_space=pltpu.SMEM)
    vmem = pl.BlockSpec(memory_space=pltpu.VMEM)
    return pl.pallas_call(
        functools.partial(pack_kernel, slots=slots),
        out_shape=jax.ShapeDtypeStruct(
            (device_count, slots * depth + 8, lanes), grain_blocks.dtype
        ),
        in_specs=[smem, smem, smem, vmem],
        out_specs=pl.BlockSpec(memory_space=pltpu.HBM),
        scratch_shapes=[
            pltpu.VMEM((device_count, slots * depth, lanes), grain_blocks.dtype),
            pltpu.SMEM((device_count, 128), jnp.int32),
            pltpu.VMEM((device_count, 128), jnp.int32),
            pltpu.VMEM((device_count, 8, lanes), grain_blocks.dtype),
            pltpu.SemaphoreType.DMA((3,)),
        ],
        compiler_params=pltpu.CompilerParams(vmem_limit_bytes=PACK_LIMIT),
        name="pack_blocks",
    )(owner_dev, tiles, live_counts, grain_blocks)


def plan_tiles(gx, piece_bits, nowhere, got_ref, plan, ids_vec, ids, last, sems, slots):
    heads, again, earlier = plan
    nowhere_tile = last.shape[0] - 1
    sources = ids.shape[0]
    forget = pltpu.make_async_copy(nowhere, last.at[pl.ds(0, nowhere.shape[0])], sems.at[0])
    forget.start()
    for source in range(sources):
        coded = got_ref[source, got_ref.shape[1] - 8 :, :].astype(jnp.float32)
        ids_vec[source : source + 1, :] = (coded[0:1, :] * 64.0 + coded[1:2, :]).astype(jnp.int32)
    fetch = pltpu.make_async_copy(ids_vec, ids, sems.at[1])
    fetch.start()
    last[nowhere_tile] = -1
    fetch.wait()
    forget.wait()

    def from_source(source, counts):
        live = ids[source, slots]

        def some(batch, counts):
            count, more = counts
            found = []
            for place in range(UNROLL):
                slot = batch * UNROLL + place
                entry = source * slots + slot
                valid = slot < live
                tile = jnp.where(valid, ids[source, slot], nowhere_tile)
                before = last[tile]
                last[tile] = entry
                found.append((entry, tile, valid, before))
            for entry, tile, valid, before in found:
                earlier[entry] = before
                kernel = 1 - (((tile >> piece_bits) ^ gx) >> 1) & 1
                shift = kernel << 4
                heads[kernel, (count >> shift) & 65535] = entry + (tile << 16)
                count = count + (jnp.where(valid, 1, 0) << shift)

            def with_again():
                new = more
                for entry, tile, valid, before in found:
                    kernel = 1 - (((tile >> piece_bits) ^ gx) >> 1) & 1
                    shift = kernel << 4
                    again[kernel, (new >> shift) & 65535] = entry + (tile << 16)
                    seen = jnp.logical_and(valid, before >= 0)
                    new = new + (jnp.where(seen, 1, 0) << shift)
                return new

            latest = functools.reduce(
                jnp.maximum, [jnp.where(valid, before, -1) for _, _, valid, before in found]
            )
            more = lax.cond(latest >= 0, with_again, lambda: more)
            return count, more

        return lax.fori_loop(0, (live + UNROLL - 1) >> bits_of(UNROLL), some, counts)

    count, more = lax.fori_loop(0, sources, from_source, (jnp.int32(0), jnp.int32(0)))

    for kernel in range(2):
        found = (count >> (16 * kernel)) & 65535
        heads[kernel, heads.shape[1] - 1] = found
        again[kernel, heads.shape[1] - 1] = (more >> (16 * kernel)) & 65535

        @pl.when(found > 0)
        def _():
            for extra in range(UNROLL - 1):
                heads[kernel, found + extra] = heads[kernel, found - 1]


def empty_kernel(ext_ref, col_ref, por_hbm, part, por_tiles, por, turned, sems):
    depth, rows, cols = por_hbm.shape
    block_rows = por.shape[2]
    half_rows = block_rows // 2
    col_blocks = cols // 128
    steps = rows // block_rows
    base = -LOG2E * ext_ref[0]
    slope = LOG2E * ext_ref[0]

    def fetch(step, slot):
        start = pl.multiple_of(step * block_rows, block_rows)
        return pltpu.make_async_copy(
            por_hbm.at[:, pl.ds(start, block_rows), :], por.at[slot], sems.at[slot]
        )

    fetch(0, 0).start()

    def one_step(step, carry):
        slot = lax.rem(step, 2)

        @pl.when(step + 1 < steps)
        def _():
            fetch(step + 1, 1 - slot).start()

        fetch(step, slot).wait()

        def one_column(col, carry):
            lanes = pl.ds(pl.multiple_of(col * 128, 128), 128)
            clear = jnp.ones((block_rows, 128), jnp.float32)
            sums = [jnp.zeros((block_rows, 128), jnp.float32) for _ in range(3)]
            for z in range(depth):
                porous = por[slot, z, :, lanes].astype(jnp.float32)
                turned[z * block_rows : (z + 1) * block_rows, :] = porous
                passed = clear * jnp.exp2(base + slope * porous)
                weight = clear - passed
                clear = passed
                for c in range(3):
                    half_logit = (0.5 * col_ref[c, 0]) * porous + 0.5 * col_ref[c, 2]
                    sums[c] = sums[c] + weight * jnp.tanh(half_logit)
            for row in range(block_rows):
                tile = (step * block_rows + row) * col_blocks + col
                por_tiles[tile] = turned[pl.ds(row, depth, stride=block_rows), :].astype(
                    jnp.bfloat16
                )
            alpha = 1.0 - clear
            parts = [0.5 * (alpha + total) for total in sums] + [alpha]
            for c in range(4):
                for half in range(2):
                    part[2 * step + half, col, c * half_rows : (c + 1) * half_rows, :] = parts[c][
                        half * half_rows : (half + 1) * half_rows
                    ]
            return carry

        lax.fori_loop(0, col_blocks, one_column, 0)
        return carry

    lax.fori_loop(0, steps, one_step, 0)


def march_empty(porosity, extinction, color_weights):
    depth, rows, cols = porosity.shape
    block_rows = 16
    smem = pl.BlockSpec(memory_space=pltpu.SMEM)
    vmem = pl.BlockSpec(memory_space=pltpu.VMEM)
    return pl.pallas_call(
        empty_kernel,
        out_shape=[
            jax.ShapeDtypeStruct((rows // 8, cols // 128, 32, 128), jnp.float32),
            jax.ShapeDtypeStruct((rows * cols // 128, depth, 128), porosity.dtype),
        ],
        in_specs=[smem, smem, pl.BlockSpec(memory_space=pl.ANY)],
        out_specs=[vmem, vmem],
        scratch_shapes=[
            pltpu.VMEM((2, depth, block_rows, cols), porosity.dtype),
            pltpu.VMEM((depth * block_rows, 128), jnp.float32),
            pltpu.SemaphoreType.DMA((2,)),
        ],
        compiler_params=pltpu.CompilerParams(vmem_limit_bytes=EMPTY_LIMIT),
        cost_estimate=pl.CostEstimate(
            flops=20 * depth * rows * cols,
            bytes_accessed=4 * depth * rows * cols + 16 * rows * cols,
            transcendentals=4 * depth * rows * cols,
        ),
        name="march_empty",
    )(extinction, color_weights, porosity)


def grain_kernel(dev_ref, ext_ref, col_ref, *refs, kernel, slots, gy_bits):
    chunks = KERNELS[kernel]
    if kernel == 0:
        nowhere, *refs = refs
    else:
        plan, refs = refs[:3], refs[3:]
    por_hbm, part_hbm, got_ref, *refs = refs
    keep_refs, send_refs = refs[: len(chunks)], refs[len(chunks) : 2 * len(chunks)]
    refs = refs[2 * len(chunks) :]
    if kernel == 0:
        plan, refs = refs[:3], refs[3:]
    por_ref, part, sems, *scratch = refs
    own_x = dev_ref[0] & 1
    gx = dev_ref[0] >> gy_bits
    col_bits = bits_of(part.shape[2])
    piece_bits = bits_of(por_ref.shape[1])
    fetches = []
    for piece in range(2):
        chunk = gx ^ (piece + 2 * (1 - kernel))
        for place, (hbm, ref) in enumerate(((part_hbm, part), (por_hbm, por_ref))):
            rows = pl.ds(chunk * ref.shape[1], ref.shape[1])
            fetches.append(
                pltpu.make_async_copy(hbm.at[rows], ref.at[piece], sems.at[2 * piece + place])
            )
    for fetch in fetches:
        fetch.start()
    if kernel == 0:
        plan_tiles(gx, piece_bits, nowhere, got_ref, plan, *scratch, slots)
    heads, again, earlier = plan
    for fetch in fetches:
        fetch.wait()

    def block_of(entry):
        depth = por_ref.shape[2]
        start = pl.multiple_of((entry & (slots - 1)) * depth, depth)
        block = got_ref[entry >> bits_of(slots), pl.ds(start, depth), :]
        return block.astype(jnp.float32)

    base = -LOG2E * ext_ref[0]
    slope = LOG2E * ext_ref[0]
    grain_slope = -LOG2E * ext_ref[1]
    depth_of = lax.broadcasted_iota(jnp.int32, (8, 128), 0)

    def running(value):
        for shift in (1, 2, 4):
            value = value + jnp.where(depth_of >= shift, pltpu.roll(value, shift, 0), 0.0)
        return value

    def march_tiles(work):
        for code, grain in work:
            tile = code >> 16
            piece = ((tile >> piece_bits) ^ gx) & 1
            tile = tile & ((1 << piece_bits) - 1)
            porous = por_ref[piece, tile].astype(jnp.float32)
            exponent = (base + slope * porous) + grain_slope * grain
            front = running(exponent[:8])
            back = running(exponent[8:]) + front[7:8]
            optical = jnp.concatenate([front, back], axis=0)
            weight = jnp.exp2(optical - exponent) - jnp.exp2(optical)
            alpha = 1.0 - jnp.exp2(back[7:8])
            results = []
            for c in range(3):
                half_logit = (
                    (0.5 * col_ref[c, 0]) * porous
                    + (0.5 * col_ref[c, 1]) * grain
                    + 0.5 * col_ref[c, 2]
                )
                shaded = weight * jnp.tanh(half_logit)
                total = jnp.sum(shaded[:8] + shaded[8:], axis=0, keepdims=True)
                results.append(0.5 * (alpha + total))
            results.append(alpha)
            group, row = tile >> (3 + col_bits), (tile >> col_bits) & 7
            col = tile & ((1 << col_bits) - 1)
            for c in range(4):
                part[piece, group, col, pl.ds(c * 8 + row, 1), :] = results[c]

    def some_tiles(batch, carry):
        codes = [heads[kernel, batch * UNROLL + place] for place in range(UNROLL)]
        march_tiles([(code, block_of(code & 65535)) for code in codes])
        return carry

    found = heads[kernel, heads.shape[1] - 1]
    lax.fori_loop(0, (found + UNROLL - 1) >> bits_of(UNROLL), some_tiles, 0)

    def one_again(index, carry):
        code = again[kernel, index]
        entry = code & 65535

        def add_earlier(state):
            at, total = state
            return earlier[at], total + block_of(at)

        _, grain = lax.while_loop(
            lambda state: state[0] >= 0, add_earlier, (earlier[entry], block_of(entry))
        )
        march_tiles([(code, grain)])
        return carry

    lax.fori_loop(0, again[kernel, heads.shape[1] - 1], one_again, 0)

    pairs = part.shape[1] // 2
    for flips, keep_ref, send_ref in zip(chunks, keep_refs, send_refs):
        for place, flip in enumerate(flips):

            def split(pair, carry):
                at = place * pairs + pair
                send_ref[at] = part[flip & 1, 2 * pair + 1 - own_x].astype(jnp.bfloat16)
                keep_ref[at] = part[flip & 1, 2 * pair + own_x]
                return carry

            lax.fori_loop(0, pairs, split, 0)


def march_grain(kernel, plan, got, porous_tiles, part, dev, extinction, color_weights, slots, mesh):
    width_x, width_y = mesh
    chunks = KERNELS[kernel]
    smem = pl.BlockSpec(memory_space=pltpu.SMEM)
    vmem = pl.BlockSpec(memory_space=pltpu.VMEM)
    hbm = pl.BlockSpec(memory_space=pltpu.HBM)
    sources = got.shape[0]
    entries = sources * slots
    tile_count = porous_tiles.shape[0]
    groups = part.shape[0] // width_x
    split = [(len(flips) * groups // 2,) + part.shape[1:] for flips in chunks]
    scratch = [
        pltpu.VMEM((2, tile_count // width_x) + porous_tiles.shape[1:], porous_tiles.dtype),
        pltpu.VMEM((2, groups) + part.shape[1:], part.dtype),
        pltpu.SemaphoreType.DMA((4,)),
    ]
    plan_shapes = []
    if kernel == 0:
        most = -(-(entries + UNROLL + 1) // 128) * 128
        plan_shapes = [
            jax.ShapeDtypeStruct((2, most), jnp.int32),
            jax.ShapeDtypeStruct((2, most), jnp.int32),
            jax.ShapeDtypeStruct((entries + UNROLL,), jnp.int32),
        ]
        scratch += [
            pltpu.VMEM((sources, 128), jnp.int32),
            pltpu.SMEM((sources, 128), jnp.int32),
            pltpu.SMEM((tile_count + 1,), jnp.int32),
            pltpu.SemaphoreType.DMA((2,)),
        ]
        before, before_specs = [jnp.full((tile_count,), -1, jnp.int32)], [hbm]
    else:
        before, before_specs = plan, [smem] * 3
    outs = pl.pallas_call(
        functools.partial(grain_kernel, kernel=kernel, slots=slots, gy_bits=bits_of(width_y)),
        out_shape=[jax.ShapeDtypeStruct(shape, jnp.float32) for shape in split]
        + [jax.ShapeDtypeStruct(shape, jnp.bfloat16) for shape in split]
        + plan_shapes,
        in_specs=[smem] * 3 + before_specs + [hbm] * 2 + [vmem],
        out_specs=[vmem] * (2 * len(chunks)) + [smem] * len(plan_shapes),
        scratch_shapes=scratch,
        compiler_params=pltpu.CompilerParams(vmem_limit_bytes=GRAIN_LIMIT),
        cost_estimate=pl.CostEstimate(flops=1000, bytes_accessed=1000, transcendentals=0),
        name=f"march_grain_{kernel}",
    )(dev, extinction, color_weights, *before, porous_tiles, part, got)
    keeps, sends = outs[: len(chunks)], outs[len(chunks) : 2 * len(chunks)]
    return list(zip(chunks, keeps, sends)), outs[2 * len(chunks) :]


def ordered(mine, theirs, mine_near):
    nearer = [jnp.where(mine_near, a, b) for a, b in zip(mine, theirs)]
    farther = [jnp.where(mine_near, b, a) for a, b in zip(mine, theirs)]
    open_part = 1.0 - nearer[3]
    return [n + open_part * f for n, f in zip(nearer, farther)]


def channels_of(block):
    block = block.astype(jnp.float32)
    rows = block.shape[0] // 4
    return [block[c * rows : (c + 1) * rows] for c in range(4)]


def swap_kernel(dev_ref, rank_ref, mine_ref, got_ref, *out_refs, stage, pieces):
    device = dev_ref[0]
    mine_near = (rank_ref[device] >> stage) & 1 == 0
    low, high = (device >> 1) & 1, (device >> 2) & 1
    piece_groups = got_ref.shape[0] // pieces

    def one_column(col, carry):
        for piece in range(pieces):
            for way, out_ref in enumerate(out_refs):
                for place in range(out_ref.shape[0] // pieces):
                    group = [2 * place + (low ^ way), high ^ way, 0][stage] + piece * piece_groups
                    merged = ordered(
                        channels_of(mine_ref[group, col]),
                        channels_of(got_ref[group, col]),
                        mine_near,
                    )
                    merged = jnp.concatenate(merged, axis=0).astype(out_ref.dtype)
                    out_ref[piece * (out_ref.shape[0] // pieces) + place, col] = merged
        return carry

    lax.fori_loop(0, got_ref.shape[1], one_column, 0)


def swap_rows(mine, got, dev, ranks, stage, pieces):
    smem = pl.BlockSpec(memory_space=pltpu.SMEM)
    vmem = pl.BlockSpec(memory_space=pltpu.VMEM)
    kept = (max(1, got.shape[0] // 2) if stage < 2 else got.shape[0],) + got.shape[1:]
    out_shape = [jax.ShapeDtypeStruct(kept, jnp.float32)]
    if stage < 2:
        out_shape.append(jax.ShapeDtypeStruct(kept, jnp.bfloat16))
    return pl.pallas_call(
        functools.partial(swap_kernel, stage=stage, pieces=pieces),
        out_shape=out_shape,
        in_specs=[smem, smem, vmem, vmem],
        out_specs=[vmem] * len(out_shape),
        compiler_params=pltpu.CompilerParams(vmem_limit_bytes=SMALL_LIMIT),
        cost_estimate=pl.CostEstimate(flops=1000, bytes_accessed=1000, transcendentals=0),
        name=f"swap_rows_{stage}",
    )(dev, ranks, mine, got)


def four_way(device, rank_ref, parts, stride, bit):
    low = (rank_ref[device] >> bit) & 1 == 0
    far_low = (rank_ref[device ^ (2 * stride)] >> bit) & 1 == 0
    high = (rank_ref[device] >> (bit + 1)) & 1 == 0
    return ordered(
        ordered(parts[0], parts[1], low), ordered(parts[2], parts[3], far_low), high
    )


def last_kernel(dev_ref, rank_ref, mine_ref, got_ref, q1, q2, q3, out_ref, *, width_y):
    device = dev_ref[0]
    mine_near = (rank_ref[device] >> 2) & 1 == 0
    col_blocks = mine_ref.shape[1]
    for col in range(col_blocks):
        mine = ordered(channels_of(mine_ref[0, col]), channels_of(got_ref[0, col]), mine_near)
        parts = [mine] + [channels_of(ref[0, col]) for ref in (q1, q2, q3)]
        merged = four_way(device, rank_ref, parts, width_y, bits_of(width_y))
        for c in range(4):
            for row in range(merged[c].shape[0]):
                start = (row * col_blocks + col) * 128
                out_ref[c : c + 1, start : start + 128] = merged[c][row : row + 1]


def last_rows(mine, got, ready, dev, ranks, width_y):
    smem = pl.BlockSpec(memory_space=pltpu.SMEM)
    vmem = pl.BlockSpec(memory_space=pltpu.VMEM)
    return pl.pallas_call(
        functools.partial(last_kernel, width_y=width_y),
        out_shape=jax.ShapeDtypeStruct((4, mine.size // 4), jnp.float32),
        in_specs=[smem, smem] + [vmem] * 5,
        out_specs=vmem,
        compiler_params=pltpu.CompilerParams(vmem_limit_bytes=SMALL_LIMIT),
        name="last_rows",
    )(dev, ranks, mine, got, *ready)


def shards(porosity, grain_blocks, owners, tiles, live_counts, ranks, extinction, color_weights):
    width_x = lax.axis_size("gx")
    width_y = lax.axis_size("gy")
    device_count = width_x * width_y
    block_count = grain_blocks.shape[0]
    slots = max(2, 2 * block_count // device_count)
    dev = lax.axis_index(("gx", "gy")).astype(jnp.int32).reshape(1)
    packed = pack_blocks(grain_blocks, owners[:, 0], tiles, live_counts, device_count, slots)
    got = lax.all_to_all(packed, ("gx", "gy"), split_axis=0, concat_axis=0, tiled=True)
    porosity, _ = lax.optimization_barrier((porosity, packed))
    part, porous_tiles = march_empty(porosity, extinction, color_weights)
    got, part, porous_tiles = lax.optimization_barrier((got, part, porous_tiles))
    work, plan = [], None
    for kernel in range(len(KERNELS)):
        made, planned = march_grain(
            kernel,
            plan,
            got,
            porous_tiles,
            part,
            dev,
            extinction,
            color_weights,
            slots,
            (width_x, width_y),
        )
        plan = plan or planned
        for flips, keep, send in made:
            work.append((flips, keep, exchanged(send, "gy", 1)))
    ready = [None] * (width_x - 1)
    token = work[-1][1]
    for chunk, stage in ORDER:
        flips, mine, got = work[chunk]
        got, token = lax.optimization_barrier((got, token))
        if flips == (0,) and stage == 2:
            return last_rows(mine, got, ready, dev, ranks, width_y)
        mine, *send = swap_rows(mine, got, dev, ranks, stage, len(flips))
        token = mine
        if stage < 2:
            work[chunk] = flips, mine, exchanged(send[0], "gy", 2 << stage)
            continue
        for piece, flip in enumerate(flips):
            ready[flip - 1] = exchanged(mine[piece : piece + 1], "gx", flip)


def march_flat(porous_flat, grain_flat, extinction, color_weights):
    porous = porous_flat.astype(jnp.float32)
    extinct = extinction[0] * (1.0 - porous) + extinction[1] * grain_flat
    optical = jnp.cumsum(extinct, axis=0)
    before = optical - extinct
    weight = jnp.exp(-before) * (1.0 - jnp.exp(-extinct))
    channels = []
    for channel in range(3):
        colour = jax.nn.sigmoid(
            color_weights[channel, 0] * porous
            + color_weights[channel, 1] * grain_flat
            + color_weights[channel, 2]
        )
        channels.append(jnp.sum(weight * colour, axis=0))
    channels.append(1.0 - jnp.exp(-optical[-1]))
    return jnp.stack(channels, axis=0)


def composite(nearer, farther):
    return nearer + (1.0 - nearer[3:4]) * farther


def shards_any(
    porosity, grain_blocks, owners, tiles, live_counts, ranks, extinction, color_weights
):
    width_x = lax.axis_size("gx")
    width_y = lax.axis_size("gy")
    device_count = width_x * width_y
    depth_cells, image_rows, image_cols = porosity.shape
    block_count, _, block_cols = grain_blocks.shape
    slots = max(2, 2 * block_count // device_count)
    tile_count = image_rows * image_cols // block_cols
    pixel_count = image_rows * image_cols
    block_len = pixel_count // device_count
    packed = pack_blocks(grain_blocks, owners[:, 0], tiles, live_counts, device_count, slots)
    got = lax.all_to_all(packed, ("gx", "gy"), split_axis=0, concat_axis=0, tiled=True)
    coded = got[:, slots * depth_cells : slots * depth_cells + 2, : slots + 1].astype(jnp.int32)
    table = coded[:, 0] * 64 + coded[:, 1]
    used = jnp.arange(slots, dtype=jnp.int32)[None, :] < table[:, slots:]
    got_tile = jnp.where(used, table[:, :slots], tile_count)
    got_data = got[:, : slots * depth_cells].reshape(-1, slots, depth_cells, block_cols)
    got_data = jnp.where(used[:, :, None, None], got_data, jnp.bfloat16(0))
    grain_tiles = (
        jnp.zeros((tile_count, depth_cells, block_cols), jnp.float32)
        .at[got_tile.reshape(-1)]
        .add(
            got_data.reshape(device_count * slots, depth_cells, block_cols).astype(jnp.float32),
            mode="drop",
        )
    )
    grain_flat = jnp.transpose(grain_tiles, (1, 0, 2)).reshape(depth_cells, pixel_count)
    porous_flat = porosity.reshape(depth_cells, pixel_count)
    partial_value = march_flat(porous_flat, grain_flat, extinction, color_weights)
    my_rank = ranks[lax.axis_index(("gx", "gy"))]
    bits_y = width_y.bit_length() - 1
    bits_x = width_x.bit_length() - 1
    current = partial_value.reshape(4, width_x, width_y, block_len)
    for axis, dim, bits, first in (("gy", 2, bits_y, 0), ("gx", 1, bits_x, bits_y)):
        for section_bit in range(bits):
            shape = current.shape
            paired = current.reshape(
                shape[:dim] + (shape[dim] // 2, 2) + shape[dim + 1 :]
            )
            own_bit = lax.axis_index(axis) >> section_bit & 1
            kept_half = lax.dynamic_index_in_dim(paired, own_bit, dim + 1, keepdims=False)
            sent_half = lax.dynamic_index_in_dim(paired, 1 - own_bit, dim + 1, keepdims=False)
            partner = exchanged(sent_half, axis, 1 << section_bit)
            nearer_side = my_rank >> first + section_bit & 1 == 0
            current = composite(
                jnp.where(nearer_side, kept_half, partner),
                jnp.where(nearer_side, partner, kept_half),
            )
        if dim == 2:
            current = current.reshape(4, width_x, 1, block_len).reshape(4, width_x, block_len)
    return current.reshape(4, block_len)


def solution(mesh):
    in_specs = (
        P(("gx", "gy"), None, None),
        P(("gx", "gy"), None, None),
        P(("gx", "gy"), None),
        P(("gx", "gy")),
        P(("gx", "gy")),
        P(),
        P(),
        P(),
    )
    out_specs = P(None, ("gx", "gy"))

    def run(porosity, *rest):
        rows = porosity.shape[1] // (mesh.shape["gx"] * mesh.shape["gy"])
        fits = mesh.shape["gx"] == 4 and mesh.shape["gy"] == 8 and rows == 8
        return jax.shard_map(
            shards if fits else shards_any,
            mesh=mesh,
            in_specs=in_specs,
            out_specs=out_specs,
            check_vma=False,
        )(porosity, *rest)

    return run
```

```python
import functools

import jax
import jax.numpy as jnp
from jax import lax
from jax.experimental import pallas as pl
from jax.experimental.pallas import tpu as pltpu
from jax.sharding import PartitionSpec as P

LOG2E = 1.4426950408889634
PACK_LIMIT = 56 * 1024 * 1024
EMPTY_LIMIT = 24 * 1024 * 1024
GRAIN_LIMIT = 47 * 1024 * 1024
SMALL_LIMIT = 8 * 1024 * 1024
UNROLL = 4
KERNELS = (((3, 2),), ((1,), (0,)))
ORDER = ((0, 0), (1, 0), (0, 1), (1, 1), (2, 0), (1, 2), (0, 2), (2, 1), (2, 2))


def exchanged(block, axis, distance):
    route = [(low, low ^ distance) for low in range(lax.axis_size(axis))]
    return lax.ppermute(block, axis, route)


def bits_of(size):
    assert size & (size - 1) == 0
    return size.bit_length() - 1


def pack_kernel(
    owner_ref, tile_ref, live_ref, block_ref, out_hbm, rows, table, table_vec, coded, sems, *, slots
):
    owners_all = rows.shape[0]
    depth = block_ref.shape[1]

    def clear(owner, carry):
        table[owner, slots] = 0
        return carry

    lax.fori_loop(0, owners_all, clear, 0)

    def place(index, carry):
        owner = owner_ref[index]
        slot = table[owner, slots]
        table[owner, slots] = slot + 1
        table[owner, slot] = tile_ref[index]
        rows[owner, pl.ds(pl.multiple_of(slot * depth, depth), depth), :] = block_ref[index]
        return carry

    lax.fori_loop(0, live_ref[0], place, 0)
    data = pltpu.make_async_copy(rows, out_hbm.at[:, pl.ds(0, rows.shape[1]), :], sems.at[0])
    data.start()
    copy = pltpu.make_async_copy(table, table_vec, sems.at[1])
    copy.start()
    copy.wait()
    first = lax.broadcasted_iota(jnp.int32, (8, 128), 0) == 0
    for owner in range(owners_all):
        row = jnp.broadcast_to(table_vec[owner : owner + 1, :], (8, 128))
        coded[owner] = jnp.where(first, row >> 6, row & 63).astype(jnp.float32).astype(jnp.bfloat16)
    copy = pltpu.make_async_copy(coded, out_hbm.at[:, pl.ds(rows.shape[1], 8), :], sems.at[2])
    copy.start()
    copy.wait()
    data.wait()


def pack_blocks(grain_blocks, owner_dev, tiles, live_counts, device_count, slots):
    _, depth, lanes = grain_blocks.shape
    smem = pl.BlockSpec(memory_space=pltpu.SMEM)
    vmem = pl.BlockSpec(memory_space=pltpu.VMEM)
    return pl.pallas_call(
        functools.partial(pack_kernel, slots=slots),
        out_shape=jax.ShapeDtypeStruct(
            (device_count, slots * depth + 8, lanes), grain_blocks.dtype
        ),
        in_specs=[smem, smem, smem, vmem],
        out_specs=pl.BlockSpec(memory_space=pltpu.HBM),
        scratch_shapes=[
            pltpu.VMEM((device_count, slots * depth, lanes), grain_blocks.dtype),
            pltpu.SMEM((device_count, 128), jnp.int32),
            pltpu.VMEM((device_count, 128), jnp.int32),
            pltpu.VMEM((device_count, 8, lanes), grain_blocks.dtype),
            pltpu.SemaphoreType.DMA((3,)),
        ],
        compiler_params=pltpu.CompilerParams(vmem_limit_bytes=PACK_LIMIT),
        name="pack_blocks",
    )(owner_dev, tiles, live_counts, grain_blocks)


def plan_tiles(gx, piece_bits, nowhere, got_ref, plan, ids_vec, ids, last, sems, slots):
    heads, again, earlier = plan
    nowhere_tile = last.shape[0] - 1
    sources = ids.shape[0]
    forget = pltpu.make_async_copy(nowhere, last.at[pl.ds(0, nowhere.shape[0])], sems.at[0])
    forget.start()
    for source in range(sources):
        coded = got_ref[source, got_ref.shape[1] - 8 :, :].astype(jnp.float32)
        ids_vec[source : source + 1, :] = (coded[0:1, :] * 64.0 + coded[1:2, :]).astype(jnp.int32)
    fetch = pltpu.make_async_copy(ids_vec, ids, sems.at[1])
    fetch.start()
    last[nowhere_tile] = -1
    fetch.wait()
    forget.wait()

    def from_source(source, counts):
        live = ids[source, slots]

        def some(batch, counts):
            count, more = counts
            found = []
            for place in range(UNROLL):
                slot = batch * UNROLL + place
                entry = source * slots + slot
                valid = slot < live
                tile = jnp.where(valid, ids[source, slot], nowhere_tile)
                before = last[tile]
                last[tile] = entry
                found.append((entry, tile, valid, before))
            for entry, tile, valid, before in found:
                earlier[entry] = before
                kernel = 1 - (((tile >> piece_bits) ^ gx) >> 1) & 1
                shift = kernel << 4
                code = entry + (tile << 16)
                heads[kernel, (count >> shift) & 65535] = code
                again[kernel, (more >> shift) & 65535] = code
                one = jnp.where(valid, 1, 0) << shift
                count = count + one
                more = more + jnp.where(before >= 0, one, 0)
            return count, more

        return lax.fori_loop(0, (live + UNROLL - 1) >> bits_of(UNROLL), some, counts)

    count, more = lax.fori_loop(0, sources, from_source, (jnp.int32(0), jnp.int32(0)))

    for kernel in range(2):
        found = (count >> (16 * kernel)) & 65535
        heads[kernel, heads.shape[1] - 1] = found
        again[kernel, heads.shape[1] - 1] = (more >> (16 * kernel)) & 65535

        @pl.when(found > 0)
        def _():
            for extra in range(UNROLL - 1):
                heads[kernel, found + extra] = heads[kernel, found - 1]


def empty_kernel(ext_ref, col_ref, por_hbm, part, por_tiles, por, turned, sems):
    depth, rows, cols = por_hbm.shape
    block_rows = por.shape[2]
    half_rows = block_rows // 2
    col_blocks = cols // 128
    steps = rows // block_rows
    base = -LOG2E * ext_ref[0]
    slope = LOG2E * ext_ref[0]

    def fetch(step, slot):
        start = pl.multiple_of(step * block_rows, block_rows)
        return pltpu.make_async_copy(
            por_hbm.at[:, pl.ds(start, block_rows), :], por.at[slot], sems.at[slot]
        )

    fetch(0, 0).start()

    def one_step(step, carry):
        slot = lax.rem(step, 2)

        @pl.when(step + 1 < steps)
        def _():
            fetch(step + 1, 1 - slot).start()

        fetch(step, slot).wait()

        def one_column(col, carry):
            lanes = pl.ds(pl.multiple_of(col * 128, 128), 128)
            clear = jnp.ones((block_rows, 128), jnp.float32)
            sums = [jnp.zeros((block_rows, 128), jnp.float32) for _ in range(3)]
            for z in range(depth):
                porous = por[slot, z, :, lanes].astype(jnp.float32)
                turned[z * block_rows : (z + 1) * block_rows, :] = porous
                passed = clear * jnp.exp2(base + slope * porous)
                weight = clear - passed
                clear = passed
                for c in range(3):
                    half_logit = (0.5 * col_ref[c, 0]) * porous + 0.5 * col_ref[c, 2]
                    sums[c] = sums[c] + weight * jnp.tanh(half_logit)
            for row in range(block_rows):
                tile = (step * block_rows + row) * col_blocks + col
                por_tiles[tile] = turned[pl.ds(row, depth, stride=block_rows), :].astype(
                    jnp.bfloat16
                )
            alpha = 1.0 - clear
            parts = [0.5 * (alpha + total) for total in sums] + [alpha]
            for c in range(4):
                for half in range(2):
                    part[2 * step + half, col, c * half_rows : (c + 1) * half_rows, :] = parts[c][
                        half * half_rows : (half + 1) * half_rows
                    ]
            return carry

        lax.fori_loop(0, col_blocks, one_column, 0)
        return carry

    lax.fori_loop(0, steps, one_step, 0)


def march_empty(porosity, extinction, color_weights):
    depth, rows, cols = porosity.shape
    block_rows = 16
    smem = pl.BlockSpec(memory_space=pltpu.SMEM)
    vmem = pl.BlockSpec(memory_space=pltpu.VMEM)
    return pl.pallas_call(
        empty_kernel,
        out_shape=[
            jax.ShapeDtypeStruct((rows // 8, cols // 128, 32, 128), jnp.float32),
            jax.ShapeDtypeStruct((rows * cols // 128, depth, 128), porosity.dtype),
        ],
        in_specs=[smem, smem, pl.BlockSpec(memory_space=pl.ANY)],
        out_specs=[vmem, vmem],
        scratch_shapes=[
            pltpu.VMEM((2, depth, block_rows, cols), porosity.dtype),
            pltpu.VMEM((depth * block_rows, 128), jnp.float32),
            pltpu.SemaphoreType.DMA((2,)),
        ],
        compiler_params=pltpu.CompilerParams(vmem_limit_bytes=EMPTY_LIMIT),
        cost_estimate=pl.CostEstimate(
            flops=20 * depth * rows * cols,
            bytes_accessed=4 * depth * rows * cols + 16 * rows * cols,
            transcendentals=4 * depth * rows * cols,
        ),
        name="march_empty",
    )(extinction, color_weights, porosity)


def grain_kernel(dev_ref, ext_ref, col_ref, *refs, kernel, slots, gy_bits):
    chunks = KERNELS[kernel]
    if kernel == 0:
        nowhere, *refs = refs
    else:
        plan, refs = refs[:3], refs[3:]
    por_hbm, part_hbm, got_ref, *refs = refs
    keep_refs, send_refs = refs[: len(chunks)], refs[len(chunks) : 2 * len(chunks)]
    refs = refs[2 * len(chunks) :]
    if kernel == 0:
        plan, refs = refs[:3], refs[3:]
    por_ref, part, sems, *scratch = refs
    own_x = dev_ref[0] & 1
    gx = dev_ref[0] >> gy_bits
    col_bits = bits_of(part.shape[2])
    piece_bits = bits_of(por_ref.shape[1])
    fetches = []
    for piece in range(2):
        chunk = gx ^ (piece + 2 * (1 - kernel))
        for place, (hbm, ref) in enumerate(((part_hbm, part), (por_hbm, por_ref))):
            rows = pl.ds(chunk * ref.shape[1], ref.shape[1])
            fetches.append(
                pltpu.make_async_copy(hbm.at[rows], ref.at[piece], sems.at[2 * piece + place])
            )
    for fetch in fetches:
        fetch.start()
    if kernel == 0:
        plan_tiles(gx, piece_bits, nowhere, got_ref, plan, *scratch, slots)
    heads, again, earlier = plan
    for fetch in fetches:
        fetch.wait()

    def block_of(entry):
        depth = por_ref.shape[2]
        start = pl.multiple_of((entry & (slots - 1)) * depth, depth)
        block = got_ref[entry >> bits_of(slots), pl.ds(start, depth), :]
        return block.astype(jnp.float32)

    base = -LOG2E * ext_ref[0]
    slope = LOG2E * ext_ref[0]
    grain_slope = -LOG2E * ext_ref[1]
    depth_of = lax.broadcasted_iota(jnp.int32, (8, 128), 0)

    def running(value):
        for shift in (1, 2, 4):
            value = value + jnp.where(depth_of >= shift, pltpu.roll(value, shift, 0), 0.0)
        return value

    def march_tiles(work):
        for code, grain in work:
            tile = code >> 16
            piece = ((tile >> piece_bits) ^ gx) & 1
            tile = tile & ((1 << piece_bits) - 1)
            porous = por_ref[piece, tile].astype(jnp.float32)
            exponent = (base + slope * porous) + grain_slope * grain
            front = running(exponent[:8])
            back = running(exponent[8:]) + front[7:8]
            optical = jnp.concatenate([front, back], axis=0)
            weight = jnp.exp2(optical - exponent) - jnp.exp2(optical)
            alpha = 1.0 - jnp.exp2(back[7:8])
            results = []
            for c in range(3):
                half_logit = (
                    (0.5 * col_ref[c, 0]) * porous
                    + (0.5 * col_ref[c, 1]) * grain
                    + 0.5 * col_ref[c, 2]
                )
                shaded = weight * jnp.tanh(half_logit)
                total = jnp.sum(shaded[:8] + shaded[8:], axis=0, keepdims=True)
                results.append(0.5 * (alpha + total))
            results.append(alpha)
            group, row = tile >> (3 + col_bits), (tile >> col_bits) & 7
            col = tile & ((1 << col_bits) - 1)
            for c in range(4):
                part[piece, group, col, pl.ds(c * 8 + row, 1), :] = results[c]

    def some_tiles(batch, carry):
        codes = [heads[kernel, batch * UNROLL + place] for place in range(UNROLL)]
        march_tiles([(code, block_of(code & 65535)) for code in codes])
        return carry

    found = heads[kernel, heads.shape[1] - 1]
    lax.fori_loop(0, (found + UNROLL - 1) >> bits_of(UNROLL), some_tiles, 0)

    def one_again(index, carry):
        code = again[kernel, index]
        entry = code & 65535

        def add_earlier(state):
            at, total = state
            return earlier[at], total + block_of(at)

        _, grain = lax.while_loop(
            lambda state: state[0] >= 0, add_earlier, (earlier[entry], block_of(entry))
        )
        march_tiles([(code, grain)])
        return carry

    lax.fori_loop(0, again[kernel, heads.shape[1] - 1], one_again, 0)

    pairs = part.shape[1] // 2
    for flips, keep_ref, send_ref in zip(chunks, keep_refs, send_refs):
        for place, flip in enumerate(flips):

            def split(pair, carry):
                at = place * pairs + pair
                send_ref[at] = part[flip & 1, 2 * pair + 1 - own_x].astype(jnp.bfloat16)
                keep_ref[at] = part[flip & 1, 2 * pair + own_x]
                return carry

            lax.fori_loop(0, pairs, split, 0)


def march_grain(kernel, plan, got, porous_tiles, part, dev, extinction, color_weights, slots, mesh):
    width_x, width_y = mesh
    chunks = KERNELS[kernel]
    smem = pl.BlockSpec(memory_space=pltpu.SMEM)
    vmem = pl.BlockSpec(memory_space=pltpu.VMEM)
    hbm = pl.BlockSpec(memory_space=pltpu.HBM)
    sources = got.shape[0]
    entries = sources * slots
    tile_count = porous_tiles.shape[0]
    groups = part.shape[0] // width_x
    split = [(len(flips) * groups // 2,) + part.shape[1:] for flips in chunks]
    scratch = [
        pltpu.VMEM((2, tile_count // width_x) + porous_tiles.shape[1:], porous_tiles.dtype),
        pltpu.VMEM((2, groups) + part.shape[1:], part.dtype),
        pltpu.SemaphoreType.DMA((4,)),
    ]
    plan_shapes = []
    if kernel == 0:
        most = -(-(entries + UNROLL + 1) // 128) * 128
        plan_shapes = [
            jax.ShapeDtypeStruct((2, most), jnp.int32),
            jax.ShapeDtypeStruct((2, most), jnp.int32),
            jax.ShapeDtypeStruct((entries + UNROLL,), jnp.int32),
        ]
        scratch += [
            pltpu.VMEM((sources, 128), jnp.int32),
            pltpu.SMEM((sources, 128), jnp.int32),
            pltpu.SMEM((tile_count + 1,), jnp.int32),
            pltpu.SemaphoreType.DMA((2,)),
        ]
        before, before_specs = [jnp.full((tile_count,), -1, jnp.int32)], [hbm]
    else:
        before, before_specs = plan, [smem] * 3
    outs = pl.pallas_call(
        functools.partial(grain_kernel, kernel=kernel, slots=slots, gy_bits=bits_of(width_y)),
        out_shape=[jax.ShapeDtypeStruct(shape, jnp.float32) for shape in split]
        + [jax.ShapeDtypeStruct(shape, jnp.bfloat16) for shape in split]
        + plan_shapes,
        in_specs=[smem] * 3 + before_specs + [hbm] * 2 + [vmem],
        out_specs=[vmem] * (2 * len(chunks)) + [smem] * len(plan_shapes),
        scratch_shapes=scratch,
        compiler_params=pltpu.CompilerParams(vmem_limit_bytes=GRAIN_LIMIT),
        cost_estimate=pl.CostEstimate(flops=1000, bytes_accessed=1000, transcendentals=0),
        name=f"march_grain_{kernel}",
    )(dev, extinction, color_weights, *before, porous_tiles, part, got)
    keeps, sends = outs[: len(chunks)], outs[len(chunks) : 2 * len(chunks)]
    return list(zip(chunks, keeps, sends)), outs[2 * len(chunks) :]


def ordered(mine, theirs, mine_near):
    nearer = [jnp.where(mine_near, a, b) for a, b in zip(mine, theirs)]
    farther = [jnp.where(mine_near, b, a) for a, b in zip(mine, theirs)]
    open_part = 1.0 - nearer[3]
    return [n + open_part * f for n, f in zip(nearer, farther)]


def channels_of(block):
    block = block.astype(jnp.float32)
    rows = block.shape[0] // 4
    return [block[c * rows : (c + 1) * rows] for c in range(4)]


def swap_kernel(dev_ref, rank_ref, mine_ref, got_ref, *out_refs, stage, pieces):
    device = dev_ref[0]
    mine_near = (rank_ref[device] >> stage) & 1 == 0
    low, high = (device >> 1) & 1, (device >> 2) & 1
    piece_groups = got_ref.shape[0] // pieces

    def one_column(col, carry):
        for piece in range(pieces):
            for way, out_ref in enumerate(out_refs):
                for place in range(out_ref.shape[0] // pieces):
                    group = [2 * place + (low ^ way), high ^ way, 0][stage] + piece * piece_groups
                    merged = ordered(
                        channels_of(mine_ref[group, col]),
                        channels_of(got_ref[group, col]),
                        mine_near,
                    )
                    merged = jnp.concatenate(merged, axis=0).astype(out_ref.dtype)
                    out_ref[piece * (out_ref.shape[0] // pieces) + place, col] = merged
        return carry

    lax.fori_loop(0, got_ref.shape[1], one_column, 0)


def swap_rows(mine, got, dev, ranks, stage, pieces):
    smem = pl.BlockSpec(memory_space=pltpu.SMEM)
    vmem = pl.BlockSpec(memory_space=pltpu.VMEM)
    kept = (max(1, got.shape[0] // 2) if stage < 2 else got.shape[0],) + got.shape[1:]
    out_shape = [jax.ShapeDtypeStruct(kept, jnp.float32)]
    if stage < 2:
        out_shape.append(jax.ShapeDtypeStruct(kept, jnp.bfloat16))
    return pl.pallas_call(
        functools.partial(swap_kernel, stage=stage, pieces=pieces),
        out_shape=out_shape,
        in_specs=[smem, smem, vmem, vmem],
        out_specs=[vmem] * len(out_shape),
        compiler_params=pltpu.CompilerParams(vmem_limit_bytes=SMALL_LIMIT),
        cost_estimate=pl.CostEstimate(flops=1000, bytes_accessed=1000, transcendentals=0),
        name=f"swap_rows_{stage}",
    )(dev, ranks, mine, got)


def four_way(device, rank_ref, parts, stride, bit):
    low = (rank_ref[device] >> bit) & 1 == 0
    far_low = (rank_ref[device ^ (2 * stride)] >> bit) & 1 == 0
    high = (rank_ref[device] >> (bit + 1)) & 1 == 0
    return ordered(
        ordered(parts[0], parts[1], low), ordered(parts[2], parts[3], far_low), high
    )


def last_kernel(dev_ref, rank_ref, mine_ref, got_ref, q1, q2, q3, out_ref, *, width_y):
    device = dev_ref[0]
    mine_near = (rank_ref[device] >> 2) & 1 == 0
    col_blocks = mine_ref.shape[1]
    for col in range(col_blocks):
        mine = ordered(channels_of(mine_ref[0, col]), channels_of(got_ref[0, col]), mine_near)
        parts = [mine] + [channels_of(ref[0, col]) for ref in (q1, q2, q3)]
        merged = four_way(device, rank_ref, parts, width_y, bits_of(width_y))
        for c in range(4):
            for row in range(merged[c].shape[0]):
                start = (row * col_blocks + col) * 128
                out_ref[c : c + 1, start : start + 128] = merged[c][row : row + 1]


def last_rows(mine, got, ready, dev, ranks, width_y):
    smem = pl.BlockSpec(memory_space=pltpu.SMEM)
    vmem = pl.BlockSpec(memory_space=pltpu.VMEM)
    return pl.pallas_call(
        functools.partial(last_kernel, width_y=width_y),
        out_shape=jax.ShapeDtypeStruct((4, mine.size // 4), jnp.float32),
        in_specs=[smem, smem] + [vmem] * 5,
        out_specs=vmem,
        compiler_params=pltpu.CompilerParams(vmem_limit_bytes=SMALL_LIMIT),
        name="last_rows",
    )(dev, ranks, mine, got, *ready)


def shards(porosity, grain_blocks, owners, tiles, live_counts, ranks, extinction, color_weights):
    width_x = lax.axis_size("gx")
    width_y = lax.axis_size("gy")
    device_count = width_x * width_y
    block_count = grain_blocks.shape[0]
    slots = max(2, 2 * block_count // device_count)
    dev = lax.axis_index(("gx", "gy")).astype(jnp.int32).reshape(1)
    packed = pack_blocks(grain_blocks, owners[:, 0], tiles, live_counts, device_count, slots)
    got = lax.all_to_all(packed, ("gx", "gy"), split_axis=0, concat_axis=0, tiled=True)
    porosity, _ = lax.optimization_barrier((porosity, packed))
    part, porous_tiles = march_empty(porosity, extinction, color_weights)
    got, part, porous_tiles = lax.optimization_barrier((got, part, porous_tiles))
    work, plan = [], None
    for kernel in range(len(KERNELS)):
        made, planned = march_grain(
            kernel,
            plan,
            got,
            porous_tiles,
            part,
            dev,
            extinction,
            color_weights,
            slots,
            (width_x, width_y),
        )
        plan = plan or planned
        for flips, keep, send in made:
            work.append((flips, keep, exchanged(send, "gy", 1)))
    ready = [None] * (width_x - 1)
    token = work[-1][1]
    for chunk, stage in ORDER:
        flips, mine, got = work[chunk]
        got, token = lax.optimization_barrier((got, token))
        if flips == (0,) and stage == 2:
            return last_rows(mine, got, ready, dev, ranks, width_y)
        mine, *send = swap_rows(mine, got, dev, ranks, stage, len(flips))
        token = mine
        if stage < 2:
            work[chunk] = flips, mine, exchanged(send[0], "gy", 2 << stage)
            continue
        for piece, flip in enumerate(flips):
            ready[flip - 1] = exchanged(mine[piece : piece + 1], "gx", flip)


def march_flat(porous_flat, grain_flat, extinction, color_weights):
    porous = porous_flat.astype(jnp.float32)
    extinct = extinction[0] * (1.0 - porous) + extinction[1] * grain_flat
    optical = jnp.cumsum(extinct, axis=0)
    before = optical - extinct
    weight = jnp.exp(-before) * (1.0 - jnp.exp(-extinct))
    channels = []
    for channel in range(3):
        colour = jax.nn.sigmoid(
            color_weights[channel, 0] * porous
            + color_weights[channel, 1] * grain_flat
            + color_weights[channel, 2]
        )
        channels.append(jnp.sum(weight * colour, axis=0))
    channels.append(1.0 - jnp.exp(-optical[-1]))
    return jnp.stack(channels, axis=0)


def composite(nearer, farther):
    return nearer + (1.0 - nearer[3:4]) * farther


def shards_any(
    porosity, grain_blocks, owners, tiles, live_counts, ranks, extinction, color_weights
):
    width_x = lax.axis_size("gx")
    width_y = lax.axis_size("gy")
    device_count = width_x * width_y
    depth_cells, image_rows, image_cols = porosity.shape
    block_count, _, block_cols = grain_blocks.shape
    slots = max(2, 2 * block_count // device_count)
    tile_count = image_rows * image_cols // block_cols
    pixel_count = image_rows * image_cols
    block_len = pixel_count // device_count
    packed = pack_blocks(grain_blocks, owners[:, 0], tiles, live_counts, device_count, slots)
    got = lax.all_to_all(packed, ("gx", "gy"), split_axis=0, concat_axis=0, tiled=True)
    coded = got[:, slots * depth_cells : slots * depth_cells + 2, : slots + 1].astype(jnp.int32)
    table = coded[:, 0] * 64 + coded[:, 1]
    used = jnp.arange(slots, dtype=jnp.int32)[None, :] < table[:, slots:]
    got_tile = jnp.where(used, table[:, :slots], tile_count)
    got_data = got[:, : slots * depth_cells].reshape(-1, slots, depth_cells, block_cols)
    got_data = jnp.where(used[:, :, None, None], got_data, jnp.bfloat16(0))
    grain_tiles = (
        jnp.zeros((tile_count, depth_cells, block_cols), jnp.float32)
        .at[got_tile.reshape(-1)]
        .add(
            got_data.reshape(device_count * slots, depth_cells, block_cols).astype(jnp.float32),
            mode="drop",
        )
    )
    grain_flat = jnp.transpose(grain_tiles, (1, 0, 2)).reshape(depth_cells, pixel_count)
    porous_flat = porosity.reshape(depth_cells, pixel_count)
    partial_value = march_flat(porous_flat, grain_flat, extinction, color_weights)
    my_rank = ranks[lax.axis_index(("gx", "gy"))]
    bits_y = width_y.bit_length() - 1
    bits_x = width_x.bit_length() - 1
    current = partial_value.reshape(4, width_x, width_y, block_len)
    for axis, dim, bits, first in (("gy", 2, bits_y, 0), ("gx", 1, bits_x, bits_y)):
        for section_bit in range(bits):
            shape = current.shape
            paired = current.reshape(
                shape[:dim] + (shape[dim] // 2, 2) + shape[dim + 1 :]
            )
            own_bit = lax.axis_index(axis) >> section_bit & 1
            kept_half = lax.dynamic_index_in_dim(paired, own_bit, dim + 1, keepdims=False)
            sent_half = lax.dynamic_index_in_dim(paired, 1 - own_bit, dim + 1, keepdims=False)
            partner = exchanged(sent_half, axis, 1 << section_bit)
            nearer_side = my_rank >> first + section_bit & 1 == 0
            current = composite(
                jnp.where(nearer_side, kept_half, partner),
                jnp.where(nearer_side, partner, kept_half),
            )
        if dim == 2:
            current = current.reshape(4, width_x, 1, block_len).reshape(4, width_x, block_len)
    return current.reshape(4, block_len)


def solution(mesh):
    in_specs = (
        P(("gx", "gy"), None, None),
        P(("gx", "gy"), None, None),
        P(("gx", "gy"), None),
        P(("gx", "gy")),
        P(("gx", "gy")),
        P(),
        P(),
        P(),
    )
    out_specs = P(None, ("gx", "gy"))

    def run(porosity, *rest):
        rows = porosity.shape[1] // (mesh.shape["gx"] * mesh.shape["gy"])
        fits = mesh.shape["gx"] == 4 and mesh.shape["gy"] == 8 and rows == 8
        return jax.shard_map(
            shards if fits else shards_any,
            mesh=mesh,
            in_specs=in_specs,
            out_specs=out_specs,
            check_vma=False,
        )(porosity, *rest)

    return run
```

```python
import functools

import jax
import jax.numpy as jnp
from jax import lax
from jax.experimental import pallas as pl
from jax.experimental.pallas import tpu as pltpu
from jax.sharding import PartitionSpec as P

LOG2E = 1.4426950408889634
PACK_LIMIT = 56 * 1024 * 1024
EMPTY_LIMIT = 24 * 1024 * 1024
GRAIN_LIMIT = 47 * 1024 * 1024
SMALL_LIMIT = 8 * 1024 * 1024
UNROLL = 4
KERNELS = (((3, 2),), ((1,), (0,)))
ORDER = ((0, 0), (1, 0), (0, 1), (1, 1), (2, 0), (0, 2), (2, 1), (1, 2), (2, 2))


def exchanged(block, axis, distance):
    route = [(low, low ^ distance) for low in range(lax.axis_size(axis))]
    return lax.ppermute(block, axis, route)


def bits_of(size):
    assert size & (size - 1) == 0
    return size.bit_length() - 1


def pack_kernel(
    owner_ref, tile_ref, live_ref, block_ref, out_hbm, rows, table, table_vec, coded, sems, *, slots
):
    owners_all = rows.shape[0]
    depth = block_ref.shape[1]

    def clear(owner, carry):
        table[owner, slots] = 0
        return carry

    lax.fori_loop(0, owners_all, clear, 0)

    def place(index, carry):
        owner = owner_ref[index]
        slot = table[owner, slots]
        table[owner, slots] = slot + 1
        table[owner, slot] = tile_ref[index]
        rows[owner, pl.ds(pl.multiple_of(slot * depth, depth), depth), :] = block_ref[index]
        return carry

    lax.fori_loop(0, live_ref[0], place, 0)
    data = pltpu.make_async_copy(rows, out_hbm.at[:, pl.ds(0, rows.shape[1]), :], sems.at[0])
    data.start()
    copy = pltpu.make_async_copy(table, table_vec, sems.at[1])
    copy.start()
    copy.wait()
    first = lax.broadcasted_iota(jnp.int32, (8, 128), 0) == 0
    for owner in range(owners_all):
        row = jnp.broadcast_to(table_vec[owner : owner + 1, :], (8, 128))
        coded[owner] = jnp.where(first, row >> 6, row & 63).astype(jnp.float32).astype(jnp.bfloat16)
    copy = pltpu.make_async_copy(coded, out_hbm.at[:, pl.ds(rows.shape[1], 8), :], sems.at[2])
    copy.start()
    copy.wait()
    data.wait()


def pack_blocks(grain_blocks, owner_dev, tiles, live_counts, device_count, slots):
    _, depth, lanes = grain_blocks.shape
    smem = pl.BlockSpec(memory_space=pltpu.SMEM)
    vmem = pl.BlockSpec(memory_space=pltpu.VMEM)
    return pl.pallas_call(
        functools.partial(pack_kernel, slots=slots),
        out_shape=jax.ShapeDtypeStruct(
            (device_count, slots * depth + 8, lanes), grain_blocks.dtype
        ),
        in_specs=[smem, smem, smem, vmem],
        out_specs=pl.BlockSpec(memory_space=pltpu.HBM),
        scratch_shapes=[
            pltpu.VMEM((device_count, slots * depth, lanes), grain_blocks.dtype),
            pltpu.SMEM((device_count, 128), jnp.int32),
            pltpu.VMEM((device_count, 128), jnp.int32),
            pltpu.VMEM((device_count, 8, lanes), grain_blocks.dtype),
            pltpu.SemaphoreType.DMA((3,)),
        ],
        compiler_params=pltpu.CompilerParams(vmem_limit_bytes=PACK_LIMIT),
        name="pack_blocks",
    )(owner_dev, tiles, live_counts, grain_blocks)


def plan_tiles(gx, piece_bits, nowhere, got_ref, plan, ids_vec, ids, last, sems, slots):
    heads, again, earlier = plan
    nowhere_tile = last.shape[0] - 1
    sources = ids.shape[0]
    forget = pltpu.make_async_copy(nowhere, last.at[pl.ds(0, nowhere.shape[0])], sems.at[0])
    forget.start()
    for source in range(sources):
        coded = got_ref[source, got_ref.shape[1] - 8 :, :].astype(jnp.float32)
        ids_vec[source : source + 1, :] = (coded[0:1, :] * 64.0 + coded[1:2, :]).astype(jnp.int32)
    fetch = pltpu.make_async_copy(ids_vec, ids, sems.at[1])
    fetch.start()
    last[nowhere_tile] = -1
    fetch.wait()
    forget.wait()

    def from_source(source, counts):
        live = ids[source, slots]

        def some(batch, counts):
            count, more = counts
            found = []
            for place in range(UNROLL):
                slot = batch * UNROLL + place
                entry = source * slots + slot
                valid = slot < live
                tile = jnp.where(valid, ids[source, slot], nowhere_tile)
                before = last[tile]
                last[tile] = entry
                found.append((entry, tile, valid, before))
            for entry, tile, valid, before in found:
                earlier[entry] = before
                kernel = 1 - (((tile >> piece_bits) ^ gx) >> 1) & 1
                shift = kernel << 4
                code = entry + (tile << 16)
                heads[kernel, (count >> shift) & 65535] = code
                again[kernel, (more >> shift) & 65535] = code
                one = jnp.where(valid, 1, 0) << shift
                count = count + one
                more = more + jnp.where(before >= 0, one, 0)
            return count, more

        return lax.fori_loop(0, (live + UNROLL - 1) >> bits_of(UNROLL), some, counts)

    count, more = lax.fori_loop(0, sources, from_source, (jnp.int32(0), jnp.int32(0)))

    for kernel in range(2):
        found = (count >> (16 * kernel)) & 65535
        heads[kernel, heads.shape[1] - 1] = found
        again[kernel, heads.shape[1] - 1] = (more >> (16 * kernel)) & 65535

        @pl.when(found > 0)
        def _():
            for extra in range(UNROLL - 1):
                heads[kernel, found + extra] = heads[kernel, found - 1]


def empty_kernel(ext_ref, col_ref, por_hbm, part, por_tiles, por, turned, sems):
    depth, rows, cols = por_hbm.shape
    block_rows = por.shape[2]
    half_rows = block_rows // 2
    col_blocks = cols // 128
    steps = rows // block_rows
    base = -LOG2E * ext_ref[0]
    slope = LOG2E * ext_ref[0]

    def fetch(step, slot):
        start = pl.multiple_of(step * block_rows, block_rows)
        return pltpu.make_async_copy(
            por_hbm.at[:, pl.ds(start, block_rows), :], por.at[slot], sems.at[slot]
        )

    fetch(0, 0).start()

    def one_step(step, carry):
        slot = lax.rem(step, 2)

        @pl.when(step + 1 < steps)
        def _():
            fetch(step + 1, 1 - slot).start()

        fetch(step, slot).wait()

        def one_column(col, carry):
            lanes = pl.ds(pl.multiple_of(col * 128, 128), 128)
            clear = jnp.ones((block_rows, 128), jnp.float32)
            sums = [jnp.zeros((block_rows, 128), jnp.float32) for _ in range(3)]
            for z in range(depth):
                porous = por[slot, z, :, lanes].astype(jnp.float32)
                turned[z * block_rows : (z + 1) * block_rows, :] = porous
                passed = clear * jnp.exp2(base + slope * porous)
                weight = clear - passed
                clear = passed
                for c in range(3):
                    half_logit = (0.5 * col_ref[c, 0]) * porous + 0.5 * col_ref[c, 2]
                    sums[c] = sums[c] + weight * jnp.tanh(half_logit)
            for row in range(block_rows):
                tile = (step * block_rows + row) * col_blocks + col
                por_tiles[tile] = turned[pl.ds(row, depth, stride=block_rows), :].astype(
                    jnp.bfloat16
                )
            alpha = 1.0 - clear
            parts = [0.5 * (alpha + total) for total in sums] + [alpha]
            for c in range(4):
                for half in range(2):
                    part[2 * step + half, col, c * half_rows : (c + 1) * half_rows, :] = parts[c][
                        half * half_rows : (half + 1) * half_rows
                    ]
            return carry

        lax.fori_loop(0, col_blocks, one_column, 0)
        return carry

    lax.fori_loop(0, steps, one_step, 0)


def march_empty(porosity, extinction, color_weights):
    depth, rows, cols = porosity.shape
    block_rows = 16
    smem = pl.BlockSpec(memory_space=pltpu.SMEM)
    vmem = pl.BlockSpec(memory_space=pltpu.VMEM)
    return pl.pallas_call(
        empty_kernel,
        out_shape=[
            jax.ShapeDtypeStruct((rows // 8, cols // 128, 32, 128), jnp.float32),
            jax.ShapeDtypeStruct((rows * cols // 128, depth, 128), porosity.dtype),
        ],
        in_specs=[smem, smem, pl.BlockSpec(memory_space=pl.ANY)],
        out_specs=[vmem, vmem],
        scratch_shapes=[
            pltpu.VMEM((2, depth, block_rows, cols), porosity.dtype),
            pltpu.VMEM((depth * block_rows, 128), jnp.float32),
            pltpu.SemaphoreType.DMA((2,)),
        ],
        compiler_params=pltpu.CompilerParams(vmem_limit_bytes=EMPTY_LIMIT),
        cost_estimate=pl.CostEstimate(
            flops=20 * depth * rows * cols,
            bytes_accessed=4 * depth * rows * cols + 16 * rows * cols,
            transcendentals=4 * depth * rows * cols,
        ),
        name="march_empty",
    )(extinction, color_weights, porosity)


def grain_kernel(dev_ref, ext_ref, col_ref, *refs, kernel, slots, gy_bits):
    chunks = KERNELS[kernel]
    if kernel == 0:
        nowhere, *refs = refs
    else:
        plan, refs = refs[:3], refs[3:]
    por_hbm, part_hbm, got_ref, *refs = refs
    keep_refs, send_refs = refs[: len(chunks)], refs[len(chunks) : 2 * len(chunks)]
    refs = refs[2 * len(chunks) :]
    if kernel == 0:
        plan, refs = refs[:3], refs[3:]
    por_ref, part, sems, *scratch = refs
    own_x = dev_ref[0] & 1
    gx = dev_ref[0] >> gy_bits
    col_bits = bits_of(part.shape[2])
    piece_bits = bits_of(por_ref.shape[1])
    fetches = []
    for piece in range(2):
        chunk = gx ^ (piece + 2 * (1 - kernel))
        for place, (hbm, ref) in enumerate(((part_hbm, part), (por_hbm, por_ref))):
            rows = pl.ds(chunk * ref.shape[1], ref.shape[1])
            fetches.append(
                pltpu.make_async_copy(hbm.at[rows], ref.at[piece], sems.at[2 * piece + place])
            )
    for fetch in fetches:
        fetch.start()
    if kernel == 0:
        plan_tiles(gx, piece_bits, nowhere, got_ref, plan, *scratch, slots)
    heads, again, earlier = plan
    for fetch in fetches:
        fetch.wait()

    def block_of(entry):
        depth = por_ref.shape[2]
        start = pl.multiple_of((entry & (slots - 1)) * depth, depth)
        block = got_ref[entry >> bits_of(slots), pl.ds(start, depth), :]
        return block.astype(jnp.float32)

    base = -LOG2E * ext_ref[0]
    slope = LOG2E * ext_ref[0]
    grain_slope = -LOG2E * ext_ref[1]
    depth_of = lax.broadcasted_iota(jnp.int32, (8, 128), 0)

    def running(value):
        for shift in (1, 2, 4):
            value = value + jnp.where(depth_of >= shift, pltpu.roll(value, shift, 0), 0.0)
        return value

    def march_tiles(work):
        for code, grain in work:
            tile = code >> 16
            piece = ((tile >> piece_bits) ^ gx) & 1
            tile = tile & ((1 << piece_bits) - 1)
            porous = por_ref[piece, tile].astype(jnp.float32)
            exponent = (base + slope * porous) + grain_slope * grain
            front = running(exponent[:8])
            back = running(exponent[8:]) + front[7:8]
            optical = jnp.concatenate([front, back], axis=0)
            weight = jnp.exp2(optical - exponent) - jnp.exp2(optical)
            alpha = 1.0 - jnp.exp2(back[7:8])
            results = []
            for c in range(3):
                half_logit = (
                    (0.5 * col_ref[c, 0]) * porous
                    + (0.5 * col_ref[c, 1]) * grain
                    + 0.5 * col_ref[c, 2]
                )
                shaded = weight * jnp.tanh(half_logit)
                total = jnp.sum(shaded[:8] + shaded[8:], axis=0, keepdims=True)
                results.append(0.5 * (alpha + total))
            results.append(alpha)
            group, row = tile >> (3 + col_bits), (tile >> col_bits) & 7
            col = tile & ((1 << col_bits) - 1)
            for c in range(4):
                part[piece, group, col, pl.ds(c * 8 + row, 1), :] = results[c]

    def some_tiles(batch, carry):
        codes = [heads[kernel, batch * UNROLL + place] for place in range(UNROLL)]
        march_tiles([(code, block_of(code & 65535)) for code in codes])
        return carry

    found = heads[kernel, heads.shape[1] - 1]
    lax.fori_loop(0, (found + UNROLL - 1) >> bits_of(UNROLL), some_tiles, 0)

    def one_again(index, carry):
        code = again[kernel, index]
        entry = code & 65535

        def add_earlier(state):
            at, total = state
            return earlier[at], total + block_of(at)

        _, grain = lax.while_loop(
            lambda state: state[0] >= 0, add_earlier, (earlier[entry], block_of(entry))
        )
        march_tiles([(code, grain)])
        return carry

    lax.fori_loop(0, again[kernel, heads.shape[1] - 1], one_again, 0)

    pairs = part.shape[1] // 2
    for flips, keep_ref, send_ref in zip(chunks, keep_refs, send_refs):
        for place, flip in enumerate(flips):

            def split(pair, carry):
                at = place * pairs + pair
                send_ref[at] = part[flip & 1, 2 * pair + 1 - own_x].astype(jnp.bfloat16)
                keep_ref[at] = part[flip & 1, 2 * pair + own_x]
                return carry

            lax.fori_loop(0, pairs, split, 0)


def march_grain(kernel, plan, got, porous_tiles, part, dev, extinction, color_weights, slots, mesh):
    width_x, width_y = mesh
    chunks = KERNELS[kernel]
    smem = pl.BlockSpec(memory_space=pltpu.SMEM)
    vmem = pl.BlockSpec(memory_space=pltpu.VMEM)
    hbm = pl.BlockSpec(memory_space=pltpu.HBM)
    sources = got.shape[0]
    entries = sources * slots
    tile_count = porous_tiles.shape[0]
    groups = part.shape[0] // width_x
    split = [(len(flips) * groups // 2,) + part.shape[1:] for flips in chunks]
    scratch = [
        pltpu.VMEM((2, tile_count // width_x) + porous_tiles.shape[1:], porous_tiles.dtype),
        pltpu.VMEM((2, groups) + part.shape[1:], part.dtype),
        pltpu.SemaphoreType.DMA((4,)),
    ]
    plan_shapes = []
    if kernel == 0:
        most = -(-(entries + UNROLL + 1) // 128) * 128
        plan_shapes = [
            jax.ShapeDtypeStruct((2, most), jnp.int32),
            jax.ShapeDtypeStruct((2, most), jnp.int32),
            jax.ShapeDtypeStruct((entries + UNROLL,), jnp.int32),
        ]
        scratch += [
            pltpu.VMEM((sources, 128), jnp.int32),
            pltpu.SMEM((sources, 128), jnp.int32),
            pltpu.SMEM((tile_count + 1,), jnp.int32),
            pltpu.SemaphoreType.DMA((2,)),
        ]
        before, before_specs = [jnp.full((tile_count,), -1, jnp.int32)], [hbm]
    else:
        before, before_specs = plan, [smem] * 3
    outs = pl.pallas_call(
        functools.partial(grain_kernel, kernel=kernel, slots=slots, gy_bits=bits_of(width_y)),
        out_shape=[jax.ShapeDtypeStruct(shape, jnp.float32) for shape in split]
        + [jax.ShapeDtypeStruct(shape, jnp.bfloat16) for shape in split]
        + plan_shapes,
        in_specs=[smem] * 3 + before_specs + [hbm] * 2 + [vmem],
        out_specs=[vmem] * (2 * len(chunks)) + [smem] * len(plan_shapes),
        scratch_shapes=scratch,
        compiler_params=pltpu.CompilerParams(vmem_limit_bytes=GRAIN_LIMIT),
        cost_estimate=pl.CostEstimate(flops=1000, bytes_accessed=1000, transcendentals=0),
        name=f"march_grain_{kernel}",
    )(dev, extinction, color_weights, *before, porous_tiles, part, got)
    keeps, sends = outs[: len(chunks)], outs[len(chunks) : 2 * len(chunks)]
    return list(zip(chunks, keeps, sends)), outs[2 * len(chunks) :]


def ordered(mine, theirs, mine_near):
    nearer = [jnp.where(mine_near, a, b) for a, b in zip(mine, theirs)]
    farther = [jnp.where(mine_near, b, a) for a, b in zip(mine, theirs)]
    open_part = 1.0 - nearer[3]
    return [n + open_part * f for n, f in zip(nearer, farther)]


def channels_of(block):
    block = block.astype(jnp.float32)
    rows = block.shape[0] // 4
    return [block[c * rows : (c + 1) * rows] for c in range(4)]


def swap_kernel(dev_ref, rank_ref, mine_ref, got_ref, *out_refs, stage, pieces):
    device = dev_ref[0]
    mine_near = (rank_ref[device] >> stage) & 1 == 0
    low, high = (device >> 1) & 1, (device >> 2) & 1
    piece_groups = got_ref.shape[0] // pieces

    def one_column(col, carry):
        for piece in range(pieces):
            for way, out_ref in enumerate(out_refs):
                for place in range(out_ref.shape[0] // pieces):
                    group = [2 * place + (low ^ way), high ^ way, 0][stage] + piece * piece_groups
                    merged = ordered(
                        channels_of(mine_ref[group, col]),
                        channels_of(got_ref[group, col]),
                        mine_near,
                    )
                    merged = jnp.concatenate(merged, axis=0).astype(out_ref.dtype)
                    out_ref[piece * (out_ref.shape[0] // pieces) + place, col] = merged
        return carry

    lax.fori_loop(0, got_ref.shape[1], one_column, 0)


def swap_rows(mine, got, dev, ranks, stage, pieces):
    smem = pl.BlockSpec(memory_space=pltpu.SMEM)
    vmem = pl.BlockSpec(memory_space=pltpu.VMEM)
    kept = (max(1, got.shape[0] // 2) if stage < 2 else got.shape[0],) + got.shape[1:]
    out_shape = [jax.ShapeDtypeStruct(kept, jnp.float32)]
    if stage < 2:
        out_shape.append(jax.ShapeDtypeStruct(kept, jnp.bfloat16))
    return pl.pallas_call(
        functools.partial(swap_kernel, stage=stage, pieces=pieces),
        out_shape=out_shape,
        in_specs=[smem, smem, vmem, vmem],
        out_specs=[vmem] * len(out_shape),
        compiler_params=pltpu.CompilerParams(vmem_limit_bytes=SMALL_LIMIT),
        cost_estimate=pl.CostEstimate(flops=1000, bytes_accessed=1000, transcendentals=0),
        name=f"swap_rows_{stage}",
    )(dev, ranks, mine, got)


def four_way(device, rank_ref, parts, stride, bit):
    low = (rank_ref[device] >> bit) & 1 == 0
    far_low = (rank_ref[device ^ (2 * stride)] >> bit) & 1 == 0
    high = (rank_ref[device] >> (bit + 1)) & 1 == 0
    return ordered(
        ordered(parts[0], parts[1], low), ordered(parts[2], parts[3], far_low), high
    )


def last_kernel(dev_ref, rank_ref, mine_ref, got_ref, q1, q2, q3, out_ref, *, width_y):
    device = dev_ref[0]
    mine_near = (rank_ref[device] >> 2) & 1 == 0
    col_blocks = mine_ref.shape[1]
    for col in range(col_blocks):
        mine = ordered(channels_of(mine_ref[0, col]), channels_of(got_ref[0, col]), mine_near)
        parts = [mine] + [channels_of(ref[0, col]) for ref in (q1, q2, q3)]
        merged = four_way(device, rank_ref, parts, width_y, bits_of(width_y))
        for c in range(4):
            for row in range(merged[c].shape[0]):
                start = (row * col_blocks + col) * 128
                out_ref[c : c + 1, start : start + 128] = merged[c][row : row + 1]


def last_rows(mine, got, ready, dev, ranks, width_y):
    smem = pl.BlockSpec(memory_space=pltpu.SMEM)
    vmem = pl.BlockSpec(memory_space=pltpu.VMEM)
    return pl.pallas_call(
        functools.partial(last_kernel, width_y=width_y),
        out_shape=jax.ShapeDtypeStruct((4, mine.size // 4), jnp.float32),
        in_specs=[smem, smem] + [vmem] * 5,
        out_specs=vmem,
        compiler_params=pltpu.CompilerParams(vmem_limit_bytes=SMALL_LIMIT),
        name="last_rows",
    )(dev, ranks, mine, got, *ready)


def shards(porosity, grain_blocks, owners, tiles, live_counts, ranks, extinction, color_weights):
    width_x = lax.axis_size("gx")
    width_y = lax.axis_size("gy")
    device_count = width_x * width_y
    block_count = grain_blocks.shape[0]
    slots = max(2, 2 * block_count // device_count)
    dev = lax.axis_index(("gx", "gy")).astype(jnp.int32).reshape(1)
    packed = pack_blocks(grain_blocks, owners[:, 0], tiles, live_counts, device_count, slots)
    got = lax.all_to_all(packed, ("gx", "gy"), split_axis=0, concat_axis=0, tiled=True)
    porosity, _ = lax.optimization_barrier((porosity, packed))
    part, porous_tiles = march_empty(porosity, extinction, color_weights)
    got, part, porous_tiles = lax.optimization_barrier((got, part, porous_tiles))
    work, plan = [], None
    for kernel in range(len(KERNELS)):
        made, planned = march_grain(
            kernel,
            plan,
            got,
            porous_tiles,
            part,
            dev,
            extinction,
            color_weights,
            slots,
            (width_x, width_y),
        )
        plan = plan or planned
        for flips, keep, send in made:
            work.append((flips, keep, exchanged(send, "gy", 1)))
    ready = [None] * (width_x - 1)
    token = work[-1][1]
    for chunk, stage in ORDER:
        flips, mine, got = work[chunk]
        got, token = lax.optimization_barrier((got, token))
        if flips == (0,) and stage == 2:
            return last_rows(mine, got, ready, dev, ranks, width_y)
        mine, *send = swap_rows(mine, got, dev, ranks, stage, len(flips))
        token = mine
        if stage < 2:
            work[chunk] = flips, mine, exchanged(send[0], "gy", 2 << stage)
            continue
        for piece, flip in enumerate(flips):
            ready[flip - 1] = exchanged(mine[piece : piece + 1], "gx", flip)


def march_flat(porous_flat, grain_flat, extinction, color_weights):
    porous = porous_flat.astype(jnp.float32)
    extinct = extinction[0] * (1.0 - porous) + extinction[1] * grain_flat
    optical = jnp.cumsum(extinct, axis=0)
    before = optical - extinct
    weight = jnp.exp(-before) * (1.0 - jnp.exp(-extinct))
    channels = []
    for channel in range(3):
        colour = jax.nn.sigmoid(
            color_weights[channel, 0] * porous
            + color_weights[channel, 1] * grain_flat
            + color_weights[channel, 2]
        )
        channels.append(jnp.sum(weight * colour, axis=0))
    channels.append(1.0 - jnp.exp(-optical[-1]))
    return jnp.stack(channels, axis=0)


def composite(nearer, farther):
    return nearer + (1.0 - nearer[3:4]) * farther


def shards_any(
    porosity, grain_blocks, owners, tiles, live_counts, ranks, extinction, color_weights
):
    width_x = lax.axis_size("gx")
    width_y = lax.axis_size("gy")
    device_count = width_x * width_y
    depth_cells, image_rows, image_cols = porosity.shape
    block_count, _, block_cols = grain_blocks.shape
    slots = max(2, 2 * block_count // device_count)
    tile_count = image_rows * image_cols // block_cols
    pixel_count = image_rows * image_cols
    block_len = pixel_count // device_count
    packed = pack_blocks(grain_blocks, owners[:, 0], tiles, live_counts, device_count, slots)
    got = lax.all_to_all(packed, ("gx", "gy"), split_axis=0, concat_axis=0, tiled=True)
    coded = got[:, slots * depth_cells : slots * depth_cells + 2, : slots + 1].astype(jnp.int32)
    table = coded[:, 0] * 64 + coded[:, 1]
    used = jnp.arange(slots, dtype=jnp.int32)[None, :] < table[:, slots:]
    got_tile = jnp.where(used, table[:, :slots], tile_count)
    got_data = got[:, : slots * depth_cells].reshape(-1, slots, depth_cells, block_cols)
    got_data = jnp.where(used[:, :, None, None], got_data, jnp.bfloat16(0))
    grain_tiles = (
        jnp.zeros((tile_count, depth_cells, block_cols), jnp.float32)
        .at[got_tile.reshape(-1)]
        .add(
            got_data.reshape(device_count * slots, depth_cells, block_cols).astype(jnp.float32),
            mode="drop",
        )
    )
    grain_flat = jnp.transpose(grain_tiles, (1, 0, 2)).reshape(depth_cells, pixel_count)
    porous_flat = porosity.reshape(depth_cells, pixel_count)
    partial_value = march_flat(porous_flat, grain_flat, extinction, color_weights)
    my_rank = ranks[lax.axis_index(("gx", "gy"))]
    bits_y = width_y.bit_length() - 1
    bits_x = width_x.bit_length() - 1
    current = partial_value.reshape(4, width_x, width_y, block_len)
    for axis, dim, bits, first in (("gy", 2, bits_y, 0), ("gx", 1, bits_x, bits_y)):
        for section_bit in range(bits):
            shape = current.shape
            paired = current.reshape(
                shape[:dim] + (shape[dim] // 2, 2) + shape[dim + 1 :]
            )
            own_bit = lax.axis_index(axis) >> section_bit & 1
            kept_half = lax.dynamic_index_in_dim(paired, own_bit, dim + 1, keepdims=False)
            sent_half = lax.dynamic_index_in_dim(paired, 1 - own_bit, dim + 1, keepdims=False)
            partner = exchanged(sent_half, axis, 1 << section_bit)
            nearer_side = my_rank >> first + section_bit & 1 == 0
            current = composite(
                jnp.where(nearer_side, kept_half, partner),
                jnp.where(nearer_side, partner, kept_half),
            )
        if dim == 2:
            current = current.reshape(4, width_x, 1, block_len).reshape(4, width_x, block_len)
    return current.reshape(4, block_len)


def solution(mesh):
    in_specs = (
        P(("gx", "gy"), None, None),
        P(("gx", "gy"), None, None),
        P(("gx", "gy"), None),
        P(("gx", "gy")),
        P(("gx", "gy")),
        P(),
        P(),
        P(),
    )
    out_specs = P(None, ("gx", "gy"))

    def run(porosity, *rest):
        rows = porosity.shape[1] // (mesh.shape["gx"] * mesh.shape["gy"])
        fits = mesh.shape["gx"] == 4 and mesh.shape["gy"] == 8 and rows == 8
        return jax.shard_map(
            shards if fits else shards_any,
            mesh=mesh,
            in_specs=in_specs,
            out_specs=out_specs,
            check_vma=False,
        )(porosity, *rest)

    return run
```

```python
import functools

import jax
import jax.numpy as jnp
from jax import lax
from jax.experimental import pallas as pl
from jax.experimental.pallas import tpu as pltpu
from jax.sharding import PartitionSpec as P

LOG2E = 1.4426950408889634
PACK_LIMIT = 56 * 1024 * 1024
EMPTY_LIMIT = 24 * 1024 * 1024
GRAIN_LIMIT = 47 * 1024 * 1024
SMALL_LIMIT = 8 * 1024 * 1024
UNROLL = 4
KERNELS = (((3, 2),), ((1,), (0,)))
ORDER = ((0, 0), (1, 0), (0, 1), (1, 1), (2, 0), (1, 2), (0, 2), (2, 1), (2, 2))


def exchanged(block, axis, distance):
    route = [(low, low ^ distance) for low in range(lax.axis_size(axis))]
    return lax.ppermute(block, axis, route)


def bits_of(size):
    assert size & (size - 1) == 0
    return size.bit_length() - 1


def pack_kernel(
    owner_ref, tile_ref, live_ref, block_ref, out_hbm, rows, table, table_vec, coded, sems, *, slots
):
    owners_all = rows.shape[0]
    depth = block_ref.shape[1]

    def clear(owner, carry):
        table[owner, slots] = 0
        return carry

    lax.fori_loop(0, owners_all, clear, 0)

    def place(index, carry):
        owner = owner_ref[index]
        slot = table[owner, slots]
        table[owner, slots] = slot + 1
        table[owner, slot] = tile_ref[index]
        rows[owner, pl.ds(pl.multiple_of(slot * depth, depth), depth), :] = block_ref[index]
        return carry

    lax.fori_loop(0, live_ref[0], place, 0)
    data = pltpu.make_async_copy(rows, out_hbm.at[:, pl.ds(0, rows.shape[1]), :], sems.at[0])
    data.start()
    copy = pltpu.make_async_copy(table, table_vec, sems.at[1])
    copy.start()
    copy.wait()
    first = lax.broadcasted_iota(jnp.int32, (8, 128), 0) == 0
    for owner in range(owners_all):
        row = jnp.broadcast_to(table_vec[owner : owner + 1, :], (8, 128))
        coded[owner] = jnp.where(first, row >> 6, row & 63).astype(jnp.float32).astype(jnp.bfloat16)
    copy = pltpu.make_async_copy(coded, out_hbm.at[:, pl.ds(rows.shape[1], 8), :], sems.at[2])
    copy.start()
    copy.wait()
    data.wait()


def pack_blocks(grain_blocks, owner_dev, tiles, live_counts, device_count, slots):
    _, depth, lanes = grain_blocks.shape
    smem = pl.BlockSpec(memory_space=pltpu.SMEM)
    vmem = pl.BlockSpec(memory_space=pltpu.VMEM)
    return pl.pallas_call(
        functools.partial(pack_kernel, slots=slots),
        out_shape=jax.ShapeDtypeStruct(
            (device_count, slots * depth + 8, lanes), grain_blocks.dtype
        ),
        in_specs=[smem, smem, smem, vmem],
        out_specs=pl.BlockSpec(memory_space=pltpu.HBM),
        scratch_shapes=[
            pltpu.VMEM((device_count, slots * depth, lanes), grain_blocks.dtype),
            pltpu.SMEM((device_count, 128), jnp.int32),
            pltpu.VMEM((device_count, 128), jnp.int32),
            pltpu.VMEM((device_count, 8, lanes), grain_blocks.dtype),
            pltpu.SemaphoreType.DMA((3,)),
        ],
        compiler_params=pltpu.CompilerParams(vmem_limit_bytes=PACK_LIMIT),
        name="pack_blocks",
    )(owner_dev, tiles, live_counts, grain_blocks)


def plan_tiles(gx, piece_bits, nowhere, got_ref, plan, ids_vec, ids, last, sems, slots):
    heads, again, earlier = plan
    nowhere_tile = last.shape[0] - 1
    sources = ids.shape[0]
    forget = pltpu.make_async_copy(nowhere, last.at[pl.ds(0, nowhere.shape[0])], sems.at[0])
    forget.start()
    for source in range(sources):
        coded = got_ref[source, got_ref.shape[1] - 8 :, :].astype(jnp.float32)
        ids_vec[source : source + 1, :] = (coded[0:1, :] * 64.0 + coded[1:2, :]).astype(jnp.int32)
    fetch = pltpu.make_async_copy(ids_vec, ids, sems.at[1])
    fetch.start()
    last[nowhere_tile] = -1
    fetch.wait()
    forget.wait()

    def from_source(source, counts):
        live = ids[source, slots]

        def some(batch, counts):
            count, more = counts
            found = []
            for place in range(UNROLL):
                slot = batch * UNROLL + place
                entry = source * slots + slot
                valid = slot < live
                tile = jnp.where(valid, ids[source, slot], nowhere_tile)
                before = last[tile]
                last[tile] = entry
                found.append((entry, tile, valid, before))
            for entry, tile, valid, before in found:
                earlier[entry] = before
                kernel = 1 - (((tile >> piece_bits) ^ gx) >> 1) & 1
                shift = kernel << 4
                code = entry + (tile << 16)
                heads[kernel, (count >> shift) & 65535] = code
                again[kernel, (more >> shift) & 65535] = code
                one = jnp.where(valid, 1, 0) << shift
                count = count + one
                more = more + jnp.where(before >= 0, one, 0)
            return count, more

        return lax.fori_loop(0, (live + UNROLL - 1) >> bits_of(UNROLL), some, counts)

    count, more = lax.fori_loop(0, sources, from_source, (jnp.int32(0), jnp.int32(0)))

    for kernel in range(2):
        found = (count >> (16 * kernel)) & 65535
        heads[kernel, heads.shape[1] - 1] = found
        again[kernel, heads.shape[1] - 1] = (more >> (16 * kernel)) & 65535

        @pl.when(found > 0)
        def _():
            for extra in range(UNROLL - 1):
                heads[kernel, found + extra] = heads[kernel, found - 1]


def empty_kernel(ext_ref, col_ref, por_hbm, part, por_tiles, por, turned, sems):
    depth, rows, cols = por_hbm.shape
    block_rows = por.shape[2]
    half_rows = block_rows // 2
    col_blocks = cols // 128
    steps = rows // block_rows
    base = -LOG2E * ext_ref[0]
    slope = LOG2E * ext_ref[0]

    def fetch(step, slot):
        start = pl.multiple_of(step * block_rows, block_rows)
        return pltpu.make_async_copy(
            por_hbm.at[:, pl.ds(start, block_rows), :], por.at[slot], sems.at[slot]
        )

    fetch(0, 0).start()

    def one_step(step, carry):
        slot = lax.rem(step, 2)

        @pl.when(step + 1 < steps)
        def _():
            fetch(step + 1, 1 - slot).start()

        fetch(step, slot).wait()

        def one_column(col, carry):
            lanes = pl.ds(pl.multiple_of(col * 128, 128), 128)
            clear = jnp.ones((block_rows, 128), jnp.float32)
            sums = [jnp.zeros((block_rows, 128), jnp.float32) for _ in range(3)]
            for z in range(depth):
                porous = por[slot, z, :, lanes].astype(jnp.float32)
                turned[z * block_rows : (z + 1) * block_rows, :] = porous
                passed = clear * jnp.exp2(base + slope * porous)
                weight = clear - passed
                clear = passed
                for c in range(3):
                    half_logit = (0.5 * col_ref[c, 0]) * porous + 0.5 * col_ref[c, 2]
                    sums[c] = sums[c] + weight * jnp.tanh(half_logit)
            for row in range(block_rows):
                tile = (step * block_rows + row) * col_blocks + col
                por_tiles[tile] = turned[pl.ds(row, depth, stride=block_rows), :].astype(
                    jnp.bfloat16
                )
            alpha = 1.0 - clear
            parts = [0.5 * (alpha + total) for total in sums] + [alpha]
            for c in range(4):
                for half in range(2):
                    part[2 * step + half, col, c * half_rows : (c + 1) * half_rows, :] = parts[c][
                        half * half_rows : (half + 1) * half_rows
                    ]
            return carry

        lax.fori_loop(0, col_blocks, one_column, 0)
        return carry

    lax.fori_loop(0, steps, one_step, 0)


def march_empty(porosity, extinction, color_weights):
    depth, rows, cols = porosity.shape
    block_rows = 16
    smem = pl.BlockSpec(memory_space=pltpu.SMEM)
    vmem = pl.BlockSpec(memory_space=pltpu.VMEM)
    return pl.pallas_call(
        empty_kernel,
        out_shape=[
            jax.ShapeDtypeStruct((rows // 8, cols // 128, 32, 128), jnp.float32),
            jax.ShapeDtypeStruct((rows * cols // 128, depth, 128), porosity.dtype),
        ],
        in_specs=[smem, smem, pl.BlockSpec(memory_space=pl.ANY)],
        out_specs=[vmem, vmem],
        scratch_shapes=[
            pltpu.VMEM((2, depth, block_rows, cols), porosity.dtype),
            pltpu.VMEM(((depth + 1) * block_rows, 128), jnp.float32),
            pltpu.SemaphoreType.DMA((2,)),
        ],
        compiler_params=pltpu.CompilerParams(vmem_limit_bytes=EMPTY_LIMIT),
        cost_estimate=pl.CostEstimate(
            flops=20 * depth * rows * cols,
            bytes_accessed=4 * depth * rows * cols + 16 * rows * cols,
            transcendentals=4 * depth * rows * cols,
        ),
        name="march_empty",
    )(extinction, color_weights, porosity)


def grain_kernel(dev_ref, ext_ref, col_ref, *refs, kernel, slots, gy_bits):
    chunks = KERNELS[kernel]
    if kernel == 0:
        nowhere, *refs = refs
    else:
        plan, refs = refs[:3], refs[3:]
    por_hbm, part_hbm, got_ref, *refs = refs
    keep_refs, send_refs = refs[: len(chunks)], refs[len(chunks) : 2 * len(chunks)]
    refs = refs[2 * len(chunks) :]
    if kernel == 0:
        plan, refs = refs[:3], refs[3:]
    por_ref, part, sems, *scratch = refs
    own_x = dev_ref[0] & 1
    gx = dev_ref[0] >> gy_bits
    col_bits = bits_of(part.shape[2])
    piece_bits = bits_of(por_ref.shape[1])
    fetches = []
    for piece in range(2):
        chunk = gx ^ (piece + 2 * (1 - kernel))
        for place, (hbm, ref) in enumerate(((part_hbm, part), (por_hbm, por_ref))):
            rows = pl.ds(chunk * ref.shape[1], ref.shape[1])
            fetches.append(
                pltpu.make_async_copy(hbm.at[rows], ref.at[piece], sems.at[2 * piece + place])
            )
    for fetch in fetches:
        fetch.start()
    if kernel == 0:
        plan_tiles(gx, piece_bits, nowhere, got_ref, plan, *scratch, slots)
    heads, again, earlier = plan
    for fetch in fetches:
        fetch.wait()

    def block_of(entry):
        depth = por_ref.shape[2]
        start = pl.multiple_of((entry & (slots - 1)) * depth, depth)
        block = got_ref[entry >> bits_of(slots), pl.ds(start, depth), :]
        return block.astype(jnp.float32)

    base = -LOG2E * ext_ref[0]
    slope = LOG2E * ext_ref[0]
    grain_slope = -LOG2E * ext_ref[1]
    depth_of = lax.broadcasted_iota(jnp.int32, (8, 128), 0)

    def running(value):
        for shift in (1, 2, 4):
            value = value + jnp.where(depth_of >= shift, pltpu.roll(value, shift, 0), 0.0)
        return value

    def march_tiles(work):
        for code, grain in work:
            tile = code >> 16
            piece = ((tile >> piece_bits) ^ gx) & 1
            tile = tile & ((1 << piece_bits) - 1)
            porous = por_ref[piece, tile].astype(jnp.float32)
            exponent = (base + slope * porous) + grain_slope * grain
            front = running(exponent[:8])
            back = running(exponent[8:]) + front[7:8]
            optical = jnp.concatenate([front, back], axis=0)
            weight = jnp.exp2(optical - exponent) - jnp.exp2(optical)
            alpha = 1.0 - jnp.exp2(back[7:8])
            results = []
            for c in range(3):
                half_logit = (
                    (0.5 * col_ref[c, 0]) * porous
                    + (0.5 * col_ref[c, 1]) * grain
                    + 0.5 * col_ref[c, 2]
                )
                shaded = weight * jnp.tanh(half_logit)
                total = jnp.sum(shaded[:8] + shaded[8:], axis=0, keepdims=True)
                results.append(0.5 * (alpha + total))
            results.append(alpha)
            group, row = tile >> (3 + col_bits), (tile >> col_bits) & 7
            col = tile & ((1 << col_bits) - 1)
            for c in range(4):
                part[piece, group, col, pl.ds(c * 8 + row, 1), :] = results[c]

    def some_tiles(batch, carry):
        codes = [heads[kernel, batch * UNROLL + place] for place in range(UNROLL)]
        march_tiles([(code, block_of(code & 65535)) for code in codes])
        return carry

    found = heads[kernel, heads.shape[1] - 1]
    lax.fori_loop(0, (found + UNROLL - 1) >> bits_of(UNROLL), some_tiles, 0)

    def one_again(index, carry):
        code = again[kernel, index]
        entry = code & 65535

        def add_earlier(state):
            at, total = state
            return earlier[at], total + block_of(at)

        _, grain = lax.while_loop(
            lambda state: state[0] >= 0, add_earlier, (earlier[entry], block_of(entry))
        )
        march_tiles([(code, grain)])
        return carry

    lax.fori_loop(0, again[kernel, heads.shape[1] - 1], one_again, 0)

    pairs = part.shape[1] // 2
    for flips, keep_ref, send_ref in zip(chunks, keep_refs, send_refs):
        for place, flip in enumerate(flips):

            def split(pair, carry):
                at = place * pairs + pair
                send_ref[at] = part[flip & 1, 2 * pair + 1 - own_x].astype(jnp.bfloat16)
                keep_ref[at] = part[flip & 1, 2 * pair + own_x]
                return carry

            lax.fori_loop(0, pairs, split, 0)


def march_grain(kernel, plan, got, porous_tiles, part, dev, extinction, color_weights, slots, mesh):
    width_x, width_y = mesh
    chunks = KERNELS[kernel]
    smem = pl.BlockSpec(memory_space=pltpu.SMEM)
    vmem = pl.BlockSpec(memory_space=pltpu.VMEM)
    hbm = pl.BlockSpec(memory_space=pltpu.HBM)
    sources = got.shape[0]
    entries = sources * slots
    tile_count = porous_tiles.shape[0]
    groups = part.shape[0] // width_x
    split = [(len(flips) * groups // 2,) + part.shape[1:] for flips in chunks]
    scratch = [
        pltpu.VMEM((2, tile_count // width_x) + porous_tiles.shape[1:], porous_tiles.dtype),
        pltpu.VMEM((2, groups) + part.shape[1:], part.dtype),
        pltpu.SemaphoreType.DMA((4,)),
    ]
    plan_shapes = []
    if kernel == 0:
        most = -(-(entries + UNROLL + 1) // 128) * 128
        plan_shapes = [
            jax.ShapeDtypeStruct((2, most), jnp.int32),
            jax.ShapeDtypeStruct((2, most), jnp.int32),
            jax.ShapeDtypeStruct((entries + UNROLL,), jnp.int32),
        ]
        scratch += [
            pltpu.VMEM((sources, 128), jnp.int32),
            pltpu.SMEM((sources, 128), jnp.int32),
            pltpu.SMEM((tile_count + 1,), jnp.int32),
            pltpu.SemaphoreType.DMA((2,)),
        ]
        before, before_specs = [jnp.full((tile_count,), -1, jnp.int32)], [hbm]
    else:
        before, before_specs = plan, [smem] * 3
    outs = pl.pallas_call(
        functools.partial(grain_kernel, kernel=kernel, slots=slots, gy_bits=bits_of(width_y)),
        out_shape=[jax.ShapeDtypeStruct(shape, jnp.float32) for shape in split]
        + [jax.ShapeDtypeStruct(shape, jnp.bfloat16) for shape in split]
        + plan_shapes,
        in_specs=[smem] * 3 + before_specs + [hbm] * 2 + [vmem],
        out_specs=[vmem] * (2 * len(chunks)) + [smem] * len(plan_shapes),
        scratch_shapes=scratch,
        compiler_params=pltpu.CompilerParams(vmem_limit_bytes=GRAIN_LIMIT),
        cost_estimate=pl.CostEstimate(flops=1000, bytes_accessed=1000, transcendentals=0),
        name=f"march_grain_{kernel}",
    )(dev, extinction, color_weights, *before, porous_tiles, part, got)
    keeps, sends = outs[: len(chunks)], outs[len(chunks) : 2 * len(chunks)]
    return list(zip(chunks, keeps, sends)), outs[2 * len(chunks) :]


def ordered(mine, theirs, mine_near):
    nearer = [jnp.where(mine_near, a, b) for a, b in zip(mine, theirs)]
    farther = [jnp.where(mine_near, b, a) for a, b in zip(mine, theirs)]
    open_part = 1.0 - nearer[3]
    return [n + open_part * f for n, f in zip(nearer, farther)]


def channels_of(block):
    block = block.astype(jnp.float32)
    rows = block.shape[0] // 4
    return [block[c * rows : (c + 1) * rows] for c in range(4)]


def swap_kernel(dev_ref, rank_ref, mine_ref, got_ref, *out_refs, stage, pieces):
    device = dev_ref[0]
    mine_near = (rank_ref[device] >> stage) & 1 == 0
    low, high = (device >> 1) & 1, (device >> 2) & 1
    piece_groups = got_ref.shape[0] // pieces

    def one_column(col, carry):
        for piece in range(pieces):
            for way, out_ref in enumerate(out_refs):
                for place in range(out_ref.shape[0] // pieces):
                    group = [2 * place + (low ^ way), high ^ way, 0][stage] + piece * piece_groups
                    merged = ordered(
                        channels_of(mine_ref[group, col]),
                        channels_of(got_ref[group, col]),
                        mine_near,
                    )
                    merged = jnp.concatenate(merged, axis=0).astype(out_ref.dtype)
                    out_ref[piece * (out_ref.shape[0] // pieces) + place, col] = merged
        return carry

    lax.fori_loop(0, got_ref.shape[1], one_column, 0)


def swap_rows(mine, got, dev, ranks, stage, pieces):
    smem = pl.BlockSpec(memory_space=pltpu.SMEM)
    vmem = pl.BlockSpec(memory_space=pltpu.VMEM)
    kept = (max(1, got.shape[0] // 2) if stage < 2 else got.shape[0],) + got.shape[1:]
    out_shape = [jax.ShapeDtypeStruct(kept, jnp.float32)]
    if stage < 2:
        out_shape.append(jax.ShapeDtypeStruct(kept, jnp.bfloat16))
    return pl.pallas_call(
        functools.partial(swap_kernel, stage=stage, pieces=pieces),
        out_shape=out_shape,
        in_specs=[smem, smem, vmem, vmem],
        out_specs=[vmem] * len(out_shape),
        compiler_params=pltpu.CompilerParams(vmem_limit_bytes=SMALL_LIMIT),
        cost_estimate=pl.CostEstimate(flops=1000, bytes_accessed=1000, transcendentals=0),
        name=f"swap_rows_{stage}",
    )(dev, ranks, mine, got)


def four_way(device, rank_ref, parts, stride, bit):
    low = (rank_ref[device] >> bit) & 1 == 0
    far_low = (rank_ref[device ^ (2 * stride)] >> bit) & 1 == 0
    high = (rank_ref[device] >> (bit + 1)) & 1 == 0
    return ordered(
        ordered(parts[0], parts[1], low), ordered(parts[2], parts[3], far_low), high
    )


def last_kernel(dev_ref, rank_ref, mine_ref, got_ref, q1, q2, q3, out_ref, *, width_y):
    device = dev_ref[0]
    mine_near = (rank_ref[device] >> 2) & 1 == 0
    col_blocks = mine_ref.shape[1]
    for col in range(col_blocks):
        mine = ordered(channels_of(mine_ref[0, col]), channels_of(got_ref[0, col]), mine_near)
        parts = [mine] + [channels_of(ref[0, col]) for ref in (q1, q2, q3)]
        merged = four_way(device, rank_ref, parts, width_y, bits_of(width_y))
        for c in range(4):
            for row in range(merged[c].shape[0]):
                start = (row * col_blocks + col) * 128
                out_ref[c : c + 1, start : start + 128] = merged[c][row : row + 1]


def last_rows(mine, got, ready, dev, ranks, width_y):
    smem = pl.BlockSpec(memory_space=pltpu.SMEM)
    vmem = pl.BlockSpec(memory_space=pltpu.VMEM)
    return pl.pallas_call(
        functools.partial(last_kernel, width_y=width_y),
        out_shape=jax.ShapeDtypeStruct((4, mine.size // 4), jnp.float32),
        in_specs=[smem, smem] + [vmem] * 5,
        out_specs=vmem,
        compiler_params=pltpu.CompilerParams(vmem_limit_bytes=SMALL_LIMIT),
        name="last_rows",
    )(dev, ranks, mine, got, *ready)


def shards(porosity, grain_blocks, owners, tiles, live_counts, ranks, extinction, color_weights):
    width_x = lax.axis_size("gx")
    width_y = lax.axis_size("gy")
    device_count = width_x * width_y
    block_count = grain_blocks.shape[0]
    slots = max(2, 2 * block_count // device_count)
    dev = lax.axis_index(("gx", "gy")).astype(jnp.int32).reshape(1)
    packed = pack_blocks(grain_blocks, owners[:, 0], tiles, live_counts, device_count, slots)
    got = lax.all_to_all(packed, ("gx", "gy"), split_axis=0, concat_axis=0, tiled=True)
    porosity, _ = lax.optimization_barrier((porosity, packed))
    part, porous_tiles = march_empty(porosity, extinction, color_weights)
    got, part, porous_tiles = lax.optimization_barrier((got, part, porous_tiles))
    work, plan = [], None
    for kernel in range(len(KERNELS)):
        made, planned = march_grain(
            kernel,
            plan,
            got,
            porous_tiles,
            part,
            dev,
            extinction,
            color_weights,
            slots,
            (width_x, width_y),
        )
        plan = plan or planned
        for flips, keep, send in made:
            work.append((flips, keep, exchanged(send, "gy", 1)))
    ready = [None] * (width_x - 1)
    token = work[-1][1]
    for chunk, stage in ORDER:
        flips, mine, got = work[chunk]
        got, token = lax.optimization_barrier((got, token))
        if flips == (0,) and stage == 2:
            return last_rows(mine, got, ready, dev, ranks, width_y)
        mine, *send = swap_rows(mine, got, dev, ranks, stage, len(flips))
        token = mine
        if stage < 2:
            work[chunk] = flips, mine, exchanged(send[0], "gy", 2 << stage)
            continue
        for piece, flip in enumerate(flips):
            ready[flip - 1] = exchanged(mine[piece : piece + 1], "gx", flip)


def march_flat(porous_flat, grain_flat, extinction, color_weights):
    porous = porous_flat.astype(jnp.float32)
    extinct = extinction[0] * (1.0 - porous) + extinction[1] * grain_flat
    optical = jnp.cumsum(extinct, axis=0)
    before = optical - extinct
    weight = jnp.exp(-before) * (1.0 - jnp.exp(-extinct))
    channels = []
    for channel in range(3):
        colour = jax.nn.sigmoid(
            color_weights[channel, 0] * porous
            + color_weights[channel, 1] * grain_flat
            + color_weights[channel, 2]
        )
        channels.append(jnp.sum(weight * colour, axis=0))
    channels.append(1.0 - jnp.exp(-optical[-1]))
    return jnp.stack(channels, axis=0)


def composite(nearer, farther):
    return nearer + (1.0 - nearer[3:4]) * farther


def shards_any(
    porosity, grain_blocks, owners, tiles, live_counts, ranks, extinction, color_weights
):
    width_x = lax.axis_size("gx")
    width_y = lax.axis_size("gy")
    device_count = width_x * width_y
    depth_cells, image_rows, image_cols = porosity.shape
    block_count, _, block_cols = grain_blocks.shape
    slots = max(2, 2 * block_count // device_count)
    tile_count = image_rows * image_cols // block_cols
    pixel_count = image_rows * image_cols
    block_len = pixel_count // device_count
    packed = pack_blocks(grain_blocks, owners[:, 0], tiles, live_counts, device_count, slots)
    got = lax.all_to_all(packed, ("gx", "gy"), split_axis=0, concat_axis=0, tiled=True)
    coded = got[:, slots * depth_cells : slots * depth_cells + 2, : slots + 1].astype(jnp.int32)
    table = coded[:, 0] * 64 + coded[:, 1]
    used = jnp.arange(slots, dtype=jnp.int32)[None, :] < table[:, slots:]
    got_tile = jnp.where(used, table[:, :slots], tile_count)
    got_data = got[:, : slots * depth_cells].reshape(-1, slots, depth_cells, block_cols)
    got_data = jnp.where(used[:, :, None, None], got_data, jnp.bfloat16(0))
    grain_tiles = (
        jnp.zeros((tile_count, depth_cells, block_cols), jnp.float32)
        .at[got_tile.reshape(-1)]
        .add(
            got_data.reshape(device_count * slots, depth_cells, block_cols).astype(jnp.float32),
            mode="drop",
        )
    )
    grain_flat = jnp.transpose(grain_tiles, (1, 0, 2)).reshape(depth_cells, pixel_count)
    porous_flat = porosity.reshape(depth_cells, pixel_count)
    partial_value = march_flat(porous_flat, grain_flat, extinction, color_weights)
    my_rank = ranks[lax.axis_index(("gx", "gy"))]
    bits_y = width_y.bit_length() - 1
    bits_x = width_x.bit_length() - 1
    current = partial_value.reshape(4, width_x, width_y, block_len)
    for axis, dim, bits, first in (("gy", 2, bits_y, 0), ("gx", 1, bits_x, bits_y)):
        for section_bit in range(bits):
            shape = current.shape
            paired = current.reshape(
                shape[:dim] + (shape[dim] // 2, 2) + shape[dim + 1 :]
            )
            own_bit = lax.axis_index(axis) >> section_bit & 1
            kept_half = lax.dynamic_index_in_dim(paired, own_bit, dim + 1, keepdims=False)
            sent_half = lax.dynamic_index_in_dim(paired, 1 - own_bit, dim + 1, keepdims=False)
            partner = exchanged(sent_half, axis, 1 << section_bit)
            nearer_side = my_rank >> first + section_bit & 1 == 0
            current = composite(
                jnp.where(nearer_side, kept_half, partner),
                jnp.where(nearer_side, partner, kept_half),
            )
        if dim == 2:
            current = current.reshape(4, width_x, 1, block_len).reshape(4, width_x, block_len)
    return current.reshape(4, block_len)


def solution(mesh):
    in_specs = (
        P(("gx", "gy"), None, None),
        P(("gx", "gy"), None, None),
        P(("gx", "gy"), None),
        P(("gx", "gy")),
        P(("gx", "gy")),
        P(),
        P(),
        P(),
    )
    out_specs = P(None, ("gx", "gy"))

    def run(porosity, *rest):
        rows = porosity.shape[1] // (mesh.shape["gx"] * mesh.shape["gy"])
        fits = mesh.shape["gx"] == 4 and mesh.shape["gy"] == 8 and rows == 8
        return jax.shard_map(
            shards if fits else shards_any,
            mesh=mesh,
            in_specs=in_specs,
            out_specs=out_specs,
            check_vma=False,
        )(porosity, *rest)

    return run
```
